32 devices in a mesh: groups: 2 (over y), sess: 4 (over z), inner: 2 (over x), rep: 2 (over core).
Axes of the slice: x: 2, y: 2, z: 4, core: 2. Of those that a mesh axis runs over, the one named last changes fastest.
Arguments:
- thinker_rows: bfloat16 [4096, 3584], P(('groups', 'sess', 'rep'), 'inner'), parts along dimension 0, may hold values from -6 to 6
- row_session: int32 [4096, 1], P(('groups', 'sess', 'rep')), parts along dimension 0, may hold values from 0 to 31; in each aligned block of 256 rows (0 to 255, 256 to 511, ...) at most 12 rows name the same one
- speaker_of: int32 [64], P('groups'), parts along dimension 0, may hold values from 0 to 7
- prompt_slot: int32 [16], P('groups'), parts along dimension 0, may hold values from 0 to 7, each once
- prompt_cache: bfloat16 [16, 1024, 1024], P(('groups', 'sess'), ('inner', 'rep')), parts along dimension 0, may hold values from -64 to 64
- proj_weight: bfloat16 [3584, 896], P('inner'), may hold values from -0.09375 to 0.09375
- attn_gain: bfloat16 [896], replicated, may hold values from 0.5 to 1.5
- q_weight: bfloat16 [896, 1536], replicated, may hold values from -0.1875 to 0.1875
- k_weight: bfloat16 [896, 512], replicated, may hold values from -0.625 to 0.625
- v_weight: bfloat16 [896, 512], replicated, may hold values from -0.1875 to 0.1875
- o_weight: bfloat16 [1536, 896], replicated, may hold values from -0.15625 to 0.15625
Outputs:
- voice_states: bfloat16 [64, 96, 896], P(('groups', 'sess', 'inner', 'rep')), parts along dimension 0
The draws below stay inside these ranges and needn't reach their ends.
There are 2 independent parts, one for each index of `groups`. The reference program is written for one: setup_inputs(seed, part) draws one part's arguments, and reference() takes and returns one part's arrays. A program takes and returns all parts, laid end to end along the dimension named above; an argument that names none is the same for every part. Nothing has to cross between parts.
Inputs may be any that keep to these rules, and one draw needn't show every extreme that they name: `row_session`: column 0 names the session of the row. Within each block of 256 rows (rows b * 256 to (b + 1) * 256 - 1, the rows of one index of sess+rep) no session is named by more than 12 rows, a bound that some block reaches; every session is named by some row. `prompt_slot`: each slot holds exactly one speaker's prompt.
All inputs are finite; a program needn't handle non-finite values.
Results may differ from the reference program's by a relative error of at most 0.0071.
Values may be sent and summed in bfloat16 or wider, within the bound.
No kernel may reach another device: no remote copies, remote signals or barrier semaphores. Data moves between devices by JAX's collectives and lax.ppermute only.
A program may use at most 128 MiB of HBM per device.

```python
import math
import jax
import jax.numpy as jnp
import numpy as np
from jax import lax

D = 896
H = 12
KVH = 4
HD = 128
THINK = 3584
PROMPT = 1024
SESS_DEV = 2
SLOTS = 96
MOST = 12
SESSIONS = 32
ROWS_SRC = 256
ROWS = 2048
SPEAKERS = 8


def draw_prompt_cache(key, part):
    channel_total = 2 * KVH * HD
    base = jnp.clip(jax.random.normal(key, (SPEAKERS, PROMPT, channel_total), jnp.float32), -6.0, 6.0)
    return base.astype(jnp.bfloat16)


def place_ends(array, key, low, high):
    longest = array.shape.index(max(array.shape))
    spots = []
    for shift in (0, 1):
        where = [jax.random.randint(jax.random.fold_in(key, axis), (), 0, length) for axis, length in enumerate(array.shape)]
        where[longest] = (where[longest] + shift) % array.shape[longest]
        spots.append(tuple(where))
    return array.at[spots[0]].set(low).at[spots[1]].set(high)


def block_levels(stream_key, extent, shards, smallest, top_value):
    def one(position, parts):
        heights = jax.random.uniform(jax.random.fold_in(jax.random.fold_in(stream_key, 6), position), (parts,), jnp.float32, smallest / len(shards), top_value / len(shards))
        return jnp.repeat(jnp.exp(heights), extent[position] // parts).reshape((-1,) + (1,) * (len(extent) - position - 1))

    loudness = one(*shards[0])
    for cut in shards[1:]:
        loudness = loudness * one(*cut)
    return loudness


def rank_table(amount, lean):
    portions = [(1 << 20) // math.isqrt(grade ** lean) + 1 for grade in range(1, amount + 1)]
    width = 1 + sum(portions) // (1 << 30)
    return np.cumsum(np.array([max(1, weight // width) for weight in portions]))


def ranked(key, extent, number_of, lean):
    grid = rank_table(number_of, lean)
    pick = jax.random.randint(jax.random.fold_in(key, 1), extent, 0, int(grid[number_of - 1]))
    rank = jnp.searchsorted(jnp.asarray(grid, jnp.int32), pick, side="right")
    return jax.random.permutation(jax.random.fold_in(key, 2), number_of)[rank].astype(jnp.int32)


def shared_out(key, own, number, rows, number_of, top, most, lean):
    sequence = jax.random.permutation(key, number_of)
    crowded, usual = portions_of(number_of, rows * top, most, lean, True), portions_of(number_of, rows * top, most, lean, False)
    places = jnp.arange(number_of)

    def named(tallies, turn):
        used = int((tallies > 0).sum())
        fixed = max(1, used // 4)
        passed = fixed + (places - fixed + turn * (used - fixed)) % max(1, number_of - fixed)
        return jnp.zeros((number_of,), jnp.int32).at[sequence[jnp.where(places < fixed, places, passed)]].set(jnp.asarray(tallies, jnp.int32))

    tallies = jnp.where(number % 4 == 0, named(crowded, number // 4), named(usual, number - number // 4 - 1))
    mixed = jax.random.permutation(jax.random.fold_in(own, 3), number_of)
    source_of, receiver = mixed[0:number_of // 2 * 2:2], mixed[1:number_of // 2 * 2:2]
    room = jnp.minimum(tallies[source_of] - 1, most - tallies[receiver]) // 2
    room = jnp.where((source_of == sequence[0]) | (receiver == sequence[0]) | (tallies[receiver] == 0), 0, jnp.maximum(room, 0))
    passed = jax.random.randint(jax.random.fold_in(own, 4), (number_of // 2,), 0, 1 << 20) % (room + 1)
    tallies = tallies.at[source_of].add(-passed).at[receiver].add(passed)
    items = jnp.searchsorted(jnp.cumsum(tallies), jnp.arange(rows * top), side="right").astype(jnp.int32)
    table = items.reshape(top, rows).T
    table = table[jax.random.permutation(jax.random.fold_in(own, 1), rows)]
    turn = jax.random.randint(jax.random.fold_in(own, 2), (rows, 1), 0, top)
    return jnp.take_along_axis(table, (jnp.arange(top)[None, :] + turn) % top, axis=1)


def portions_of(amount, total, most, lean, full):
    portions = [(1 << 20) // math.isqrt(standing ** lean) + 1 for standing in range(1, amount + 1)]
    largest = most if full else min(most, max(-(-total // amount), total * portions[0] // sum(portions)))
    least = 1 if total - largest >= amount - 1 else 0
    given, spare = [largest] + [least] * (amount - 1), total - largest - least * (amount - 1)
    while spare > 0:
        candidates = [i for i in range(1, amount) if given[i] < largest] or [i for i in range(1, amount) if given[i] < most]
        pool, remaining = sum([portions[i] for i in candidates]), spare
        for i in candidates:
            extra = min(most - given[i], max(1, remaining * portions[i] // pool), spare)
            given[i] = given[i] + extra
            spare = spare - extra
    return np.array(given)


def gaussian(rng, dims, deviation, bound, cuts=(), held_as=jnp.bfloat16):
    drawn = deviation * jax.random.normal(rng, dims, jnp.float32)
    if cuts:
        drawn = drawn * block_levels(rng, dims, cuts, -0.22, 0.18)
    return jnp.clip(drawn, -bound, bound).astype(held_as)


def setup_inputs(seed: int = 0, part: int = 0) -> dict:
    arg_keys = jax.random.split(jax.random.key(seed), 12)
    part_keys = jax.random.split(jax.random.fold_in(arg_keys[11], part), 12)
    thinker_rows = gaussian(part_keys[0], (ROWS, THINK), 1.0, 6.0, ((0, 8), (1, 2)))
    row_session_keys = jax.random.split(jax.random.fold_in(part_keys[1], 1), ROWS // ROWS_SRC)
    row_session_turns = jax.random.permutation(jax.random.fold_in(part_keys[1], 3), ROWS // ROWS_SRC)
    row_session = jax.vmap(lambda own, number: shared_out(jax.random.fold_in(part_keys[1], 2), own, number, ROWS_SRC, SESSIONS, 1, MOST, 1))(row_session_keys, row_session_turns).reshape((ROWS, 1))
    speaker_of = place_ends(ranked(part_keys[2], (SESSIONS,), SPEAKERS, 2), jax.random.fold_in(part_keys[2], 3), 0, SPEAKERS - 1).astype(jnp.int32)
    prompt_slot = jax.random.permutation(part_keys[3], SPEAKERS).astype(jnp.int32)
    prompt_cache = draw_prompt_cache(jax.random.fold_in(jax.random.fold_in(arg_keys[11], part), 71), part)
    proj_weight = gaussian(arg_keys[5], (THINK, D), THINK ** -0.5, 0.09375, ((0, 2),))
    attn_gain = jnp.clip(jax.random.uniform(arg_keys[6], (D,), jnp.float32, 0.5, 1.5), 0.5, 1.5).astype(jnp.bfloat16)
    q_weight = gaussian(arg_keys[7], (D, H * HD), D ** -0.5, 0.1875)
    k_weight = gaussian(arg_keys[8], (D, KVH * HD), (D // 9) ** -0.5, 0.625)
    v_weight = gaussian(arg_keys[9], (D, KVH * HD), D ** -0.5, 0.1875)
    o_weight = gaussian(arg_keys[10], (H * HD, D), (H * HD) ** -0.5, 0.15625)
    return dict(thinker_rows=thinker_rows, row_session=row_session, speaker_of=speaker_of, prompt_slot=prompt_slot, prompt_cache=prompt_cache, proj_weight=proj_weight, attn_gain=attn_gain, q_weight=q_weight, k_weight=k_weight, v_weight=v_weight, o_weight=o_weight)


EPSILON = 1e-06
ROPE_BASE = 1000000.0

def rms_scale(states, gain):
    widened = states.astype(jnp.float32)
    factor = lax.rsqrt(lax.optimization_barrier(jnp.mean(widened * widened, axis=-1, keepdims=True)) + EPSILON)
    return (widened * factor * gain.astype(jnp.float32)).astype(jnp.bfloat16)

def rope_tables(slot_total):
    half_width = HD // 2
    inverse = ROPE_BASE ** (-(jnp.arange(half_width, dtype=jnp.float32) * 2.0) / HD)
    angles = (PROMPT + jnp.arange(slot_total)).astype(jnp.float32)[:, None] * inverse[None, :]
    cosine = jnp.concatenate([jnp.cos(angles), jnp.cos(angles)], axis=1)[:, None, :]
    sine_table = jnp.concatenate([jnp.sin(angles), jnp.sin(angles)], axis=1)[:, None, :]
    return (cosine, sine_table)

def rotate(vectors, cosine, sine_table):
    half_width = vectors.shape[-1] // 2
    turned = jnp.concatenate([-vectors[..., half_width:], vectors[..., :half_width]], axis=-1)
    return vectors * cosine + turned * sine_table

def attend(states, lengths, prompts, attn_gain, q_weight, k_weight, v_weight, o_weight):
    session_total, slot_total, model_width = states.shape
    flat_rows = states.reshape(session_total * slot_total, model_width)
    normed = rms_scale(flat_rows, attn_gain)
    cosine, sine_table = rope_tables(slot_total)
    query = rotate(jnp.dot(normed, q_weight, preferred_element_type=jnp.float32).reshape(session_total, slot_total, H, HD), cosine, sine_table).astype(jnp.bfloat16)
    own_keys = rotate(jnp.dot(normed, k_weight, preferred_element_type=jnp.float32).reshape(session_total, slot_total, KVH, HD), cosine, sine_table).astype(jnp.bfloat16)
    own_values = jnp.dot(normed, v_weight, preferred_element_type=jnp.float32).reshape(session_total, slot_total, KVH, HD).astype(jnp.bfloat16)
    prompt_keys = prompts[:, :, :KVH * HD].reshape(session_total, PROMPT, KVH, HD)
    prompt_values = prompts[:, :, KVH * HD:].reshape(session_total, PROMPT, KVH, HD)
    all_keys = jnp.concatenate([prompt_keys, own_keys], axis=1)
    all_values = jnp.concatenate([prompt_values, own_values], axis=1)
    key_place = jnp.arange(PROMPT + slot_total) - PROMPT
    query_place = jnp.arange(slot_total)
    allowed = (key_place[None, None, :] < 0) | (key_place[None, None, :] <= query_place[None, :, None]) & (key_place[None, None, :] < lengths[:, None, None])
    per_group = H // KVH
    outputs = []
    for kv_head in range(KVH):
        query_group = query[:, :, kv_head * per_group:(kv_head + 1) * per_group].astype(jnp.float32)
        scores = jnp.einsum('cqhd,ckd->chqk', query_group, all_keys[:, :, kv_head].astype(jnp.float32)) * HD ** (-0.5)
        scores = jnp.where(allowed[:, None], scores, -1e+30)
        highest = lax.optimization_barrier(jnp.max(scores, axis=-1, keepdims=True))
        powers = jnp.exp(scores - highest)
        weights = (powers / lax.optimization_barrier(jnp.sum(powers, axis=-1, keepdims=True))).astype(jnp.bfloat16)
        outputs.append(jnp.einsum('chqk,ckd->cqhd', weights.astype(jnp.float32), all_values[:, :, kv_head].astype(jnp.float32)))
    attended = jnp.concatenate(outputs, axis=2).reshape(session_total * slot_total, H * HD).astype(jnp.bfloat16)
    return flat_rows.astype(jnp.float32) + jnp.dot(attended, o_weight, preferred_element_type=jnp.float32)

def reference(thinker_rows, row_session, speaker_of, prompt_slot, prompt_cache, proj_weight, attn_gain, q_weight, k_weight, v_weight, o_weight):
    owner_of_row = row_session[:, 0].astype(jnp.int32)
    projected = jnp.dot(thinker_rows, proj_weight, preferred_element_type=jnp.float32).astype(jnp.bfloat16)
    matches = (owner_of_row[:, None] == jnp.arange(SESSIONS, dtype=jnp.int32)[None, :]).astype(jnp.int32)
    earlier = lax.optimization_barrier(jnp.sum((jnp.cumsum(matches, axis=0) - matches) * matches, axis=1)).astype(jnp.int32)
    lengths = lax.optimization_barrier(jnp.sum(matches, axis=0)).astype(jnp.int32)
    compact = jnp.zeros((SESSIONS, SLOTS, D), jnp.bfloat16).at[owner_of_row, earlier].set(projected)
    chosen_slot = jnp.take(prompt_slot, speaker_of).astype(jnp.int32)

    def one_block(inputs):
        states, block_lengths, block_slots = inputs
        prompts = jnp.take(prompt_cache, block_slots, axis=0)
        summed = attend(states, block_lengths, prompts, attn_gain, q_weight, k_weight, v_weight, o_weight)
        live_rows = (jnp.arange(SLOTS)[None, :] < block_lengths[:, None]).reshape(-1, 1)
        return jnp.where(live_rows, summed, 0.0).astype(jnp.bfloat16).reshape(states.shape)
    block_total = SESSIONS // SESS_DEV
    result = lax.map(one_block, (compact.reshape(block_total, SESS_DEV, SLOTS, D), lengths.reshape(block_total, SESS_DEV), chosen_slot.reshape(block_total, SESS_DEV)))
    return result.reshape(SESSIONS, SLOTS, D)
```

```python
import functools
import math

import jax
import jax.numpy as jnp
import numpy as np
from jax import lax
from jax.experimental import pallas as pl
from jax.experimental.pallas import tpu as pltpu
from jax.sharding import PartitionSpec as P

H = 12
KVH = 4
HD = 128
PROMPT = 1024
SLOTS = 96
PER_GROUP = H // KVH

EPSILON = 1e-06
ROPE_BASE = 1000000.0
NT = (((1,), (1,)), ((), ()))


def rope_tables(copies):
    half_width = HD // 2
    inverse = ROPE_BASE ** (-(np.arange(half_width, dtype=np.float64) * 2.0) / HD)
    angles = (PROMPT + np.arange(SLOTS, dtype=np.float64))[:, None] * inverse[None, :]
    cosine = np.concatenate([np.cos(angles), np.cos(angles)], axis=1)
    sine = np.concatenate([-np.sin(angles), np.sin(angles)], axis=1)
    return (
        np.tile(cosine, (copies, 1)).astype(np.float32),
        np.tile(sine, (copies, 1)).astype(np.float32),
    )


def states_kernel(code_ref, slots_ref, gain_ref, weight_ref, cos_ref, sin_ref,
                  states_ref, query_ref, key_ref, value_ref):
    halves, blocks, rows, width = slots_ref.shape
    total = states_ref.shape[0]
    place = lax.broadcasted_iota(jnp.int32, (total, blocks * rows), 0)
    pick = (place == code_ref[0]).astype(jnp.bfloat16)
    parts = [
        jnp.dot(
            pick,
            slots_ref[half].reshape(blocks * rows, width),
            preferred_element_type=jnp.float32,
        )
        for half in range(halves)
    ]
    widened = jnp.concatenate(parts, axis=1)
    states_ref[...] = widened.astype(jnp.bfloat16)
    factor = lax.rsqrt(jnp.mean(widened * widened, axis=-1, keepdims=True) + EPSILON)
    normed = (widened * factor * gain_ref[...].astype(jnp.float32)).astype(jnp.bfloat16)
    both = jnp.dot(normed, weight_ref[...], preferred_element_type=jnp.float32)
    cosine, sine = cos_ref[...], sin_ref[...]
    for head in range(PER_GROUP + 1):
        vector = both[:, head * HD : (head + 1) * HD]
        turned = vector * cosine + pltpu.roll(vector, HD // 2, 1) * sine
        if head < PER_GROUP:
            query_ref[:, head * HD : (head + 1) * HD] = turned.astype(jnp.bfloat16)
        else:
            key_ref[...] = turned.astype(jnp.bfloat16)
    value_ref[...] = both[:, (PER_GROUP + 1) * HD :].astype(jnp.bfloat16)


def attention_kernel(place_ref, length_ref, query_ref, key_ref, value_ref, prompt_ref, out_ref):
    session = pl.program_id(0)
    length = length_ref[session]
    scale = HD ** (-0.5) * math.log2(math.e)
    query = jnp.concatenate(
        [query_ref[:, h * HD : (h + 1) * HD] for h in range(PER_GROUP)], axis=0
    )
    ahead = lax.dot_general(query, prompt_ref[0, :, :HD], NT, preferred_element_type=jnp.float32)
    own = lax.dot_general(query, key_ref[...], NT, preferred_element_type=jnp.float32)
    row = lax.broadcasted_iota(jnp.int32, (SLOTS, SLOTS), 0)
    column = lax.broadcasted_iota(jnp.int32, (SLOTS, SLOTS), 1)
    allowed = (column <= row) & (column < length)
    own = jnp.where(jnp.concatenate([allowed] * PER_GROUP, axis=0), own, -1e30)
    highest = jnp.maximum(
        jnp.max(ahead, axis=-1, keepdims=True), jnp.max(own, axis=-1, keepdims=True)
    )
    powers = jnp.exp2((ahead - highest) * scale)
    own_powers = jnp.exp2((own - highest) * scale)
    total = jnp.sum(powers, axis=-1, keepdims=True) + jnp.sum(own_powers, axis=-1, keepdims=True)
    mixed = jnp.dot(
        powers.astype(jnp.bfloat16), prompt_ref[0, :, HD:], preferred_element_type=jnp.float32
    ) + jnp.dot(own_powers.astype(jnp.bfloat16), value_ref[...], preferred_element_type=jnp.float32)
    mixed = (mixed / total).astype(jnp.bfloat16)
    for h in range(PER_GROUP):
        out_ref[:, h * HD : (h + 1) * HD] = mixed[h * SLOTS : (h + 1) * SLOTS]


def make_states(code, slots, gain, weight, sessions, together):
    halves, blocks, rows, width = slots.shape
    steps = sessions // together
    model = halves * width
    cosine, sine = rope_tables(together)
    total = together * SLOTS
    out = jax.ShapeDtypeStruct
    row_spec = lambda w: pl.BlockSpec((total, w), lambda i: (i, 0))
    whole = lambda a: pl.BlockSpec(a.shape, lambda i: (0,) * a.ndim)
    gain = gain.reshape(1, model)
    return pl.pallas_call(
        states_kernel,
        grid=(steps,),
        in_specs=[
            pl.BlockSpec((1, 1, code.shape[2]), lambda i: (i, 0, 0)),
            pl.BlockSpec((halves, blocks, rows // steps, width), lambda i: (0, 0, i, 0)),
            whole(gain),
            whole(weight),
            whole(cosine),
            whole(sine),
        ],
        out_specs=[row_spec(model), row_spec(PER_GROUP * HD), row_spec(HD), row_spec(HD)],
        out_shape=[
            out((sessions * SLOTS, model), jnp.bfloat16),
            out((sessions * SLOTS, PER_GROUP * HD), jnp.bfloat16),
            out((sessions * SLOTS, HD), jnp.bfloat16),
            out((sessions * SLOTS, HD), jnp.bfloat16),
        ],
        compiler_params=pltpu.CompilerParams(vmem_limit_bytes=40 << 20),
        name="states",
    )(code, slots, gain, weight, jnp.asarray(cosine), jnp.asarray(sine))


def attend(place, lengths, query, key, value, prompts):
    sessions = place.shape[0]
    row_spec = lambda w: pl.BlockSpec((SLOTS, w), lambda i, place, length: (i, 0))
    return pl.pallas_call(
        attention_kernel,
        grid_spec=pltpu.PrefetchScalarGridSpec(
            num_scalar_prefetch=2,
            grid=(sessions,),
            in_specs=[
                row_spec(PER_GROUP * HD),
                row_spec(HD),
                row_spec(HD),
                pl.BlockSpec((1, PROMPT, 2 * HD), lambda i, place, length: (place[i], 0, 0)),
            ],
            out_specs=row_spec(PER_GROUP * HD),
        ),
        out_shape=jax.ShapeDtypeStruct((sessions * SLOTS, PER_GROUP * HD), jnp.bfloat16),
        compiler_params=pltpu.CompilerParams(vmem_limit_bytes=40 << 20),
        name="attend",
    )(place, lengths, query, key, value, prompts)


def body(
    thinker_rows,
    row_session,
    speaker_of,
    prompt_slot,
    prompt_cache,
    proj_weight,
    attn_gain,
    q_weight,
    k_weight,
    v_weight,
    o_weight,
):
    sess_count = lax.axis_size("sess")
    inner_count = lax.axis_size("inner")
    rep_count = lax.axis_size("rep")
    plane = inner_count * rep_count
    blocks = sess_count * rep_count
    session_all = speaker_of.shape[0]
    per_plane = session_all // sess_count
    per_device = per_plane // plane
    slot_cap = SLOTS // blocks
    held, tokens, channels = prompt_cache.shape
    model = proj_weight.shape[1]
    sharers = plane // KVH
    held_part = held // sharers
    sess_place = lax.axis_index("sess")
    plane_place = lax.axis_index("inner") * rep_count + lax.axis_index("rep")
    head = plane_place // sharers
    sharer = plane_place % sharers

    outgoing = jnp.transpose(
        prompt_cache.reshape(sharers, held_part, tokens, 2, KVH, HD), (4, 0, 1, 2, 3, 5)
    ).reshape(plane, held_part, tokens, 2 * HD)
    own_head = lax.all_to_all(outgoing, ("inner", "rep"), split_axis=0, concat_axis=2, tiled=True)
    own_head = own_head.reshape(held_part, plane * tokens, 2 * HD)
    prompts = lax.all_gather(own_head, "sess", axis=0, tiled=True)

    row_owner = row_session[:, 0]
    order = jnp.arange(row_owner.shape[0])
    same = row_owner[:, None] == row_owner[None, :]
    earlier = jnp.sum((same & (order[None, :] < order[:, None])).astype(jnp.int32), axis=1)
    row_slot = row_owner * slot_cap + earlier
    counts = jnp.sum(
        (row_owner[:, None] == jnp.arange(session_all)[None, :]).astype(jnp.int32), axis=0
    )
    all_counts = lax.all_gather(counts, ("sess", "rep"), axis=0, tiled=False)

    partial_sum = jnp.dot(thinker_rows, proj_weight, preferred_element_type=jnp.float32)
    width = model // inner_count
    if inner_count == 2:
        inner_place = lax.axis_index("inner")
        kept = lax.dynamic_slice_in_dim(partial_sum, inner_place * width, width, 1)
        sent = lax.dynamic_slice_in_dim(partial_sum, (1 - inner_place) * width, width, 1)
        came = lax.ppermute(sent.astype(jnp.bfloat16), "inner", [(0, 1), (1, 0)])
        own_columns = (kept + came.astype(jnp.float32)).astype(jnp.bfloat16)
    else:
        own_columns = lax.psum_scatter(
            partial_sum, "inner", scatter_dimension=1, tiled=True
        ).astype(jnp.bfloat16)
    into = (jnp.arange(session_all * slot_cap)[:, None] == row_slot[None, :]).astype(jnp.bfloat16)
    buffer = jnp.dot(into, own_columns, preferred_element_type=jnp.float32).astype(jnp.bfloat16)
    arrived = lax.all_to_all(
        buffer.reshape(sess_count, per_plane * slot_cap, width),
        "sess",
        split_axis=0,
        concat_axis=0,
        tiled=True,
    )
    spread = lax.all_gather(arrived, ("inner", "rep"), axis=0, tiled=False)
    slots = spread.reshape(inner_count, rep_count * sess_count, per_plane * slot_cap, width)

    offsets = jnp.cumsum(all_counts, axis=0) - all_counts
    lengths_all = jnp.sum(all_counts, axis=0)
    mine = lambda a: lax.dynamic_slice_in_dim(a, sess_place * per_plane, per_plane, a.ndim - 1)
    by_block = lambda a: jnp.transpose(
        mine(a).reshape(sess_count, rep_count, per_plane), (1, 0, 2)
    ).reshape(blocks, per_plane)
    lengths = mine(lengths_all)
    together = 16 // math.gcd(16, slot_cap)
    within = jnp.arange(slot_cap)
    local = (jnp.arange(per_plane) % together)[None, :, None] * SLOTS
    code = jnp.where(
        within[None, None, :] < by_block(all_counts)[:, :, None],
        by_block(offsets)[:, :, None] + within[None, None, :] + local,
        -1,
    )
    steps = per_plane // together
    code = jnp.transpose(
        code.reshape(blocks, steps, together * slot_cap), (1, 0, 2)
    ).reshape(steps, 1, blocks * together * slot_cap)

    group_width = PER_GROUP * HD
    weight = jnp.concatenate(
        [
            lax.dynamic_slice_in_dim(q_weight, head * group_width, group_width, 1),
            lax.dynamic_slice_in_dim(k_weight, head * HD, HD, 1),
            lax.dynamic_slice_in_dim(v_weight, head * HD, HD, 1),
        ],
        axis=1,
    )
    states, query, key, value = make_states(
        code, slots, attn_gain, weight, per_plane, together
    )

    wanted_slot = jnp.sum(
        jnp.where(
            mine(speaker_of)[:, None] == jnp.arange(prompt_slot.shape[0])[None, :],
            prompt_slot[None, :],
            0,
        ),
        axis=1,
    )
    place = wanted_slot // held * held_part + wanted_slot % held_part
    attended = attend(place, lengths, query, key, value, prompts)
    returned = lax.all_to_all(
        attended.reshape(plane, per_device * SLOTS, group_width),
        ("inner", "rep"),
        split_axis=0,
        concat_axis=0,
        tiled=True,
    ).reshape(KVH, sharers, per_device, SLOTS, group_width)
    first = plane_place * per_device
    if sharers > 1:
        holder = lax.dynamic_slice_in_dim(wanted_slot % held // held_part, first, per_device)
        chosen = jnp.zeros_like(returned[:, 0])
        for t in range(sharers):
            chosen = jnp.where((holder == t)[None, :, None, None], returned[:, t], chosen)
    else:
        chosen = returned[:, 0]
    gathered = jnp.transpose(chosen, (1, 2, 0, 3)).reshape(per_device * SLOTS, H * HD)
    own_states = lax.dynamic_slice_in_dim(states, first * SLOTS, per_device * SLOTS, 0)
    own_lengths = lax.dynamic_slice_in_dim(lengths, first, per_device)
    summed = own_states.astype(jnp.float32) + jnp.dot(
        gathered, o_weight, preferred_element_type=jnp.float32
    )
    live_rows = (jnp.arange(SLOTS)[None, :] < own_lengths[:, None]).reshape(-1, 1)
    return (
        jnp.where(live_rows, summed, 0.0)
        .astype(jnp.bfloat16)
        .reshape(per_device, SLOTS, model)
    )


def solution(mesh):
    in_specs = (
        P(("groups", "sess", "rep"), "inner"),
        P(("groups", "sess", "rep"), None),
        P("groups"),
        P("groups"),
        P(("groups", "sess"), ("inner", "rep"), None),
        P("inner", None),
        P(),
        P(),
        P(),
        P(),
        P(),
    )
    out_specs = P(("groups", "sess", "inner", "rep"), None, None)
    return jax.shard_map(body, mesh=mesh, in_specs=in_specs, out_specs=out_specs, check_vma=False)
```

```python
import functools
import math

import jax
import jax.numpy as jnp
import numpy as np
from jax import lax
from jax.experimental import pallas as pl
from jax.experimental.pallas import tpu as pltpu
from jax.sharding import PartitionSpec as P

H = 12
KVH = 4
HD = 128
PROMPT = 1024
SLOTS = 96
PER_GROUP = H // KVH

EPSILON = 1e-06
ROPE_BASE = 1000000.0
NT = (((1,), (1,)), ((), ()))


def rope_tables(copies):
    half_width = HD // 2
    inverse = ROPE_BASE ** (-(np.arange(half_width, dtype=np.float64) * 2.0) / HD)
    angles = (PROMPT + np.arange(SLOTS, dtype=np.float64))[:, None] * inverse[None, :]
    cosine = np.concatenate([np.cos(angles), np.cos(angles)], axis=1)
    sine = np.concatenate([-np.sin(angles), np.sin(angles)], axis=1)
    return (
        np.tile(cosine, (copies, 1)).astype(np.float32),
        np.tile(sine, (copies, 1)).astype(np.float32),
    )


def states_kernel(code_ref, slots_ref, gain_ref, weight_ref, cos_ref, sin_ref,
                  states_ref, query_ref, key_ref, value_ref):
    halves, blocks, rows, width = slots_ref.shape
    total = states_ref.shape[0]
    place = lax.broadcasted_iota(jnp.int32, (total, blocks * rows), 0)
    pick = (place == code_ref[0]).astype(jnp.bfloat16)
    parts = [
        jnp.dot(
            pick,
            slots_ref[half].reshape(blocks * rows, width),
            preferred_element_type=jnp.float32,
        )
        for half in range(halves)
    ]
    widened = jnp.concatenate(parts, axis=1)
    states_ref[...] = widened.astype(jnp.bfloat16)
    factor = lax.rsqrt(jnp.mean(widened * widened, axis=-1, keepdims=True) + EPSILON)
    normed = (widened * factor * gain_ref[...].astype(jnp.float32)).astype(jnp.bfloat16)
    both = jnp.dot(normed, weight_ref[...], preferred_element_type=jnp.float32)
    cosine, sine = cos_ref[...], sin_ref[...]
    for head in range(PER_GROUP + 1):
        vector = both[:, head * HD : (head + 1) * HD]
        turned = vector * cosine + pltpu.roll(vector, HD // 2, 1) * sine
        if head < PER_GROUP:
            query_ref[:, head * HD : (head + 1) * HD] = turned.astype(jnp.bfloat16)
        else:
            key_ref[...] = turned.astype(jnp.bfloat16)
    value_ref[...] = both[:, (PER_GROUP + 1) * HD :].astype(jnp.bfloat16)


def attention_kernel(place_ref, length_ref, query_ref, key_ref, value_ref, prompt_ref, out_ref):
    session = pl.program_id(0)
    length = length_ref[session]
    scale = HD ** (-0.5) * math.log2(math.e)
    query = jnp.concatenate(
        [query_ref[:, h * HD : (h + 1) * HD] for h in range(PER_GROUP)], axis=0
    )
    ahead = lax.dot_general(query, prompt_ref[0, :, :HD], NT, preferred_element_type=jnp.float32)
    own = lax.dot_general(query, key_ref[...], NT, preferred_element_type=jnp.float32)
    row = lax.broadcasted_iota(jnp.int32, (SLOTS, SLOTS), 0)
    column = lax.broadcasted_iota(jnp.int32, (SLOTS, SLOTS), 1)
    allowed = (column <= row) & (column < length)
    own = jnp.where(jnp.concatenate([allowed] * PER_GROUP, axis=0), own, -1e30)
    highest = jnp.maximum(
        jnp.max(ahead, axis=-1, keepdims=True), jnp.max(own, axis=-1, keepdims=True)
    )
    powers = jnp.exp2((ahead - highest) * scale)
    own_powers = jnp.exp2((own - highest) * scale)
    total = jnp.sum(powers, axis=-1, keepdims=True) + jnp.sum(own_powers, axis=-1, keepdims=True)
    mixed = jnp.dot(
        powers.astype(jnp.bfloat16), prompt_ref[0, :, HD:], preferred_element_type=jnp.float32
    ) + jnp.dot(own_powers.astype(jnp.bfloat16), value_ref[...], preferred_element_type=jnp.float32)
    mixed = (mixed / total).astype(jnp.bfloat16)
    for h in range(PER_GROUP):
        out_ref[:, h * HD : (h + 1) * HD] = mixed[h * SLOTS : (h + 1) * SLOTS]


def make_states(code, slots, gain, weight, sessions, together):
    halves, blocks, rows, width = slots.shape
    steps = sessions // together
    model = halves * width
    cosine, sine = rope_tables(together)
    total = together * SLOTS
    out = jax.ShapeDtypeStruct
    row_spec = lambda w: pl.BlockSpec((total, w), lambda i: (i, 0))
    whole = lambda a: pl.BlockSpec(a.shape, lambda i: (0,) * a.ndim)
    gain = gain.reshape(1, model)
    return pl.pallas_call(
        states_kernel,
        grid=(steps,),
        in_specs=[
            pl.BlockSpec((1, 1, code.shape[2]), lambda i: (i, 0, 0)),
            pl.BlockSpec((halves, blocks, rows // steps, width), lambda i: (0, 0, i, 0)),
            whole(gain),
            whole(weight),
            whole(cosine),
            whole(sine),
        ],
        out_specs=[row_spec(model), row_spec(PER_GROUP * HD), row_spec(HD), row_spec(HD)],
        out_shape=[
            out((sessions * SLOTS, model), jnp.bfloat16),
            out((sessions * SLOTS, PER_GROUP * HD), jnp.bfloat16),
            out((sessions * SLOTS, HD), jnp.bfloat16),
            out((sessions * SLOTS, HD), jnp.bfloat16),
        ],
        compiler_params=pltpu.CompilerParams(vmem_limit_bytes=40 << 20),
        name="states",
    )(code, slots, gain, weight, jnp.asarray(cosine), jnp.asarray(sine))


def attend(place, lengths, query, key, value, prompts):
    sessions = place.shape[0]
    row_spec = lambda w: pl.BlockSpec((SLOTS, w), lambda i, place, length: (i, 0))
    return pl.pallas_call(
        attention_kernel,
        grid_spec=pltpu.PrefetchScalarGridSpec(
            num_scalar_prefetch=2,
            grid=(sessions,),
            in_specs=[
                row_spec(PER_GROUP * HD),
                row_spec(HD),
                row_spec(HD),
                pl.BlockSpec((1, PROMPT, 2 * HD), lambda i, place, length: (place[i], 0, 0)),
            ],
            out_specs=row_spec(PER_GROUP * HD),
        ),
        out_shape=jax.ShapeDtypeStruct((sessions * SLOTS, PER_GROUP * HD), jnp.bfloat16),
        compiler_params=pltpu.CompilerParams(vmem_limit_bytes=40 << 20),
        name="attend",
    )(place, lengths, query, key, value, prompts)


def general_body(
    thinker_rows,
    row_session,
    speaker_of,
    prompt_slot,
    prompt_cache,
    proj_weight,
    attn_gain,
    q_weight,
    k_weight,
    v_weight,
    o_weight,
):
    sess_count = lax.axis_size("sess")
    inner_count = lax.axis_size("inner")
    rep_count = lax.axis_size("rep")
    plane = inner_count * rep_count
    blocks = sess_count * rep_count
    session_all = speaker_of.shape[0]
    per_plane = session_all // sess_count
    per_device = per_plane // plane
    slot_cap = SLOTS // blocks
    held, tokens, channels = prompt_cache.shape
    model = proj_weight.shape[1]
    sharers = plane // KVH
    held_part = held // sharers
    sess_place = lax.axis_index("sess")
    plane_place = lax.axis_index("inner") * rep_count + lax.axis_index("rep")
    head = plane_place // sharers
    sharer = plane_place % sharers

    outgoing = jnp.transpose(
        prompt_cache.reshape(sharers, held_part, tokens, 2, KVH, HD), (4, 0, 1, 2, 3, 5)
    ).reshape(plane, held_part, tokens, 2 * HD)
    own_head = lax.all_to_all(outgoing, ("inner", "rep"), split_axis=0, concat_axis=2, tiled=True)
    own_head = own_head.reshape(held_part, plane * tokens, 2 * HD)
    prompts = lax.all_gather(own_head, "sess", axis=0, tiled=True)

    row_owner = row_session[:, 0]
    order = jnp.arange(row_owner.shape[0])
    same = row_owner[:, None] == row_owner[None, :]
    earlier = jnp.sum((same & (order[None, :] < order[:, None])).astype(jnp.int32), axis=1)
    row_slot = row_owner * slot_cap + earlier
    counts = jnp.sum(
        (row_owner[:, None] == jnp.arange(session_all)[None, :]).astype(jnp.int32), axis=0
    )
    all_counts = lax.all_gather(counts, ("sess", "rep"), axis=0, tiled=False)

    partial_sum = jnp.dot(thinker_rows, proj_weight, preferred_element_type=jnp.float32)
    width = model // inner_count
    if inner_count == 2:
        inner_place = lax.axis_index("inner")
        kept = lax.dynamic_slice_in_dim(partial_sum, inner_place * width, width, 1)
        sent = lax.dynamic_slice_in_dim(partial_sum, (1 - inner_place) * width, width, 1)
        came = lax.ppermute(sent.astype(jnp.bfloat16), "inner", [(0, 1), (1, 0)])
        own_columns = (kept + came.astype(jnp.float32)).astype(jnp.bfloat16)
    else:
        own_columns = lax.psum_scatter(
            partial_sum, "inner", scatter_dimension=1, tiled=True
        ).astype(jnp.bfloat16)
    into = (jnp.arange(session_all * slot_cap)[:, None] == row_slot[None, :]).astype(jnp.bfloat16)
    buffer = jnp.dot(into, own_columns, preferred_element_type=jnp.float32).astype(jnp.bfloat16)
    arrived = lax.all_to_all(
        buffer.reshape(sess_count, per_plane * slot_cap, width),
        "sess",
        split_axis=0,
        concat_axis=0,
        tiled=True,
    )
    spread = lax.all_gather(arrived, ("inner", "rep"), axis=0, tiled=False)
    slots = spread.reshape(inner_count, rep_count * sess_count, per_plane * slot_cap, width)

    offsets = jnp.cumsum(all_counts, axis=0) - all_counts
    lengths_all = jnp.sum(all_counts, axis=0)
    mine = lambda a: lax.dynamic_slice_in_dim(a, sess_place * per_plane, per_plane, a.ndim - 1)
    by_block = lambda a: jnp.transpose(
        mine(a).reshape(sess_count, rep_count, per_plane), (1, 0, 2)
    ).reshape(blocks, per_plane)
    lengths = mine(lengths_all)
    together = 16 // math.gcd(16, slot_cap)
    within = jnp.arange(slot_cap)
    local = (jnp.arange(per_plane) % together)[None, :, None] * SLOTS
    code = jnp.where(
        within[None, None, :] < by_block(all_counts)[:, :, None],
        by_block(offsets)[:, :, None] + within[None, None, :] + local,
        -1,
    )
    steps = per_plane // together
    code = jnp.transpose(
        code.reshape(blocks, steps, together * slot_cap), (1, 0, 2)
    ).reshape(steps, 1, blocks * together * slot_cap)

    group_width = PER_GROUP * HD
    weight = jnp.concatenate(
        [
            lax.dynamic_slice_in_dim(q_weight, head * group_width, group_width, 1),
            lax.dynamic_slice_in_dim(k_weight, head * HD, HD, 1),
            lax.dynamic_slice_in_dim(v_weight, head * HD, HD, 1),
        ],
        axis=1,
    )
    states, query, key, value = make_states(
        code, slots, attn_gain, weight, per_plane, together
    )

    wanted_slot = jnp.sum(
        jnp.where(
            mine(speaker_of)[:, None] == jnp.arange(prompt_slot.shape[0])[None, :],
            prompt_slot[None, :],
            0,
        ),
        axis=1,
    )
    place = wanted_slot // held * held_part + wanted_slot % held_part
    attended = attend(place, lengths, query, key, value, prompts)
    returned = lax.all_to_all(
        attended.reshape(plane, per_device * SLOTS, group_width),
        ("inner", "rep"),
        split_axis=0,
        concat_axis=0,
        tiled=True,
    ).reshape(KVH, sharers, per_device, SLOTS, group_width)
    first = plane_place * per_device
    if sharers > 1:
        holder = lax.dynamic_slice_in_dim(wanted_slot % held // held_part, first, per_device)
        chosen = jnp.zeros_like(returned[:, 0])
        for t in range(sharers):
            chosen = jnp.where((holder == t)[None, :, None, None], returned[:, t], chosen)
    else:
        chosen = returned[:, 0]
    gathered = jnp.transpose(chosen, (1, 2, 0, 3)).reshape(per_device * SLOTS, H * HD)
    own_states = lax.dynamic_slice_in_dim(states, first * SLOTS, per_device * SLOTS, 0)
    own_lengths = lax.dynamic_slice_in_dim(lengths, first, per_device)
    summed = own_states.astype(jnp.float32) + jnp.dot(
        gathered, o_weight, preferred_element_type=jnp.float32
    )
    live_rows = (jnp.arange(SLOTS)[None, :] < own_lengths[:, None]).reshape(-1, 1)
    return (
        jnp.where(live_rows, summed, 0.0)
        .astype(jnp.bfloat16)
        .reshape(per_device, SLOTS, model)
    )


def session_attention(query_ref, key_ref, value_ref, kv, out_ref, session, length):
    scale = HD ** (-0.5) * math.log2(math.e)
    rows = pl.ds(pl.multiple_of(session * SLOTS, SLOTS), SLOTS)
    query = jnp.concatenate(
        [query_ref[rows, h * HD : (h + 1) * HD] for h in range(PER_GROUP)], axis=0
    )
    tokens = kv.reshape(PROMPT, 2 * HD)
    ahead = lax.dot_general(query, tokens[:, :HD], NT, preferred_element_type=jnp.float32)
    own = lax.dot_general(query, key_ref[rows, :], NT, preferred_element_type=jnp.float32)
    row = lax.broadcasted_iota(jnp.int32, (SLOTS, SLOTS), 0)
    column = lax.broadcasted_iota(jnp.int32, (SLOTS, SLOTS), 1)
    allowed = (column <= row) & (column < length)
    own = jnp.where(jnp.concatenate([allowed] * PER_GROUP, axis=0), own, -1e30)
    highest = jnp.maximum(
        jnp.max(ahead, axis=-1, keepdims=True), jnp.max(own, axis=-1, keepdims=True)
    )
    powers = jnp.exp2((ahead - highest) * scale)
    own_powers = jnp.exp2((own - highest) * scale)
    total = jnp.sum(powers, axis=-1, keepdims=True) + jnp.sum(own_powers, axis=-1, keepdims=True)
    mixed = jnp.dot(
        powers.astype(jnp.bfloat16), tokens[:, HD:], preferred_element_type=jnp.float32
    ) + jnp.dot(own_powers.astype(jnp.bfloat16), value_ref[rows, :], preferred_element_type=jnp.float32)
    mixed = (mixed / total).astype(jnp.bfloat16)
    for h in range(PER_GROUP):
        out_ref[rows, h * HD : (h + 1) * HD] = mixed[h * SLOTS : (h + 1) * SLOTS]


def hops_kernel(hop_ref, held_ref, length_ref, query_ref, key_ref, value_ref, *refs, hops, carried):
    if carried:
        before_ref, *refs = refs
    prompt_refs, (out_ref, kv, sem) = refs[: 2 * len(hops)], refs[2 * len(hops) :]
    sessions = hop_ref.shape[0]

    def copies(session, which):
        return [
            pltpu.make_async_copy(
                prompt_refs[2 * which + chunk].at[:, held_ref[session]],
                kv.at[session, chunk],
                sem.at[session, chunk],
            )
            for chunk in range(2)
        ]

    def fetch(session, _):
        for which, hop in enumerate(hops):
            @pl.when(hop_ref[session] == hop)
            def _():
                for copy in copies(session, which):
                    copy.start()
        return 0

    lax.fori_loop(0, sessions, fetch, 0)
    if carried:
        out_ref[...] = before_ref[...]

    def work(session, _):
        ours = hop_ref[session] == hops[0]
        for hop in hops[1:]:
            ours = ours | (hop_ref[session] == hop)

        @pl.when(ours)
        def _():
            for copy in copies(session, 0):
                copy.wait()
            session_attention(
                query_ref, key_ref, value_ref, kv[session], out_ref, session, length_ref[session]
            )

        return 0

    lax.fori_loop(0, sessions, work, 0)


def attend_hops(hop, held, lengths, query, key, value, prompts, hops, before):
    sessions = hop.shape[0]
    carried = before is not None
    smem = pl.BlockSpec(memory_space=pltpu.SMEM)
    vmem = pl.BlockSpec(memory_space=pltpu.VMEM)
    anywhere = pl.BlockSpec(memory_space=pl.ANY)
    pieces = [piece for h in hops for piece in prompts[h]]
    work = sessions * len(hops) // 7 + 1
    return pl.pallas_call(
        functools.partial(hops_kernel, hops=hops, carried=carried),
        in_specs=[smem] * 3 + [vmem] * (3 + carried) + [anywhere] * len(pieces),
        out_specs=vmem,
        out_shape=jax.ShapeDtypeStruct((sessions * SLOTS, PER_GROUP * HD), jnp.bfloat16),
        scratch_shapes=[
            pltpu.VMEM((sessions, 2, 2, PROMPT // 4, 2 * HD), jnp.bfloat16),
            pltpu.SemaphoreType.DMA((sessions, 2)),
        ],
        compiler_params=pltpu.CompilerParams(vmem_limit_bytes=40 << 20),
        cost_estimate=pl.CostEstimate(
            flops=work * 4 * PER_GROUP * SLOTS * (PROMPT + SLOTS) * HD,
            bytes_accessed=work * PROMPT * 4 * HD,
            transcendentals=work * PER_GROUP * SLOTS * (PROMPT + SLOTS),
        ),
        name="attend",
    )(hop, held, lengths, query, key, value, *([before] if carried else []), *pieces)


def shifted(n, by):
    return [(i, i + by) for i in range(n) if 0 <= i + by < n]


def swapped(n, by):
    return [(i, i ^ by) for i in range(n)]


def line_body(
    thinker_rows,
    row_session,
    speaker_of,
    prompt_slot,
    prompt_cache,
    proj_weight,
    attn_gain,
    q_weight,
    k_weight,
    v_weight,
    o_weight,
):
    planes, plane, rep_count = lax.axis_size("sess"), KVH, 2
    blocks = planes * rep_count
    session_all = speaker_of.shape[0]
    per_plane = session_all // planes
    per_device = per_plane // plane
    slot_cap = SLOTS // blocks
    held = prompt_cache.shape[0]
    model = proj_weight.shape[1]
    width = model // 2
    z, x, c = lax.axis_index("sess"), lax.axis_index("inner"), lax.axis_index("rep")
    head = x * rep_count + c
    pair = ("inner", "rep")

    def of_head(h):
        parts = [
            lax.dynamic_slice_in_dim(prompt_cache, h * HD + side * KVH * HD, HD, 2)
            for side in range(2)
        ]
        return jnp.concatenate(parts, axis=2)

    from_core = lax.ppermute(of_head(head ^ 1), pair, swapped(4, 1))
    from_x = lax.ppermute(of_head(head ^ 2), pair, swapped(4, 2))
    from_far = lax.ppermute(of_head(head ^ 3), pair, swapped(4, 3))
    right = [jnp.stack([of_head(head), from_core]), jnp.stack([from_x, from_far])]
    left = list(right)
    prompts = {0: tuple(right)}
    for hop in range(1, planes):
        for chunk in range(2):
            right[chunk] = lax.ppermute(right[chunk], "sess", shifted(planes, 1))
            left[chunk] = lax.ppermute(left[chunk], "sess", shifted(planes, -1))
        prompts[-hop], prompts[hop] = tuple(right), tuple(left)

    row_owner = row_session[:, 0]
    order = jnp.arange(row_owner.shape[0])
    same = row_owner[:, None] == row_owner[None, :]
    earlier = jnp.sum((same & (order[None, :] < order[:, None])).astype(jnp.int32), axis=1)
    row_slot = row_owner * slot_cap + earlier
    all_owners = lax.all_gather(
        row_owner.reshape(-1, 128), ("sess", "rep"), axis=0, tiled=True
    ).reshape(blocks, -1)

    partial_sum = jnp.dot(thinker_rows, proj_weight, preferred_element_type=jnp.float32)
    kept = lax.dynamic_slice_in_dim(partial_sum, x * width, width, 1)
    sent = lax.dynamic_slice_in_dim(partial_sum, (1 - x) * width, width, 1)
    came = lax.ppermute(sent.astype(jnp.bfloat16), "inner", swapped(2, 1))
    own_columns = (kept + came.astype(jnp.float32)).astype(jnp.bfloat16)
    into = (jnp.arange(session_all * slot_cap)[:, None] == row_slot[None, :]).astype(jnp.bfloat16)
    buffer = jnp.dot(into, own_columns, preferred_element_type=jnp.float32).astype(jnp.bfloat16)
    buffer = buffer.reshape(planes, per_plane * slot_cap, width)
    arrived = [lax.dynamic_index_in_dim(buffer, z, 0, keepdims=False)]
    for by in range(1, planes):
        outgoing = lax.dynamic_index_in_dim(buffer, z ^ by, 0, keepdims=False)
        arrived.append(lax.ppermute(outgoing, "sess", swapped(planes, by)))
    arrived = jnp.stack(arrived)
    other_x = lax.ppermute(arrived, "inner", swapped(2, 1))
    low = jnp.where(x == 0, arrived, other_x)
    high = jnp.where(x == 0, other_x, arrived)
    halves = jnp.stack([low, high])
    other_core = lax.ppermute(halves, "rep", swapped(2, 1))
    slots = jnp.concatenate([halves, other_core], axis=1)

    mine = lambda a: lax.dynamic_slice_in_dim(a, z * per_plane, per_plane, a.ndim - 1)
    ours = z * per_plane + jnp.arange(per_plane)
    counts = jnp.sum(
        (all_owners[:, None, :] == ours[None, :, None]).astype(jnp.int32), axis=2
    )
    lengths = jnp.sum(counts, axis=0)
    kind = jnp.arange(blocks)
    block = (z ^ (kind % planes)) * rep_count + (c ^ (kind // planes))
    is_block = block[:, None] == kind[None, :]
    is_before = kind[None, :] < block[:, None]
    here = jnp.sum(jnp.where(is_block[:, :, None], counts[None], 0), axis=1)
    offsets = jnp.sum(jnp.where(is_before[:, :, None], counts[None], 0), axis=1)
    together = 16 // math.gcd(16, slot_cap)
    steps = per_plane // together
    within = jnp.arange(slot_cap)
    local = (jnp.arange(per_plane) % together)[None, :, None] * SLOTS
    code = jnp.where(
        within[None, None, :] < here[:, :, None],
        offsets[:, :, None] + within[None, None, :] + local,
        -1,
    )
    code = jnp.transpose(
        code.reshape(blocks, steps, together * slot_cap), (1, 0, 2)
    ).reshape(steps, 1, blocks * together * slot_cap)

    group_width = PER_GROUP * HD
    weight = jnp.concatenate(
        [
            lax.dynamic_slice_in_dim(q_weight, head * group_width, group_width, 1),
            lax.dynamic_slice_in_dim(k_weight, head * HD, HD, 1),
            lax.dynamic_slice_in_dim(v_weight, head * HD, HD, 1),
        ],
        axis=1,
    )
    states, query, key, value = make_states(
        code, slots, attn_gain, weight, per_plane, together
    )

    wanted_slot = jnp.sum(
        jnp.where(
            mine(speaker_of)[:, None] == jnp.arange(prompt_slot.shape[0])[None, :],
            prompt_slot[None, :],
            0,
        ),
        axis=1,
    )
    hop = wanted_slot // held - z
    which = wanted_slot % held
    near = attend_hops(
        hop, which, lengths, query, key, value, prompts, (0, -1, 1, -2, 2), None
    )
    attended = attend_hops(hop, which, lengths, query, key, value, prompts, (-3, 3), near)

    attended = attended.reshape(plane, per_device * SLOTS, group_width)
    pieces = [lax.dynamic_index_in_dim(attended, head, 0, keepdims=False)]
    for by in (2, 3, 1):
        outgoing = lax.dynamic_index_in_dim(attended, head ^ by, 0, keepdims=False)
        pieces.append(lax.ppermute(outgoing, pair, swapped(4, by)))
    o_rows = o_weight.reshape(KVH, group_width, model)
    first = head * per_device
    summed = lax.dynamic_slice_in_dim(states, first * SLOTS, per_device * SLOTS, 0).astype(
        jnp.float32
    )
    gathered = jnp.concatenate(pieces, axis=1)
    turned = jnp.concatenate(
        [
            lax.dynamic_index_in_dim(o_rows, head ^ by, 0, keepdims=False)
            for by in (0, 2, 3, 1)
        ],
        axis=0,
    )
    summed = summed + jnp.dot(gathered, turned, preferred_element_type=jnp.float32)
    own_lengths = lax.dynamic_slice_in_dim(lengths, first, per_device)
    live_rows = (jnp.arange(SLOTS)[None, :] < own_lengths[:, None]).reshape(-1, 1)
    return (
        jnp.where(live_rows, summed, 0.0)
        .astype(jnp.bfloat16)
        .reshape(per_device, SLOTS, model)
    )


def solution(mesh):
    in_specs = (
        P(("groups", "sess", "rep"), "inner"),
        P(("groups", "sess", "rep"), None),
        P("groups"),
        P("groups"),
        P(("groups", "sess"), ("inner", "rep"), None),
        P("inner", None),
        P(),
        P(),
        P(),
        P(),
        P(),
    )
    out_specs = P(("groups", "sess", "inner", "rep"), None, None)
    sizes = tuple(mesh.shape[name] for name in ("sess", "inner", "rep"))
    body = line_body if sizes == (4, 2, 2) else general_body
    return jax.shard_map(body, mesh=mesh, in_specs=in_specs, out_specs=out_specs, check_vma=False)
```

```python
import functools
import math

import jax
import jax.numpy as jnp
import numpy as np
from jax import lax
from jax.experimental import pallas as pl
from jax.experimental.pallas import tpu as pltpu
from jax.sharding import PartitionSpec as P

H = 12
KVH = 4
HD = 128
PROMPT = 1024
SLOTS = 96
PER_GROUP = H // KVH

EPSILON = 1e-06
ROPE_BASE = 1000000.0
NT = (((1,), (1,)), ((), ()))


def rope_tables(copies):
    half_width = HD // 2
    inverse = ROPE_BASE ** (-(np.arange(half_width, dtype=np.float64) * 2.0) / HD)
    angles = (PROMPT + np.arange(SLOTS, dtype=np.float64))[:, None] * inverse[None, :]
    cosine = np.concatenate([np.cos(angles), np.cos(angles)], axis=1)
    sine = np.concatenate([-np.sin(angles), np.sin(angles)], axis=1)
    return (
        np.tile(cosine, (copies, 1)).astype(np.float32),
        np.tile(sine, (copies, 1)).astype(np.float32),
    )


def states_kernel(code_ref, slots_ref, gain_ref, weight_ref, cos_ref, sin_ref,
                  states_ref, query_ref, key_ref, value_ref):
    halves, blocks, rows, width = slots_ref.shape
    total = states_ref.shape[0]
    place = lax.broadcasted_iota(jnp.int32, (total, blocks * rows), 0)
    pick = (place == code_ref[0]).astype(jnp.bfloat16)
    parts = [
        jnp.dot(
            pick,
            slots_ref[half].reshape(blocks * rows, width),
            preferred_element_type=jnp.float32,
        )
        for half in range(halves)
    ]
    widened = jnp.concatenate(parts, axis=1)
    states_ref[...] = widened.astype(jnp.bfloat16)
    factor = lax.rsqrt(jnp.mean(widened * widened, axis=-1, keepdims=True) + EPSILON)
    normed = (widened * factor * gain_ref[...].astype(jnp.float32)).astype(jnp.bfloat16)
    both = jnp.dot(normed, weight_ref[...], preferred_element_type=jnp.float32)
    cosine, sine = cos_ref[...], sin_ref[...]
    for head in range(PER_GROUP + 1):
        vector = both[:, head * HD : (head + 1) * HD]
        turned = vector * cosine + pltpu.roll(vector, HD // 2, 1) * sine
        if head < PER_GROUP:
            query_ref[:, head * HD : (head + 1) * HD] = turned.astype(jnp.bfloat16)
        else:
            key_ref[...] = turned.astype(jnp.bfloat16)
    value_ref[...] = both[:, (PER_GROUP + 1) * HD :].astype(jnp.bfloat16)


def attention_kernel(place_ref, length_ref, query_ref, key_ref, value_ref, prompt_ref, out_ref):
    session = pl.program_id(0)
    length = length_ref[session]
    scale = HD ** (-0.5) * math.log2(math.e)
    query = jnp.concatenate(
        [query_ref[:, h * HD : (h + 1) * HD] for h in range(PER_GROUP)], axis=0
    )
    ahead = lax.dot_general(query, prompt_ref[0, :, :HD], NT, preferred_element_type=jnp.float32)
    own = lax.dot_general(query, key_ref[...], NT, preferred_element_type=jnp.float32)
    row = lax.broadcasted_iota(jnp.int32, (SLOTS, SLOTS), 0)
    column = lax.broadcasted_iota(jnp.int32, (SLOTS, SLOTS), 1)
    allowed = (column <= row) & (column < length)
    own = jnp.where(jnp.concatenate([allowed] * PER_GROUP, axis=0), own, -1e30)
    highest = jnp.maximum(
        jnp.max(ahead, axis=-1, keepdims=True), jnp.max(own, axis=-1, keepdims=True)
    )
    powers = jnp.exp2((ahead - highest) * scale)
    own_powers = jnp.exp2((own - highest) * scale)
    total = jnp.sum(powers, axis=-1, keepdims=True) + jnp.sum(own_powers, axis=-1, keepdims=True)
    mixed = jnp.dot(
        powers.astype(jnp.bfloat16), prompt_ref[0, :, HD:], preferred_element_type=jnp.float32
    ) + jnp.dot(own_powers.astype(jnp.bfloat16), value_ref[...], preferred_element_type=jnp.float32)
    mixed = (mixed / total).astype(jnp.bfloat16)
    for h in range(PER_GROUP):
        out_ref[:, h * HD : (h + 1) * HD] = mixed[h * SLOTS : (h + 1) * SLOTS]


def make_states(code, slots, gain, weight, sessions, together):
    halves, blocks, rows, width = slots.shape
    steps = sessions // together
    model = halves * width
    cosine, sine = rope_tables(together)
    total = together * SLOTS
    out = jax.ShapeDtypeStruct
    row_spec = lambda w: pl.BlockSpec((total, w), lambda i: (i, 0))
    whole = lambda a: pl.BlockSpec(a.shape, lambda i: (0,) * a.ndim)
    gain = gain.reshape(1, model)
    return pl.pallas_call(
        states_kernel,
        grid=(steps,),
        in_specs=[
            pl.BlockSpec((1, 1, code.shape[2]), lambda i: (i, 0, 0)),
            pl.BlockSpec((halves, blocks, rows // steps, width), lambda i: (0, 0, i, 0)),
            whole(gain),
            whole(weight),
            whole(cosine),
            whole(sine),
        ],
        out_specs=[row_spec(model), row_spec(PER_GROUP * HD), row_spec(HD), row_spec(HD)],
        out_shape=[
            out((sessions * SLOTS, model), jnp.bfloat16),
            out((sessions * SLOTS, PER_GROUP * HD), jnp.bfloat16),
            out((sessions * SLOTS, HD), jnp.bfloat16),
            out((sessions * SLOTS, HD), jnp.bfloat16),
        ],
        compiler_params=pltpu.CompilerParams(vmem_limit_bytes=40 << 20),
        name="states",
    )(code, slots, gain, weight, jnp.asarray(cosine), jnp.asarray(sine))


def attend(place, lengths, query, key, value, prompts):
    sessions = place.shape[0]
    row_spec = lambda w: pl.BlockSpec((SLOTS, w), lambda i, place, length: (i, 0))
    return pl.pallas_call(
        attention_kernel,
        grid_spec=pltpu.PrefetchScalarGridSpec(
            num_scalar_prefetch=2,
            grid=(sessions,),
            in_specs=[
                row_spec(PER_GROUP * HD),
                row_spec(HD),
                row_spec(HD),
                pl.BlockSpec((1, PROMPT, 2 * HD), lambda i, place, length: (place[i], 0, 0)),
            ],
            out_specs=row_spec(PER_GROUP * HD),
        ),
        out_shape=jax.ShapeDtypeStruct((sessions * SLOTS, PER_GROUP * HD), jnp.bfloat16),
        compiler_params=pltpu.CompilerParams(vmem_limit_bytes=40 << 20),
        name="attend",
    )(place, lengths, query, key, value, prompts)


def general_body(
    thinker_rows,
    row_session,
    speaker_of,
    prompt_slot,
    prompt_cache,
    proj_weight,
    attn_gain,
    q_weight,
    k_weight,
    v_weight,
    o_weight,
):
    sess_count = lax.axis_size("sess")
    inner_count = lax.axis_size("inner")
    rep_count = lax.axis_size("rep")
    plane = inner_count * rep_count
    blocks = sess_count * rep_count
    session_all = speaker_of.shape[0]
    per_plane = session_all // sess_count
    per_device = per_plane // plane
    slot_cap = SLOTS // blocks
    held, tokens, channels = prompt_cache.shape
    model = proj_weight.shape[1]
    sharers = plane // KVH
    held_part = held // sharers
    sess_place = lax.axis_index("sess")
    plane_place = lax.axis_index("inner") * rep_count + lax.axis_index("rep")
    head = plane_place // sharers
    sharer = plane_place % sharers

    outgoing = jnp.transpose(
        prompt_cache.reshape(sharers, held_part, tokens, 2, KVH, HD), (4, 0, 1, 2, 3, 5)
    ).reshape(plane, held_part, tokens, 2 * HD)
    own_head = lax.all_to_all(outgoing, ("inner", "rep"), split_axis=0, concat_axis=2, tiled=True)
    own_head = own_head.reshape(held_part, plane * tokens, 2 * HD)
    prompts = lax.all_gather(own_head, "sess", axis=0, tiled=True)

    row_owner = row_session[:, 0]
    order = jnp.arange(row_owner.shape[0])
    same = row_owner[:, None] == row_owner[None, :]
    earlier = jnp.sum((same & (order[None, :] < order[:, None])).astype(jnp.int32), axis=1)
    row_slot = row_owner * slot_cap + earlier
    counts = jnp.sum(
        (row_owner[:, None] == jnp.arange(session_all)[None, :]).astype(jnp.int32), axis=0
    )
    all_counts = lax.all_gather(counts, ("sess", "rep"), axis=0, tiled=False)

    partial_sum = jnp.dot(thinker_rows, proj_weight, preferred_element_type=jnp.float32)
    width = model // inner_count
    if inner_count == 2:
        inner_place = lax.axis_index("inner")
        kept = lax.dynamic_slice_in_dim(partial_sum, inner_place * width, width, 1)
        sent = lax.dynamic_slice_in_dim(partial_sum, (1 - inner_place) * width, width, 1)
        came = lax.ppermute(sent.astype(jnp.bfloat16), "inner", [(0, 1), (1, 0)])
        own_columns = (kept + came.astype(jnp.float32)).astype(jnp.bfloat16)
    else:
        own_columns = lax.psum_scatter(
            partial_sum, "inner", scatter_dimension=1, tiled=True
        ).astype(jnp.bfloat16)
    into = (jnp.arange(session_all * slot_cap)[:, None] == row_slot[None, :]).astype(jnp.bfloat16)
    buffer = jnp.dot(into, own_columns, preferred_element_type=jnp.float32).astype(jnp.bfloat16)
    arrived = lax.all_to_all(
        buffer.reshape(sess_count, per_plane * slot_cap, width),
        "sess",
        split_axis=0,
        concat_axis=0,
        tiled=True,
    )
    spread = lax.all_gather(arrived, ("inner", "rep"), axis=0, tiled=False)
    slots = spread.reshape(inner_count, rep_count * sess_count, per_plane * slot_cap, width)

    offsets = jnp.cumsum(all_counts, axis=0) - all_counts
    lengths_all = jnp.sum(all_counts, axis=0)
    mine = lambda a: lax.dynamic_slice_in_dim(a, sess_place * per_plane, per_plane, a.ndim - 1)
    by_block = lambda a: jnp.transpose(
        mine(a).reshape(sess_count, rep_count, per_plane), (1, 0, 2)
    ).reshape(blocks, per_plane)
    lengths = mine(lengths_all)
    together = 16 // math.gcd(16, slot_cap)
    within = jnp.arange(slot_cap)
    local = (jnp.arange(per_plane) % together)[None, :, None] * SLOTS
    code = jnp.where(
        within[None, None, :] < by_block(all_counts)[:, :, None],
        by_block(offsets)[:, :, None] + within[None, None, :] + local,
        -1,
    )
    steps = per_plane // together
    code = jnp.transpose(
        code.reshape(blocks, steps, together * slot_cap), (1, 0, 2)
    ).reshape(steps, 1, blocks * together * slot_cap)

    group_width = PER_GROUP * HD
    weight = jnp.concatenate(
        [
            lax.dynamic_slice_in_dim(q_weight, head * group_width, group_width, 1),
            lax.dynamic_slice_in_dim(k_weight, head * HD, HD, 1),
            lax.dynamic_slice_in_dim(v_weight, head * HD, HD, 1),
        ],
        axis=1,
    )
    states, query, key, value = make_states(
        code, slots, attn_gain, weight, per_plane, together
    )

    wanted_slot = jnp.sum(
        jnp.where(
            mine(speaker_of)[:, None] == jnp.arange(prompt_slot.shape[0])[None, :],
            prompt_slot[None, :],
            0,
        ),
        axis=1,
    )
    place = wanted_slot // held * held_part + wanted_slot % held_part
    attended = attend(place, lengths, query, key, value, prompts)
    returned = lax.all_to_all(
        attended.reshape(plane, per_device * SLOTS, group_width),
        ("inner", "rep"),
        split_axis=0,
        concat_axis=0,
        tiled=True,
    ).reshape(KVH, sharers, per_device, SLOTS, group_width)
    first = plane_place * per_device
    if sharers > 1:
        holder = lax.dynamic_slice_in_dim(wanted_slot % held // held_part, first, per_device)
        chosen = jnp.zeros_like(returned[:, 0])
        for t in range(sharers):
            chosen = jnp.where((holder == t)[None, :, None, None], returned[:, t], chosen)
    else:
        chosen = returned[:, 0]
    gathered = jnp.transpose(chosen, (1, 2, 0, 3)).reshape(per_device * SLOTS, H * HD)
    own_states = lax.dynamic_slice_in_dim(states, first * SLOTS, per_device * SLOTS, 0)
    own_lengths = lax.dynamic_slice_in_dim(lengths, first, per_device)
    summed = own_states.astype(jnp.float32) + jnp.dot(
        gathered, o_weight, preferred_element_type=jnp.float32
    )
    live_rows = (jnp.arange(SLOTS)[None, :] < own_lengths[:, None]).reshape(-1, 1)
    return (
        jnp.where(live_rows, summed, 0.0)
        .astype(jnp.bfloat16)
        .reshape(per_device, SLOTS, model)
    )


EXTRA = 16
SMEM = pl.BlockSpec(memory_space=pltpu.SMEM)
VMEM = pl.BlockSpec(memory_space=pltpu.VMEM)
ANY = pl.BlockSpec(memory_space=pl.ANY)


def split_heads_kernel(head_ref, cache_ref, *refs):
    out_refs, sem = refs[:-1], refs[-1]
    copies = []
    for by, out_ref in enumerate(out_refs):
        for side in range(2):
            start = pl.multiple_of((head_ref[0] ^ by) * HD + side * KVH * HD, HD)
            copies.append(
                pltpu.make_async_copy(
                    cache_ref.at[:, :, pl.ds(start, HD)],
                    out_ref.at[:, :, side * HD : (side + 1) * HD],
                    sem.at[by, side],
                )
            )
    for copy in copies:
        copy.start()
    for copy in copies:
        copy.wait()


def split_heads(head, cache):
    held, tokens, _ = cache.shape
    shape = jax.ShapeDtypeStruct((held, tokens, 2 * HD), cache.dtype)
    return pl.pallas_call(
        split_heads_kernel,
        in_specs=[SMEM, ANY],
        out_specs=[ANY] * KVH,
        out_shape=[shape] * KVH,
        scratch_shapes=[pltpu.SemaphoreType.DMA((KVH, 2))],
        cost_estimate=pl.CostEstimate(flops=0, bytes_accessed=2 * cache.size * 2, transcendentals=0),
        name="split_heads",
    )(head, cache)


def stack_kernel(*refs):
    in_refs, (out_ref, sem) = refs[:-2], refs[-2:]
    copies = []
    place = 0
    for i, in_ref in enumerate(in_refs):
        count = in_ref.shape[0]
        copies.append(
            pltpu.make_async_copy(in_ref, out_ref.at[place : place + count], sem.at[i])
        )
        place += count
    for copy in copies:
        copy.start()
    for copy in copies:
        copy.wait()


def stack(*arrays):
    total = sum(a.shape[0] for a in arrays)
    size = sum(a.size for a in arrays)
    return pl.pallas_call(
        stack_kernel,
        in_specs=[ANY] * len(arrays),
        out_specs=ANY,
        out_shape=jax.ShapeDtypeStruct((total,) + arrays[0].shape[1:], arrays[0].dtype),
        scratch_shapes=[pltpu.SemaphoreType.DMA((len(arrays),))],
        cost_estimate=pl.CostEstimate(flops=0, bytes_accessed=4 * size, transcendentals=0),
        name="stack",
    )(*arrays)


def route_kernel(z_ref, kept_ref, came_ref, owner_ref, owner_row_ref, *out_refs,
                 slot_cap, per_plane):
    rows = kept_ref.shape[0]
    planes = len(out_refs)
    size = out_refs[0].shape[0]
    live = per_plane * slot_cap
    columns = (kept_ref[...] + came_ref[...].astype(jnp.float32)).astype(jnp.bfloat16)
    owner, owner_row = owner_ref[...], owner_row_ref[...]
    above = lax.broadcasted_iota(jnp.int32, (rows, rows), 0)
    beside = lax.broadcasted_iota(jnp.int32, (rows, rows), 1)
    earlier = jnp.sum(
        jnp.where((owner == owner_row) & (above < beside), 1.0, 0.0), axis=0, keepdims=True
    ).astype(jnp.int32)
    target = lax.div(owner_row, per_plane) ^ z_ref[0]
    code = target * size + lax.rem(owner_row, per_plane) * slot_cap + earlier
    place = lax.broadcasted_iota(jnp.int32, (planes * size, rows), 0)
    into = (place == code).astype(jnp.bfloat16)
    routed = jnp.dot(into, columns, preferred_element_type=jnp.float32).astype(jnp.bfloat16)
    lane = lax.broadcasted_iota(jnp.int32, (rows, HD), 1)
    named = (lane == owner).astype(jnp.bfloat16)
    counts = jnp.dot(
        jnp.ones((EXTRA, rows), jnp.bfloat16), named, preferred_element_type=jnp.float32
    ).astype(jnp.bfloat16)
    for k, out_ref in enumerate(out_refs):
        out_ref[:live] = routed[k * size : k * size + live]
        out_ref[live:] = jnp.zeros((EXTRA, out_ref.shape[1]), jnp.bfloat16)
        out_ref[live:, :HD] = counts


def route(z, kept, came, row_session, planes, per_plane, slot_cap):
    width = kept.shape[1]
    rows = row_session.shape[0]
    size = per_plane * slot_cap + EXTRA
    return pl.pallas_call(
        functools.partial(route_kernel, slot_cap=slot_cap, per_plane=per_plane),
        in_specs=[SMEM] + [VMEM] * 4,
        out_specs=[VMEM] * planes,
        out_shape=[jax.ShapeDtypeStruct((size, width), jnp.bfloat16)] * planes,
        cost_estimate=pl.CostEstimate(
            flops=2 * planes * size * rows * width, bytes_accessed=rows * width * 8, transcendentals=0
        ),
        name="route",
    )(z, kept, came, row_session, row_session.reshape(1, rows))


def place_kernel(index_ref, mine_ref, core_ref, gain_ref, weight_ref, cos_ref, sin_ref,
                 states_ref, query_ref, key_ref, value_ref, length_ref, *, slot_cap, together):
    z, x, c = index_ref[0], index_ref[1], index_ref[2]
    planes = mine_ref.shape[0] // 2
    blocks = 2 * planes
    width = mine_ref.shape[2]
    live = mine_ref.shape[1] - EXTRA
    per_plane = live // slot_cap
    steps = per_plane // together
    window = together * slot_cap
    total = together * SLOTS
    counts = jnp.concatenate(
        [ref[k, live : live + 1, :HD] for ref in (mine_ref, core_ref) for k in range(planes)],
        axis=0,
    ).astype(jnp.float32)
    kind = lambda axis: lax.broadcasted_iota(jnp.int32, (blocks, blocks), axis)
    true_block = lambda k: (z ^ (k % planes)) * 2 + (c ^ (k // planes))
    before = (true_block(kind(1)) < true_block(kind(0))).astype(jnp.float32)
    offsets = jnp.dot(before, counts, preferred_element_type=jnp.float32)
    session_lane = lax.broadcasted_iota(jnp.int32, (HD, HD), 0)
    local_lane = lax.broadcasted_iota(jnp.int32, (HD, HD), 1)
    ours = (session_lane == z * per_plane + local_lane).astype(jnp.float32)
    sums = jnp.dot(
        jnp.broadcast_to(jnp.sum(counts, axis=0, keepdims=True), (8, HD)),
        ours,
        preferred_element_type=jnp.float32,
    )
    length_ref[...] = sums[:1].astype(jnp.int32)
    cosine, sine = cos_ref[...], sin_ref[...]
    gain = gain_ref[...].astype(jnp.float32)
    for step in range(steps):
        slot = lax.broadcasted_iota(jnp.int32, (blocks, blocks * window), 1)
        in_block = slot % window
        spread = lax.broadcasted_iota(jnp.int32, (HD, blocks * window), 1) % window // slot_cap
        from_lane = lax.broadcasted_iota(jnp.int32, (HD, blocks * window), 0)
        expand = (from_lane == z * per_plane + step * together + spread).astype(jnp.float32)
        here = jnp.dot(counts, expand, preferred_element_type=jnp.float32).astype(jnp.int32)
        start = jnp.dot(offsets, expand, preferred_element_type=jnp.float32).astype(jnp.int32)
        within = in_block % slot_cap
        row = jnp.where(within < here, start + within + in_block // slot_cap * SLOTS, -1)
        block = lax.broadcasted_iota(jnp.int32, (blocks, blocks * window), 0)
        code = jnp.max(jnp.where(slot // window == block, row, -1), axis=0, keepdims=True)
        place = lax.broadcasted_iota(jnp.int32, (total, blocks * window), 0)
        pick = (place == code).astype(jnp.bfloat16)
        slots = slice(step * window, (step + 1) * window)
        near, far = [
            jnp.dot(
                pick,
                jnp.concatenate(
                    [ref[half * planes + k, slots] for ref in (mine_ref, core_ref) for k in range(planes)],
                    axis=0,
                ),
                preferred_element_type=jnp.float32,
            )
            for half in range(2)
        ]
        widened = jnp.concatenate(
            [jnp.where(x == 0, near, far), jnp.where(x == 0, far, near)], axis=1
        )
        rows = slice(step * total, (step + 1) * total)
        states_ref[rows] = widened.astype(jnp.bfloat16)
        factor = lax.rsqrt(jnp.mean(widened * widened, axis=-1, keepdims=True) + EPSILON)
        normed = (widened * factor * gain).astype(jnp.bfloat16)
        both = jnp.dot(normed, weight_ref[...], preferred_element_type=jnp.float32)
        for h in range(PER_GROUP + 1):
            vector = both[:, h * HD : (h + 1) * HD]
            turned = vector * cosine + pltpu.roll(vector, HD // 2, 1) * sine
            if h < PER_GROUP:
                query_ref[rows, h * HD : (h + 1) * HD] = turned.astype(jnp.bfloat16)
            else:
                key_ref[rows] = turned.astype(jnp.bfloat16)
        value_ref[rows] = both[:, (PER_GROUP + 1) * HD :].astype(jnp.bfloat16)


def place_rows(index, mine, core, gain, weight, sessions, slot_cap):
    together = 16 // math.gcd(16, slot_cap)
    cosine, sine = rope_tables(together)
    model = 2 * mine.shape[2]
    total = sessions * SLOTS
    out = lambda w: jax.ShapeDtypeStruct((total, w), jnp.bfloat16)
    return pl.pallas_call(
        functools.partial(place_kernel, slot_cap=slot_cap, together=together),
        in_specs=[SMEM] + [VMEM] * 6,
        out_specs=[VMEM] * 5,
        out_shape=[
            out(model), out(PER_GROUP * HD), out(HD), out(HD),
            jax.ShapeDtypeStruct((1, HD), jnp.int32),
        ],
        compiler_params=pltpu.CompilerParams(vmem_limit_bytes=40 << 20),
        cost_estimate=pl.CostEstimate(
            flops=4 * total * model * weight.shape[1], bytes_accessed=6 << 20, transcendentals=0
        ),
        name="place_rows",
    )(index, mine, core, gain.reshape(1, model), weight, jnp.asarray(cosine), jnp.asarray(sine))


def session_attention(query_ref, key_ref, value_ref, kv, session, length):
    scale = HD ** (-0.5) * math.log2(math.e)
    rows = pl.ds(pl.multiple_of(session * SLOTS, SLOTS), SLOTS)
    query = jnp.concatenate(
        [query_ref[rows, h * HD : (h + 1) * HD] for h in range(PER_GROUP)], axis=0
    )
    tokens = kv.reshape(PROMPT, 2 * HD)
    ahead = lax.dot_general(query, tokens[:, :HD], NT, preferred_element_type=jnp.float32)
    own = lax.dot_general(query, key_ref[rows, :], NT, preferred_element_type=jnp.float32)
    row = lax.broadcasted_iota(jnp.int32, (SLOTS, SLOTS), 0)
    column = lax.broadcasted_iota(jnp.int32, (SLOTS, SLOTS), 1)
    allowed = (column <= row) & (column < length)
    own = jnp.where(jnp.concatenate([allowed] * PER_GROUP, axis=0), own, -1e30)
    highest = jnp.maximum(
        jnp.max(ahead, axis=-1, keepdims=True), jnp.max(own, axis=-1, keepdims=True)
    )
    powers = jnp.exp2((ahead - highest) * scale)
    own_powers = jnp.exp2((own - highest) * scale)
    total = jnp.sum(powers, axis=-1, keepdims=True) + jnp.sum(own_powers, axis=-1, keepdims=True)
    mixed = jnp.dot(
        powers.astype(jnp.bfloat16), tokens[:, HD:], preferred_element_type=jnp.float32
    ) + jnp.dot(own_powers.astype(jnp.bfloat16), value_ref[rows, :], preferred_element_type=jnp.float32)
    return (mixed / total).astype(jnp.bfloat16)


def hops_kernel(index_ref, hop_ref, held_ref, length_ref, query_ref, key_ref, value_ref, *refs,
                hops, carried):
    if carried:
        before_ref, *refs = refs
    count = KVH if carried else 1
    prompt_refs, out_refs = refs[: 2 * len(hops)], refs[2 * len(hops) : 2 * len(hops) + count]
    kv, sem = refs[-2:]
    sessions = hop_ref.shape[0]
    per_device = sessions // KVH

    def copies(session, which):
        return [
            pltpu.make_async_copy(
                prompt_refs[2 * which + chunk].at[:, held_ref[session]],
                kv.at[session, chunk],
                sem.at[session, chunk],
            )
            for chunk in range(2)
        ]

    def fetch(session, _):
        for which, hop in enumerate(hops):
            @pl.when(hop_ref[session] == hop)
            def _():
                for copy in copies(session, which):
                    copy.start()
        return 0

    def store(session, block):
        def into(out_ref, first):
            rows = pl.ds(pl.multiple_of(first * SLOTS, SLOTS), SLOTS)
            if block.shape[0] == SLOTS:
                out_ref[rows] = block
            else:
                for h in range(PER_GROUP):
                    out_ref[rows, h * HD : (h + 1) * HD] = block[h * SLOTS : (h + 1) * SLOTS]

        if not carried:
            into(out_refs[0], session)
            return
        for by, out_ref in enumerate(out_refs):
            @pl.when((lax.div(session, per_device) ^ index_ref[3]) == by)
            def _():
                into(out_ref, lax.rem(session, per_device))

    lax.fori_loop(0, sessions, fetch, 0)

    def work(session, _):
        ours = hop_ref[session] == hops[0]
        for hop in hops[1:]:
            ours = ours | (hop_ref[session] == hop)
        if carried:
            @pl.when(jnp.logical_not(ours))
            def _():
                rows = pl.ds(pl.multiple_of(session * SLOTS, SLOTS), SLOTS)
                store(session, before_ref[rows])

        @pl.when(ours)
        def _():
            for copy in copies(session, 0):
                copy.wait()
            store(
                session,
                session_attention(
                    query_ref, key_ref, value_ref, kv[session], session, length_ref[0, session]
                ),
            )

        return 0

    lax.fori_loop(0, sessions, work, 0)


def attend_hops(index, hop, held, lengths, query, key, value, prompts, hops, before):
    sessions = hop.shape[0]
    carried = before is not None
    pieces = [piece for h in hops for piece in prompts[h]]
    work = sessions * len(hops) // 7 + 1
    width = PER_GROUP * HD
    if carried:
        out_shape = [jax.ShapeDtypeStruct((sessions // KVH * SLOTS, width), jnp.bfloat16)] * KVH
    else:
        out_shape = jax.ShapeDtypeStruct((sessions * SLOTS, width), jnp.bfloat16)
    return pl.pallas_call(
        functools.partial(hops_kernel, hops=hops, carried=carried),
        in_specs=[SMEM] * 4 + [VMEM] * (3 + carried) + [ANY] * len(pieces),
        out_specs=[VMEM] * KVH if carried else VMEM,
        out_shape=out_shape,
        scratch_shapes=[
            pltpu.VMEM((sessions, 2, 2, PROMPT // 4, 2 * HD), jnp.bfloat16),
            pltpu.SemaphoreType.DMA((sessions, 2)),
        ],
        compiler_params=pltpu.CompilerParams(vmem_limit_bytes=40 << 20),
        cost_estimate=pl.CostEstimate(
            flops=work * 4 * PER_GROUP * SLOTS * (PROMPT + SLOTS) * HD,
            bytes_accessed=work * PROMPT * 4 * HD,
            transcendentals=work * PER_GROUP * SLOTS * (PROMPT + SLOTS),
        ),
        name="attend",
    )(index, hop, held, lengths, query, key, value, *([before] if carried else []), *pieces)


def output_kernel(index_ref, length_ref, states_ref, weight_ref, *refs):
    piece_refs, out_ref = refs[:-1], refs[-1]
    head = index_ref[3]
    group_width = PER_GROUP * HD
    per_device = out_ref.shape[0]
    total = per_device * SLOTS
    summed = states_ref[pl.ds(pl.multiple_of(head * total, SLOTS), total)].astype(jnp.float32)
    for by, piece_ref in enumerate(piece_refs):
        start = pl.multiple_of((head ^ by) * group_width, group_width)
        summed = summed + jnp.dot(
            piece_ref[...], weight_ref[pl.ds(start, group_width)], preferred_element_type=jnp.float32
        )
    row = lax.broadcasted_iota(jnp.int32, (SLOTS, 1), 0)
    for i in range(per_device):
        live = row < length_ref[0, head * per_device + i]
        part = summed[i * SLOTS : (i + 1) * SLOTS]
        out_ref[i] = jnp.where(live, part, 0.0).astype(jnp.bfloat16)


def output(index, lengths, states, o_weight, pieces, per_device):
    model = o_weight.shape[1]
    return pl.pallas_call(
        output_kernel,
        in_specs=[SMEM] * 2 + [VMEM] * (2 + len(pieces)),
        out_specs=VMEM,
        out_shape=jax.ShapeDtypeStruct((per_device, SLOTS, model), jnp.bfloat16),
        compiler_params=pltpu.CompilerParams(vmem_limit_bytes=40 << 20),
        cost_estimate=pl.CostEstimate(
            flops=2 * per_device * SLOTS * o_weight.size, bytes_accessed=o_weight.size * 2, transcendentals=0
        ),
        name="output",
    )(index, lengths, states, o_weight, *pieces)


def shifted(n, by):
    return [(i, i + by) for i in range(n) if 0 <= i + by < n]


def swapped(n, by):
    return [(i, i ^ by) for i in range(n)]


def line_body(
    thinker_rows,
    row_session,
    speaker_of,
    prompt_slot,
    prompt_cache,
    proj_weight,
    attn_gain,
    q_weight,
    k_weight,
    v_weight,
    o_weight,
):
    planes, plane, rep_count = lax.axis_size("sess"), KVH, 2
    blocks = planes * rep_count
    session_all = speaker_of.shape[0]
    per_plane = session_all // planes
    per_device = per_plane // plane
    slot_cap = SLOTS // blocks
    held = prompt_cache.shape[0]
    model = proj_weight.shape[1]
    width = model // 2
    z, x, c = lax.axis_index("sess"), lax.axis_index("inner"), lax.axis_index("rep")
    head = x * rep_count + c
    index = jnp.stack([z, x, c, head]).astype(jnp.int32)
    pair = ("inner", "rep")

    own, to_core, to_x, to_far = split_heads(head.reshape(1), prompt_cache)
    from_core = lax.ppermute(to_core, pair, swapped(4, 1))
    from_x = lax.ppermute(to_x, pair, swapped(4, 2))
    from_far = lax.ppermute(to_far, pair, swapped(4, 3))
    first = stack(own[None], from_core[None])
    second = stack(from_x[None], from_far[None])
    right = [first, second]
    left = [first, second]
    prompts = {0: (first, second)}
    for hop in range(1, planes):
        for chunk in range(2):
            right[chunk] = lax.ppermute(right[chunk], "sess", shifted(planes, 1))
            left[chunk] = lax.ppermute(left[chunk], "sess", shifted(planes, -1))
        prompts[-hop], prompts[hop] = tuple(right), tuple(left)

    thinker_rows, _ = lax.optimization_barrier((thinker_rows, (prompts[-1][0], prompts[1][0])))
    partial_sum = jnp.dot(thinker_rows, proj_weight, preferred_element_type=jnp.float32)
    kept = lax.dynamic_slice_in_dim(partial_sum, x * width, width, 1)
    sent = lax.dynamic_slice_in_dim(partial_sum, (1 - x) * width, width, 1)
    came = lax.ppermute(sent.astype(jnp.bfloat16), "inner", swapped(2, 1))
    came, _ = lax.optimization_barrier((came, (prompts[-1][1], prompts[1][1])))
    routed = route(z.reshape(1), kept, came, row_session, planes, per_plane, slot_cap)
    routed, _ = lax.optimization_barrier((tuple(routed), (prompts[-2][0], prompts[2][0])))
    arrived = [routed[0]] + [
        lax.ppermute(routed[by], "sess", swapped(planes, by)) for by in range(1, planes)
    ]
    arrived, _ = lax.optimization_barrier((arrived, (prompts[-2][1], prompts[2][1])))
    arrived = stack(*[a[None] for a in arrived])
    mine = stack(arrived, lax.ppermute(arrived, "inner", swapped(2, 1)))
    core = lax.ppermute(mine, "rep", swapped(2, 1))

    group_width = PER_GROUP * HD
    weight = jnp.concatenate(
        [
            lax.dynamic_slice_in_dim(q_weight, head * group_width, group_width, 1),
            lax.dynamic_slice_in_dim(k_weight, head * HD, HD, 1),
            lax.dynamic_slice_in_dim(v_weight, head * HD, HD, 1),
        ],
        axis=1,
    )
    states, query, key, value, lengths = place_rows(
        index, mine, core, attn_gain, weight, per_plane, slot_cap
    )

    speakers = lax.dynamic_slice_in_dim(speaker_of, z * per_plane, per_plane)
    wanted_slot = jnp.sum(
        jnp.where(
            speakers[:, None] == jnp.arange(prompt_slot.shape[0])[None, :], prompt_slot[None, :], 0
        ),
        axis=1,
    )
    hop = wanted_slot // held - z
    which = wanted_slot % held
    near = attend_hops(
        index, hop, which, lengths, query, key, value, prompts, (0, -1, 1, -2, 2), None
    )
    attended = attend_hops(
        index, hop, which, lengths, query, key, value, prompts, (-3, 3), near
    )

    pieces = [attended[0]] + [
        lax.ppermute(attended[by], pair, swapped(4, by)) for by in range(1, plane)
    ]
    return output(index, lengths, states, o_weight, pieces, per_device)


def solution(mesh):
    in_specs = (
        P(("groups", "sess", "rep"), "inner"),
        P(("groups", "sess", "rep"), None),
        P("groups"),
        P("groups"),
        P(("groups", "sess"), ("inner", "rep"), None),
        P("inner", None),
        P(),
        P(),
        P(),
        P(),
        P(),
    )
    out_specs = P(("groups", "sess", "inner", "rep"), None, None)
    sizes = tuple(mesh.shape[name] for name in ("sess", "inner", "rep"))
    body = line_body if sizes == (4, 2, 2) else general_body
    return jax.shard_map(body, mesh=mesh, in_specs=in_specs, out_specs=out_specs, check_vma=False)
```

```python
import functools
import math

import jax
import jax.numpy as jnp
import numpy as np
from jax import lax
from jax.experimental import pallas as pl
from jax.experimental.pallas import tpu as pltpu
from jax.sharding import PartitionSpec as P

H = 12
KVH = 4
HD = 128
PROMPT = 1024
SLOTS = 96
PER_GROUP = H // KVH

EPSILON = 1e-06
ROPE_BASE = 1000000.0
NT = (((1,), (1,)), ((), ()))


def rope_tables(copies):
    half_width = HD // 2
    inverse = ROPE_BASE ** (-(np.arange(half_width, dtype=np.float64) * 2.0) / HD)
    angles = (PROMPT + np.arange(SLOTS, dtype=np.float64))[:, None] * inverse[None, :]
    cosine = np.concatenate([np.cos(angles), np.cos(angles)], axis=1)
    sine = np.concatenate([-np.sin(angles), np.sin(angles)], axis=1)
    return (
        np.tile(cosine, (copies, 1)).astype(np.float32),
        np.tile(sine, (copies, 1)).astype(np.float32),
    )


def states_kernel(code_ref, slots_ref, gain_ref, weight_ref, cos_ref, sin_ref,
                  states_ref, query_ref, key_ref, value_ref):
    halves, blocks, rows, width = slots_ref.shape
    total = states_ref.shape[0]
    place = lax.broadcasted_iota(jnp.int32, (total, blocks * rows), 0)
    pick = (place == code_ref[0]).astype(jnp.bfloat16)
    parts = [
        jnp.dot(
            pick,
            slots_ref[half].reshape(blocks * rows, width),
            preferred_element_type=jnp.float32,
        )
        for half in range(halves)
    ]
    widened = jnp.concatenate(parts, axis=1)
    states_ref[...] = widened.astype(jnp.bfloat16)
    factor = lax.rsqrt(jnp.mean(widened * widened, axis=-1, keepdims=True) + EPSILON)
    normed = (widened * factor * gain_ref[...].astype(jnp.float32)).astype(jnp.bfloat16)
    both = jnp.dot(normed, weight_ref[...], preferred_element_type=jnp.float32)
    cosine, sine = cos_ref[...], sin_ref[...]
    for head in range(PER_GROUP + 1):
        vector = both[:, head * HD : (head + 1) * HD]
        turned = vector * cosine + pltpu.roll(vector, HD // 2, 1) * sine
        if head < PER_GROUP:
            query_ref[:, head * HD : (head + 1) * HD] = turned.astype(jnp.bfloat16)
        else:
            key_ref[...] = turned.astype(jnp.bfloat16)
    value_ref[...] = both[:, (PER_GROUP + 1) * HD :].astype(jnp.bfloat16)


def attention_kernel(place_ref, length_ref, query_ref, key_ref, value_ref, prompt_ref, out_ref):
    session = pl.program_id(0)
    length = length_ref[session]
    scale = HD ** (-0.5) * math.log2(math.e)
    query = jnp.concatenate(
        [query_ref[:, h * HD : (h + 1) * HD] for h in range(PER_GROUP)], axis=0
    )
    ahead = lax.dot_general(query, prompt_ref[0, :, :HD], NT, preferred_element_type=jnp.float32)
    own = lax.dot_general(query, key_ref[...], NT, preferred_element_type=jnp.float32)
    row = lax.broadcasted_iota(jnp.int32, (SLOTS, SLOTS), 0)
    column = lax.broadcasted_iota(jnp.int32, (SLOTS, SLOTS), 1)
    allowed = (column <= row) & (column < length)
    own = jnp.where(jnp.concatenate([allowed] * PER_GROUP, axis=0), own, -1e30)
    highest = jnp.maximum(
        jnp.max(ahead, axis=-1, keepdims=True), jnp.max(own, axis=-1, keepdims=True)
    )
    powers = jnp.exp2((ahead - highest) * scale)
    own_powers = jnp.exp2((own - highest) * scale)
    total = jnp.sum(powers, axis=-1, keepdims=True) + jnp.sum(own_powers, axis=-1, keepdims=True)
    mixed = jnp.dot(
        powers.astype(jnp.bfloat16), prompt_ref[0, :, HD:], preferred_element_type=jnp.float32
    ) + jnp.dot(own_powers.astype(jnp.bfloat16), value_ref[...], preferred_element_type=jnp.float32)
    mixed = (mixed / total).astype(jnp.bfloat16)
    for h in range(PER_GROUP):
        out_ref[:, h * HD : (h + 1) * HD] = mixed[h * SLOTS : (h + 1) * SLOTS]


def make_states(code, slots, gain, weight, sessions, together):
    halves, blocks, rows, width = slots.shape
    steps = sessions // together
    model = halves * width
    cosine, sine = rope_tables(together)
    total = together * SLOTS
    out = jax.ShapeDtypeStruct
    row_spec = lambda w: pl.BlockSpec((total, w), lambda i: (i, 0))
    whole = lambda a: pl.BlockSpec(a.shape, lambda i: (0,) * a.ndim)
    gain = gain.reshape(1, model)
    return pl.pallas_call(
        states_kernel,
        grid=(steps,),
        in_specs=[
            pl.BlockSpec((1, 1, code.shape[2]), lambda i: (i, 0, 0)),
            pl.BlockSpec((halves, blocks, rows // steps, width), lambda i: (0, 0, i, 0)),
            whole(gain),
            whole(weight),
            whole(cosine),
            whole(sine),
        ],
        out_specs=[row_spec(model), row_spec(PER_GROUP * HD), row_spec(HD), row_spec(HD)],
        out_shape=[
            out((sessions * SLOTS, model), jnp.bfloat16),
            out((sessions * SLOTS, PER_GROUP * HD), jnp.bfloat16),
            out((sessions * SLOTS, HD), jnp.bfloat16),
            out((sessions * SLOTS, HD), jnp.bfloat16),
        ],
        compiler_params=pltpu.CompilerParams(vmem_limit_bytes=40 << 20),
        name="states",
    )(code, slots, gain, weight, jnp.asarray(cosine), jnp.asarray(sine))


def attend(place, lengths, query, key, value, prompts):
    sessions = place.shape[0]
    row_spec = lambda w: pl.BlockSpec((SLOTS, w), lambda i, place, length: (i, 0))
    return pl.pallas_call(
        attention_kernel,
        grid_spec=pltpu.PrefetchScalarGridSpec(
            num_scalar_prefetch=2,
            grid=(sessions,),
            in_specs=[
                row_spec(PER_GROUP * HD),
                row_spec(HD),
                row_spec(HD),
                pl.BlockSpec((1, PROMPT, 2 * HD), lambda i, place, length: (place[i], 0, 0)),
            ],
            out_specs=row_spec(PER_GROUP * HD),
        ),
        out_shape=jax.ShapeDtypeStruct((sessions * SLOTS, PER_GROUP * HD), jnp.bfloat16),
        compiler_params=pltpu.CompilerParams(vmem_limit_bytes=40 << 20),
        name="attend",
    )(place, lengths, query, key, value, prompts)


def general_body(
    thinker_rows,
    row_session,
    speaker_of,
    prompt_slot,
    prompt_cache,
    proj_weight,
    attn_gain,
    q_weight,
    k_weight,
    v_weight,
    o_weight,
):
    sess_count = lax.axis_size("sess")
    inner_count = lax.axis_size("inner")
    rep_count = lax.axis_size("rep")
    plane = inner_count * rep_count
    blocks = sess_count * rep_count
    session_all = speaker_of.shape[0]
    per_plane = session_all // sess_count
    per_device = per_plane // plane
    slot_cap = SLOTS // blocks
    held, tokens, channels = prompt_cache.shape
    model = proj_weight.shape[1]
    sharers = plane // KVH
    held_part = held // sharers
    sess_place = lax.axis_index("sess")
    plane_place = lax.axis_index("inner") * rep_count + lax.axis_index("rep")
    head = plane_place // sharers
    sharer = plane_place % sharers

    outgoing = jnp.transpose(
        prompt_cache.reshape(sharers, held_part, tokens, 2, KVH, HD), (4, 0, 1, 2, 3, 5)
    ).reshape(plane, held_part, tokens, 2 * HD)
    own_head = lax.all_to_all(outgoing, ("inner", "rep"), split_axis=0, concat_axis=2, tiled=True)
    own_head = own_head.reshape(held_part, plane * tokens, 2 * HD)
    prompts = lax.all_gather(own_head, "sess", axis=0, tiled=True)

    row_owner = row_session[:, 0]
    order = jnp.arange(row_owner.shape[0])
    same = row_owner[:, None] == row_owner[None, :]
    earlier = jnp.sum((same & (order[None, :] < order[:, None])).astype(jnp.int32), axis=1)
    row_slot = row_owner * slot_cap + earlier
    counts = jnp.sum(
        (row_owner[:, None] == jnp.arange(session_all)[None, :]).astype(jnp.int32), axis=0
    )
    all_counts = lax.all_gather(counts, ("sess", "rep"), axis=0, tiled=False)

    partial_sum = jnp.dot(thinker_rows, proj_weight, preferred_element_type=jnp.float32)
    width = model // inner_count
    if inner_count == 2:
        inner_place = lax.axis_index("inner")
        kept = lax.dynamic_slice_in_dim(partial_sum, inner_place * width, width, 1)
        sent = lax.dynamic_slice_in_dim(partial_sum, (1 - inner_place) * width, width, 1)
        came = lax.ppermute(sent.astype(jnp.bfloat16), "inner", [(0, 1), (1, 0)])
        own_columns = (kept + came.astype(jnp.float32)).astype(jnp.bfloat16)
    else:
        own_columns = lax.psum_scatter(
            partial_sum, "inner", scatter_dimension=1, tiled=True
        ).astype(jnp.bfloat16)
    into = (jnp.arange(session_all * slot_cap)[:, None] == row_slot[None, :]).astype(jnp.bfloat16)
    buffer = jnp.dot(into, own_columns, preferred_element_type=jnp.float32).astype(jnp.bfloat16)
    arrived = lax.all_to_all(
        buffer.reshape(sess_count, per_plane * slot_cap, width),
        "sess",
        split_axis=0,
        concat_axis=0,
        tiled=True,
    )
    spread = lax.all_gather(arrived, ("inner", "rep"), axis=0, tiled=False)
    slots = spread.reshape(inner_count, rep_count * sess_count, per_plane * slot_cap, width)

    offsets = jnp.cumsum(all_counts, axis=0) - all_counts
    lengths_all = jnp.sum(all_counts, axis=0)
    mine = lambda a: lax.dynamic_slice_in_dim(a, sess_place * per_plane, per_plane, a.ndim - 1)
    by_block = lambda a: jnp.transpose(
        mine(a).reshape(sess_count, rep_count, per_plane), (1, 0, 2)
    ).reshape(blocks, per_plane)
    lengths = mine(lengths_all)
    together = 16 // math.gcd(16, slot_cap)
    within = jnp.arange(slot_cap)
    local = (jnp.arange(per_plane) % together)[None, :, None] * SLOTS
    code = jnp.where(
        within[None, None, :] < by_block(all_counts)[:, :, None],
        by_block(offsets)[:, :, None] + within[None, None, :] + local,
        -1,
    )
    steps = per_plane // together
    code = jnp.transpose(
        code.reshape(blocks, steps, together * slot_cap), (1, 0, 2)
    ).reshape(steps, 1, blocks * together * slot_cap)

    group_width = PER_GROUP * HD
    weight = jnp.concatenate(
        [
            lax.dynamic_slice_in_dim(q_weight, head * group_width, group_width, 1),
            lax.dynamic_slice_in_dim(k_weight, head * HD, HD, 1),
            lax.dynamic_slice_in_dim(v_weight, head * HD, HD, 1),
        ],
        axis=1,
    )
    states, query, key, value = make_states(
        code, slots, attn_gain, weight, per_plane, together
    )

    wanted_slot = jnp.sum(
        jnp.where(
            mine(speaker_of)[:, None] == jnp.arange(prompt_slot.shape[0])[None, :],
            prompt_slot[None, :],
            0,
        ),
        axis=1,
    )
    place = wanted_slot // held * held_part + wanted_slot % held_part
    attended = attend(place, lengths, query, key, value, prompts)
    returned = lax.all_to_all(
        attended.reshape(plane, per_device * SLOTS, group_width),
        ("inner", "rep"),
        split_axis=0,
        concat_axis=0,
        tiled=True,
    ).reshape(KVH, sharers, per_device, SLOTS, group_width)
    first = plane_place * per_device
    if sharers > 1:
        holder = lax.dynamic_slice_in_dim(wanted_slot % held // held_part, first, per_device)
        chosen = jnp.zeros_like(returned[:, 0])
        for t in range(sharers):
            chosen = jnp.where((holder == t)[None, :, None, None], returned[:, t], chosen)
    else:
        chosen = returned[:, 0]
    gathered = jnp.transpose(chosen, (1, 2, 0, 3)).reshape(per_device * SLOTS, H * HD)
    own_states = lax.dynamic_slice_in_dim(states, first * SLOTS, per_device * SLOTS, 0)
    own_lengths = lax.dynamic_slice_in_dim(lengths, first, per_device)
    summed = own_states.astype(jnp.float32) + jnp.dot(
        gathered, o_weight, preferred_element_type=jnp.float32
    )
    live_rows = (jnp.arange(SLOTS)[None, :] < own_lengths[:, None]).reshape(-1, 1)
    return (
        jnp.where(live_rows, summed, 0.0)
        .astype(jnp.bfloat16)
        .reshape(per_device, SLOTS, model)
    )


EXTRA = 16
SMEM = pl.BlockSpec(memory_space=pltpu.SMEM)
VMEM = pl.BlockSpec(memory_space=pltpu.VMEM)
ANY = pl.BlockSpec(memory_space=pl.ANY)


def split_heads_kernel(head_ref, cache_ref, *out_refs):
    for by, out_ref in enumerate(out_refs):
        for side in range(2):
            start = pl.multiple_of((head_ref[0] ^ by) * HD + side * KVH * HD, HD)
            out_ref[:, :, side * HD : (side + 1) * HD] = cache_ref[:, :, pl.ds(start, HD)]


def split_heads(head, cache):
    held, tokens, _ = cache.shape
    shape = jax.ShapeDtypeStruct((held, tokens, 2 * HD), cache.dtype)
    return pl.pallas_call(
        split_heads_kernel,
        in_specs=[SMEM, VMEM],
        out_specs=[VMEM] * KVH,
        out_shape=[shape] * KVH,
        cost_estimate=pl.CostEstimate(flops=0, bytes_accessed=2 * cache.size * 2, transcendentals=0),
        name="split_heads",
    )(head, cache)


def stack_kernel(*refs):
    in_refs, out_ref = refs[:-1], refs[-1]
    place = 0
    for in_ref in in_refs:
        count = in_ref.shape[0]
        out_ref[place : place + count] = in_ref[...]
        place += count


def stack(*arrays):
    total = sum(a.shape[0] for a in arrays)
    size = sum(a.size for a in arrays)
    return pl.pallas_call(
        stack_kernel,
        in_specs=[VMEM] * len(arrays),
        out_specs=VMEM,
        out_shape=jax.ShapeDtypeStruct((total,) + arrays[0].shape[1:], arrays[0].dtype),
        cost_estimate=pl.CostEstimate(flops=0, bytes_accessed=4 * size, transcendentals=0),
        name="stack",
    )(*arrays)


def route_kernel(z_ref, kept_ref, came_ref, owner_ref, owner_row_ref, *out_refs,
                 slot_cap, per_plane):
    rows = kept_ref.shape[0]
    planes = len(out_refs)
    size = out_refs[0].shape[0]
    live = per_plane * slot_cap
    columns = (kept_ref[...] + came_ref[...].astype(jnp.float32)).astype(jnp.bfloat16)
    owner, owner_row = owner_ref[...], owner_row_ref[...]
    above = lax.broadcasted_iota(jnp.int32, (rows, rows), 0)
    beside = lax.broadcasted_iota(jnp.int32, (rows, rows), 1)
    earlier = jnp.sum(
        jnp.where((owner == owner_row) & (above < beside), 1.0, 0.0), axis=0, keepdims=True
    ).astype(jnp.int32)
    target = lax.div(owner_row, per_plane) ^ z_ref[0]
    code = target * size + lax.rem(owner_row, per_plane) * slot_cap + earlier
    place = lax.broadcasted_iota(jnp.int32, (planes * size, rows), 0)
    into = (place == code).astype(jnp.bfloat16)
    routed = jnp.dot(into, columns, preferred_element_type=jnp.float32).astype(jnp.bfloat16)
    lane = lax.broadcasted_iota(jnp.int32, (rows, HD), 1)
    named = (lane == owner).astype(jnp.bfloat16)
    counts = jnp.dot(
        jnp.ones((EXTRA, rows), jnp.bfloat16), named, preferred_element_type=jnp.float32
    ).astype(jnp.bfloat16)
    for k, out_ref in enumerate(out_refs):
        out_ref[:live] = routed[k * size : k * size + live]
        out_ref[live:] = jnp.zeros((EXTRA, out_ref.shape[1]), jnp.bfloat16)
        out_ref[live:, :HD] = counts


def route(z, kept, came, row_session, planes, per_plane, slot_cap):
    width = kept.shape[1]
    rows = row_session.shape[0]
    size = per_plane * slot_cap + EXTRA
    return pl.pallas_call(
        functools.partial(route_kernel, slot_cap=slot_cap, per_plane=per_plane),
        in_specs=[SMEM] + [VMEM] * 4,
        out_specs=[VMEM] * planes,
        out_shape=[jax.ShapeDtypeStruct((size, width), jnp.bfloat16)] * planes,
        cost_estimate=pl.CostEstimate(
            flops=2 * planes * size * rows * width, bytes_accessed=rows * width * 8, transcendentals=0
        ),
        name="route",
    )(z, kept, came, row_session, row_session.reshape(1, rows))


def place_kernel(index_ref, mine_ref, core_ref, gain_ref, weight_ref, cos_ref, sin_ref,
                 states_ref, query_ref, key_ref, value_ref, length_ref, *, slot_cap, together):
    z, x, c = index_ref[0], index_ref[1], index_ref[2]
    planes = mine_ref.shape[0] // 2
    blocks = 2 * planes
    width = mine_ref.shape[2]
    live = mine_ref.shape[1] - EXTRA
    per_plane = live // slot_cap
    steps = per_plane // together
    window = together * slot_cap
    total = together * SLOTS
    counts = jnp.concatenate(
        [ref[k, live : live + 1, :HD] for ref in (mine_ref, core_ref) for k in range(planes)],
        axis=0,
    ).astype(jnp.float32)
    kind = lambda axis: lax.broadcasted_iota(jnp.int32, (blocks, blocks), axis)
    true_block = lambda k: (z ^ (k % planes)) * 2 + (c ^ (k // planes))
    before = (true_block(kind(1)) < true_block(kind(0))).astype(jnp.float32)
    offsets = jnp.dot(before, counts, preferred_element_type=jnp.float32)
    session_lane = lax.broadcasted_iota(jnp.int32, (HD, HD), 0)
    local_lane = lax.broadcasted_iota(jnp.int32, (HD, HD), 1)
    ours = (session_lane == z * per_plane + local_lane).astype(jnp.float32)
    sums = jnp.dot(
        jnp.broadcast_to(jnp.sum(counts, axis=0, keepdims=True), (8, HD)),
        ours,
        preferred_element_type=jnp.float32,
    )
    length_ref[...] = sums[:1].astype(jnp.int32)
    cosine, sine = cos_ref[...], sin_ref[...]
    gain = gain_ref[...].astype(jnp.float32)
    for step in range(steps):
        slot = lax.broadcasted_iota(jnp.int32, (blocks, blocks * window), 1)
        in_block = slot % window
        spread = lax.broadcasted_iota(jnp.int32, (HD, blocks * window), 1) % window // slot_cap
        from_lane = lax.broadcasted_iota(jnp.int32, (HD, blocks * window), 0)
        expand = (from_lane == z * per_plane + step * together + spread).astype(jnp.float32)
        here = jnp.dot(counts, expand, preferred_element_type=jnp.float32).astype(jnp.int32)
        start = jnp.dot(offsets, expand, preferred_element_type=jnp.float32).astype(jnp.int32)
        within = in_block % slot_cap
        row = jnp.where(within < here, start + within + in_block // slot_cap * SLOTS, -1)
        block = lax.broadcasted_iota(jnp.int32, (blocks, blocks * window), 0)
        code = jnp.max(jnp.where(slot // window == block, row, -1), axis=0, keepdims=True)
        place = lax.broadcasted_iota(jnp.int32, (total, blocks * window), 0)
        pick = (place == code).astype(jnp.bfloat16)
        slots = slice(step * window, (step + 1) * window)
        near, far = [
            jnp.dot(
                pick,
                jnp.concatenate(
                    [ref[half * planes + k, slots] for ref in (mine_ref, core_ref) for k in range(planes)],
                    axis=0,
                ),
                preferred_element_type=jnp.float32,
            )
            for half in range(2)
        ]
        widened = jnp.concatenate(
            [jnp.where(x == 0, near, far), jnp.where(x == 0, far, near)], axis=1
        )
        rows = slice(step * total, (step + 1) * total)
        states_ref[rows] = widened.astype(jnp.bfloat16)
        factor = lax.rsqrt(jnp.mean(widened * widened, axis=-1, keepdims=True) + EPSILON)
        normed = (widened * factor * gain).astype(jnp.bfloat16)
        both = jnp.dot(normed, weight_ref[...], preferred_element_type=jnp.float32)
        for h in range(PER_GROUP + 1):
            vector = both[:, h * HD : (h + 1) * HD]
            turned = vector * cosine + pltpu.roll(vector, HD // 2, 1) * sine
            if h < PER_GROUP:
                query_ref[rows, h * HD : (h + 1) * HD] = turned.astype(jnp.bfloat16)
            else:
                key_ref[rows] = turned.astype(jnp.bfloat16)
        value_ref[rows] = both[:, (PER_GROUP + 1) * HD :].astype(jnp.bfloat16)


def place_rows(index, mine, core, gain, weight, sessions, slot_cap):
    together = 16 // math.gcd(16, slot_cap)
    cosine, sine = rope_tables(together)
    model = 2 * mine.shape[2]
    total = sessions * SLOTS
    out = lambda w: jax.ShapeDtypeStruct((total, w), jnp.bfloat16)
    return pl.pallas_call(
        functools.partial(place_kernel, slot_cap=slot_cap, together=together),
        in_specs=[SMEM] + [VMEM] * 6,
        out_specs=[VMEM] * 5,
        out_shape=[
            out(model), out(PER_GROUP * HD), out(HD), out(HD),
            jax.ShapeDtypeStruct((1, HD), jnp.int32),
        ],
        compiler_params=pltpu.CompilerParams(vmem_limit_bytes=40 << 20),
        cost_estimate=pl.CostEstimate(
            flops=4 * total * model * weight.shape[1], bytes_accessed=6 << 20, transcendentals=0
        ),
        name="place_rows",
    )(index, mine, core, gain.reshape(1, model), weight, jnp.asarray(cosine), jnp.asarray(sine))


def session_attention(query_ref, key_ref, value_ref, kv, session, length):
    scale = HD ** (-0.5) * math.log2(math.e)
    rows = pl.ds(pl.multiple_of(session * SLOTS, SLOTS), SLOTS)
    query = jnp.concatenate(
        [query_ref[rows, h * HD : (h + 1) * HD] for h in range(PER_GROUP)], axis=0
    )
    tokens = kv.reshape(PROMPT, 2 * HD)
    ahead = lax.dot_general(query, tokens[:, :HD], NT, preferred_element_type=jnp.float32)
    own = lax.dot_general(query, key_ref[rows, :], NT, preferred_element_type=jnp.float32)
    row = lax.broadcasted_iota(jnp.int32, (SLOTS, SLOTS), 0)
    column = lax.broadcasted_iota(jnp.int32, (SLOTS, SLOTS), 1)
    allowed = (column <= row) & (column < length)
    own = jnp.where(jnp.concatenate([allowed] * PER_GROUP, axis=0), own, -1e30)
    highest = jnp.maximum(
        jnp.max(ahead, axis=-1, keepdims=True), jnp.max(own, axis=-1, keepdims=True)
    )
    powers = jnp.exp2((ahead - highest) * scale)
    own_powers = jnp.exp2((own - highest) * scale)
    total = jnp.sum(powers, axis=-1, keepdims=True) + jnp.sum(own_powers, axis=-1, keepdims=True)
    mixed = jnp.dot(
        powers.astype(jnp.bfloat16), tokens[:, HD:], preferred_element_type=jnp.float32
    ) + jnp.dot(own_powers.astype(jnp.bfloat16), value_ref[rows, :], preferred_element_type=jnp.float32)
    return (mixed / total).astype(jnp.bfloat16)


def hops_kernel(index_ref, hop_ref, held_ref, length_ref, query_ref, key_ref, value_ref, *refs,
                hops, carried):
    if carried:
        before_ref, *refs = refs
    count = KVH if carried else 1
    prompt_refs, out_refs = refs[: 2 * len(hops)], refs[2 * len(hops) : 2 * len(hops) + count]
    kv, sem = refs[-2:]
    sessions = hop_ref.shape[0]
    per_device = sessions // KVH

    def copies(session, which):
        return [
            pltpu.make_async_copy(
                prompt_refs[2 * which + chunk].at[:, held_ref[session]],
                kv.at[session, chunk],
                sem.at[session, chunk],
            )
            for chunk in range(2)
        ]

    def fetch(session, _):
        for which, hop in enumerate(hops):
            @pl.when(hop_ref[session] == hop)
            def _():
                for copy in copies(session, which):
                    copy.start()
        return 0

    def store(session, block):
        def into(out_ref, first):
            rows = pl.ds(pl.multiple_of(first * SLOTS, SLOTS), SLOTS)
            if block.shape[0] == SLOTS:
                out_ref[rows] = block
            else:
                for h in range(PER_GROUP):
                    out_ref[rows, h * HD : (h + 1) * HD] = block[h * SLOTS : (h + 1) * SLOTS]

        if not carried:
            into(out_refs[0], session)
            return
        for by, out_ref in enumerate(out_refs):
            @pl.when((lax.div(session, per_device) ^ index_ref[3]) == by)
            def _():
                into(out_ref, lax.rem(session, per_device))

    lax.fori_loop(0, sessions, fetch, 0)

    def work(session, _):
        ours = hop_ref[session] == hops[0]
        for hop in hops[1:]:
            ours = ours | (hop_ref[session] == hop)
        if carried:
            @pl.when(jnp.logical_not(ours))
            def _():
                rows = pl.ds(pl.multiple_of(session * SLOTS, SLOTS), SLOTS)
                store(session, before_ref[rows])

        @pl.when(ours)
        def _():
            for copy in copies(session, 0):
                copy.wait()
            store(
                session,
                session_attention(
                    query_ref, key_ref, value_ref, kv[session], session, length_ref[0, session]
                ),
            )

        return 0

    lax.fori_loop(0, sessions, work, 0)


def attend_hops(index, hop, held, lengths, query, key, value, prompts, hops, before):
    sessions = hop.shape[0]
    carried = before is not None
    pieces = [piece for h in hops for piece in prompts[h]]
    work = sessions * len(hops) // 7 + 1
    width = PER_GROUP * HD
    if carried:
        out_shape = [jax.ShapeDtypeStruct((sessions // KVH * SLOTS, width), jnp.bfloat16)] * KVH
    else:
        out_shape = jax.ShapeDtypeStruct((sessions * SLOTS, width), jnp.bfloat16)
    return pl.pallas_call(
        functools.partial(hops_kernel, hops=hops, carried=carried),
        in_specs=[SMEM] * 4 + [VMEM] * (3 + carried) + [ANY] * len(pieces),
        out_specs=[VMEM] * KVH if carried else VMEM,
        out_shape=out_shape,
        scratch_shapes=[
            pltpu.VMEM((sessions, 2, 2, PROMPT // 4, 2 * HD), jnp.bfloat16),
            pltpu.SemaphoreType.DMA((sessions, 2)),
        ],
        compiler_params=pltpu.CompilerParams(vmem_limit_bytes=40 << 20),
        cost_estimate=pl.CostEstimate(
            flops=work * 4 * PER_GROUP * SLOTS * (PROMPT + SLOTS) * HD,
            bytes_accessed=work * PROMPT * 4 * HD,
            transcendentals=work * PER_GROUP * SLOTS * (PROMPT + SLOTS),
        ),
        name="attend",
    )(index, hop, held, lengths, query, key, value, *([before] if carried else []), *pieces)


def output_kernel(index_ref, length_ref, states_ref, weight_ref, *refs):
    piece_refs, out_ref = refs[:-1], refs[-1]
    head = index_ref[3]
    group_width = PER_GROUP * HD
    per_device = out_ref.shape[0]
    total = per_device * SLOTS
    summed = states_ref[pl.ds(pl.multiple_of(head * total, SLOTS), total)].astype(jnp.float32)
    for by, piece_ref in enumerate(piece_refs):
        start = pl.multiple_of((head ^ by) * group_width, group_width)
        summed = summed + jnp.dot(
            piece_ref[...], weight_ref[pl.ds(start, group_width)], preferred_element_type=jnp.float32
        )
    row = lax.broadcasted_iota(jnp.int32, (SLOTS, 1), 0)
    for i in range(per_device):
        live = row < length_ref[0, head * per_device + i]
        part = summed[i * SLOTS : (i + 1) * SLOTS]
        out_ref[i] = jnp.where(live, part, 0.0).astype(jnp.bfloat16)


def output(index, lengths, states, o_weight, pieces, per_device):
    model = o_weight.shape[1]
    return pl.pallas_call(
        output_kernel,
        in_specs=[SMEM] * 2 + [VMEM] * (2 + len(pieces)),
        out_specs=VMEM,
        out_shape=jax.ShapeDtypeStruct((per_device, SLOTS, model), jnp.bfloat16),
        compiler_params=pltpu.CompilerParams(vmem_limit_bytes=40 << 20),
        cost_estimate=pl.CostEstimate(
            flops=2 * per_device * SLOTS * o_weight.size, bytes_accessed=o_weight.size * 2, transcendentals=0
        ),
        name="output",
    )(index, lengths, states, o_weight, *pieces)


def shifted(n, by):
    return [(i, i + by) for i in range(n) if 0 <= i + by < n]


def swapped(n, by):
    return [(i, i ^ by) for i in range(n)]


def line_body(
    thinker_rows,
    row_session,
    speaker_of,
    prompt_slot,
    prompt_cache,
    proj_weight,
    attn_gain,
    q_weight,
    k_weight,
    v_weight,
    o_weight,
):
    planes, plane, rep_count = lax.axis_size("sess"), KVH, 2
    blocks = planes * rep_count
    session_all = speaker_of.shape[0]
    per_plane = session_all // planes
    per_device = per_plane // plane
    slot_cap = SLOTS // blocks
    held = prompt_cache.shape[0]
    model = proj_weight.shape[1]
    width = model // 2
    z, x, c = lax.axis_index("sess"), lax.axis_index("inner"), lax.axis_index("rep")
    head = x * rep_count + c
    index = jnp.stack([z, x, c, head]).astype(jnp.int32)
    pair = ("inner", "rep")

    own, to_core, to_x, to_far = split_heads(head.reshape(1), prompt_cache)
    from_core = lax.ppermute(to_core, pair, swapped(4, 1))
    from_x = lax.ppermute(to_x, pair, swapped(4, 2))
    from_far = lax.ppermute(to_far, pair, swapped(4, 3))
    first = stack(own[None], from_core[None])
    second = stack(from_x[None], from_far[None])
    right = [first, second]
    left = [first, second]
    prompts = {0: (first, second)}
    for hop in range(1, planes):
        for chunk in range(2):
            right[chunk] = lax.ppermute(right[chunk], "sess", shifted(planes, 1))
            left[chunk] = lax.ppermute(left[chunk], "sess", shifted(planes, -1))
        prompts[-hop], prompts[hop] = tuple(right), tuple(left)

    thinker_rows, _ = lax.optimization_barrier((thinker_rows, (prompts[-1][0], prompts[1][0])))
    partial_sum = jnp.dot(thinker_rows, proj_weight, preferred_element_type=jnp.float32)
    kept = lax.dynamic_slice_in_dim(partial_sum, x * width, width, 1)
    sent = lax.dynamic_slice_in_dim(partial_sum, (1 - x) * width, width, 1)
    came = lax.ppermute(sent.astype(jnp.bfloat16), "inner", swapped(2, 1))
    came, _ = lax.optimization_barrier((came, (prompts[-1][1], prompts[1][1])))
    routed = route(z.reshape(1), kept, came, row_session, planes, per_plane, slot_cap)
    routed, _ = lax.optimization_barrier((tuple(routed), (prompts[-2][0], prompts[2][0])))
    arrived = [routed[0]] + [
        lax.ppermute(routed[by], "sess", swapped(planes, by)) for by in range(1, planes)
    ]
    arrived, _ = lax.optimization_barrier((arrived, (prompts[-2][1], prompts[2][1])))
    arrived = stack(*[a[None] for a in arrived])
    mine = stack(arrived, lax.ppermute(arrived, "inner", swapped(2, 1)))
    core = lax.ppermute(mine, "rep", swapped(2, 1))

    group_width = PER_GROUP * HD
    weight = jnp.concatenate(
        [
            lax.dynamic_slice_in_dim(q_weight, head * group_width, group_width, 1),
            lax.dynamic_slice_in_dim(k_weight, head * HD, HD, 1),
            lax.dynamic_slice_in_dim(v_weight, head * HD, HD, 1),
        ],
        axis=1,
    )
    states, query, key, value, lengths = place_rows(
        index, mine, core, attn_gain, weight, per_plane, slot_cap
    )

    speakers = lax.dynamic_slice_in_dim(speaker_of, z * per_plane, per_plane)
    wanted_slot = jnp.sum(
        jnp.where(
            speakers[:, None] == jnp.arange(prompt_slot.shape[0])[None, :], prompt_slot[None, :], 0
        ),
        axis=1,
    )
    hop = wanted_slot // held - z
    which = wanted_slot % held
    near = attend_hops(
        index, hop, which, lengths, query, key, value, prompts, (0, -1, 1, -2, 2), None
    )
    attended = attend_hops(
        index, hop, which, lengths, query, key, value, prompts, (-3, 3), near
    )

    pieces = [attended[0]] + [
        lax.ppermute(attended[by], pair, swapped(4, by)) for by in range(1, plane)
    ]
    return output(index, lengths, states, o_weight, pieces, per_device)


def solution(mesh):
    in_specs = (
        P(("groups", "sess", "rep"), "inner"),
        P(("groups", "sess", "rep"), None),
        P("groups"),
        P("groups"),
        P(("groups", "sess"), ("inner", "rep"), None),
        P("inner", None),
        P(),
        P(),
        P(),
        P(),
        P(),
    )
    out_specs = P(("groups", "sess", "inner", "rep"), None, None)
    sizes = tuple(mesh.shape[name] for name in ("sess", "inner", "rep"))
    body = line_body if sizes == (4, 2, 2) else general_body
    return jax.shard_map(body, mesh=mesh, in_specs=in_specs, out_specs=out_specs, check_vma=False)
```

```python
import functools
import math

import jax
import jax.numpy as jnp
import numpy as np
from jax import lax
from jax.experimental import pallas as pl
from jax.experimental.pallas import tpu as pltpu
from jax.sharding import PartitionSpec as P

H = 12
KVH = 4
HD = 128
PROMPT = 1024
SLOTS = 96
PER_GROUP = H // KVH

EPSILON = 1e-06
ROPE_BASE = 1000000.0
NT = (((1,), (1,)), ((), ()))


def rope_tables(copies):
    half_width = HD // 2
    inverse = ROPE_BASE ** (-(np.arange(half_width, dtype=np.float64) * 2.0) / HD)
    angles = (PROMPT + np.arange(SLOTS, dtype=np.float64))[:, None] * inverse[None, :]
    cosine = np.concatenate([np.cos(angles), np.cos(angles)], axis=1)
    sine = np.concatenate([-np.sin(angles), np.sin(angles)], axis=1)
    return (
        np.tile(cosine, (copies, 1)).astype(np.float32),
        np.tile(sine, (copies, 1)).astype(np.float32),
    )


def states_kernel(code_ref, slots_ref, gain_ref, weight_ref, cos_ref, sin_ref,
                  states_ref, query_ref, key_ref, value_ref):
    halves, blocks, rows, width = slots_ref.shape
    total = states_ref.shape[0]
    place = lax.broadcasted_iota(jnp.int32, (total, blocks * rows), 0)
    pick = (place == code_ref[0]).astype(jnp.bfloat16)
    parts = [
        jnp.dot(
            pick,
            slots_ref[half].reshape(blocks * rows, width),
            preferred_element_type=jnp.float32,
        )
        for half in range(halves)
    ]
    widened = jnp.concatenate(parts, axis=1)
    states_ref[...] = widened.astype(jnp.bfloat16)
    factor = lax.rsqrt(jnp.mean(widened * widened, axis=-1, keepdims=True) + EPSILON)
    normed = (widened * factor * gain_ref[...].astype(jnp.float32)).astype(jnp.bfloat16)
    both = jnp.dot(normed, weight_ref[...], preferred_element_type=jnp.float32)
    cosine, sine = cos_ref[...], sin_ref[...]
    for head in range(PER_GROUP + 1):
        vector = both[:, head * HD : (head + 1) * HD]
        turned = vector * cosine + pltpu.roll(vector, HD // 2, 1) * sine
        if head < PER_GROUP:
            query_ref[:, head * HD : (head + 1) * HD] = turned.astype(jnp.bfloat16)
        else:
            key_ref[...] = turned.astype(jnp.bfloat16)
    value_ref[...] = both[:, (PER_GROUP + 1) * HD :].astype(jnp.bfloat16)


def attention_kernel(place_ref, length_ref, query_ref, key_ref, value_ref, prompt_ref, out_ref):
    session = pl.program_id(0)
    length = length_ref[session]
    scale = HD ** (-0.5) * math.log2(math.e)
    query = jnp.concatenate(
        [query_ref[:, h * HD : (h + 1) * HD] for h in range(PER_GROUP)], axis=0
    )
    ahead = lax.dot_general(query, prompt_ref[0, :, :HD], NT, preferred_element_type=jnp.float32)
    own = lax.dot_general(query, key_ref[...], NT, preferred_element_type=jnp.float32)
    row = lax.broadcasted_iota(jnp.int32, (SLOTS, SLOTS), 0)
    column = lax.broadcasted_iota(jnp.int32, (SLOTS, SLOTS), 1)
    allowed = (column <= row) & (column < length)
    own = jnp.where(jnp.concatenate([allowed] * PER_GROUP, axis=0), own, -1e30)
    highest = jnp.maximum(
        jnp.max(ahead, axis=-1, keepdims=True), jnp.max(own, axis=-1, keepdims=True)
    )
    powers = jnp.exp2((ahead - highest) * scale)
    own_powers = jnp.exp2((own - highest) * scale)
    total = jnp.sum(powers, axis=-1, keepdims=True) + jnp.sum(own_powers, axis=-1, keepdims=True)
    mixed = jnp.dot(
        powers.astype(jnp.bfloat16), prompt_ref[0, :, HD:], preferred_element_type=jnp.float32
    ) + jnp.dot(own_powers.astype(jnp.bfloat16), value_ref[...], preferred_element_type=jnp.float32)
    mixed = (mixed / total).astype(jnp.bfloat16)
    for h in range(PER_GROUP):
        out_ref[:, h * HD : (h + 1) * HD] = mixed[h * SLOTS : (h + 1) * SLOTS]


def make_states(code, slots, gain, weight, sessions, together):
    halves, blocks, rows, width = slots.shape
    steps = sessions // together
    model = halves * width
    cosine, sine = rope_tables(together)
    total = together * SLOTS
    out = jax.ShapeDtypeStruct
    row_spec = lambda w: pl.BlockSpec((total, w), lambda i: (i, 0))
    whole = lambda a: pl.BlockSpec(a.shape, lambda i: (0,) * a.ndim)
    gain = gain.reshape(1, model)
    return pl.pallas_call(
        states_kernel,
        grid=(steps,),
        in_specs=[
            pl.BlockSpec((1, 1, code.shape[2]), lambda i: (i, 0, 0)),
            pl.BlockSpec((halves, blocks, rows // steps, width), lambda i: (0, 0, i, 0)),
            whole(gain),
            whole(weight),
            whole(cosine),
            whole(sine),
        ],
        out_specs=[row_spec(model), row_spec(PER_GROUP * HD), row_spec(HD), row_spec(HD)],
        out_shape=[
            out((sessions * SLOTS, model), jnp.bfloat16),
            out((sessions * SLOTS, PER_GROUP * HD), jnp.bfloat16),
            out((sessions * SLOTS, HD), jnp.bfloat16),
            out((sessions * SLOTS, HD), jnp.bfloat16),
        ],
        compiler_params=pltpu.CompilerParams(vmem_limit_bytes=40 << 20),
        name="states",
    )(code, slots, gain, weight, jnp.asarray(cosine), jnp.asarray(sine))


def attend(place, lengths, query, key, value, prompts):
    sessions = place.shape[0]
    row_spec = lambda w: pl.BlockSpec((SLOTS, w), lambda i, place, length: (i, 0))
    return pl.pallas_call(
        attention_kernel,
        grid_spec=pltpu.PrefetchScalarGridSpec(
            num_scalar_prefetch=2,
            grid=(sessions,),
            in_specs=[
                row_spec(PER_GROUP * HD),
                row_spec(HD),
                row_spec(HD),
                pl.BlockSpec((1, PROMPT, 2 * HD), lambda i, place, length: (place[i], 0, 0)),
            ],
            out_specs=row_spec(PER_GROUP * HD),
        ),
        out_shape=jax.ShapeDtypeStruct((sessions * SLOTS, PER_GROUP * HD), jnp.bfloat16),
        compiler_params=pltpu.CompilerParams(vmem_limit_bytes=40 << 20),
        name="attend",
    )(place, lengths, query, key, value, prompts)


def general_body(
    thinker_rows,
    row_session,
    speaker_of,
    prompt_slot,
    prompt_cache,
    proj_weight,
    attn_gain,
    q_weight,
    k_weight,
    v_weight,
    o_weight,
):
    sess_count = lax.axis_size("sess")
    inner_count = lax.axis_size("inner")
    rep_count = lax.axis_size("rep")
    plane = inner_count * rep_count
    blocks = sess_count * rep_count
    session_all = speaker_of.shape[0]
    per_plane = session_all // sess_count
    per_device = per_plane // plane
    slot_cap = SLOTS // blocks
    held, tokens, channels = prompt_cache.shape
    model = proj_weight.shape[1]
    sharers = plane // KVH
    held_part = held // sharers
    sess_place = lax.axis_index("sess")
    plane_place = lax.axis_index("inner") * rep_count + lax.axis_index("rep")
    head = plane_place // sharers
    sharer = plane_place % sharers

    outgoing = jnp.transpose(
        prompt_cache.reshape(sharers, held_part, tokens, 2, KVH, HD), (4, 0, 1, 2, 3, 5)
    ).reshape(plane, held_part, tokens, 2 * HD)
    own_head = lax.all_to_all(outgoing, ("inner", "rep"), split_axis=0, concat_axis=2, tiled=True)
    own_head = own_head.reshape(held_part, plane * tokens, 2 * HD)
    prompts = lax.all_gather(own_head, "sess", axis=0, tiled=True)

    row_owner = row_session[:, 0]
    order = jnp.arange(row_owner.shape[0])
    same = row_owner[:, None] == row_owner[None, :]
    earlier = jnp.sum((same & (order[None, :] < order[:, None])).astype(jnp.int32), axis=1)
    row_slot = row_owner * slot_cap + earlier
    counts = jnp.sum(
        (row_owner[:, None] == jnp.arange(session_all)[None, :]).astype(jnp.int32), axis=0
    )
    all_counts = lax.all_gather(counts, ("sess", "rep"), axis=0, tiled=False)

    partial_sum = jnp.dot(thinker_rows, proj_weight, preferred_element_type=jnp.float32)
    width = model // inner_count
    if inner_count == 2:
        inner_place = lax.axis_index("inner")
        kept = lax.dynamic_slice_in_dim(partial_sum, inner_place * width, width, 1)
        sent = lax.dynamic_slice_in_dim(partial_sum, (1 - inner_place) * width, width, 1)
        came = lax.ppermute(sent.astype(jnp.bfloat16), "inner", [(0, 1), (1, 0)])
        own_columns = (kept + came.astype(jnp.float32)).astype(jnp.bfloat16)
    else:
        own_columns = lax.psum_scatter(
            partial_sum, "inner", scatter_dimension=1, tiled=True
        ).astype(jnp.bfloat16)
    into = (jnp.arange(session_all * slot_cap)[:, None] == row_slot[None, :]).astype(jnp.bfloat16)
    buffer = jnp.dot(into, own_columns, preferred_element_type=jnp.float32).astype(jnp.bfloat16)
    arrived = lax.all_to_all(
        buffer.reshape(sess_count, per_plane * slot_cap, width),
        "sess",
        split_axis=0,
        concat_axis=0,
        tiled=True,
    )
    spread = lax.all_gather(arrived, ("inner", "rep"), axis=0, tiled=False)
    slots = spread.reshape(inner_count, rep_count * sess_count, per_plane * slot_cap, width)

    offsets = jnp.cumsum(all_counts, axis=0) - all_counts
    lengths_all = jnp.sum(all_counts, axis=0)
    mine = lambda a: lax.dynamic_slice_in_dim(a, sess_place * per_plane, per_plane, a.ndim - 1)
    by_block = lambda a: jnp.transpose(
        mine(a).reshape(sess_count, rep_count, per_plane), (1, 0, 2)
    ).reshape(blocks, per_plane)
    lengths = mine(lengths_all)
    together = 16 // math.gcd(16, slot_cap)
    within = jnp.arange(slot_cap)
    local = (jnp.arange(per_plane) % together)[None, :, None] * SLOTS
    code = jnp.where(
        within[None, None, :] < by_block(all_counts)[:, :, None],
        by_block(offsets)[:, :, None] + within[None, None, :] + local,
        -1,
    )
    steps = per_plane // together
    code = jnp.transpose(
        code.reshape(blocks, steps, together * slot_cap), (1, 0, 2)
    ).reshape(steps, 1, blocks * together * slot_cap)

    group_width = PER_GROUP * HD
    weight = jnp.concatenate(
        [
            lax.dynamic_slice_in_dim(q_weight, head * group_width, group_width, 1),
            lax.dynamic_slice_in_dim(k_weight, head * HD, HD, 1),
            lax.dynamic_slice_in_dim(v_weight, head * HD, HD, 1),
        ],
        axis=1,
    )
    states, query, key, value = make_states(
        code, slots, attn_gain, weight, per_plane, together
    )

    wanted_slot = jnp.sum(
        jnp.where(
            mine(speaker_of)[:, None] == jnp.arange(prompt_slot.shape[0])[None, :],
            prompt_slot[None, :],
            0,
        ),
        axis=1,
    )
    place = wanted_slot // held * held_part + wanted_slot % held_part
    attended = attend(place, lengths, query, key, value, prompts)
    returned = lax.all_to_all(
        attended.reshape(plane, per_device * SLOTS, group_width),
        ("inner", "rep"),
        split_axis=0,
        concat_axis=0,
        tiled=True,
    ).reshape(KVH, sharers, per_device, SLOTS, group_width)
    first = plane_place * per_device
    if sharers > 1:
        holder = lax.dynamic_slice_in_dim(wanted_slot % held // held_part, first, per_device)
        chosen = jnp.zeros_like(returned[:, 0])
        for t in range(sharers):
            chosen = jnp.where((holder == t)[None, :, None, None], returned[:, t], chosen)
    else:
        chosen = returned[:, 0]
    gathered = jnp.transpose(chosen, (1, 2, 0, 3)).reshape(per_device * SLOTS, H * HD)
    own_states = lax.dynamic_slice_in_dim(states, first * SLOTS, per_device * SLOTS, 0)
    own_lengths = lax.dynamic_slice_in_dim(lengths, first, per_device)
    summed = own_states.astype(jnp.float32) + jnp.dot(
        gathered, o_weight, preferred_element_type=jnp.float32
    )
    live_rows = (jnp.arange(SLOTS)[None, :] < own_lengths[:, None]).reshape(-1, 1)
    return (
        jnp.where(live_rows, summed, 0.0)
        .astype(jnp.bfloat16)
        .reshape(per_device, SLOTS, model)
    )


EXTRA = 16
SMEM = pl.BlockSpec(memory_space=pltpu.SMEM)
VMEM = pl.BlockSpec(memory_space=pltpu.VMEM)
ANY = pl.BlockSpec(memory_space=pl.ANY)


def split_heads_kernel(head_ref, cache_ref, *out_refs):
    for by, out_ref in enumerate(out_refs):
        for side in range(2):
            start = pl.multiple_of((head_ref[0] ^ by) * HD + side * KVH * HD, HD)
            out_ref[:, :, side * HD : (side + 1) * HD] = cache_ref[:, :, pl.ds(start, HD)]


def split_heads(head, cache):
    held, tokens, _ = cache.shape
    shape = jax.ShapeDtypeStruct((held, tokens, 2 * HD), cache.dtype)
    return pl.pallas_call(
        split_heads_kernel,
        in_specs=[SMEM, VMEM],
        out_specs=[VMEM] * KVH,
        out_shape=[shape] * KVH,
        cost_estimate=pl.CostEstimate(flops=0, bytes_accessed=2 * cache.size * 2, transcendentals=0),
        name="split_heads",
    )(head, cache)


def stack_kernel(*refs):
    in_refs, out_ref = refs[:-1], refs[-1]
    place = 0
    for in_ref in in_refs:
        count = in_ref.shape[0]
        out_ref[place : place + count] = in_ref[...]
        place += count


def stack(*arrays):
    total = sum(a.shape[0] for a in arrays)
    size = sum(a.size for a in arrays)
    return pl.pallas_call(
        stack_kernel,
        in_specs=[VMEM] * len(arrays),
        out_specs=VMEM,
        out_shape=jax.ShapeDtypeStruct((total,) + arrays[0].shape[1:], arrays[0].dtype),
        cost_estimate=pl.CostEstimate(flops=0, bytes_accessed=4 * size, transcendentals=0),
        name="stack",
    )(*arrays)


def route_kernel(z_ref, kept_ref, came_ref, owner_ref, owner_row_ref, *out_refs,
                 slot_cap, per_plane):
    rows = kept_ref.shape[0]
    planes = len(out_refs)
    size = out_refs[0].shape[0]
    live = per_plane * slot_cap
    columns = (kept_ref[...] + came_ref[...].astype(jnp.float32)).astype(jnp.bfloat16)
    owner, owner_row = owner_ref[...], owner_row_ref[...]
    above = lax.broadcasted_iota(jnp.int32, (rows, rows), 0)
    beside = lax.broadcasted_iota(jnp.int32, (rows, rows), 1)
    earlier = jnp.sum(
        jnp.where((owner == owner_row) & (above < beside), 1.0, 0.0), axis=0, keepdims=True
    ).astype(jnp.int32)
    target = lax.div(owner_row, per_plane) ^ z_ref[0]
    code = target * size + lax.rem(owner_row, per_plane) * slot_cap + earlier
    place = lax.broadcasted_iota(jnp.int32, (planes * size, rows), 0)
    into = (place == code).astype(jnp.bfloat16)
    routed = jnp.dot(into, columns, preferred_element_type=jnp.float32).astype(jnp.bfloat16)
    lane = lax.broadcasted_iota(jnp.int32, (rows, HD), 1)
    named = (lane == owner).astype(jnp.bfloat16)
    counts = jnp.dot(
        jnp.ones((EXTRA, rows), jnp.bfloat16), named, preferred_element_type=jnp.float32
    ).astype(jnp.bfloat16)
    for k, out_ref in enumerate(out_refs):
        out_ref[:live] = routed[k * size : k * size + live]
        out_ref[live:] = jnp.zeros((EXTRA, out_ref.shape[1]), jnp.bfloat16)
        out_ref[live:, :HD] = counts


def route(z, kept, came, row_session, planes, per_plane, slot_cap):
    width = kept.shape[1]
    rows = row_session.shape[0]
    size = per_plane * slot_cap + EXTRA
    return pl.pallas_call(
        functools.partial(route_kernel, slot_cap=slot_cap, per_plane=per_plane),
        in_specs=[SMEM] + [VMEM] * 4,
        out_specs=[VMEM] * planes,
        out_shape=[jax.ShapeDtypeStruct((size, width), jnp.bfloat16)] * planes,
        cost_estimate=pl.CostEstimate(
            flops=2 * planes * size * rows * width, bytes_accessed=rows * width * 8, transcendentals=0
        ),
        name="route",
    )(z, kept, came, row_session, row_session.reshape(1, rows))


def place_kernel(index_ref, mine_ref, core_ref, gain_ref, weight_ref, cos_ref, sin_ref,
                 states_ref, query_ref, key_ref, value_ref, length_ref, *, slot_cap, together):
    z, x, c = index_ref[0], index_ref[1], index_ref[2]
    planes = mine_ref.shape[0] // 2
    blocks = 2 * planes
    width = mine_ref.shape[2]
    live = mine_ref.shape[1] - EXTRA
    per_plane = live // slot_cap
    steps = per_plane // together
    window = together * slot_cap
    total = together * SLOTS
    counts = jnp.concatenate(
        [ref[k, live : live + 1, :HD] for ref in (mine_ref, core_ref) for k in range(planes)],
        axis=0,
    ).astype(jnp.float32)
    kind = lambda axis: lax.broadcasted_iota(jnp.int32, (blocks, blocks), axis)
    true_block = lambda k: (z ^ (k % planes)) * 2 + (c ^ (k // planes))
    before = (true_block(kind(1)) < true_block(kind(0))).astype(jnp.float32)
    offsets = jnp.dot(before, counts, preferred_element_type=jnp.float32)
    session_lane = lax.broadcasted_iota(jnp.int32, (HD, HD), 0)
    local_lane = lax.broadcasted_iota(jnp.int32, (HD, HD), 1)
    ours = (session_lane == z * per_plane + local_lane).astype(jnp.float32)
    sums = jnp.dot(
        jnp.broadcast_to(jnp.sum(counts, axis=0, keepdims=True), (8, HD)),
        ours,
        preferred_element_type=jnp.float32,
    )
    length_ref[...] = sums[:1].astype(jnp.int32)
    cosine, sine = cos_ref[...], sin_ref[...]
    gain = gain_ref[...].astype(jnp.float32)
    for step in range(steps):
        slot = lax.broadcasted_iota(jnp.int32, (blocks, blocks * window), 1)
        in_block = slot % window
        spread = lax.broadcasted_iota(jnp.int32, (HD, blocks * window), 1) % window // slot_cap
        from_lane = lax.broadcasted_iota(jnp.int32, (HD, blocks * window), 0)
        expand = (from_lane == z * per_plane + step * together + spread).astype(jnp.float32)
        here = jnp.dot(counts, expand, preferred_element_type=jnp.float32).astype(jnp.int32)
        start = jnp.dot(offsets, expand, preferred_element_type=jnp.float32).astype(jnp.int32)
        within = in_block % slot_cap
        row = jnp.where(within < here, start + within + in_block // slot_cap * SLOTS, -1)
        block = lax.broadcasted_iota(jnp.int32, (blocks, blocks * window), 0)
        code = jnp.max(jnp.where(slot // window == block, row, -1), axis=0, keepdims=True)
        place = lax.broadcasted_iota(jnp.int32, (total, blocks * window), 0)
        pick = (place == code).astype(jnp.bfloat16)
        slots = slice(step * window, (step + 1) * window)
        near, far = [
            jnp.dot(
                pick,
                jnp.concatenate(
                    [ref[half * planes + k, slots] for ref in (mine_ref, core_ref) for k in range(planes)],
                    axis=0,
                ),
                preferred_element_type=jnp.float32,
            )
            for half in range(2)
        ]
        widened = jnp.concatenate(
            [jnp.where(x == 0, near, far), jnp.where(x == 0, far, near)], axis=1
        )
        rows = slice(step * total, (step + 1) * total)
        states_ref[rows] = widened.astype(jnp.bfloat16)
        factor = lax.rsqrt(jnp.mean(widened * widened, axis=-1, keepdims=True) + EPSILON)
        normed = (widened * factor * gain).astype(jnp.bfloat16)
        both = jnp.dot(normed, weight_ref[...], preferred_element_type=jnp.float32)
        for h in range(PER_GROUP + 1):
            vector = both[:, h * HD : (h + 1) * HD]
            turned = vector * cosine + pltpu.roll(vector, HD // 2, 1) * sine
            if h < PER_GROUP:
                query_ref[rows, h * HD : (h + 1) * HD] = turned.astype(jnp.bfloat16)
            else:
                key_ref[rows] = turned.astype(jnp.bfloat16)
        value_ref[rows] = both[:, (PER_GROUP + 1) * HD :].astype(jnp.bfloat16)


def place_rows(index, mine, core, gain, weight, sessions, slot_cap):
    together = 16 // math.gcd(16, slot_cap)
    cosine, sine = rope_tables(together)
    model = 2 * mine.shape[2]
    total = sessions * SLOTS
    out = lambda w: jax.ShapeDtypeStruct((total, w), jnp.bfloat16)
    return pl.pallas_call(
        functools.partial(place_kernel, slot_cap=slot_cap, together=together),
        in_specs=[SMEM] + [VMEM] * 6,
        out_specs=[VMEM] * 5,
        out_shape=[
            out(model), out(PER_GROUP * HD), out(HD), out(HD),
            jax.ShapeDtypeStruct((1, HD), jnp.int32),
        ],
        compiler_params=pltpu.CompilerParams(vmem_limit_bytes=40 << 20),
        cost_estimate=pl.CostEstimate(
            flops=4 * total * model * weight.shape[1], bytes_accessed=6 << 20, transcendentals=0
        ),
        name="place_rows",
    )(index, mine, core, gain.reshape(1, model), weight, jnp.asarray(cosine), jnp.asarray(sine))


def session_attention(query_ref, key_ref, value_ref, kv, session, length):
    scale = HD ** (-0.5) * math.log2(math.e)
    rows = pl.ds(pl.multiple_of(session * SLOTS, SLOTS), SLOTS)
    query = jnp.concatenate(
        [query_ref[rows, h * HD : (h + 1) * HD] for h in range(PER_GROUP)], axis=0
    )
    tokens = kv.reshape(PROMPT, 2 * HD)
    ahead = lax.dot_general(query, tokens[:, :HD], NT, preferred_element_type=jnp.float32)
    own = lax.dot_general(query, key_ref[rows, :], NT, preferred_element_type=jnp.float32)
    row = lax.broadcasted_iota(jnp.int32, (SLOTS, SLOTS), 0)
    column = lax.broadcasted_iota(jnp.int32, (SLOTS, SLOTS), 1)
    allowed = (column <= row) & (column < length)
    own = jnp.where(jnp.concatenate([allowed] * PER_GROUP, axis=0), own, -1e30)
    highest = jnp.maximum(
        jnp.max(ahead, axis=-1, keepdims=True), jnp.max(own, axis=-1, keepdims=True)
    )
    powers = jnp.exp2((ahead - highest) * scale)
    own_powers = jnp.exp2((own - highest) * scale)
    total = jnp.sum(powers, axis=-1, keepdims=True) + jnp.sum(own_powers, axis=-1, keepdims=True)
    mixed = jnp.dot(
        powers.astype(jnp.bfloat16), tokens[:, HD:], preferred_element_type=jnp.float32
    ) + jnp.dot(own_powers.astype(jnp.bfloat16), value_ref[rows, :], preferred_element_type=jnp.float32)
    return (mixed / total).astype(jnp.bfloat16)


def hops_kernel(index_ref, hop_ref, held_ref, length_ref, query_ref, key_ref, value_ref, *refs,
                hops, carried):
    if carried:
        before_ref, *refs = refs
    count = KVH if carried else 1
    prompt_refs, out_refs = refs[: 2 * len(hops)], refs[2 * len(hops) : 2 * len(hops) + count]
    kv, sem = refs[-2:]
    sessions = hop_ref.shape[0]
    per_device = sessions // KVH

    def copies(session, which):
        return [
            pltpu.make_async_copy(
                prompt_refs[2 * which + chunk].at[:, held_ref[session]],
                kv.at[session, chunk],
                sem.at[session, chunk],
            )
            for chunk in range(2)
        ]

    def fetch(session, _):
        for which, hop in enumerate(hops):
            @pl.when(hop_ref[session] == hop)
            def _():
                for copy in copies(session, which):
                    copy.start()
        return 0

    def store(session, block):
        def into(out_ref, first):
            rows = pl.ds(pl.multiple_of(first * SLOTS, SLOTS), SLOTS)
            if block.shape[0] == SLOTS:
                out_ref[rows] = block
            else:
                for h in range(PER_GROUP):
                    out_ref[rows, h * HD : (h + 1) * HD] = block[h * SLOTS : (h + 1) * SLOTS]

        if not carried:
            into(out_refs[0], session)
            return
        for by, out_ref in enumerate(out_refs):
            @pl.when((lax.div(session, per_device) ^ index_ref[3]) == by)
            def _():
                into(out_ref, lax.rem(session, per_device))

    lax.fori_loop(0, sessions, fetch, 0)

    def work(session, _):
        ours = hop_ref[session] == hops[0]
        for hop in hops[1:]:
            ours = ours | (hop_ref[session] == hop)
        if carried:
            @pl.when(jnp.logical_not(ours))
            def _():
                rows = pl.ds(pl.multiple_of(session * SLOTS, SLOTS), SLOTS)
                store(session, before_ref[rows])

        @pl.when(ours)
        def _():
            for copy in copies(session, 0):
                copy.wait()
            store(
                session,
                session_attention(
                    query_ref, key_ref, value_ref, kv[session], session, length_ref[0, session]
                ),
            )

        return 0

    lax.fori_loop(0, sessions, work, 0)


def attend_hops(index, hop, held, lengths, query, key, value, prompts, hops, before):
    sessions = hop.shape[0]
    carried = before is not None
    pieces = [piece for h in hops for piece in prompts[h]]
    work = sessions * len(hops) // 7 + 1
    width = PER_GROUP * HD
    if carried:
        out_shape = [jax.ShapeDtypeStruct((sessions // KVH * SLOTS, width), jnp.bfloat16)] * KVH
    else:
        out_shape = jax.ShapeDtypeStruct((sessions * SLOTS, width), jnp.bfloat16)
    return pl.pallas_call(
        functools.partial(hops_kernel, hops=hops, carried=carried),
        in_specs=[SMEM] * 4 + [VMEM] * (3 + carried) + [ANY] * len(pieces),
        out_specs=[VMEM] * KVH if carried else VMEM,
        out_shape=out_shape,
        scratch_shapes=[
            pltpu.VMEM((sessions, 2, 2, PROMPT // 4, 2 * HD), jnp.bfloat16),
            pltpu.SemaphoreType.DMA((sessions, 2)),
        ],
        compiler_params=pltpu.CompilerParams(vmem_limit_bytes=40 << 20),
        cost_estimate=pl.CostEstimate(
            flops=work * 4 * PER_GROUP * SLOTS * (PROMPT + SLOTS) * HD,
            bytes_accessed=work * PROMPT * 4 * HD,
            transcendentals=work * PER_GROUP * SLOTS * (PROMPT + SLOTS),
        ),
        name="attend",
    )(index, hop, held, lengths, query, key, value, *([before] if carried else []), *pieces)


def output_kernel(index_ref, length_ref, states_ref, weight_ref, *refs):
    piece_refs, out_ref = refs[:-1], refs[-1]
    head = index_ref[3]
    group_width = PER_GROUP * HD
    per_device = out_ref.shape[0]
    total = per_device * SLOTS
    summed = states_ref[pl.ds(pl.multiple_of(head * total, SLOTS), total)].astype(jnp.float32)
    for by, piece_ref in enumerate(piece_refs):
        start = pl.multiple_of((head ^ by) * group_width, group_width)
        summed = summed + jnp.dot(
            piece_ref[...], weight_ref[pl.ds(start, group_width)], preferred_element_type=jnp.float32
        )
    row = lax.broadcasted_iota(jnp.int32, (SLOTS, 1), 0)
    for i in range(per_device):
        live = row < length_ref[0, head * per_device + i]
        part = summed[i * SLOTS : (i + 1) * SLOTS]
        out_ref[i] = jnp.where(live, part, 0.0).astype(jnp.bfloat16)


def output(index, lengths, states, o_weight, pieces, per_device):
    model = o_weight.shape[1]
    return pl.pallas_call(
        output_kernel,
        in_specs=[SMEM] * 2 + [VMEM] * (2 + len(pieces)),
        out_specs=VMEM,
        out_shape=jax.ShapeDtypeStruct((per_device, SLOTS, model), jnp.bfloat16),
        compiler_params=pltpu.CompilerParams(vmem_limit_bytes=40 << 20),
        cost_estimate=pl.CostEstimate(
            flops=2 * per_device * SLOTS * o_weight.size, bytes_accessed=o_weight.size * 2, transcendentals=0
        ),
        name="output",
    )(index, lengths, states, o_weight, *pieces)


def shifted(n, by):
    return [(i, i + by) for i in range(n) if 0 <= i + by < n]


def swapped(n, by):
    return [(i, i ^ by) for i in range(n)]


def line_body(
    thinker_rows,
    row_session,
    speaker_of,
    prompt_slot,
    prompt_cache,
    proj_weight,
    attn_gain,
    q_weight,
    k_weight,
    v_weight,
    o_weight,
):
    planes, plane, rep_count = lax.axis_size("sess"), KVH, 2
    blocks = planes * rep_count
    session_all = speaker_of.shape[0]
    per_plane = session_all // planes
    per_device = per_plane // plane
    slot_cap = SLOTS // blocks
    held = prompt_cache.shape[0]
    model = proj_weight.shape[1]
    width = model // 2
    z, x, c = lax.axis_index("sess"), lax.axis_index("inner"), lax.axis_index("rep")
    head = x * rep_count + c
    index = jnp.stack([z, x, c, head]).astype(jnp.int32)
    pair = ("inner", "rep")

    own, to_core, to_x, to_far = split_heads(head.reshape(1), prompt_cache)
    from_core = lax.ppermute(to_core, pair, swapped(4, 1))
    from_x = lax.ppermute(to_x, pair, swapped(4, 2))
    from_far = lax.ppermute(to_far, pair, swapped(4, 3))
    first = stack(own[None], from_core[None])
    second = stack(from_x[None], from_far[None])
    right = [first, second]
    left = [first, second]
    prompts = {0: (first, second)}
    for hop in range(1, planes):
        for chunk in range(2):
            right[chunk] = lax.ppermute(right[chunk], "sess", shifted(planes, 1))
            left[chunk] = lax.ppermute(left[chunk], "sess", shifted(planes, -1))
        prompts[-hop], prompts[hop] = tuple(right), tuple(left)

    thinker_rows, _ = lax.optimization_barrier((thinker_rows, (prompts[-1][0], prompts[1][0])))
    partial_sum = jnp.dot(thinker_rows, proj_weight, preferred_element_type=jnp.float32)
    kept = lax.dynamic_slice_in_dim(partial_sum, x * width, width, 1)
    sent = lax.dynamic_slice_in_dim(partial_sum, (1 - x) * width, width, 1)
    came = lax.ppermute(sent.astype(jnp.bfloat16), "inner", swapped(2, 1))
    came, _ = lax.optimization_barrier((came, (prompts[-1][1], prompts[1][1])))
    routed = route(z.reshape(1), kept, came, row_session, planes, per_plane, slot_cap)
    routed, _ = lax.optimization_barrier((tuple(routed), (prompts[-2][0], prompts[2][0])))
    arrived = [routed[0]] + [
        lax.ppermute(routed[by], "sess", swapped(planes, by)) for by in range(1, planes)
    ]
    arrived, _ = lax.optimization_barrier((arrived, (prompts[-2][1], prompts[2][1])))
    arrived = stack(*[a[None] for a in arrived])
    other = lax.ppermute(arrived, "inner", swapped(2, 1))
    other, _ = lax.optimization_barrier((other, (prompts[-3][0], prompts[3][0])))
    mine = stack(arrived, other)
    core = lax.ppermute(mine, "rep", swapped(2, 1))

    group_width = PER_GROUP * HD
    weight = jnp.concatenate(
        [
            lax.dynamic_slice_in_dim(q_weight, head * group_width, group_width, 1),
            lax.dynamic_slice_in_dim(k_weight, head * HD, HD, 1),
            lax.dynamic_slice_in_dim(v_weight, head * HD, HD, 1),
        ],
        axis=1,
    )
    states, query, key, value, lengths = place_rows(
        index, mine, core, attn_gain, weight, per_plane, slot_cap
    )

    speakers = lax.dynamic_slice_in_dim(speaker_of, z * per_plane, per_plane)
    wanted_slot = jnp.sum(
        jnp.where(
            speakers[:, None] == jnp.arange(prompt_slot.shape[0])[None, :], prompt_slot[None, :], 0
        ),
        axis=1,
    )
    hop = wanted_slot // held - z
    which = wanted_slot % held
    near = attend_hops(
        index, hop, which, lengths, query, key, value, prompts, (0, -1, 1, -2, 2), None
    )
    attended = attend_hops(
        index, hop, which, lengths, query, key, value, prompts, (-3, 3), near
    )

    pieces = [attended[0]] + [
        lax.ppermute(attended[by], pair, swapped(4, by)) for by in range(1, plane)
    ]
    return output(index, lengths, states, o_weight, pieces, per_device)


def solution(mesh):
    in_specs = (
        P(("groups", "sess", "rep"), "inner"),
        P(("groups", "sess", "rep"), None),
        P("groups"),
        P("groups"),
        P(("groups", "sess"), ("inner", "rep"), None),
        P("inner", None),
        P(),
        P(),
        P(),
        P(),
        P(),
    )
    out_specs = P(("groups", "sess", "inner", "rep"), None, None)
    sizes = tuple(mesh.shape[name] for name in ("sess", "inner", "rep"))
    body = line_body if sizes == (4, 2, 2) else general_body
    return jax.shard_map(body, mesh=mesh, in_specs=in_specs, out_specs=out_specs, check_vma=False)
```

```python
import functools
import math

import jax
import jax.numpy as jnp
import numpy as np
from jax import lax
from jax.experimental import pallas as pl
from jax.experimental.pallas import tpu as pltpu
from jax.sharding import PartitionSpec as P

H = 12
KVH = 4
HD = 128
PROMPT = 1024
SLOTS = 96
PER_GROUP = H // KVH

EPSILON = 1e-06
ROPE_BASE = 1000000.0
NT = (((1,), (1,)), ((), ()))


def rope_tables(copies):
    half_width = HD // 2
    inverse = ROPE_BASE ** (-(np.arange(half_width, dtype=np.float64) * 2.0) / HD)
    angles = (PROMPT + np.arange(SLOTS, dtype=np.float64))[:, None] * inverse[None, :]
    cosine = np.concatenate([np.cos(angles), np.cos(angles)], axis=1)
    sine = np.concatenate([-np.sin(angles), np.sin(angles)], axis=1)
    return (
        np.tile(cosine, (copies, 1)).astype(np.float32),
        np.tile(sine, (copies, 1)).astype(np.float32),
    )


def states_kernel(code_ref, slots_ref, gain_ref, weight_ref, cos_ref, sin_ref,
                  states_ref, query_ref, key_ref, value_ref):
    halves, blocks, rows, width = slots_ref.shape
    total = states_ref.shape[0]
    place = lax.broadcasted_iota(jnp.int32, (total, blocks * rows), 0)
    pick = (place == code_ref[0]).astype(jnp.bfloat16)
    parts = [
        jnp.dot(
            pick,
            slots_ref[half].reshape(blocks * rows, width),
            preferred_element_type=jnp.float32,
        )
        for half in range(halves)
    ]
    widened = jnp.concatenate(parts, axis=1)
    states_ref[...] = widened.astype(jnp.bfloat16)
    factor = lax.rsqrt(jnp.mean(widened * widened, axis=-1, keepdims=True) + EPSILON)
    normed = (widened * factor * gain_ref[...].astype(jnp.float32)).astype(jnp.bfloat16)
    both = jnp.dot(normed, weight_ref[...], preferred_element_type=jnp.float32)
    cosine, sine = cos_ref[...], sin_ref[...]
    for head in range(PER_GROUP + 1):
        vector = both[:, head * HD : (head + 1) * HD]
        turned = vector * cosine + pltpu.roll(vector, HD // 2, 1) * sine
        if head < PER_GROUP:
            query_ref[:, head * HD : (head + 1) * HD] = turned.astype(jnp.bfloat16)
        else:
            key_ref[...] = turned.astype(jnp.bfloat16)
    value_ref[...] = both[:, (PER_GROUP + 1) * HD :].astype(jnp.bfloat16)


def attention_kernel(place_ref, length_ref, query_ref, key_ref, value_ref, prompt_ref, out_ref):
    session = pl.program_id(0)
    length = length_ref[session]
    scale = HD ** (-0.5) * math.log2(math.e)
    query = jnp.concatenate(
        [query_ref[:, h * HD : (h + 1) * HD] for h in range(PER_GROUP)], axis=0
    )
    ahead = lax.dot_general(query, prompt_ref[0, :, :HD], NT, preferred_element_type=jnp.float32)
    own = lax.dot_general(query, key_ref[...], NT, preferred_element_type=jnp.float32)
    row = lax.broadcasted_iota(jnp.int32, (SLOTS, SLOTS), 0)
    column = lax.broadcasted_iota(jnp.int32, (SLOTS, SLOTS), 1)
    allowed = (column <= row) & (column < length)
    own = jnp.where(jnp.concatenate([allowed] * PER_GROUP, axis=0), own, -1e30)
    highest = jnp.maximum(
        jnp.max(ahead, axis=-1, keepdims=True), jnp.max(own, axis=-1, keepdims=True)
    )
    powers = jnp.exp2((ahead - highest) * scale)
    own_powers = jnp.exp2((own - highest) * scale)
    total = jnp.sum(powers, axis=-1, keepdims=True) + jnp.sum(own_powers, axis=-1, keepdims=True)
    mixed = jnp.dot(
        powers.astype(jnp.bfloat16), prompt_ref[0, :, HD:], preferred_element_type=jnp.float32
    ) + jnp.dot(own_powers.astype(jnp.bfloat16), value_ref[...], preferred_element_type=jnp.float32)
    mixed = (mixed / total).astype(jnp.bfloat16)
    for h in range(PER_GROUP):
        out_ref[:, h * HD : (h + 1) * HD] = mixed[h * SLOTS : (h + 1) * SLOTS]


def make_states(code, slots, gain, weight, sessions, together):
    halves, blocks, rows, width = slots.shape
    steps = sessions // together
    model = halves * width
    cosine, sine = rope_tables(together)
    total = together * SLOTS
    out = jax.ShapeDtypeStruct
    row_spec = lambda w: pl.BlockSpec((total, w), lambda i: (i, 0))
    whole = lambda a: pl.BlockSpec(a.shape, lambda i: (0,) * a.ndim)
    gain = gain.reshape(1, model)
    return pl.pallas_call(
        states_kernel,
        grid=(steps,),
        in_specs=[
            pl.BlockSpec((1, 1, code.shape[2]), lambda i: (i, 0, 0)),
            pl.BlockSpec((halves, blocks, rows // steps, width), lambda i: (0, 0, i, 0)),
            whole(gain),
            whole(weight),
            whole(cosine),
            whole(sine),
        ],
        out_specs=[row_spec(model), row_spec(PER_GROUP * HD), row_spec(HD), row_spec(HD)],
        out_shape=[
            out((sessions * SLOTS, model), jnp.bfloat16),
            out((sessions * SLOTS, PER_GROUP * HD), jnp.bfloat16),
            out((sessions * SLOTS, HD), jnp.bfloat16),
            out((sessions * SLOTS, HD), jnp.bfloat16),
        ],
        compiler_params=pltpu.CompilerParams(vmem_limit_bytes=40 << 20),
        name="states",
    )(code, slots, gain, weight, jnp.asarray(cosine), jnp.asarray(sine))


def attend(place, lengths, query, key, value, prompts):
    sessions = place.shape[0]
    row_spec = lambda w: pl.BlockSpec((SLOTS, w), lambda i, place, length: (i, 0))
    return pl.pallas_call(
        attention_kernel,
        grid_spec=pltpu.PrefetchScalarGridSpec(
            num_scalar_prefetch=2,
            grid=(sessions,),
            in_specs=[
                row_spec(PER_GROUP * HD),
                row_spec(HD),
                row_spec(HD),
                pl.BlockSpec((1, PROMPT, 2 * HD), lambda i, place, length: (place[i], 0, 0)),
            ],
            out_specs=row_spec(PER_GROUP * HD),
        ),
        out_shape=jax.ShapeDtypeStruct((sessions * SLOTS, PER_GROUP * HD), jnp.bfloat16),
        compiler_params=pltpu.CompilerParams(vmem_limit_bytes=40 << 20),
        name="attend",
    )(place, lengths, query, key, value, prompts)


def general_body(
    thinker_rows,
    row_session,
    speaker_of,
    prompt_slot,
    prompt_cache,
    proj_weight,
    attn_gain,
    q_weight,
    k_weight,
    v_weight,
    o_weight,
):
    sess_count = lax.axis_size("sess")
    inner_count = lax.axis_size("inner")
    rep_count = lax.axis_size("rep")
    plane = inner_count * rep_count
    blocks = sess_count * rep_count
    session_all = speaker_of.shape[0]
    per_plane = session_all // sess_count
    per_device = per_plane // plane
    slot_cap = SLOTS // blocks
    held, tokens, channels = prompt_cache.shape
    model = proj_weight.shape[1]
    sharers = plane // KVH
    held_part = held // sharers
    sess_place = lax.axis_index("sess")
    plane_place = lax.axis_index("inner") * rep_count + lax.axis_index("rep")
    head = plane_place // sharers
    sharer = plane_place % sharers

    outgoing = jnp.transpose(
        prompt_cache.reshape(sharers, held_part, tokens, 2, KVH, HD), (4, 0, 1, 2, 3, 5)
    ).reshape(plane, held_part, tokens, 2 * HD)
    own_head = lax.all_to_all(outgoing, ("inner", "rep"), split_axis=0, concat_axis=2, tiled=True)
    own_head = own_head.reshape(held_part, plane * tokens, 2 * HD)
    prompts = lax.all_gather(own_head, "sess", axis=0, tiled=True)

    row_owner = row_session[:, 0]
    order = jnp.arange(row_owner.shape[0])
    same = row_owner[:, None] == row_owner[None, :]
    earlier = jnp.sum((same & (order[None, :] < order[:, None])).astype(jnp.int32), axis=1)
    row_slot = row_owner * slot_cap + earlier
    counts = jnp.sum(
        (row_owner[:, None] == jnp.arange(session_all)[None, :]).astype(jnp.int32), axis=0
    )
    all_counts = lax.all_gather(counts, ("sess", "rep"), axis=0, tiled=False)

    partial_sum = jnp.dot(thinker_rows, proj_weight, preferred_element_type=jnp.float32)
    width = model // inner_count
    if inner_count == 2:
        inner_place = lax.axis_index("inner")
        kept = lax.dynamic_slice_in_dim(partial_sum, inner_place * width, width, 1)
        sent = lax.dynamic_slice_in_dim(partial_sum, (1 - inner_place) * width, width, 1)
        came = lax.ppermute(sent.astype(jnp.bfloat16), "inner", [(0, 1), (1, 0)])
        own_columns = (kept + came.astype(jnp.float32)).astype(jnp.bfloat16)
    else:
        own_columns = lax.psum_scatter(
            partial_sum, "inner", scatter_dimension=1, tiled=True
        ).astype(jnp.bfloat16)
    into = (jnp.arange(session_all * slot_cap)[:, None] == row_slot[None, :]).astype(jnp.bfloat16)
    buffer = jnp.dot(into, own_columns, preferred_element_type=jnp.float32).astype(jnp.bfloat16)
    arrived = lax.all_to_all(
        buffer.reshape(sess_count, per_plane * slot_cap, width),
        "sess",
        split_axis=0,
        concat_axis=0,
        tiled=True,
    )
    spread = lax.all_gather(arrived, ("inner", "rep"), axis=0, tiled=False)
    slots = spread.reshape(inner_count, rep_count * sess_count, per_plane * slot_cap, width)

    offsets = jnp.cumsum(all_counts, axis=0) - all_counts
    lengths_all = jnp.sum(all_counts, axis=0)
    mine = lambda a: lax.dynamic_slice_in_dim(a, sess_place * per_plane, per_plane, a.ndim - 1)
    by_block = lambda a: jnp.transpose(
        mine(a).reshape(sess_count, rep_count, per_plane), (1, 0, 2)
    ).reshape(blocks, per_plane)
    lengths = mine(lengths_all)
    together = 16 // math.gcd(16, slot_cap)
    within = jnp.arange(slot_cap)
    local = (jnp.arange(per_plane) % together)[None, :, None] * SLOTS
    code = jnp.where(
        within[None, None, :] < by_block(all_counts)[:, :, None],
        by_block(offsets)[:, :, None] + within[None, None, :] + local,
        -1,
    )
    steps = per_plane // together
    code = jnp.transpose(
        code.reshape(blocks, steps, together * slot_cap), (1, 0, 2)
    ).reshape(steps, 1, blocks * together * slot_cap)

    group_width = PER_GROUP * HD
    weight = jnp.concatenate(
        [
            lax.dynamic_slice_in_dim(q_weight, head * group_width, group_width, 1),
            lax.dynamic_slice_in_dim(k_weight, head * HD, HD, 1),
            lax.dynamic_slice_in_dim(v_weight, head * HD, HD, 1),
        ],
        axis=1,
    )
    states, query, key, value = make_states(
        code, slots, attn_gain, weight, per_plane, together
    )

    wanted_slot = jnp.sum(
        jnp.where(
            mine(speaker_of)[:, None] == jnp.arange(prompt_slot.shape[0])[None, :],
            prompt_slot[None, :],
            0,
        ),
        axis=1,
    )
    place = wanted_slot // held * held_part + wanted_slot % held_part
    attended = attend(place, lengths, query, key, value, prompts)
    returned = lax.all_to_all(
        attended.reshape(plane, per_device * SLOTS, group_width),
        ("inner", "rep"),
        split_axis=0,
        concat_axis=0,
        tiled=True,
    ).reshape(KVH, sharers, per_device, SLOTS, group_width)
    first = plane_place * per_device
    if sharers > 1:
        holder = lax.dynamic_slice_in_dim(wanted_slot % held // held_part, first, per_device)
        chosen = jnp.zeros_like(returned[:, 0])
        for t in range(sharers):
            chosen = jnp.where((holder == t)[None, :, None, None], returned[:, t], chosen)
    else:
        chosen = returned[:, 0]
    gathered = jnp.transpose(chosen, (1, 2, 0, 3)).reshape(per_device * SLOTS, H * HD)
    own_states = lax.dynamic_slice_in_dim(states, first * SLOTS, per_device * SLOTS, 0)
    own_lengths = lax.dynamic_slice_in_dim(lengths, first, per_device)
    summed = own_states.astype(jnp.float32) + jnp.dot(
        gathered, o_weight, preferred_element_type=jnp.float32
    )
    live_rows = (jnp.arange(SLOTS)[None, :] < own_lengths[:, None]).reshape(-1, 1)
    return (
        jnp.where(live_rows, summed, 0.0)
        .astype(jnp.bfloat16)
        .reshape(per_device, SLOTS, model)
    )


EXTRA = 16
SMEM = pl.BlockSpec(memory_space=pltpu.SMEM)
VMEM = pl.BlockSpec(memory_space=pltpu.VMEM)
ANY = pl.BlockSpec(memory_space=pl.ANY)


def split_heads_kernel(head_ref, cache_ref, *out_refs):
    for by, out_ref in enumerate(out_refs):
        for side in range(2):
            start = pl.multiple_of((head_ref[0] ^ by) * HD + side * KVH * HD, HD)
            out_ref[:, :, side * HD : (side + 1) * HD] = cache_ref[:, :, pl.ds(start, HD)]


def split_heads(head, cache):
    held, tokens, _ = cache.shape
    shape = jax.ShapeDtypeStruct((held, tokens, 2 * HD), cache.dtype)
    return pl.pallas_call(
        split_heads_kernel,
        in_specs=[SMEM, VMEM],
        out_specs=[VMEM] * KVH,
        out_shape=[shape] * KVH,
        cost_estimate=pl.CostEstimate(flops=0, bytes_accessed=2 * cache.size * 2, transcendentals=0),
        name="split_heads",
    )(head, cache)


def stack_kernel(*refs):
    in_refs, out_ref = refs[:-1], refs[-1]
    place = 0
    for in_ref in in_refs:
        count = in_ref.shape[0]
        out_ref[place : place + count] = in_ref[...]
        place += count


def stack(*arrays):
    total = sum(a.shape[0] for a in arrays)
    size = sum(a.size for a in arrays)
    return pl.pallas_call(
        stack_kernel,
        in_specs=[VMEM] * len(arrays),
        out_specs=VMEM,
        out_shape=jax.ShapeDtypeStruct((total,) + arrays[0].shape[1:], arrays[0].dtype),
        cost_estimate=pl.CostEstimate(flops=0, bytes_accessed=4 * size, transcendentals=0),
        name="stack",
    )(*arrays)


def route_kernel(z_ref, kept_ref, came_ref, owner_ref, owner_row_ref, *out_refs,
                 slot_cap, per_plane):
    rows = kept_ref.shape[0]
    planes = len(out_refs)
    size = out_refs[0].shape[0]
    live = per_plane * slot_cap
    columns = (kept_ref[...] + came_ref[...].astype(jnp.float32)).astype(jnp.bfloat16)
    owner, owner_row = owner_ref[...], owner_row_ref[...]
    above = lax.broadcasted_iota(jnp.int32, (rows, rows), 0)
    beside = lax.broadcasted_iota(jnp.int32, (rows, rows), 1)
    earlier = jnp.sum(
        jnp.where((owner == owner_row) & (above < beside), 1.0, 0.0), axis=0, keepdims=True
    ).astype(jnp.int32)
    target = lax.div(owner_row, per_plane) ^ z_ref[0]
    code = target * size + lax.rem(owner_row, per_plane) * slot_cap + earlier
    place = lax.broadcasted_iota(jnp.int32, (planes * size, rows), 0)
    into = (place == code).astype(jnp.bfloat16)
    routed = jnp.dot(into, columns, preferred_element_type=jnp.float32).astype(jnp.bfloat16)
    lane = lax.broadcasted_iota(jnp.int32, (rows, HD), 1)
    named = (lane == owner).astype(jnp.bfloat16)
    counts = jnp.dot(
        jnp.ones((EXTRA, rows), jnp.bfloat16), named, preferred_element_type=jnp.float32
    ).astype(jnp.bfloat16)
    for k, out_ref in enumerate(out_refs):
        out_ref[:live] = routed[k * size : k * size + live]
        out_ref[live:] = jnp.zeros((EXTRA, out_ref.shape[1]), jnp.bfloat16)
        out_ref[live:, :HD] = counts


def route(z, kept, came, row_session, planes, per_plane, slot_cap):
    width = kept.shape[1]
    rows = row_session.shape[0]
    size = per_plane * slot_cap + EXTRA
    return pl.pallas_call(
        functools.partial(route_kernel, slot_cap=slot_cap, per_plane=per_plane),
        in_specs=[SMEM] + [VMEM] * 4,
        out_specs=[VMEM] * planes,
        out_shape=[jax.ShapeDtypeStruct((size, width), jnp.bfloat16)] * planes,
        cost_estimate=pl.CostEstimate(
            flops=2 * planes * size * rows * width, bytes_accessed=rows * width * 8, transcendentals=0
        ),
        name="route",
    )(z, kept, came, row_session, row_session.reshape(1, rows))


def place_kernel(index_ref, mine_ref, core_ref, gain_ref, weight_ref, cos_ref, sin_ref,
                 states_ref, query_ref, key_ref, value_ref, length_ref, *, slot_cap, together):
    z, x, c = index_ref[0], index_ref[1], index_ref[2]
    planes = mine_ref.shape[0] // 2
    blocks = 2 * planes
    width = mine_ref.shape[2]
    live = mine_ref.shape[1] - EXTRA
    per_plane = live // slot_cap
    steps = per_plane // together
    window = together * slot_cap
    total = together * SLOTS
    counts = jnp.concatenate(
        [ref[k, live : live + 1, :HD] for ref in (mine_ref, core_ref) for k in range(planes)],
        axis=0,
    ).astype(jnp.float32)
    kind = lambda axis: lax.broadcasted_iota(jnp.int32, (blocks, blocks), axis)
    true_block = lambda k: (z ^ (k % planes)) * 2 + (c ^ (k // planes))
    before = (true_block(kind(1)) < true_block(kind(0))).astype(jnp.float32)
    offsets = jnp.dot(before, counts, preferred_element_type=jnp.float32)
    session_lane = lax.broadcasted_iota(jnp.int32, (HD, HD), 0)
    local_lane = lax.broadcasted_iota(jnp.int32, (HD, HD), 1)
    ours = (session_lane == z * per_plane + local_lane).astype(jnp.float32)
    sums = jnp.dot(
        jnp.broadcast_to(jnp.sum(counts, axis=0, keepdims=True), (8, HD)),
        ours,
        preferred_element_type=jnp.float32,
    )
    length_ref[...] = sums[:1].astype(jnp.int32)
    cosine, sine = cos_ref[...], sin_ref[...]
    gain = gain_ref[...].astype(jnp.float32)
    for step in range(steps):
        slot = lax.broadcasted_iota(jnp.int32, (blocks, blocks * window), 1)
        in_block = slot % window
        spread = lax.broadcasted_iota(jnp.int32, (HD, blocks * window), 1) % window // slot_cap
        from_lane = lax.broadcasted_iota(jnp.int32, (HD, blocks * window), 0)
        expand = (from_lane == z * per_plane + step * together + spread).astype(jnp.float32)
        here = jnp.dot(counts, expand, preferred_element_type=jnp.float32).astype(jnp.int32)
        start = jnp.dot(offsets, expand, preferred_element_type=jnp.float32).astype(jnp.int32)
        within = in_block % slot_cap
        row = jnp.where(within < here, start + within + in_block // slot_cap * SLOTS, -1)
        block = lax.broadcasted_iota(jnp.int32, (blocks, blocks * window), 0)
        code = jnp.max(jnp.where(slot // window == block, row, -1), axis=0, keepdims=True)
        place = lax.broadcasted_iota(jnp.int32, (total, blocks * window), 0)
        pick = (place == code).astype(jnp.bfloat16)
        slots = slice(step * window, (step + 1) * window)
        near, far = [
            jnp.dot(
                pick,
                jnp.concatenate(
                    [ref[half * planes + k, slots] for ref in (mine_ref, core_ref) for k in range(planes)],
                    axis=0,
                ),
                preferred_element_type=jnp.float32,
            )
            for half in range(2)
        ]
        widened = jnp.concatenate(
            [jnp.where(x == 0, near, far), jnp.where(x == 0, far, near)], axis=1
        )
        rows = slice(step * total, (step + 1) * total)
        states_ref[rows] = widened.astype(jnp.bfloat16)
        factor = lax.rsqrt(jnp.mean(widened * widened, axis=-1, keepdims=True) + EPSILON)
        normed = (widened * factor * gain).astype(jnp.bfloat16)
        both = jnp.dot(normed, weight_ref[...], preferred_element_type=jnp.float32)
        for h in range(PER_GROUP + 1):
            vector = both[:, h * HD : (h + 1) * HD]
            turned = vector * cosine + pltpu.roll(vector, HD // 2, 1) * sine
            if h < PER_GROUP:
                query_ref[rows, h * HD : (h + 1) * HD] = turned.astype(jnp.bfloat16)
            else:
                key_ref[rows] = turned.astype(jnp.bfloat16)
        value_ref[rows] = both[:, (PER_GROUP + 1) * HD :].astype(jnp.bfloat16)


def place_rows(index, mine, core, gain, weight, sessions, slot_cap):
    together = 16 // math.gcd(16, slot_cap)
    cosine, sine = rope_tables(together)
    model = 2 * mine.shape[2]
    total = sessions * SLOTS
    out = lambda w: jax.ShapeDtypeStruct((total, w), jnp.bfloat16)
    return pl.pallas_call(
        functools.partial(place_kernel, slot_cap=slot_cap, together=together),
        in_specs=[SMEM] + [VMEM] * 6,
        out_specs=[VMEM] * 5,
        out_shape=[
            out(model), out(PER_GROUP * HD), out(HD), out(HD),
            jax.ShapeDtypeStruct((1, HD), jnp.int32),
        ],
        compiler_params=pltpu.CompilerParams(vmem_limit_bytes=40 << 20),
        cost_estimate=pl.CostEstimate(
            flops=4 * total * model * weight.shape[1], bytes_accessed=6 << 20, transcendentals=0
        ),
        name="place_rows",
    )(index, mine, core, gain.reshape(1, model), weight, jnp.asarray(cosine), jnp.asarray(sine))


def session_attention(query, key, value, tokens, length):
    scale = HD ** (-0.5) * math.log2(math.e)
    query = jnp.concatenate([query[:, h * HD : (h + 1) * HD] for h in range(PER_GROUP)], axis=0)
    ahead = lax.dot_general(query, tokens[:, :HD], NT, preferred_element_type=jnp.float32)
    own = lax.dot_general(query, key, NT, preferred_element_type=jnp.float32)
    row = lax.broadcasted_iota(jnp.int32, (SLOTS, SLOTS), 0)
    column = lax.broadcasted_iota(jnp.int32, (SLOTS, SLOTS), 1)
    allowed = (column <= row) & (column < length)
    own = jnp.where(jnp.concatenate([allowed] * PER_GROUP, axis=0), own, -1e30)
    highest = jnp.maximum(
        jnp.max(ahead, axis=-1, keepdims=True), jnp.max(own, axis=-1, keepdims=True)
    )
    powers = jnp.exp2((ahead - highest) * scale)
    own_powers = jnp.exp2((own - highest) * scale)
    total = jnp.sum(powers, axis=-1, keepdims=True) + jnp.sum(own_powers, axis=-1, keepdims=True)
    mixed = jnp.dot(
        powers.astype(jnp.bfloat16), tokens[:, HD:], preferred_element_type=jnp.float32
    ) + jnp.dot(own_powers.astype(jnp.bfloat16), value, preferred_element_type=jnp.float32)
    return (mixed / total).astype(jnp.bfloat16)


def attend_kernel(index_ref, hop_ref, held_ref, length_ref, query_ref, key_ref, value_ref,
                  gathered_ref, *refs, targets, hops):
    chain_refs, refs = refs[: len(hops)], refs[len(hops) :]
    out_refs, (kv, sem) = refs[: len(targets)], refs[len(targets) :]
    z, head = index_ref[0], index_ref[3]
    per_device = out_refs[0].shape[0] // SLOTS
    places = [(t, j) for t in range(len(targets)) for j in range(per_device)]

    def session_of(i):
        t, j = places[i]
        return (head ^ targets[t]) * per_device + j

    def from_gathered(i):
        session = session_of(i)
        plane = z + hop_ref[session]
        return pltpu.make_async_copy(
            gathered_ref.at[pl.ds(2 * plane, 2), held_ref[session]], kv.at[i, 0], sem.at[i, 0]
        )

    def from_chain(i, which):
        return pltpu.make_async_copy(
            chain_refs[which].at[:, held_ref[session_of(i)]], kv.at[i, 1], sem.at[i, 1]
        )

    for i in range(len(places)):
        from_gathered(i).start()
        for which, hop in enumerate(hops):
            @pl.when(hop_ref[session_of(i)] == hop)
            def _():
                from_chain(i, which).start()
    for i in range(len(places)):
        from_gathered(i).wait()
        from_chain(i, 0).wait()
    for i, (t, j) in enumerate(places):
        session = session_of(i)
        rows = pl.ds(pl.multiple_of(session * SLOTS, SLOTS), SLOTS)
        mixed = session_attention(
            query_ref[rows],
            key_ref[rows],
            value_ref[rows],
            kv[i].reshape(PROMPT, 2 * HD),
            length_ref[0, session],
        )
        for h in range(PER_GROUP):
            out_refs[t][j * SLOTS : (j + 1) * SLOTS, h * HD : (h + 1) * HD] = mixed[
                h * SLOTS : (h + 1) * SLOTS
            ]


def attend_for(index, hop, held, lengths, query, key, value, gathered, chain, targets):
    per_device = hop.shape[0] // KVH
    hops = tuple(sorted(chain))
    work = per_device * len(targets)
    width = PER_GROUP * HD
    return pl.pallas_call(
        functools.partial(attend_kernel, targets=targets, hops=hops),
        in_specs=[SMEM] * 4 + [VMEM] * 3 + [ANY] * (1 + len(hops)),
        out_specs=[VMEM] * len(targets),
        out_shape=[jax.ShapeDtypeStruct((per_device * SLOTS, width), jnp.bfloat16)] * len(targets),
        scratch_shapes=[
            pltpu.VMEM((work, 2, 2, PROMPT // 4, 2 * HD), jnp.bfloat16),
            pltpu.SemaphoreType.DMA((work, 2)),
        ],
        compiler_params=pltpu.CompilerParams(vmem_limit_bytes=40 << 20),
        cost_estimate=pl.CostEstimate(
            flops=work * 4 * PER_GROUP * SLOTS * (PROMPT + SLOTS) * HD,
            bytes_accessed=work * PROMPT * 4 * HD,
            transcendentals=work * PER_GROUP * SLOTS * (PROMPT + SLOTS),
        ),
        name="attend",
    )(index, hop, held, lengths, query, key, value, gathered, *[chain[h] for h in hops])


def output_kernel(index_ref, length_ref, states_ref, weight_ref, *refs):
    piece_refs, out_ref = refs[:-1], refs[-1]
    head = index_ref[3]
    group_width = PER_GROUP * HD
    per_device = out_ref.shape[0]
    total = per_device * SLOTS
    summed = states_ref[pl.ds(pl.multiple_of(head * total, SLOTS), total)].astype(jnp.float32)
    for by, piece_ref in enumerate(piece_refs):
        start = pl.multiple_of((head ^ by) * group_width, group_width)
        summed = summed + jnp.dot(
            piece_ref[...], weight_ref[pl.ds(start, group_width)], preferred_element_type=jnp.float32
        )
    row = lax.broadcasted_iota(jnp.int32, (SLOTS, 1), 0)
    for i in range(per_device):
        live = row < length_ref[0, head * per_device + i]
        part = summed[i * SLOTS : (i + 1) * SLOTS]
        out_ref[i] = jnp.where(live, part, 0.0).astype(jnp.bfloat16)


def output(index, lengths, states, o_weight, pieces, per_device):
    model = o_weight.shape[1]
    return pl.pallas_call(
        output_kernel,
        in_specs=[SMEM] * 2 + [VMEM] * (2 + len(pieces)),
        out_specs=VMEM,
        out_shape=jax.ShapeDtypeStruct((per_device, SLOTS, model), jnp.bfloat16),
        compiler_params=pltpu.CompilerParams(vmem_limit_bytes=40 << 20),
        cost_estimate=pl.CostEstimate(
            flops=2 * per_device * SLOTS * o_weight.size, bytes_accessed=o_weight.size * 2, transcendentals=0
        ),
        name="output",
    )(index, lengths, states, o_weight, *pieces)


def shifted(n, by):
    return [(i, i + by) for i in range(n) if 0 <= i + by < n]


def swapped(n, by):
    return [(i, i ^ by) for i in range(n)]


def line_body(
    thinker_rows,
    row_session,
    speaker_of,
    prompt_slot,
    prompt_cache,
    proj_weight,
    attn_gain,
    q_weight,
    k_weight,
    v_weight,
    o_weight,
):
    planes, plane, rep_count = lax.axis_size("sess"), KVH, 2
    blocks = planes * rep_count
    session_all = speaker_of.shape[0]
    per_plane = session_all // planes
    per_device = per_plane // plane
    slot_cap = SLOTS // blocks
    held = prompt_cache.shape[0]
    model = proj_weight.shape[1]
    width = model // 2
    z, x, c = lax.axis_index("sess"), lax.axis_index("inner"), lax.axis_index("rep")
    head = x * rep_count + c
    index = jnp.stack([z, x, c, head]).astype(jnp.int32)
    pair = ("inner", "rep")

    own, to_core, to_x, to_far = split_heads(head.reshape(1), prompt_cache)
    from_core = lax.ppermute(to_core, pair, swapped(4, 1))
    from_x = lax.ppermute(to_x, pair, swapped(4, 2))
    from_far = lax.ppermute(to_far, pair, swapped(4, 3))
    first = stack(own[None], from_core[None])
    second = stack(from_x[None], from_far[None])
    gathered = lax.all_gather(first, "sess", axis=0, tiled=True)
    right = left = second
    chain = {0: second}
    for hop in range(1, planes):
        right = lax.ppermute(right, "sess", shifted(planes, 1))
        left = lax.ppermute(left, "sess", shifted(planes, -1))
        chain[-hop], chain[hop] = right, left

    thinker_rows, _ = lax.optimization_barrier((thinker_rows, first))
    partial_sum = jnp.dot(thinker_rows, proj_weight, preferred_element_type=jnp.float32)
    kept = lax.dynamic_slice_in_dim(partial_sum, x * width, width, 1)
    sent = lax.dynamic_slice_in_dim(partial_sum, (1 - x) * width, width, 1)
    came = lax.ppermute(sent.astype(jnp.bfloat16), "inner", swapped(2, 1))
    came, _ = lax.optimization_barrier((came, second))
    routed = route(z.reshape(1), kept, came, row_session, planes, per_plane, slot_cap)
    arrived = [routed[0]] + [
        lax.ppermute(routed[by], "sess", swapped(planes, by)) for by in range(1, planes)
    ]
    arrived = stack(*[a[None] for a in arrived])
    other = lax.ppermute(arrived, "inner", swapped(2, 1))
    other, _ = lax.optimization_barrier((other, (chain[-1], chain[1])))
    mine = stack(arrived, other)
    core = lax.ppermute(mine, "rep", swapped(2, 1))
    core, _ = lax.optimization_barrier((core, (chain[-2], chain[2])))

    group_width = PER_GROUP * HD
    weight = jnp.concatenate(
        [
            lax.dynamic_slice_in_dim(q_weight, head * group_width, group_width, 1),
            lax.dynamic_slice_in_dim(k_weight, head * HD, HD, 1),
            lax.dynamic_slice_in_dim(v_weight, head * HD, HD, 1),
        ],
        axis=1,
    )
    states, query, key, value, lengths = place_rows(
        index, mine, core, attn_gain, weight, per_plane, slot_cap
    )

    speakers = lax.dynamic_slice_in_dim(speaker_of, z * per_plane, per_plane)
    wanted_slot = jnp.sum(
        jnp.where(
            speakers[:, None] == jnp.arange(prompt_slot.shape[0])[None, :], prompt_slot[None, :], 0
        ),
        axis=1,
    )
    hop = wanted_slot // held - z
    which = wanted_slot % held
    run = functools.partial(attend_for, index, hop, which, lengths)
    attended = {}
    attended[2], attended[3] = run(query, key, value, gathered, chain, (2, 3))
    query, _ = lax.optimization_barrier((query, attended[2]))
    attended[0], attended[1] = run(query, key, value, gathered, chain, (0, 1))
    pieces = [attended[0]] + [
        lax.ppermute(attended[by], pair, swapped(4, by)) for by in range(1, plane)
    ]
    return output(index, lengths, states, o_weight, pieces, per_device)


def solution(mesh):
    in_specs = (
        P(("groups", "sess", "rep"), "inner"),
        P(("groups", "sess", "rep"), None),
        P("groups"),
        P("groups"),
        P(("groups", "sess"), ("inner", "rep"), None),
        P("inner", None),
        P(),
        P(),
        P(),
        P(),
        P(),
    )
    out_specs = P(("groups", "sess", "inner", "rep"), None, None)
    sizes = tuple(mesh.shape[name] for name in ("sess", "inner", "rep"))
    body = line_body if sizes == (4, 2, 2) else general_body
    return jax.shard_map(body, mesh=mesh, in_specs=in_specs, out_specs=out_specs, check_vma=False)
```

```python
import functools
import math

import jax
import jax.numpy as jnp
import numpy as np
from jax import lax
from jax.experimental import pallas as pl
from jax.experimental.pallas import tpu as pltpu
from jax.sharding import PartitionSpec as P

H = 12
KVH = 4
HD = 128
PROMPT = 1024
SLOTS = 96
PER_GROUP = H // KVH

EPSILON = 1e-06
ROPE_BASE = 1000000.0
NT = (((1,), (1,)), ((), ()))


def rope_tables(copies):
    half_width = HD // 2
    inverse = ROPE_BASE ** (-(np.arange(half_width, dtype=np.float64) * 2.0) / HD)
    angles = (PROMPT + np.arange(SLOTS, dtype=np.float64))[:, None] * inverse[None, :]
    cosine = np.concatenate([np.cos(angles), np.cos(angles)], axis=1)
    sine = np.concatenate([-np.sin(angles), np.sin(angles)], axis=1)
    return (
        np.tile(cosine, (copies, 1)).astype(np.float32),
        np.tile(sine, (copies, 1)).astype(np.float32),
    )


def states_kernel(code_ref, slots_ref, gain_ref, weight_ref, cos_ref, sin_ref,
                  states_ref, query_ref, key_ref, value_ref):
    halves, blocks, rows, width = slots_ref.shape
    total = states_ref.shape[0]
    place = lax.broadcasted_iota(jnp.int32, (total, blocks * rows), 0)
    pick = (place == code_ref[0]).astype(jnp.bfloat16)
    parts = [
        jnp.dot(
            pick,
            slots_ref[half].reshape(blocks * rows, width),
            preferred_element_type=jnp.float32,
        )
        for half in range(halves)
    ]
    widened = jnp.concatenate(parts, axis=1)
    states_ref[...] = widened.astype(jnp.bfloat16)
    factor = lax.rsqrt(jnp.mean(widened * widened, axis=-1, keepdims=True) + EPSILON)
    normed = (widened * factor * gain_ref[...].astype(jnp.float32)).astype(jnp.bfloat16)
    both = jnp.dot(normed, weight_ref[...], preferred_element_type=jnp.float32)
    cosine, sine = cos_ref[...], sin_ref[...]
    for head in range(PER_GROUP + 1):
        vector = both[:, head * HD : (head + 1) * HD]
        turned = vector * cosine + pltpu.roll(vector, HD // 2, 1) * sine
        if head < PER_GROUP:
            query_ref[:, head * HD : (head + 1) * HD] = turned.astype(jnp.bfloat16)
        else:
            key_ref[...] = turned.astype(jnp.bfloat16)
    value_ref[...] = both[:, (PER_GROUP + 1) * HD :].astype(jnp.bfloat16)


def attention_kernel(place_ref, length_ref, query_ref, key_ref, value_ref, prompt_ref, out_ref):
    session = pl.program_id(0)
    length = length_ref[session]
    scale = HD ** (-0.5) * math.log2(math.e)
    query = jnp.concatenate(
        [query_ref[:, h * HD : (h + 1) * HD] for h in range(PER_GROUP)], axis=0
    )
    ahead = lax.dot_general(query, prompt_ref[0, :, :HD], NT, preferred_element_type=jnp.float32)
    own = lax.dot_general(query, key_ref[...], NT, preferred_element_type=jnp.float32)
    row = lax.broadcasted_iota(jnp.int32, (SLOTS, SLOTS), 0)
    column = lax.broadcasted_iota(jnp.int32, (SLOTS, SLOTS), 1)
    allowed = (column <= row) & (column < length)
    own = jnp.where(jnp.concatenate([allowed] * PER_GROUP, axis=0), own, -1e30)
    highest = jnp.maximum(
        jnp.max(ahead, axis=-1, keepdims=True), jnp.max(own, axis=-1, keepdims=True)
    )
    powers = jnp.exp2((ahead - highest) * scale)
    own_powers = jnp.exp2((own - highest) * scale)
    total = jnp.sum(powers, axis=-1, keepdims=True) + jnp.sum(own_powers, axis=-1, keepdims=True)
    mixed = jnp.dot(
        powers.astype(jnp.bfloat16), prompt_ref[0, :, HD:], preferred_element_type=jnp.float32
    ) + jnp.dot(own_powers.astype(jnp.bfloat16), value_ref[...], preferred_element_type=jnp.float32)
    mixed = (mixed / total).astype(jnp.bfloat16)
    for h in range(PER_GROUP):
        out_ref[:, h * HD : (h + 1) * HD] = mixed[h * SLOTS : (h + 1) * SLOTS]


def make_states(code, slots, gain, weight, sessions, together):
    halves, blocks, rows, width = slots.shape
    steps = sessions // together
    model = halves * width
    cosine, sine = rope_tables(together)
    total = together * SLOTS
    out = jax.ShapeDtypeStruct
    row_spec = lambda w: pl.BlockSpec((total, w), lambda i: (i, 0))
    whole = lambda a: pl.BlockSpec(a.shape, lambda i: (0,) * a.ndim)
    gain = gain.reshape(1, model)
    return pl.pallas_call(
        states_kernel,
        grid=(steps,),
        in_specs=[
            pl.BlockSpec((1, 1, code.shape[2]), lambda i: (i, 0, 0)),
            pl.BlockSpec((halves, blocks, rows // steps, width), lambda i: (0, 0, i, 0)),
            whole(gain),
            whole(weight),
            whole(cosine),
            whole(sine),
        ],
        out_specs=[row_spec(model), row_spec(PER_GROUP * HD), row_spec(HD), row_spec(HD)],
        out_shape=[
            out((sessions * SLOTS, model), jnp.bfloat16),
            out((sessions * SLOTS, PER_GROUP * HD), jnp.bfloat16),
            out((sessions * SLOTS, HD), jnp.bfloat16),
            out((sessions * SLOTS, HD), jnp.bfloat16),
        ],
        compiler_params=pltpu.CompilerParams(vmem_limit_bytes=40 << 20),
        name="states",
    )(code, slots, gain, weight, jnp.asarray(cosine), jnp.asarray(sine))


def attend(place, lengths, query, key, value, prompts):
    sessions = place.shape[0]
    row_spec = lambda w: pl.BlockSpec((SLOTS, w), lambda i, place, length: (i, 0))
    return pl.pallas_call(
        attention_kernel,
        grid_spec=pltpu.PrefetchScalarGridSpec(
            num_scalar_prefetch=2,
            grid=(sessions,),
            in_specs=[
                row_spec(PER_GROUP * HD),
                row_spec(HD),
                row_spec(HD),
                pl.BlockSpec((1, PROMPT, 2 * HD), lambda i, place, length: (place[i], 0, 0)),
            ],
            out_specs=row_spec(PER_GROUP * HD),
        ),
        out_shape=jax.ShapeDtypeStruct((sessions * SLOTS, PER_GROUP * HD), jnp.bfloat16),
        compiler_params=pltpu.CompilerParams(vmem_limit_bytes=40 << 20),
        name="attend",
    )(place, lengths, query, key, value, prompts)


def general_body(
    thinker_rows,
    row_session,
    speaker_of,
    prompt_slot,
    prompt_cache,
    proj_weight,
    attn_gain,
    q_weight,
    k_weight,
    v_weight,
    o_weight,
):
    sess_count = lax.axis_size("sess")
    inner_count = lax.axis_size("inner")
    rep_count = lax.axis_size("rep")
    plane = inner_count * rep_count
    blocks = sess_count * rep_count
    session_all = speaker_of.shape[0]
    per_plane = session_all // sess_count
    per_device = per_plane // plane
    slot_cap = SLOTS // blocks
    held, tokens, channels = prompt_cache.shape
    model = proj_weight.shape[1]
    sharers = plane // KVH
    held_part = held // sharers
    sess_place = lax.axis_index("sess")
    plane_place = lax.axis_index("inner") * rep_count + lax.axis_index("rep")
    head = plane_place // sharers
    sharer = plane_place % sharers

    outgoing = jnp.transpose(
        prompt_cache.reshape(sharers, held_part, tokens, 2, KVH, HD), (4, 0, 1, 2, 3, 5)
    ).reshape(plane, held_part, tokens, 2 * HD)
    own_head = lax.all_to_all(outgoing, ("inner", "rep"), split_axis=0, concat_axis=2, tiled=True)
    own_head = own_head.reshape(held_part, plane * tokens, 2 * HD)
    prompts = lax.all_gather(own_head, "sess", axis=0, tiled=True)

    row_owner = row_session[:, 0]
    order = jnp.arange(row_owner.shape[0])
    same = row_owner[:, None] == row_owner[None, :]
    earlier = jnp.sum((same & (order[None, :] < order[:, None])).astype(jnp.int32), axis=1)
    row_slot = row_owner * slot_cap + earlier
    counts = jnp.sum(
        (row_owner[:, None] == jnp.arange(session_all)[None, :]).astype(jnp.int32), axis=0
    )
    all_counts = lax.all_gather(counts, ("sess", "rep"), axis=0, tiled=False)

    partial_sum = jnp.dot(thinker_rows, proj_weight, preferred_element_type=jnp.float32)
    width = model // inner_count
    if inner_count == 2:
        inner_place = lax.axis_index("inner")
        kept = lax.dynamic_slice_in_dim(partial_sum, inner_place * width, width, 1)
        sent = lax.dynamic_slice_in_dim(partial_sum, (1 - inner_place) * width, width, 1)
        came = lax.ppermute(sent.astype(jnp.bfloat16), "inner", [(0, 1), (1, 0)])
        own_columns = (kept + came.astype(jnp.float32)).astype(jnp.bfloat16)
    else:
        own_columns = lax.psum_scatter(
            partial_sum, "inner", scatter_dimension=1, tiled=True
        ).astype(jnp.bfloat16)
    into = (jnp.arange(session_all * slot_cap)[:, None] == row_slot[None, :]).astype(jnp.bfloat16)
    buffer = jnp.dot(into, own_columns, preferred_element_type=jnp.float32).astype(jnp.bfloat16)
    arrived = lax.all_to_all(
        buffer.reshape(sess_count, per_plane * slot_cap, width),
        "sess",
        split_axis=0,
        concat_axis=0,
        tiled=True,
    )
    spread = lax.all_gather(arrived, ("inner", "rep"), axis=0, tiled=False)
    slots = spread.reshape(inner_count, rep_count * sess_count, per_plane * slot_cap, width)

    offsets = jnp.cumsum(all_counts, axis=0) - all_counts
    lengths_all = jnp.sum(all_counts, axis=0)
    mine = lambda a: lax.dynamic_slice_in_dim(a, sess_place * per_plane, per_plane, a.ndim - 1)
    by_block = lambda a: jnp.transpose(
        mine(a).reshape(sess_count, rep_count, per_plane), (1, 0, 2)
    ).reshape(blocks, per_plane)
    lengths = mine(lengths_all)
    together = 16 // math.gcd(16, slot_cap)
    within = jnp.arange(slot_cap)
    local = (jnp.arange(per_plane) % together)[None, :, None] * SLOTS
    code = jnp.where(
        within[None, None, :] < by_block(all_counts)[:, :, None],
        by_block(offsets)[:, :, None] + within[None, None, :] + local,
        -1,
    )
    steps = per_plane // together
    code = jnp.transpose(
        code.reshape(blocks, steps, together * slot_cap), (1, 0, 2)
    ).reshape(steps, 1, blocks * together * slot_cap)

    group_width = PER_GROUP * HD
    weight = jnp.concatenate(
        [
            lax.dynamic_slice_in_dim(q_weight, head * group_width, group_width, 1),
            lax.dynamic_slice_in_dim(k_weight, head * HD, HD, 1),
            lax.dynamic_slice_in_dim(v_weight, head * HD, HD, 1),
        ],
        axis=1,
    )
    states, query, key, value = make_states(
        code, slots, attn_gain, weight, per_plane, together
    )

    wanted_slot = jnp.sum(
        jnp.where(
            mine(speaker_of)[:, None] == jnp.arange(prompt_slot.shape[0])[None, :],
            prompt_slot[None, :],
            0,
        ),
        axis=1,
    )
    place = wanted_slot // held * held_part + wanted_slot % held_part
    attended = attend(place, lengths, query, key, value, prompts)
    returned = lax.all_to_all(
        attended.reshape(plane, per_device * SLOTS, group_width),
        ("inner", "rep"),
        split_axis=0,
        concat_axis=0,
        tiled=True,
    ).reshape(KVH, sharers, per_device, SLOTS, group_width)
    first = plane_place * per_device
    if sharers > 1:
        holder = lax.dynamic_slice_in_dim(wanted_slot % held // held_part, first, per_device)
        chosen = jnp.zeros_like(returned[:, 0])
        for t in range(sharers):
            chosen = jnp.where((holder == t)[None, :, None, None], returned[:, t], chosen)
    else:
        chosen = returned[:, 0]
    gathered = jnp.transpose(chosen, (1, 2, 0, 3)).reshape(per_device * SLOTS, H * HD)
    own_states = lax.dynamic_slice_in_dim(states, first * SLOTS, per_device * SLOTS, 0)
    own_lengths = lax.dynamic_slice_in_dim(lengths, first, per_device)
    summed = own_states.astype(jnp.float32) + jnp.dot(
        gathered, o_weight, preferred_element_type=jnp.float32
    )
    live_rows = (jnp.arange(SLOTS)[None, :] < own_lengths[:, None]).reshape(-1, 1)
    return (
        jnp.where(live_rows, summed, 0.0)
        .astype(jnp.bfloat16)
        .reshape(per_device, SLOTS, model)
    )


EXTRA = 16
SMEM = pl.BlockSpec(memory_space=pltpu.SMEM)
VMEM = pl.BlockSpec(memory_space=pltpu.VMEM)
ANY = pl.BlockSpec(memory_space=pl.ANY)


def split_heads_kernel(head_ref, cache_ref, *out_refs):
    for by, out_ref in enumerate(out_refs):
        for side in range(2):
            start = pl.multiple_of((head_ref[0] ^ by) * HD + side * KVH * HD, HD)
            out_ref[:, :, side * HD : (side + 1) * HD] = cache_ref[:, :, pl.ds(start, HD)]


def split_heads(head, cache):
    held, tokens, _ = cache.shape
    shape = jax.ShapeDtypeStruct((held, tokens, 2 * HD), cache.dtype)
    return pl.pallas_call(
        split_heads_kernel,
        in_specs=[SMEM, VMEM],
        out_specs=[VMEM] * KVH,
        out_shape=[shape] * KVH,
        cost_estimate=pl.CostEstimate(flops=0, bytes_accessed=2 * cache.size * 2, transcendentals=0),
        name="split_heads",
    )(head, cache)


def stack_kernel(*refs):
    in_refs, out_ref = refs[:-1], refs[-1]
    place = 0
    for in_ref in in_refs:
        count = in_ref.shape[0]
        out_ref[place : place + count] = in_ref[...]
        place += count


def stack(*arrays):
    total = sum(a.shape[0] for a in arrays)
    size = sum(a.size for a in arrays)
    return pl.pallas_call(
        stack_kernel,
        in_specs=[VMEM] * len(arrays),
        out_specs=VMEM,
        out_shape=jax.ShapeDtypeStruct((total,) + arrays[0].shape[1:], arrays[0].dtype),
        cost_estimate=pl.CostEstimate(flops=0, bytes_accessed=4 * size, transcendentals=0),
        name="stack",
    )(*arrays)


def route_kernel(z_ref, kept_ref, came_ref, owner_ref, owner_row_ref, *out_refs,
                 slot_cap, per_plane):
    rows = kept_ref.shape[0]
    planes = len(out_refs)
    size = out_refs[0].shape[0]
    live = per_plane * slot_cap
    columns = (kept_ref[...] + came_ref[...].astype(jnp.float32)).astype(jnp.bfloat16)
    owner, owner_row = owner_ref[...], owner_row_ref[...]
    above = lax.broadcasted_iota(jnp.int32, (rows, rows), 0)
    beside = lax.broadcasted_iota(jnp.int32, (rows, rows), 1)
    earlier = jnp.sum(
        jnp.where((owner == owner_row) & (above < beside), 1.0, 0.0), axis=0, keepdims=True
    ).astype(jnp.int32)
    target = lax.div(owner_row, per_plane) ^ z_ref[0]
    code = target * size + lax.rem(owner_row, per_plane) * slot_cap + earlier
    place = lax.broadcasted_iota(jnp.int32, (planes * size, rows), 0)
    into = (place == code).astype(jnp.bfloat16)
    routed = jnp.dot(into, columns, preferred_element_type=jnp.float32).astype(jnp.bfloat16)
    lane = lax.broadcasted_iota(jnp.int32, (rows, HD), 1)
    named = (lane == owner).astype(jnp.bfloat16)
    counts = jnp.dot(
        jnp.ones((EXTRA, rows), jnp.bfloat16), named, preferred_element_type=jnp.float32
    ).astype(jnp.bfloat16)
    for k, out_ref in enumerate(out_refs):
        out_ref[:live] = routed[k * size : k * size + live]
        out_ref[live:] = jnp.zeros((EXTRA, out_ref.shape[1]), jnp.bfloat16)
        out_ref[live:, :HD] = counts


def route(z, kept, came, row_session, planes, per_plane, slot_cap):
    width = kept.shape[1]
    rows = row_session.shape[0]
    size = per_plane * slot_cap + EXTRA
    return pl.pallas_call(
        functools.partial(route_kernel, slot_cap=slot_cap, per_plane=per_plane),
        in_specs=[SMEM] + [VMEM] * 4,
        out_specs=[VMEM] * planes,
        out_shape=[jax.ShapeDtypeStruct((size, width), jnp.bfloat16)] * planes,
        cost_estimate=pl.CostEstimate(
            flops=2 * planes * size * rows * width, bytes_accessed=rows * width * 8, transcendentals=0
        ),
        name="route",
    )(z, kept, came, row_session, row_session.reshape(1, rows))


def place_kernel(index_ref, mine_ref, core_ref, gain_ref, weight_ref, cos_ref, sin_ref,
                 states_ref, query_ref, key_ref, value_ref, length_ref, *, slot_cap, together):
    z, x, c = index_ref[0], index_ref[1], index_ref[2]
    planes = mine_ref.shape[0] // 2
    blocks = 2 * planes
    width = mine_ref.shape[2]
    live = mine_ref.shape[1] - EXTRA
    per_plane = live // slot_cap
    steps = per_plane // together
    window = together * slot_cap
    total = together * SLOTS
    counts = jnp.concatenate(
        [ref[k, live : live + 1, :HD] for ref in (mine_ref, core_ref) for k in range(planes)],
        axis=0,
    ).astype(jnp.float32)
    kind = lambda axis: lax.broadcasted_iota(jnp.int32, (blocks, blocks), axis)
    true_block = lambda k: (z ^ (k % planes)) * 2 + (c ^ (k // planes))
    before = (true_block(kind(1)) < true_block(kind(0))).astype(jnp.float32)
    offsets = jnp.dot(before, counts, preferred_element_type=jnp.float32)
    session_lane = lax.broadcasted_iota(jnp.int32, (HD, HD), 0)
    local_lane = lax.broadcasted_iota(jnp.int32, (HD, HD), 1)
    ours = (session_lane == z * per_plane + local_lane).astype(jnp.float32)
    sums = jnp.dot(
        jnp.broadcast_to(jnp.sum(counts, axis=0, keepdims=True), (8, HD)),
        ours,
        preferred_element_type=jnp.float32,
    )
    length_ref[...] = sums[:1].astype(jnp.int32)
    cosine, sine = cos_ref[...], sin_ref[...]
    gain = gain_ref[...].astype(jnp.float32)
    for step in range(steps):
        slot = lax.broadcasted_iota(jnp.int32, (blocks, blocks * window), 1)
        in_block = slot % window
        spread = lax.broadcasted_iota(jnp.int32, (HD, blocks * window), 1) % window // slot_cap
        from_lane = lax.broadcasted_iota(jnp.int32, (HD, blocks * window), 0)
        expand = (from_lane == z * per_plane + step * together + spread).astype(jnp.float32)
        here = jnp.dot(counts, expand, preferred_element_type=jnp.float32).astype(jnp.int32)
        start = jnp.dot(offsets, expand, preferred_element_type=jnp.float32).astype(jnp.int32)
        within = in_block % slot_cap
        row = jnp.where(within < here, start + within + in_block // slot_cap * SLOTS, -1)
        block = lax.broadcasted_iota(jnp.int32, (blocks, blocks * window), 0)
        code = jnp.max(jnp.where(slot // window == block, row, -1), axis=0, keepdims=True)
        place = lax.broadcasted_iota(jnp.int32, (total, blocks * window), 0)
        pick = (place == code).astype(jnp.bfloat16)
        slots = slice(step * window, (step + 1) * window)
        near, far = [
            jnp.dot(
                pick,
                jnp.concatenate(
                    [ref[half * planes + k, slots] for ref in (mine_ref, core_ref) for k in range(planes)],
                    axis=0,
                ),
                preferred_element_type=jnp.float32,
            )
            for half in range(2)
        ]
        widened = jnp.concatenate(
            [jnp.where(x == 0, near, far), jnp.where(x == 0, far, near)], axis=1
        )
        rows = slice(step * total, (step + 1) * total)
        states_ref[rows] = widened.astype(jnp.bfloat16)
        factor = lax.rsqrt(jnp.mean(widened * widened, axis=-1, keepdims=True) + EPSILON)
        normed = (widened * factor * gain).astype(jnp.bfloat16)
        both = jnp.dot(normed, weight_ref[...], preferred_element_type=jnp.float32)
        for h in range(PER_GROUP + 1):
            vector = both[:, h * HD : (h + 1) * HD]
            turned = vector * cosine + pltpu.roll(vector, HD // 2, 1) * sine
            if h < PER_GROUP:
                query_ref[rows, h * HD : (h + 1) * HD] = turned.astype(jnp.bfloat16)
            else:
                key_ref[rows] = turned.astype(jnp.bfloat16)
        value_ref[rows] = both[:, (PER_GROUP + 1) * HD :].astype(jnp.bfloat16)


def place_rows(index, mine, core, gain, weight, sessions, slot_cap):
    together = 16 // math.gcd(16, slot_cap)
    cosine, sine = rope_tables(together)
    model = 2 * mine.shape[2]
    total = sessions * SLOTS
    out = lambda w: jax.ShapeDtypeStruct((total, w), jnp.bfloat16)
    return pl.pallas_call(
        functools.partial(place_kernel, slot_cap=slot_cap, together=together),
        in_specs=[SMEM] + [VMEM] * 6,
        out_specs=[VMEM] * 5,
        out_shape=[
            out(model), out(PER_GROUP * HD), out(HD), out(HD),
            jax.ShapeDtypeStruct((1, HD), jnp.int32),
        ],
        compiler_params=pltpu.CompilerParams(vmem_limit_bytes=40 << 20),
        cost_estimate=pl.CostEstimate(
            flops=4 * total * model * weight.shape[1], bytes_accessed=6 << 20, transcendentals=0
        ),
        name="place_rows",
    )(index, mine, core, gain.reshape(1, model), weight, jnp.asarray(cosine), jnp.asarray(sine))


def session_attention(query, key, value, tokens, length):
    scale = HD ** (-0.5) * math.log2(math.e)
    query = jnp.concatenate([query[:, h * HD : (h + 1) * HD] for h in range(PER_GROUP)], axis=0)
    ahead = lax.dot_general(query, tokens[:, :HD], NT, preferred_element_type=jnp.float32)
    own = lax.dot_general(query, key, NT, preferred_element_type=jnp.float32)
    row = lax.broadcasted_iota(jnp.int32, (SLOTS, SLOTS), 0)
    column = lax.broadcasted_iota(jnp.int32, (SLOTS, SLOTS), 1)
    allowed = (column <= row) & (column < length)
    own = jnp.where(jnp.concatenate([allowed] * PER_GROUP, axis=0), own, -1e30)
    highest = jnp.maximum(
        jnp.max(ahead, axis=-1, keepdims=True), jnp.max(own, axis=-1, keepdims=True)
    )
    powers = jnp.exp2((ahead - highest) * scale)
    own_powers = jnp.exp2((own - highest) * scale)
    total = jnp.sum(powers, axis=-1, keepdims=True) + jnp.sum(own_powers, axis=-1, keepdims=True)
    mixed = jnp.dot(
        powers.astype(jnp.bfloat16), tokens[:, HD:], preferred_element_type=jnp.float32
    ) + jnp.dot(own_powers.astype(jnp.bfloat16), value, preferred_element_type=jnp.float32)
    return (mixed / total).astype(jnp.bfloat16)


def fetches(hop, refs, held, kv, sem, hops, start):
    for which, source in enumerate(hops):
        copies = [
            pltpu.make_async_copy(refs[2 * which + chunk].at[:, held], kv.at[chunk], sem.at[chunk])
            for chunk in range(2)
        ]
        if start:
            @pl.when(hop == source)
            def _():
                for copy in copies:
                    copy.start()
        elif which == 0:
            for copy in copies:
                copy.wait()


def among(hop, hops):
    ours = hop == hops[0]
    for other in hops[1:]:
        ours = ours | (hop == other)
    return ours


def near_kernel(hop_ref, held_ref, length_ref, query_ref, key_ref, value_ref, *refs, hops):
    prompt_refs, (out_ref, kv, sem) = refs[: 2 * len(hops)], refs[2 * len(hops) :]
    sessions = hop_ref.shape[0]
    for i in range(sessions):
        fetches(hop_ref[i], prompt_refs, held_ref[i], kv.at[i], sem.at[i], hops, True)

    def work(i, _):
        @pl.when(among(hop_ref[i], hops))
        def _():
            fetches(hop_ref[i], prompt_refs, held_ref[i], kv.at[i], sem.at[i], hops, False)
            rows = pl.ds(pl.multiple_of(i * SLOTS, SLOTS), SLOTS)
            mixed = session_attention(
                query_ref[rows], key_ref[rows], value_ref[rows],
                kv[i].reshape(PROMPT, 2 * HD), length_ref[0, i],
            )
            for h in range(PER_GROUP):
                out_ref[rows, h * HD : (h + 1) * HD] = mixed[h * SLOTS : (h + 1) * SLOTS]

        return 0

    lax.fori_loop(0, sessions, work, 0)


def far_kernel(index_ref, hop_ref, held_ref, length_ref, query_ref, key_ref, value_ref, near_ref,
               *refs, targets, hops):
    prompt_refs, refs = refs[: 2 * len(hops)], refs[2 * len(hops) :]
    out_refs, (kv, sem) = refs[: len(targets)], refs[len(targets) :]
    head = index_ref[3]
    per_device = out_refs[0].shape[0] // SLOTS
    places = [(t, j) for t in range(len(targets)) for j in range(per_device)]
    sessions = [(head ^ targets[t]) * per_device + j for t, j in places]
    for i, session in enumerate(sessions):
        fetches(
            hop_ref[session], prompt_refs, held_ref[session], kv.at[i], sem.at[i], hops, True
        )
    for i, (session, (t, j)) in enumerate(zip(sessions, places)):
        rows = pl.ds(pl.multiple_of(session * SLOTS, SLOTS), SLOTS)
        target = slice(j * SLOTS, (j + 1) * SLOTS)
        ours = among(hop_ref[session], hops)

        @pl.when(jnp.logical_not(ours))
        def _():
            out_refs[t][target] = near_ref[rows]

        @pl.when(ours)
        def _():
            fetches(
                hop_ref[session], prompt_refs, held_ref[session], kv.at[i], sem.at[i], hops, False
            )
            mixed = session_attention(
                query_ref[rows], key_ref[rows], value_ref[rows],
                kv[i].reshape(PROMPT, 2 * HD), length_ref[0, session],
            )
            for h in range(PER_GROUP):
                out_refs[t][target, h * HD : (h + 1) * HD] = mixed[h * SLOTS : (h + 1) * SLOTS]


HBM = pl.BlockSpec(memory_space=pltpu.HBM)


def attention_call(kernel, out_specs, out_shape, places, name, scalars, arrays, prompts, hops):
    pieces = [piece for h in hops for piece in prompts[h]]
    work = places * PER_GROUP * SLOTS * (PROMPT + SLOTS) // 2
    return pl.pallas_call(
        kernel,
        in_specs=[SMEM] * len(scalars) + [VMEM] * len(arrays) + [HBM] * len(pieces),
        out_specs=out_specs,
        out_shape=out_shape,
        scratch_shapes=[
            pltpu.VMEM((places, 2, 2, PROMPT // 4, 2 * HD), jnp.bfloat16),
            pltpu.SemaphoreType.DMA((places, 2)),
        ],
        compiler_params=pltpu.CompilerParams(vmem_limit_bytes=40 << 20),
        cost_estimate=pl.CostEstimate(
            flops=4 * work * HD, bytes_accessed=places * PROMPT * 2 * HD, transcendentals=work
        ),
        name=name,
    )(*scalars, *arrays, *pieces)


def attend_near(hop, held, lengths, query, key, value, prompts, hops):
    out_shape = jax.ShapeDtypeStruct(query.shape, jnp.bfloat16)
    return attention_call(
        functools.partial(near_kernel, hops=hops),
        VMEM, out_shape, hop.shape[0], "near", (hop, held, lengths), (query, key, value),
        prompts, hops,
    )


def attend_far(index, hop, held, lengths, query, key, value, near, prompts, hops, targets):
    per_device = hop.shape[0] // KVH
    out_shape = jax.ShapeDtypeStruct((per_device * SLOTS, query.shape[1]), jnp.bfloat16)
    return attention_call(
        functools.partial(far_kernel, hops=hops, targets=targets),
        [VMEM] * len(targets), [out_shape] * len(targets), per_device * len(targets), "far",
        (index, hop, held, lengths), (query, key, value, near), prompts, hops,
    )


def output_kernel(index_ref, length_ref, states_ref, weight_ref, *refs):
    piece_refs, out_ref = refs[:-1], refs[-1]
    head = index_ref[3]
    group_width = PER_GROUP * HD
    per_device = out_ref.shape[0]
    total = per_device * SLOTS
    summed = states_ref[pl.ds(pl.multiple_of(head * total, SLOTS), total)].astype(jnp.float32)
    for by, piece_ref in enumerate(piece_refs):
        start = pl.multiple_of((head ^ by) * group_width, group_width)
        summed = summed + jnp.dot(
            piece_ref[...], weight_ref[pl.ds(start, group_width)], preferred_element_type=jnp.float32
        )
    row = lax.broadcasted_iota(jnp.int32, (SLOTS, 1), 0)
    for i in range(per_device):
        live = row < length_ref[0, head * per_device + i]
        part = summed[i * SLOTS : (i + 1) * SLOTS]
        out_ref[i] = jnp.where(live, part, 0.0).astype(jnp.bfloat16)


def output(index, lengths, states, o_weight, pieces, per_device):
    model = o_weight.shape[1]
    return pl.pallas_call(
        output_kernel,
        in_specs=[SMEM] * 2 + [VMEM] * (2 + len(pieces)),
        out_specs=VMEM,
        out_shape=jax.ShapeDtypeStruct((per_device, SLOTS, model), jnp.bfloat16),
        compiler_params=pltpu.CompilerParams(vmem_limit_bytes=40 << 20),
        cost_estimate=pl.CostEstimate(
            flops=2 * per_device * SLOTS * o_weight.size, bytes_accessed=o_weight.size * 2, transcendentals=0
        ),
        name="output",
    )(index, lengths, states, o_weight, *pieces)


def shifted(n, by):
    return [(i, i + by) for i in range(n) if 0 <= i + by < n]


def swapped(n, by):
    return [(i, i ^ by) for i in range(n)]


def line_body(
    thinker_rows,
    row_session,
    speaker_of,
    prompt_slot,
    prompt_cache,
    proj_weight,
    attn_gain,
    q_weight,
    k_weight,
    v_weight,
    o_weight,
):
    planes, plane, rep_count = lax.axis_size("sess"), KVH, 2
    blocks = planes * rep_count
    session_all = speaker_of.shape[0]
    per_plane = session_all // planes
    per_device = per_plane // plane
    slot_cap = SLOTS // blocks
    held = prompt_cache.shape[0]
    model = proj_weight.shape[1]
    width = model // 2
    z, x, c = lax.axis_index("sess"), lax.axis_index("inner"), lax.axis_index("rep")
    head = x * rep_count + c
    index = jnp.stack([z, x, c, head]).astype(jnp.int32)
    pair = ("inner", "rep")

    own, to_core, to_x, to_far = split_heads(head.reshape(1), prompt_cache)
    from_core = lax.ppermute(to_core, pair, swapped(4, 1))
    from_x = lax.ppermute(to_x, pair, swapped(4, 2))
    from_far = lax.ppermute(to_far, pair, swapped(4, 3))
    first = stack(own[None], from_core[None])
    second = stack(from_x[None], from_far[None])
    thinker_rows, _ = lax.optimization_barrier((thinker_rows, to_core))
    partial_sum = jnp.dot(thinker_rows, proj_weight, preferred_element_type=jnp.float32)
    kept = lax.dynamic_slice_in_dim(partial_sum, x * width, width, 1)
    sent = lax.dynamic_slice_in_dim(partial_sum, (1 - x) * width, width, 1)
    sent = sent.astype(jnp.bfloat16)
    came = lax.ppermute(sent, "inner", swapped(2, 1))
    routed = route(z.reshape(1), kept, came, row_session, planes, per_plane, slot_cap)
    first, _ = lax.optimization_barrier((first, sent))
    second, _ = lax.optimization_barrier((second, routed[0]))
    right, left = [first, second], [first, second]
    prompts = {0: (first, second)}
    for hop in range(1, planes):
        for chunk in range(2):
            right[chunk] = lax.ppermute(right[chunk], "sess", shifted(planes, 1))
            left[chunk] = lax.ppermute(left[chunk], "sess", shifted(planes, -1))
        prompts[-hop], prompts[hop] = tuple(right), tuple(left)

    def after(value, hop, chunk):
        return lax.optimization_barrier((value, prompts[-hop][chunk], prompts[hop][chunk]))[0]

    routed = after(tuple(routed), 1, 0)
    arrived = [routed[0]] + [
        lax.ppermute(routed[by], "sess", swapped(planes, by)) for by in range(1, planes)
    ]
    arrived = after(arrived, 1, 1)
    arrived = stack(*[a[None] for a in arrived])
    other = lax.ppermute(arrived, "inner", swapped(2, 1))
    other = after(other, 2, 0)
    mine = stack(arrived, other)
    core = lax.ppermute(mine, "rep", swapped(2, 1))
    core = after(core, 2, 1)

    group_width = PER_GROUP * HD
    weight = jnp.concatenate(
        [
            lax.dynamic_slice_in_dim(q_weight, head * group_width, group_width, 1),
            lax.dynamic_slice_in_dim(k_weight, head * HD, HD, 1),
            lax.dynamic_slice_in_dim(v_weight, head * HD, HD, 1),
        ],
        axis=1,
    )
    states, query, key, value, lengths = place_rows(
        index, mine, core, attn_gain, weight, per_plane, slot_cap
    )

    speakers = lax.dynamic_slice_in_dim(speaker_of, z * per_plane, per_plane)
    wanted_slot = jnp.sum(
        jnp.where(
            speakers[:, None] == jnp.arange(prompt_slot.shape[0])[None, :], prompt_slot[None, :], 0
        ),
        axis=1,
    )
    hop = wanted_slot // held - z
    which = wanted_slot % held
    near = attend_near(
        hop, which, lengths, after(query, 3, 0), key, value, prompts, (0, -1, 1, -2, 2)
    )
    run = functools.partial(attend_far, index, hop, which, lengths)
    attended = {}
    attended[2], attended[3] = run(query, key, value, near, prompts, (-3, 3), (2, 3))
    near, _ = lax.optimization_barrier((near, attended[2]))
    attended[0], attended[1] = run(query, key, value, near, prompts, (-3, 3), (0, 1))
    pieces = [attended[0]] + [
        lax.ppermute(attended[by], pair, swapped(4, by)) for by in range(1, plane)
    ]
    return output(index, lengths, states, o_weight, pieces, per_device)


def solution(mesh):
    in_specs = (
        P(("groups", "sess", "rep"), "inner"),
        P(("groups", "sess", "rep"), None),
        P("groups"),
        P("groups"),
        P(("groups", "sess"), ("inner", "rep"), None),
        P("inner", None),
        P(),
        P(),
        P(),
        P(),
        P(),
    )
    out_specs = P(("groups", "sess", "inner", "rep"), None, None)
    sizes = tuple(mesh.shape[name] for name in ("sess", "inner", "rep"))
    body = line_body if sizes == (4, 2, 2) else general_body
    return jax.shard_map(body, mesh=mesh, in_specs=in_specs, out_specs=out_specs, check_vma=False)
```

```python
import functools
import math

import jax
import jax.numpy as jnp
import numpy as np
from jax import lax
from jax.experimental import pallas as pl
from jax.experimental.pallas import tpu as pltpu
from jax.sharding import PartitionSpec as P

H = 12
KVH = 4
HD = 128
PROMPT = 1024
SLOTS = 96
PER_GROUP = H // KVH

EPSILON = 1e-06
ROPE_BASE = 1000000.0
NT = (((1,), (1,)), ((), ()))


def rope_tables(copies):
    half_width = HD // 2
    inverse = ROPE_BASE ** (-(np.arange(half_width, dtype=np.float64) * 2.0) / HD)
    angles = (PROMPT + np.arange(SLOTS, dtype=np.float64))[:, None] * inverse[None, :]
    cosine = np.concatenate([np.cos(angles), np.cos(angles)], axis=1)
    sine = np.concatenate([-np.sin(angles), np.sin(angles)], axis=1)
    return (
        np.tile(cosine, (copies, 1)).astype(np.float32),
        np.tile(sine, (copies, 1)).astype(np.float32),
    )


def states_kernel(code_ref, slots_ref, gain_ref, weight_ref, cos_ref, sin_ref,
                  states_ref, query_ref, key_ref, value_ref):
    halves, blocks, rows, width = slots_ref.shape
    total = states_ref.shape[0]
    place = lax.broadcasted_iota(jnp.int32, (total, blocks * rows), 0)
    pick = (place == code_ref[0]).astype(jnp.bfloat16)
    parts = [
        jnp.dot(
            pick,
            slots_ref[half].reshape(blocks * rows, width),
            preferred_element_type=jnp.float32,
        )
        for half in range(halves)
    ]
    widened = jnp.concatenate(parts, axis=1)
    states_ref[...] = widened.astype(jnp.bfloat16)
    factor = lax.rsqrt(jnp.mean(widened * widened, axis=-1, keepdims=True) + EPSILON)
    normed = (widened * factor * gain_ref[...].astype(jnp.float32)).astype(jnp.bfloat16)
    both = jnp.dot(normed, weight_ref[...], preferred_element_type=jnp.float32)
    cosine, sine = cos_ref[...], sin_ref[...]
    for head in range(PER_GROUP + 1):
        vector = both[:, head * HD : (head + 1) * HD]
        turned = vector * cosine + pltpu.roll(vector, HD // 2, 1) * sine
        if head < PER_GROUP:
            query_ref[:, head * HD : (head + 1) * HD] = turned.astype(jnp.bfloat16)
        else:
            key_ref[...] = turned.astype(jnp.bfloat16)
    value_ref[...] = both[:, (PER_GROUP + 1) * HD :].astype(jnp.bfloat16)


def attention_kernel(place_ref, length_ref, query_ref, key_ref, value_ref, prompt_ref, out_ref):
    session = pl.program_id(0)
    length = length_ref[session]
    scale = HD ** (-0.5) * math.log2(math.e)
    query = jnp.concatenate(
        [query_ref[:, h * HD : (h + 1) * HD] for h in range(PER_GROUP)], axis=0
    )
    ahead = lax.dot_general(query, prompt_ref[0, :, :HD], NT, preferred_element_type=jnp.float32)
    own = lax.dot_general(query, key_ref[...], NT, preferred_element_type=jnp.float32)
    row = lax.broadcasted_iota(jnp.int32, (SLOTS, SLOTS), 0)
    column = lax.broadcasted_iota(jnp.int32, (SLOTS, SLOTS), 1)
    allowed = (column <= row) & (column < length)
    own = jnp.where(jnp.concatenate([allowed] * PER_GROUP, axis=0), own, -1e30)
    highest = jnp.maximum(
        jnp.max(ahead, axis=-1, keepdims=True), jnp.max(own, axis=-1, keepdims=True)
    )
    powers = jnp.exp2((ahead - highest) * scale)
    own_powers = jnp.exp2((own - highest) * scale)
    total = jnp.sum(powers, axis=-1, keepdims=True) + jnp.sum(own_powers, axis=-1, keepdims=True)
    mixed = jnp.dot(
        powers.astype(jnp.bfloat16), prompt_ref[0, :, HD:], preferred_element_type=jnp.float32
    ) + jnp.dot(own_powers.astype(jnp.bfloat16), value_ref[...], preferred_element_type=jnp.float32)
    mixed = (mixed / total).astype(jnp.bfloat16)
    for h in range(PER_GROUP):
        out_ref[:, h * HD : (h + 1) * HD] = mixed[h * SLOTS : (h + 1) * SLOTS]


def make_states(code, slots, gain, weight, sessions, together):
    halves, blocks, rows, width = slots.shape
    steps = sessions // together
    model = halves * width
    cosine, sine = rope_tables(together)
    total = together * SLOTS
    out = jax.ShapeDtypeStruct
    row_spec = lambda w: pl.BlockSpec((total, w), lambda i: (i, 0))
    whole = lambda a: pl.BlockSpec(a.shape, lambda i: (0,) * a.ndim)
    gain = gain.reshape(1, model)
    return pl.pallas_call(
        states_kernel,
        grid=(steps,),
        in_specs=[
            pl.BlockSpec((1, 1, code.shape[2]), lambda i: (i, 0, 0)),
            pl.BlockSpec((halves, blocks, rows // steps, width), lambda i: (0, 0, i, 0)),
            whole(gain),
            whole(weight),
            whole(cosine),
            whole(sine),
        ],
        out_specs=[row_spec(model), row_spec(PER_GROUP * HD), row_spec(HD), row_spec(HD)],
        out_shape=[
            out((sessions * SLOTS, model), jnp.bfloat16),
            out((sessions * SLOTS, PER_GROUP * HD), jnp.bfloat16),
            out((sessions * SLOTS, HD), jnp.bfloat16),
            out((sessions * SLOTS, HD), jnp.bfloat16),
        ],
        compiler_params=pltpu.CompilerParams(vmem_limit_bytes=40 << 20),
        name="states",
    )(code, slots, gain, weight, jnp.asarray(cosine), jnp.asarray(sine))


def attend(place, lengths, query, key, value, prompts):
    sessions = place.shape[0]
    row_spec = lambda w: pl.BlockSpec((SLOTS, w), lambda i, place, length: (i, 0))
    return pl.pallas_call(
        attention_kernel,
        grid_spec=pltpu.PrefetchScalarGridSpec(
            num_scalar_prefetch=2,
            grid=(sessions,),
            in_specs=[
                row_spec(PER_GROUP * HD),
                row_spec(HD),
                row_spec(HD),
                pl.BlockSpec((1, PROMPT, 2 * HD), lambda i, place, length: (place[i], 0, 0)),
            ],
            out_specs=row_spec(PER_GROUP * HD),
        ),
        out_shape=jax.ShapeDtypeStruct((sessions * SLOTS, PER_GROUP * HD), jnp.bfloat16),
        compiler_params=pltpu.CompilerParams(vmem_limit_bytes=40 << 20),
        name="attend",
    )(place, lengths, query, key, value, prompts)


def general_body(
    thinker_rows,
    row_session,
    speaker_of,
    prompt_slot,
    prompt_cache,
    proj_weight,
    attn_gain,
    q_weight,
    k_weight,
    v_weight,
    o_weight,
):
    sess_count = lax.axis_size("sess")
    inner_count = lax.axis_size("inner")
    rep_count = lax.axis_size("rep")
    plane = inner_count * rep_count
    blocks = sess_count * rep_count
    session_all = speaker_of.shape[0]
    per_plane = session_all // sess_count
    per_device = per_plane // plane
    slot_cap = SLOTS // blocks
    held, tokens, channels = prompt_cache.shape
    model = proj_weight.shape[1]
    sharers = plane // KVH
    held_part = held // sharers
    sess_place = lax.axis_index("sess")
    plane_place = lax.axis_index("inner") * rep_count + lax.axis_index("rep")
    head = plane_place // sharers
    sharer = plane_place % sharers

    outgoing = jnp.transpose(
        prompt_cache.reshape(sharers, held_part, tokens, 2, KVH, HD), (4, 0, 1, 2, 3, 5)
    ).reshape(plane, held_part, tokens, 2 * HD)
    own_head = lax.all_to_all(outgoing, ("inner", "rep"), split_axis=0, concat_axis=2, tiled=True)
    own_head = own_head.reshape(held_part, plane * tokens, 2 * HD)
    prompts = lax.all_gather(own_head, "sess", axis=0, tiled=True)

    row_owner = row_session[:, 0]
    order = jnp.arange(row_owner.shape[0])
    same = row_owner[:, None] == row_owner[None, :]
    earlier = jnp.sum((same & (order[None, :] < order[:, None])).astype(jnp.int32), axis=1)
    row_slot = row_owner * slot_cap + earlier
    counts = jnp.sum(
        (row_owner[:, None] == jnp.arange(session_all)[None, :]).astype(jnp.int32), axis=0
    )
    all_counts = lax.all_gather(counts, ("sess", "rep"), axis=0, tiled=False)

    partial_sum = jnp.dot(thinker_rows, proj_weight, preferred_element_type=jnp.float32)
    width = model // inner_count
    if inner_count == 2:
        inner_place = lax.axis_index("inner")
        kept = lax.dynamic_slice_in_dim(partial_sum, inner_place * width, width, 1)
        sent = lax.dynamic_slice_in_dim(partial_sum, (1 - inner_place) * width, width, 1)
        came = lax.ppermute(sent.astype(jnp.bfloat16), "inner", [(0, 1), (1, 0)])
        own_columns = (kept + came.astype(jnp.float32)).astype(jnp.bfloat16)
    else:
        own_columns = lax.psum_scatter(
            partial_sum, "inner", scatter_dimension=1, tiled=True
        ).astype(jnp.bfloat16)
    into = (jnp.arange(session_all * slot_cap)[:, None] == row_slot[None, :]).astype(jnp.bfloat16)
    buffer = jnp.dot(into, own_columns, preferred_element_type=jnp.float32).astype(jnp.bfloat16)
    arrived = lax.all_to_all(
        buffer.reshape(sess_count, per_plane * slot_cap, width),
        "sess",
        split_axis=0,
        concat_axis=0,
        tiled=True,
    )
    spread = lax.all_gather(arrived, ("inner", "rep"), axis=0, tiled=False)
    slots = spread.reshape(inner_count, rep_count * sess_count, per_plane * slot_cap, width)

    offsets = jnp.cumsum(all_counts, axis=0) - all_counts
    lengths_all = jnp.sum(all_counts, axis=0)
    mine = lambda a: lax.dynamic_slice_in_dim(a, sess_place * per_plane, per_plane, a.ndim - 1)
    by_block = lambda a: jnp.transpose(
        mine(a).reshape(sess_count, rep_count, per_plane), (1, 0, 2)
    ).reshape(blocks, per_plane)
    lengths = mine(lengths_all)
    together = 16 // math.gcd(16, slot_cap)
    within = jnp.arange(slot_cap)
    local = (jnp.arange(per_plane) % together)[None, :, None] * SLOTS
    code = jnp.where(
        within[None, None, :] < by_block(all_counts)[:, :, None],
        by_block(offsets)[:, :, None] + within[None, None, :] + local,
        -1,
    )
    steps = per_plane // together
    code = jnp.transpose(
        code.reshape(blocks, steps, together * slot_cap), (1, 0, 2)
    ).reshape(steps, 1, blocks * together * slot_cap)

    group_width = PER_GROUP * HD
    weight = jnp.concatenate(
        [
            lax.dynamic_slice_in_dim(q_weight, head * group_width, group_width, 1),
            lax.dynamic_slice_in_dim(k_weight, head * HD, HD, 1),
            lax.dynamic_slice_in_dim(v_weight, head * HD, HD, 1),
        ],
        axis=1,
    )
    states, query, key, value = make_states(
        code, slots, attn_gain, weight, per_plane, together
    )

    wanted_slot = jnp.sum(
        jnp.where(
            mine(speaker_of)[:, None] == jnp.arange(prompt_slot.shape[0])[None, :],
            prompt_slot[None, :],
            0,
        ),
        axis=1,
    )
    place = wanted_slot // held * held_part + wanted_slot % held_part
    attended = attend(place, lengths, query, key, value, prompts)
    returned = lax.all_to_all(
        attended.reshape(plane, per_device * SLOTS, group_width),
        ("inner", "rep"),
        split_axis=0,
        concat_axis=0,
        tiled=True,
    ).reshape(KVH, sharers, per_device, SLOTS, group_width)
    first = plane_place * per_device
    if sharers > 1:
        holder = lax.dynamic_slice_in_dim(wanted_slot % held // held_part, first, per_device)
        chosen = jnp.zeros_like(returned[:, 0])
        for t in range(sharers):
            chosen = jnp.where((holder == t)[None, :, None, None], returned[:, t], chosen)
    else:
        chosen = returned[:, 0]
    gathered = jnp.transpose(chosen, (1, 2, 0, 3)).reshape(per_device * SLOTS, H * HD)
    own_states = lax.dynamic_slice_in_dim(states, first * SLOTS, per_device * SLOTS, 0)
    own_lengths = lax.dynamic_slice_in_dim(lengths, first, per_device)
    summed = own_states.astype(jnp.float32) + jnp.dot(
        gathered, o_weight, preferred_element_type=jnp.float32
    )
    live_rows = (jnp.arange(SLOTS)[None, :] < own_lengths[:, None]).reshape(-1, 1)
    return (
        jnp.where(live_rows, summed, 0.0)
        .astype(jnp.bfloat16)
        .reshape(per_device, SLOTS, model)
    )


EXTRA = 16
SMEM = pl.BlockSpec(memory_space=pltpu.SMEM)
VMEM = pl.BlockSpec(memory_space=pltpu.VMEM)
ANY = pl.BlockSpec(memory_space=pl.ANY)


def split_heads_kernel(head_ref, cache_ref, *out_refs):
    for by, out_ref in enumerate(out_refs):
        for side in range(2):
            start = pl.multiple_of((head_ref[0] ^ by) * HD + side * KVH * HD, HD)
            out_ref[:, :, side * HD : (side + 1) * HD] = cache_ref[:, :, pl.ds(start, HD)]


def split_heads(head, cache):
    held, tokens, _ = cache.shape
    shape = jax.ShapeDtypeStruct((held, tokens, 2 * HD), cache.dtype)
    return pl.pallas_call(
        split_heads_kernel,
        in_specs=[SMEM, VMEM],
        out_specs=[VMEM] * KVH,
        out_shape=[shape] * KVH,
        cost_estimate=pl.CostEstimate(flops=0, bytes_accessed=2 * cache.size * 2, transcendentals=0),
        name="split_heads",
    )(head, cache)


def stack_kernel(*refs):
    in_refs, out_ref = refs[:-1], refs[-1]
    place = 0
    for in_ref in in_refs:
        count = in_ref.shape[0]
        out_ref[place : place + count] = in_ref[...]
        place += count


def stack(*arrays):
    total = sum(a.shape[0] for a in arrays)
    size = sum(a.size for a in arrays)
    return pl.pallas_call(
        stack_kernel,
        in_specs=[VMEM] * len(arrays),
        out_specs=VMEM,
        out_shape=jax.ShapeDtypeStruct((total,) + arrays[0].shape[1:], arrays[0].dtype),
        cost_estimate=pl.CostEstimate(flops=0, bytes_accessed=4 * size, transcendentals=0),
        name="stack",
    )(*arrays)


def route_kernel(z_ref, kept_ref, came_ref, owner_ref, owner_row_ref, *out_refs,
                 slot_cap, per_plane):
    rows = kept_ref.shape[0]
    planes = len(out_refs)
    size = out_refs[0].shape[0]
    live = per_plane * slot_cap
    columns = (kept_ref[...] + came_ref[...].astype(jnp.float32)).astype(jnp.bfloat16)
    owner, owner_row = owner_ref[...], owner_row_ref[...]
    above = lax.broadcasted_iota(jnp.int32, (rows, rows), 0)
    beside = lax.broadcasted_iota(jnp.int32, (rows, rows), 1)
    earlier = jnp.sum(
        jnp.where((owner == owner_row) & (above < beside), 1.0, 0.0), axis=0, keepdims=True
    ).astype(jnp.int32)
    target = lax.div(owner_row, per_plane) ^ z_ref[0]
    code = target * size + lax.rem(owner_row, per_plane) * slot_cap + earlier
    place = lax.broadcasted_iota(jnp.int32, (planes * size, rows), 0)
    into = (place == code).astype(jnp.bfloat16)
    routed = jnp.dot(into, columns, preferred_element_type=jnp.float32).astype(jnp.bfloat16)
    lane = lax.broadcasted_iota(jnp.int32, (rows, HD), 1)
    named = (lane == owner).astype(jnp.bfloat16)
    counts = jnp.dot(
        jnp.ones((EXTRA, rows), jnp.bfloat16), named, preferred_element_type=jnp.float32
    ).astype(jnp.bfloat16)
    for k, out_ref in enumerate(out_refs):
        out_ref[:live] = routed[k * size : k * size + live]
        out_ref[live:] = jnp.zeros((EXTRA, out_ref.shape[1]), jnp.bfloat16)
        out_ref[live:, :HD] = counts


def route(z, kept, came, row_session, planes, per_plane, slot_cap):
    width = kept.shape[1]
    rows = row_session.shape[0]
    size = per_plane * slot_cap + EXTRA
    return pl.pallas_call(
        functools.partial(route_kernel, slot_cap=slot_cap, per_plane=per_plane),
        in_specs=[SMEM] + [VMEM] * 4,
        out_specs=[VMEM] * planes,
        out_shape=[jax.ShapeDtypeStruct((size, width), jnp.bfloat16)] * planes,
        cost_estimate=pl.CostEstimate(
            flops=2 * planes * size * rows * width, bytes_accessed=rows * width * 8, transcendentals=0
        ),
        name="route",
    )(z, kept, came, row_session, row_session.reshape(1, rows))


def place_kernel(index_ref, mine_ref, core_ref, gain_ref, weight_ref, cos_ref, sin_ref,
                 states_ref, query_ref, key_ref, value_ref, length_ref, *, slot_cap, together):
    z, x, c = index_ref[0], index_ref[1], index_ref[2]
    planes = mine_ref.shape[0] // 2
    blocks = 2 * planes
    width = mine_ref.shape[2]
    live = mine_ref.shape[1] - EXTRA
    per_plane = live // slot_cap
    steps = per_plane // together
    window = together * slot_cap
    total = together * SLOTS
    counts = jnp.concatenate(
        [ref[k, live : live + 1, :HD] for ref in (mine_ref, core_ref) for k in range(planes)],
        axis=0,
    ).astype(jnp.float32)
    kind = lambda axis: lax.broadcasted_iota(jnp.int32, (blocks, blocks), axis)
    true_block = lambda k: (z ^ (k % planes)) * 2 + (c ^ (k // planes))
    before = (true_block(kind(1)) < true_block(kind(0))).astype(jnp.float32)
    offsets = jnp.dot(before, counts, preferred_element_type=jnp.float32)
    session_lane = lax.broadcasted_iota(jnp.int32, (HD, HD), 0)
    local_lane = lax.broadcasted_iota(jnp.int32, (HD, HD), 1)
    ours = (session_lane == z * per_plane + local_lane).astype(jnp.float32)
    sums = jnp.dot(
        jnp.broadcast_to(jnp.sum(counts, axis=0, keepdims=True), (8, HD)),
        ours,
        preferred_element_type=jnp.float32,
    )
    length_ref[...] = sums[:1].astype(jnp.int32)
    cosine, sine = cos_ref[...], sin_ref[...]
    gain = gain_ref[...].astype(jnp.float32)
    for step in range(steps):
        slot = lax.broadcasted_iota(jnp.int32, (blocks, blocks * window), 1)
        in_block = slot % window
        spread = lax.broadcasted_iota(jnp.int32, (HD, blocks * window), 1) % window // slot_cap
        from_lane = lax.broadcasted_iota(jnp.int32, (HD, blocks * window), 0)
        expand = (from_lane == z * per_plane + step * together + spread).astype(jnp.float32)
        here = jnp.dot(counts, expand, preferred_element_type=jnp.float32).astype(jnp.int32)
        start = jnp.dot(offsets, expand, preferred_element_type=jnp.float32).astype(jnp.int32)
        within = in_block % slot_cap
        row = jnp.where(within < here, start + within + in_block // slot_cap * SLOTS, -1)
        block = lax.broadcasted_iota(jnp.int32, (blocks, blocks * window), 0)
        code = jnp.max(jnp.where(slot // window == block, row, -1), axis=0, keepdims=True)
        place = lax.broadcasted_iota(jnp.int32, (total, blocks * window), 0)
        pick = (place == code).astype(jnp.bfloat16)
        slots = slice(step * window, (step + 1) * window)
        near, far = [
            jnp.dot(
                pick,
                jnp.concatenate(
                    [ref[half * planes + k, slots] for ref in (mine_ref, core_ref) for k in range(planes)],
                    axis=0,
                ),
                preferred_element_type=jnp.float32,
            )
            for half in range(2)
        ]
        widened = jnp.concatenate(
            [jnp.where(x == 0, near, far), jnp.where(x == 0, far, near)], axis=1
        )
        rows = slice(step * total, (step + 1) * total)
        states_ref[rows] = widened.astype(jnp.bfloat16)
        factor = lax.rsqrt(jnp.mean(widened * widened, axis=-1, keepdims=True) + EPSILON)
        normed = (widened * factor * gain).astype(jnp.bfloat16)
        both = jnp.dot(normed, weight_ref[...], preferred_element_type=jnp.float32)
        for h in range(PER_GROUP + 1):
            vector = both[:, h * HD : (h + 1) * HD]
            turned = vector * cosine + pltpu.roll(vector, HD // 2, 1) * sine
            if h < PER_GROUP:
                query_ref[rows, h * HD : (h + 1) * HD] = turned.astype(jnp.bfloat16)
            else:
                key_ref[rows] = turned.astype(jnp.bfloat16)
        value_ref[rows] = both[:, (PER_GROUP + 1) * HD :].astype(jnp.bfloat16)


def place_rows(index, mine, core, gain, weight, sessions, slot_cap):
    together = 16 // math.gcd(16, slot_cap)
    cosine, sine = rope_tables(together)
    model = 2 * mine.shape[2]
    total = sessions * SLOTS
    out = lambda w: jax.ShapeDtypeStruct((total, w), jnp.bfloat16)
    return pl.pallas_call(
        functools.partial(place_kernel, slot_cap=slot_cap, together=together),
        in_specs=[SMEM] + [VMEM] * 6,
        out_specs=[VMEM] * 5,
        out_shape=[
            out(model), out(PER_GROUP * HD), out(HD), out(HD),
            jax.ShapeDtypeStruct((1, HD), jnp.int32),
        ],
        compiler_params=pltpu.CompilerParams(vmem_limit_bytes=40 << 20),
        cost_estimate=pl.CostEstimate(
            flops=4 * total * model * weight.shape[1], bytes_accessed=6 << 20, transcendentals=0
        ),
        name="place_rows",
    )(index, mine, core, gain.reshape(1, model), weight, jnp.asarray(cosine), jnp.asarray(sine))


def session_attention(query, key, value, tokens, length):
    scale = HD ** (-0.5) * math.log2(math.e)
    query = jnp.concatenate([query[:, h * HD : (h + 1) * HD] for h in range(PER_GROUP)], axis=0)
    ahead = lax.dot_general(query, tokens[:, :HD], NT, preferred_element_type=jnp.float32)
    own = lax.dot_general(query, key, NT, preferred_element_type=jnp.float32)
    row = lax.broadcasted_iota(jnp.int32, (SLOTS, SLOTS), 0)
    column = lax.broadcasted_iota(jnp.int32, (SLOTS, SLOTS), 1)
    allowed = (column <= row) & (column < length)
    own = jnp.where(jnp.concatenate([allowed] * PER_GROUP, axis=0), own, -1e30)
    highest = jnp.maximum(
        jnp.max(ahead, axis=-1, keepdims=True), jnp.max(own, axis=-1, keepdims=True)
    )
    powers = jnp.exp2((ahead - highest) * scale)
    own_powers = jnp.exp2((own - highest) * scale)
    total = jnp.sum(powers, axis=-1, keepdims=True) + jnp.sum(own_powers, axis=-1, keepdims=True)
    mixed = jnp.dot(
        powers.astype(jnp.bfloat16), tokens[:, HD:], preferred_element_type=jnp.float32
    ) + jnp.dot(own_powers.astype(jnp.bfloat16), value, preferred_element_type=jnp.float32)
    return (mixed / total).astype(jnp.bfloat16)


def fetches(hop, refs, held, kv, sem, hops, start):
    for which, source in enumerate(hops):
        copies = [
            pltpu.make_async_copy(refs[2 * which + chunk].at[:, held], kv.at[chunk], sem.at[chunk])
            for chunk in range(2)
        ]
        if start:
            @pl.when(hop == source)
            def _():
                for copy in copies:
                    copy.start()
        elif which == 0:
            for copy in copies:
                copy.wait()


def among(hop, hops):
    ours = hop == hops[0]
    for other in hops[1:]:
        ours = ours | (hop == other)
    return ours


def near_kernel(hop_ref, held_ref, length_ref, query_ref, key_ref, value_ref, *refs, hops):
    prompt_refs, (out_ref, kv, sem) = refs[: 2 * len(hops)], refs[2 * len(hops) :]
    sessions = hop_ref.shape[0]
    for i in range(sessions):
        fetches(hop_ref[i], prompt_refs, held_ref[i], kv.at[i], sem.at[i], hops, True)

    def work(i, _):
        @pl.when(among(hop_ref[i], hops))
        def _():
            fetches(hop_ref[i], prompt_refs, held_ref[i], kv.at[i], sem.at[i], hops, False)
            rows = pl.ds(pl.multiple_of(i * SLOTS, SLOTS), SLOTS)
            mixed = session_attention(
                query_ref[rows], key_ref[rows], value_ref[rows],
                kv[i].reshape(PROMPT, 2 * HD), length_ref[0, i],
            )
            for h in range(PER_GROUP):
                out_ref[rows, h * HD : (h + 1) * HD] = mixed[h * SLOTS : (h + 1) * SLOTS]

        return 0

    lax.fori_loop(0, sessions, work, 0)


def far_kernel(index_ref, hop_ref, held_ref, length_ref, query_ref, key_ref, value_ref, near_ref,
               *refs, targets, hops):
    prompt_refs, refs = refs[: 2 * len(hops)], refs[2 * len(hops) :]
    out_refs, (kv, sem) = refs[: len(targets)], refs[len(targets) :]
    head = index_ref[3]
    per_device = out_refs[0].shape[0] // SLOTS
    places = [(t, j) for t in range(len(targets)) for j in range(per_device)]
    sessions = [(head ^ targets[t]) * per_device + j for t, j in places]
    for i, session in enumerate(sessions):
        fetches(
            hop_ref[session], prompt_refs, held_ref[session], kv.at[i], sem.at[i], hops, True
        )
    for i, (session, (t, j)) in enumerate(zip(sessions, places)):
        rows = pl.ds(pl.multiple_of(session * SLOTS, SLOTS), SLOTS)
        target = slice(j * SLOTS, (j + 1) * SLOTS)
        ours = among(hop_ref[session], hops)

        @pl.when(jnp.logical_not(ours))
        def _():
            out_refs[t][target] = near_ref[rows]

        @pl.when(ours)
        def _():
            fetches(
                hop_ref[session], prompt_refs, held_ref[session], kv.at[i], sem.at[i], hops, False
            )
            mixed = session_attention(
                query_ref[rows], key_ref[rows], value_ref[rows],
                kv[i].reshape(PROMPT, 2 * HD), length_ref[0, session],
            )
            for h in range(PER_GROUP):
                out_refs[t][target, h * HD : (h + 1) * HD] = mixed[h * SLOTS : (h + 1) * SLOTS]


HBM = pl.BlockSpec(memory_space=pltpu.HBM)


def attention_call(kernel, out_specs, out_shape, places, name, scalars, arrays, prompts, hops):
    pieces = [piece for h in hops for piece in prompts[h]]
    work = places * PER_GROUP * SLOTS * (PROMPT + SLOTS) // 2
    return pl.pallas_call(
        kernel,
        in_specs=[SMEM] * len(scalars) + [VMEM] * len(arrays) + [HBM] * len(pieces),
        out_specs=out_specs,
        out_shape=out_shape,
        scratch_shapes=[
            pltpu.VMEM((places, 2, 2, PROMPT // 4, 2 * HD), jnp.bfloat16),
            pltpu.SemaphoreType.DMA((places, 2)),
        ],
        compiler_params=pltpu.CompilerParams(vmem_limit_bytes=40 << 20),
        cost_estimate=pl.CostEstimate(
            flops=4 * work * HD, bytes_accessed=places * PROMPT * 2 * HD, transcendentals=work
        ),
        name=name,
    )(*scalars, *arrays, *pieces)


def attend_near(hop, held, lengths, query, key, value, prompts, hops):
    out_shape = jax.ShapeDtypeStruct(query.shape, jnp.bfloat16)
    return attention_call(
        functools.partial(near_kernel, hops=hops),
        VMEM, out_shape, hop.shape[0], "near", (hop, held, lengths), (query, key, value),
        prompts, hops,
    )


def attend_far(index, hop, held, lengths, query, key, value, near, prompts, hops, targets):
    per_device = hop.shape[0] // KVH
    out_shape = jax.ShapeDtypeStruct((per_device * SLOTS, query.shape[1]), jnp.bfloat16)
    return attention_call(
        functools.partial(far_kernel, hops=hops, targets=targets),
        [VMEM] * len(targets), [out_shape] * len(targets), per_device * len(targets), "far",
        (index, hop, held, lengths), (query, key, value, near), prompts, hops,
    )


def output_kernel(index_ref, length_ref, states_ref, weight_ref, *refs):
    piece_refs, out_ref = refs[:-1], refs[-1]
    head = index_ref[3]
    group_width = PER_GROUP * HD
    per_device = out_ref.shape[0]
    total = per_device * SLOTS
    summed = states_ref[pl.ds(pl.multiple_of(head * total, SLOTS), total)].astype(jnp.float32)
    for by, piece_ref in enumerate(piece_refs):
        start = pl.multiple_of((head ^ by) * group_width, group_width)
        summed = summed + jnp.dot(
            piece_ref[...], weight_ref[pl.ds(start, group_width)], preferred_element_type=jnp.float32
        )
    row = lax.broadcasted_iota(jnp.int32, (SLOTS, 1), 0)
    for i in range(per_device):
        live = row < length_ref[0, head * per_device + i]
        part = summed[i * SLOTS : (i + 1) * SLOTS]
        out_ref[i] = jnp.where(live, part, 0.0).astype(jnp.bfloat16)


def output(index, lengths, states, o_weight, pieces, per_device):
    model = o_weight.shape[1]
    return pl.pallas_call(
        output_kernel,
        in_specs=[SMEM] * 2 + [VMEM] * (2 + len(pieces)),
        out_specs=VMEM,
        out_shape=jax.ShapeDtypeStruct((per_device, SLOTS, model), jnp.bfloat16),
        compiler_params=pltpu.CompilerParams(vmem_limit_bytes=40 << 20),
        cost_estimate=pl.CostEstimate(
            flops=2 * per_device * SLOTS * o_weight.size, bytes_accessed=o_weight.size * 2, transcendentals=0
        ),
        name="output",
    )(index, lengths, states, o_weight, *pieces)


def shifted(n, by):
    return [(i, i + by) for i in range(n) if 0 <= i + by < n]


def swapped(n, by):
    return [(i, i ^ by) for i in range(n)]


def line_body(
    thinker_rows,
    row_session,
    speaker_of,
    prompt_slot,
    prompt_cache,
    proj_weight,
    attn_gain,
    q_weight,
    k_weight,
    v_weight,
    o_weight,
):
    planes, plane, rep_count = lax.axis_size("sess"), KVH, 2
    blocks = planes * rep_count
    session_all = speaker_of.shape[0]
    per_plane = session_all // planes
    per_device = per_plane // plane
    slot_cap = SLOTS // blocks
    held = prompt_cache.shape[0]
    model = proj_weight.shape[1]
    width = model // 2
    z, x, c = lax.axis_index("sess"), lax.axis_index("inner"), lax.axis_index("rep")
    head = x * rep_count + c
    index = jnp.stack([z, x, c, head]).astype(jnp.int32)
    pair = ("inner", "rep")

    own, to_core, to_x, to_far = split_heads(head.reshape(1), prompt_cache)
    from_core = lax.ppermute(to_core, pair, swapped(4, 1))
    from_x = lax.ppermute(to_x, pair, swapped(4, 2))
    from_far = lax.ppermute(to_far, pair, swapped(4, 3))
    first = stack(own[None], from_core[None])
    second = stack(from_x[None], from_far[None])
    thinker_rows, _ = lax.optimization_barrier((thinker_rows, to_core))
    partial_sum = jnp.dot(thinker_rows, proj_weight, preferred_element_type=jnp.float32)
    kept = lax.dynamic_slice_in_dim(partial_sum, x * width, width, 1)
    sent = lax.dynamic_slice_in_dim(partial_sum, (1 - x) * width, width, 1)
    sent = sent.astype(jnp.bfloat16)
    came = lax.ppermute(sent, "inner", swapped(2, 1))
    routed = route(z.reshape(1), kept, came, row_session, planes, per_plane, slot_cap)
    first, _ = lax.optimization_barrier((first, sent))
    arrived = [routed[0]] + [
        lax.ppermute(routed[by], "sess", swapped(planes, by)) for by in range(1, planes)
    ]
    second, arrived = lax.optimization_barrier((second, arrived))
    right, left = [first, second], [first, second]
    prompts = {0: (first, second)}
    for hop in range(1, planes):
        for chunk in range(2):
            right[chunk] = lax.ppermute(right[chunk], "sess", shifted(planes, 1))
            left[chunk] = lax.ppermute(left[chunk], "sess", shifted(planes, -1))
        prompts[-hop], prompts[hop] = tuple(right), tuple(left)

    def after(value, hop, chunk):
        return lax.optimization_barrier((value, prompts[-hop][chunk], prompts[hop][chunk]))[0]

    arrived = stack(*[a[None] for a in arrived])
    other = lax.ppermute(arrived, "inner", swapped(2, 1))
    other = after(other, 1, 1)
    mine = stack(arrived, other)
    core = lax.ppermute(mine, "rep", swapped(2, 1))
    core = after(core, 2, 0)

    group_width = PER_GROUP * HD
    weight = jnp.concatenate(
        [
            lax.dynamic_slice_in_dim(q_weight, head * group_width, group_width, 1),
            lax.dynamic_slice_in_dim(k_weight, head * HD, HD, 1),
            lax.dynamic_slice_in_dim(v_weight, head * HD, HD, 1),
        ],
        axis=1,
    )
    states, query, key, value, lengths = place_rows(
        index, mine, core, attn_gain, weight, per_plane, slot_cap
    )

    speakers = lax.dynamic_slice_in_dim(speaker_of, z * per_plane, per_plane)
    wanted_slot = jnp.sum(
        jnp.where(
            speakers[:, None] == jnp.arange(prompt_slot.shape[0])[None, :], prompt_slot[None, :], 0
        ),
        axis=1,
    )
    hop = wanted_slot // held - z
    which = wanted_slot % held
    near = attend_near(
        hop, which, lengths, after(query, 3, 0), key, value, prompts, (0, -1, 1, -2, 2)
    )
    run = functools.partial(attend_far, index, hop, which, lengths)
    attended = {}
    attended[2], attended[3] = run(query, key, value, near, prompts, (-3, 3), (2, 3))
    near, _ = lax.optimization_barrier((near, attended[2]))
    attended[0], attended[1] = run(query, key, value, near, prompts, (-3, 3), (0, 1))
    pieces = [attended[0]] + [
        lax.ppermute(attended[by], pair, swapped(4, by)) for by in range(1, plane)
    ]
    return output(index, lengths, states, o_weight, pieces, per_device)


def solution(mesh):
    in_specs = (
        P(("groups", "sess", "rep"), "inner"),
        P(("groups", "sess", "rep"), None),
        P("groups"),
        P("groups"),
        P(("groups", "sess"), ("inner", "rep"), None),
        P("inner", None),
        P(),
        P(),
        P(),
        P(),
        P(),
    )
    out_specs = P(("groups", "sess", "inner", "rep"), None, None)
    sizes = tuple(mesh.shape[name] for name in ("sess", "inner", "rep"))
    body = line_body if sizes == (4, 2, 2) else general_body
    return jax.shard_map(body, mesh=mesh, in_specs=in_specs, out_specs=out_specs, check_vma=False)
```

```python
import functools
import math

import jax
import jax.numpy as jnp
import numpy as np
from jax import lax
from jax.experimental import pallas as pl
from jax.experimental.pallas import tpu as pltpu
from jax.sharding import PartitionSpec as P

H = 12
KVH = 4
HD = 128
PROMPT = 1024
SLOTS = 96
PER_GROUP = H // KVH

EPSILON = 1e-06
ROPE_BASE = 1000000.0
NT = (((1,), (1,)), ((), ()))


def rope_tables(copies):
    half_width = HD // 2
    inverse = ROPE_BASE ** (-(np.arange(half_width, dtype=np.float64) * 2.0) / HD)
    angles = (PROMPT + np.arange(SLOTS, dtype=np.float64))[:, None] * inverse[None, :]
    cosine = np.concatenate([np.cos(angles), np.cos(angles)], axis=1)
    sine = np.concatenate([-np.sin(angles), np.sin(angles)], axis=1)
    return (
        np.tile(cosine, (copies, 1)).astype(np.float32),
        np.tile(sine, (copies, 1)).astype(np.float32),
    )


def states_kernel(code_ref, slots_ref, gain_ref, weight_ref, cos_ref, sin_ref,
                  states_ref, query_ref, key_ref, value_ref):
    halves, blocks, rows, width = slots_ref.shape
    total = states_ref.shape[0]
    place = lax.broadcasted_iota(jnp.int32, (total, blocks * rows), 0)
    pick = (place == code_ref[0]).astype(jnp.bfloat16)
    parts = [
        jnp.dot(
            pick,
            slots_ref[half].reshape(blocks * rows, width),
            preferred_element_type=jnp.float32,
        )
        for half in range(halves)
    ]
    widened = jnp.concatenate(parts, axis=1)
    states_ref[...] = widened.astype(jnp.bfloat16)
    factor = lax.rsqrt(jnp.mean(widened * widened, axis=-1, keepdims=True) + EPSILON)
    normed = (widened * factor * gain_ref[...].astype(jnp.float32)).astype(jnp.bfloat16)
    both = jnp.dot(normed, weight_ref[...], preferred_element_type=jnp.float32)
    cosine, sine = cos_ref[...], sin_ref[...]
    for head in range(PER_GROUP + 1):
        vector = both[:, head * HD : (head + 1) * HD]
        turned = vector * cosine + pltpu.roll(vector, HD // 2, 1) * sine
        if head < PER_GROUP:
            query_ref[:, head * HD : (head + 1) * HD] = turned.astype(jnp.bfloat16)
        else:
            key_ref[...] = turned.astype(jnp.bfloat16)
    value_ref[...] = both[:, (PER_GROUP + 1) * HD :].astype(jnp.bfloat16)


def attention_kernel(place_ref, length_ref, query_ref, key_ref, value_ref, prompt_ref, out_ref):
    session = pl.program_id(0)
    length = length_ref[session]
    scale = HD ** (-0.5) * math.log2(math.e)
    query = jnp.concatenate(
        [query_ref[:, h * HD : (h + 1) * HD] for h in range(PER_GROUP)], axis=0
    )
    ahead = lax.dot_general(query, prompt_ref[0, :, :HD], NT, preferred_element_type=jnp.float32)
    own = lax.dot_general(query, key_ref[...], NT, preferred_element_type=jnp.float32)
    row = lax.broadcasted_iota(jnp.int32, (SLOTS, SLOTS), 0)
    column = lax.broadcasted_iota(jnp.int32, (SLOTS, SLOTS), 1)
    allowed = (column <= row) & (column < length)
    own = jnp.where(jnp.concatenate([allowed] * PER_GROUP, axis=0), own, -1e30)
    highest = jnp.maximum(
        jnp.max(ahead, axis=-1, keepdims=True), jnp.max(own, axis=-1, keepdims=True)
    )
    powers = jnp.exp2((ahead - highest) * scale)
    own_powers = jnp.exp2((own - highest) * scale)
    total = jnp.sum(powers, axis=-1, keepdims=True) + jnp.sum(own_powers, axis=-1, keepdims=True)
    mixed = jnp.dot(
        powers.astype(jnp.bfloat16), prompt_ref[0, :, HD:], preferred_element_type=jnp.float32
    ) + jnp.dot(own_powers.astype(jnp.bfloat16), value_ref[...], preferred_element_type=jnp.float32)
    mixed = (mixed / total).astype(jnp.bfloat16)
    for h in range(PER_GROUP):
        out_ref[:, h * HD : (h + 1) * HD] = mixed[h * SLOTS : (h + 1) * SLOTS]


def make_states(code, slots, gain, weight, sessions, together):
    halves, blocks, rows, width = slots.shape
    steps = sessions // together
    model = halves * width
    cosine, sine = rope_tables(together)
    total = together * SLOTS
    out = jax.ShapeDtypeStruct
    row_spec = lambda w: pl.BlockSpec((total, w), lambda i: (i, 0))
    whole = lambda a: pl.BlockSpec(a.shape, lambda i: (0,) * a.ndim)
    gain = gain.reshape(1, model)
    return pl.pallas_call(
        states_kernel,
        grid=(steps,),
        in_specs=[
            pl.BlockSpec((1, 1, code.shape[2]), lambda i: (i, 0, 0)),
            pl.BlockSpec((halves, blocks, rows // steps, width), lambda i: (0, 0, i, 0)),
            whole(gain),
            whole(weight),
            whole(cosine),
            whole(sine),
        ],
        out_specs=[row_spec(model), row_spec(PER_GROUP * HD), row_spec(HD), row_spec(HD)],
        out_shape=[
            out((sessions * SLOTS, model), jnp.bfloat16),
            out((sessions * SLOTS, PER_GROUP * HD), jnp.bfloat16),
            out((sessions * SLOTS, HD), jnp.bfloat16),
            out((sessions * SLOTS, HD), jnp.bfloat16),
        ],
        compiler_params=pltpu.CompilerParams(vmem_limit_bytes=40 << 20),
        name="states",
    )(code, slots, gain, weight, jnp.asarray(cosine), jnp.asarray(sine))


def attend(place, lengths, query, key, value, prompts):
    sessions = place.shape[0]
    row_spec = lambda w: pl.BlockSpec((SLOTS, w), lambda i, place, length: (i, 0))
    return pl.pallas_call(
        attention_kernel,
        grid_spec=pltpu.PrefetchScalarGridSpec(
            num_scalar_prefetch=2,
            grid=(sessions,),
            in_specs=[
                row_spec(PER_GROUP * HD),
                row_spec(HD),
                row_spec(HD),
                pl.BlockSpec((1, PROMPT, 2 * HD), lambda i, place, length: (place[i], 0, 0)),
            ],
            out_specs=row_spec(PER_GROUP * HD),
        ),
        out_shape=jax.ShapeDtypeStruct((sessions * SLOTS, PER_GROUP * HD), jnp.bfloat16),
        compiler_params=pltpu.CompilerParams(vmem_limit_bytes=40 << 20),
        name="attend",
    )(place, lengths, query, key, value, prompts)


def general_body(
    thinker_rows,
    row_session,
    speaker_of,
    prompt_slot,
    prompt_cache,
    proj_weight,
    attn_gain,
    q_weight,
    k_weight,
    v_weight,
    o_weight,
):
    sess_count = lax.axis_size("sess")
    inner_count = lax.axis_size("inner")
    rep_count = lax.axis_size("rep")
    plane = inner_count * rep_count
    blocks = sess_count * rep_count
    session_all = speaker_of.shape[0]
    per_plane = session_all // sess_count
    per_device = per_plane // plane
    slot_cap = SLOTS // blocks
    held, tokens, channels = prompt_cache.shape
    model = proj_weight.shape[1]
    sharers = plane // KVH
    held_part = held // sharers
    sess_place = lax.axis_index("sess")
    plane_place = lax.axis_index("inner") * rep_count + lax.axis_index("rep")
    head = plane_place // sharers
    sharer = plane_place % sharers

    outgoing = jnp.transpose(
        prompt_cache.reshape(sharers, held_part, tokens, 2, KVH, HD), (4, 0, 1, 2, 3, 5)
    ).reshape(plane, held_part, tokens, 2 * HD)
    own_head = lax.all_to_all(outgoing, ("inner", "rep"), split_axis=0, concat_axis=2, tiled=True)
    own_head = own_head.reshape(held_part, plane * tokens, 2 * HD)
    prompts = lax.all_gather(own_head, "sess", axis=0, tiled=True)

    row_owner = row_session[:, 0]
    order = jnp.arange(row_owner.shape[0])
    same = row_owner[:, None] == row_owner[None, :]
    earlier = jnp.sum((same & (order[None, :] < order[:, None])).astype(jnp.int32), axis=1)
    row_slot = row_owner * slot_cap + earlier
    counts = jnp.sum(
        (row_owner[:, None] == jnp.arange(session_all)[None, :]).astype(jnp.int32), axis=0
    )
    all_counts = lax.all_gather(counts, ("sess", "rep"), axis=0, tiled=False)

    partial_sum = jnp.dot(thinker_rows, proj_weight, preferred_element_type=jnp.float32)
    width = model // inner_count
    if inner_count == 2:
        inner_place = lax.axis_index("inner")
        kept = lax.dynamic_slice_in_dim(partial_sum, inner_place * width, width, 1)
        sent = lax.dynamic_slice_in_dim(partial_sum, (1 - inner_place) * width, width, 1)
        came = lax.ppermute(sent.astype(jnp.bfloat16), "inner", [(0, 1), (1, 0)])
        own_columns = (kept + came.astype(jnp.float32)).astype(jnp.bfloat16)
    else:
        own_columns = lax.psum_scatter(
            partial_sum, "inner", scatter_dimension=1, tiled=True
        ).astype(jnp.bfloat16)
    into = (jnp.arange(session_all * slot_cap)[:, None] == row_slot[None, :]).astype(jnp.bfloat16)
    buffer = jnp.dot(into, own_columns, preferred_element_type=jnp.float32).astype(jnp.bfloat16)
    arrived = lax.all_to_all(
        buffer.reshape(sess_count, per_plane * slot_cap, width),
        "sess",
        split_axis=0,
        concat_axis=0,
        tiled=True,
    )
    spread = lax.all_gather(arrived, ("inner", "rep"), axis=0, tiled=False)
    slots = spread.reshape(inner_count, rep_count * sess_count, per_plane * slot_cap, width)

    offsets = jnp.cumsum(all_counts, axis=0) - all_counts
    lengths_all = jnp.sum(all_counts, axis=0)
    mine = lambda a: lax.dynamic_slice_in_dim(a, sess_place * per_plane, per_plane, a.ndim - 1)
    by_block = lambda a: jnp.transpose(
        mine(a).reshape(sess_count, rep_count, per_plane), (1, 0, 2)
    ).reshape(blocks, per_plane)
    lengths = mine(lengths_all)
    together = 16 // math.gcd(16, slot_cap)
    within = jnp.arange(slot_cap)
    local = (jnp.arange(per_plane) % together)[None, :, None] * SLOTS
    code = jnp.where(
        within[None, None, :] < by_block(all_counts)[:, :, None],
        by_block(offsets)[:, :, None] + within[None, None, :] + local,
        -1,
    )
    steps = per_plane // together
    code = jnp.transpose(
        code.reshape(blocks, steps, together * slot_cap), (1, 0, 2)
    ).reshape(steps, 1, blocks * together * slot_cap)

    group_width = PER_GROUP * HD
    weight = jnp.concatenate(
        [
            lax.dynamic_slice_in_dim(q_weight, head * group_width, group_width, 1),
            lax.dynamic_slice_in_dim(k_weight, head * HD, HD, 1),
            lax.dynamic_slice_in_dim(v_weight, head * HD, HD, 1),
        ],
        axis=1,
    )
    states, query, key, value = make_states(
        code, slots, attn_gain, weight, per_plane, together
    )

    wanted_slot = jnp.sum(
        jnp.where(
            mine(speaker_of)[:, None] == jnp.arange(prompt_slot.shape[0])[None, :],
            prompt_slot[None, :],
            0,
        ),
        axis=1,
    )
    place = wanted_slot // held * held_part + wanted_slot % held_part
    attended = attend(place, lengths, query, key, value, prompts)
    returned = lax.all_to_all(
        attended.reshape(plane, per_device * SLOTS, group_width),
        ("inner", "rep"),
        split_axis=0,
        concat_axis=0,
        tiled=True,
    ).reshape(KVH, sharers, per_device, SLOTS, group_width)
    first = plane_place * per_device
    if sharers > 1:
        holder = lax.dynamic_slice_in_dim(wanted_slot % held // held_part, first, per_device)
        chosen = jnp.zeros_like(returned[:, 0])
        for t in range(sharers):
            chosen = jnp.where((holder == t)[None, :, None, None], returned[:, t], chosen)
    else:
        chosen = returned[:, 0]
    gathered = jnp.transpose(chosen, (1, 2, 0, 3)).reshape(per_device * SLOTS, H * HD)
    own_states = lax.dynamic_slice_in_dim(states, first * SLOTS, per_device * SLOTS, 0)
    own_lengths = lax.dynamic_slice_in_dim(lengths, first, per_device)
    summed = own_states.astype(jnp.float32) + jnp.dot(
        gathered, o_weight, preferred_element_type=jnp.float32
    )
    live_rows = (jnp.arange(SLOTS)[None, :] < own_lengths[:, None]).reshape(-1, 1)
    return (
        jnp.where(live_rows, summed, 0.0)
        .astype(jnp.bfloat16)
        .reshape(per_device, SLOTS, model)
    )


EXTRA = 16
SMEM = pl.BlockSpec(memory_space=pltpu.SMEM)
VMEM = pl.BlockSpec(memory_space=pltpu.VMEM)
ANY = pl.BlockSpec(memory_space=pl.ANY)


def split_heads_kernel(head_ref, cache_ref, *out_refs):
    for by, out_ref in enumerate(out_refs):
        for side in range(2):
            start = pl.multiple_of((head_ref[0] ^ by) * HD + side * KVH * HD, HD)
            out_ref[:, :, side * HD : (side + 1) * HD] = cache_ref[:, :, pl.ds(start, HD)]


def split_heads(head, cache):
    held, tokens, _ = cache.shape
    shape = jax.ShapeDtypeStruct((held, tokens, 2 * HD), cache.dtype)
    return pl.pallas_call(
        split_heads_kernel,
        in_specs=[SMEM, VMEM],
        out_specs=[VMEM] * KVH,
        out_shape=[shape] * KVH,
        cost_estimate=pl.CostEstimate(flops=0, bytes_accessed=2 * cache.size * 2, transcendentals=0),
        name="split_heads",
    )(head, cache)


def stack_kernel(*refs):
    in_refs, out_ref = refs[:-1], refs[-1]
    place = 0
    for in_ref in in_refs:
        count = in_ref.shape[0]
        out_ref[place : place + count] = in_ref[...]
        place += count


def stack(*arrays):
    total = sum(a.shape[0] for a in arrays)
    size = sum(a.size for a in arrays)
    return pl.pallas_call(
        stack_kernel,
        in_specs=[VMEM] * len(arrays),
        out_specs=VMEM,
        out_shape=jax.ShapeDtypeStruct((total,) + arrays[0].shape[1:], arrays[0].dtype),
        cost_estimate=pl.CostEstimate(flops=0, bytes_accessed=4 * size, transcendentals=0),
        name="stack",
    )(*arrays)


def project_kernel(index_ref, rows_ref, weight_ref, kept_ref, sent_ref):
    width = kept_ref.shape[1]
    partial_sum = jnp.dot(rows_ref[...], weight_ref[...], preferred_element_type=jnp.float32)
    low, high = partial_sum[:, :width], partial_sum[:, width:]
    is_low = index_ref[1] == 0
    kept_ref[...] = jnp.where(is_low, low, high)
    sent_ref[...] = jnp.where(is_low, high, low).astype(jnp.bfloat16)


def project(index, rows, weight):
    count, width = rows.shape[0], weight.shape[1] // 2
    return pl.pallas_call(
        project_kernel,
        in_specs=[SMEM, VMEM, VMEM],
        out_specs=[VMEM] * 2,
        out_shape=[
            jax.ShapeDtypeStruct((count, width), jnp.float32),
            jax.ShapeDtypeStruct((count, width), jnp.bfloat16),
        ],
        compiler_params=pltpu.CompilerParams(vmem_limit_bytes=40 << 20),
        cost_estimate=pl.CostEstimate(
            flops=2 * count * weight.size, bytes_accessed=2 * (rows.size + weight.size), transcendentals=0
        ),
        name="project",
    )(index, rows, weight)


def route_kernel(index_ref, kept_ref, came_ref, owner_ref, *out_refs,
                 slot_cap, per_plane):
    rows = kept_ref.shape[0]
    planes = len(out_refs)
    size = out_refs[0].shape[0]
    live = per_plane * slot_cap
    columns = (kept_ref[...] + came_ref[...].astype(jnp.float32)).astype(jnp.bfloat16)
    owner_row = owner_ref[...]
    above = lax.broadcasted_iota(jnp.int32, (rows, rows), 0)
    beside = lax.broadcasted_iota(jnp.int32, (rows, rows), 1)
    owner = jnp.sum(jnp.where(above == beside, owner_row, 0), axis=1, keepdims=True)
    earlier = jnp.sum(
        jnp.where((owner == owner_row) & (above < beside), 1.0, 0.0), axis=0, keepdims=True
    ).astype(jnp.int32)
    target = lax.div(owner_row, per_plane) ^ index_ref[0]
    code = target * size + lax.rem(owner_row, per_plane) * slot_cap + earlier
    place = lax.broadcasted_iota(jnp.int32, (planes * size, rows), 0)
    into = (place == code).astype(jnp.bfloat16)
    routed = jnp.dot(into, columns, preferred_element_type=jnp.float32).astype(jnp.bfloat16)
    lane = lax.broadcasted_iota(jnp.int32, (rows, HD), 1)
    named = (lane == owner).astype(jnp.bfloat16)
    counts = jnp.dot(
        jnp.ones((EXTRA, rows), jnp.bfloat16), named, preferred_element_type=jnp.float32
    ).astype(jnp.bfloat16)
    for k, out_ref in enumerate(out_refs):
        out_ref[:live] = routed[k * size : k * size + live]
        out_ref[live:] = jnp.zeros((EXTRA, out_ref.shape[1]), jnp.bfloat16)
        out_ref[live:, :HD] = counts


def route(index, kept, came, row_session, planes, per_plane, slot_cap):
    width = kept.shape[1]
    rows = row_session.shape[0]
    size = per_plane * slot_cap + EXTRA
    return pl.pallas_call(
        functools.partial(route_kernel, slot_cap=slot_cap, per_plane=per_plane),
        in_specs=[SMEM] + [VMEM] * 3,
        out_specs=[VMEM] * planes,
        out_shape=[jax.ShapeDtypeStruct((size, width), jnp.bfloat16)] * planes,
        cost_estimate=pl.CostEstimate(
            flops=2 * planes * size * rows * width, bytes_accessed=rows * width * 8, transcendentals=0
        ),
        name="route",
    )(index, kept, came, row_session.reshape(1, rows))


def place_kernel(index_ref, near_ref, far_ref, near_core_ref, far_core_ref, gain_ref,
                 q_ref, k_ref, v_ref, cos_ref, sin_ref, states_ref, query_ref, key_ref, value_ref, length_ref, *, slot_cap, together):
    z, x, c, head = [index_ref[i] for i in range(4)]
    planes, live, width = near_ref.shape
    blocks = 2 * planes
    live = live - EXTRA
    columns = pl.ds(pl.multiple_of(head * HD, HD), HD)
    group_columns = pl.ds(pl.multiple_of(head * PER_GROUP * HD, HD), PER_GROUP * HD)
    per_plane = live // slot_cap
    steps = per_plane // together
    window = together * slot_cap
    total = together * SLOTS
    counts = jnp.concatenate(
        [ref[k, live : live + 1, :HD] for ref in (near_ref, near_core_ref) for k in range(planes)],
        axis=0,
    ).astype(jnp.float32)
    kind = lambda axis: lax.broadcasted_iota(jnp.int32, (blocks, blocks), axis)
    true_block = lambda k: (z ^ (k % planes)) * 2 + (c ^ (k // planes))
    before = (true_block(kind(1)) < true_block(kind(0))).astype(jnp.float32)
    offsets = jnp.dot(before, counts, preferred_element_type=jnp.float32)
    session_lane = lax.broadcasted_iota(jnp.int32, (HD, HD), 0)
    local_lane = lax.broadcasted_iota(jnp.int32, (HD, HD), 1)
    ours = (session_lane == z * per_plane + local_lane).astype(jnp.float32)
    sums = jnp.dot(
        jnp.broadcast_to(jnp.sum(counts, axis=0, keepdims=True), (8, HD)),
        ours,
        preferred_element_type=jnp.float32,
    )
    length_ref[...] = sums[:1].astype(jnp.int32)
    cosine, sine = cos_ref[...], sin_ref[...]
    gain = gain_ref[...].astype(jnp.float32)
    for step in range(steps):
        slot = lax.broadcasted_iota(jnp.int32, (blocks, blocks * window), 1)
        in_block = slot % window
        spread = lax.broadcasted_iota(jnp.int32, (HD, blocks * window), 1) % window // slot_cap
        from_lane = lax.broadcasted_iota(jnp.int32, (HD, blocks * window), 0)
        expand = (from_lane == z * per_plane + step * together + spread).astype(jnp.float32)
        here = jnp.dot(counts, expand, preferred_element_type=jnp.float32).astype(jnp.int32)
        start = jnp.dot(offsets, expand, preferred_element_type=jnp.float32).astype(jnp.int32)
        within = in_block % slot_cap
        row = jnp.where(within < here, start + within + in_block // slot_cap * SLOTS, -1)
        block = lax.broadcasted_iota(jnp.int32, (blocks, blocks * window), 0)
        code = jnp.max(jnp.where(slot // window == block, row, -1), axis=0, keepdims=True)
        place = lax.broadcasted_iota(jnp.int32, (total, blocks * window), 0)
        pick = (place == code).astype(jnp.bfloat16)
        slots = slice(step * window, (step + 1) * window)
        near, far = [
            jnp.dot(
                pick,
                jnp.concatenate(
                    [ref[k, slots] for ref in refs for k in range(planes)], axis=0
                ),
                preferred_element_type=jnp.float32,
            )
            for refs in ((near_ref, near_core_ref), (far_ref, far_core_ref))
        ]
        widened = jnp.concatenate(
            [jnp.where(x == 0, near, far), jnp.where(x == 0, far, near)], axis=1
        )
        rows = slice(step * total, (step + 1) * total)
        states_ref[rows] = widened.astype(jnp.bfloat16)
        factor = lax.rsqrt(jnp.mean(widened * widened, axis=-1, keepdims=True) + EPSILON)
        normed = (widened * factor * gain).astype(jnp.bfloat16)
        queries = jnp.dot(normed, q_ref[:, group_columns], preferred_element_type=jnp.float32)
        keys = jnp.dot(normed, k_ref[:, columns], preferred_element_type=jnp.float32)
        for h in range(PER_GROUP + 1):
            vector = keys if h == PER_GROUP else queries[:, h * HD : (h + 1) * HD]
            turned = vector * cosine + pltpu.roll(vector, HD // 2, 1) * sine
            if h < PER_GROUP:
                query_ref[rows, h * HD : (h + 1) * HD] = turned.astype(jnp.bfloat16)
            else:
                key_ref[rows] = turned.astype(jnp.bfloat16)
        values = jnp.dot(normed, v_ref[:, columns], preferred_element_type=jnp.float32)
        value_ref[rows] = values.astype(jnp.bfloat16)


def place_rows(index, slots, gain, weights, sessions, slot_cap):
    together = 16 // math.gcd(16, slot_cap)
    cosine, sine = rope_tables(together)
    model = 2 * slots[0].shape[2]
    total = sessions * SLOTS
    out = lambda w: jax.ShapeDtypeStruct((total, w), jnp.bfloat16)
    return pl.pallas_call(
        functools.partial(place_kernel, slot_cap=slot_cap, together=together),
        in_specs=[SMEM] + [VMEM] * 10,
        out_specs=[VMEM] * 5,
        out_shape=[
            out(model), out(PER_GROUP * HD), out(HD), out(HD),
            jax.ShapeDtypeStruct((1, HD), jnp.int32),
        ],
        compiler_params=pltpu.CompilerParams(vmem_limit_bytes=40 << 20),
        cost_estimate=pl.CostEstimate(
            flops=4 * total * model * 5 * HD, bytes_accessed=6 << 20, transcendentals=0
        ),
        name="place_rows",
    )(index, *slots, gain.reshape(1, model), *weights, jnp.asarray(cosine), jnp.asarray(sine))


def session_attention(query, key, value, tokens, length):
    scale = HD ** (-0.5) * math.log2(math.e)
    query = jnp.concatenate([query[:, h * HD : (h + 1) * HD] for h in range(PER_GROUP)], axis=0)
    ahead = lax.dot_general(query, tokens[:, :HD], NT, preferred_element_type=jnp.float32)
    own = lax.dot_general(query, key, NT, preferred_element_type=jnp.float32)
    row = lax.broadcasted_iota(jnp.int32, (SLOTS, SLOTS), 0)
    column = lax.broadcasted_iota(jnp.int32, (SLOTS, SLOTS), 1)
    allowed = (column <= row) & (column < length)
    own = jnp.where(jnp.concatenate([allowed] * PER_GROUP, axis=0), own, -1e30)
    highest = jnp.maximum(
        jnp.max(ahead, axis=-1, keepdims=True), jnp.max(own, axis=-1, keepdims=True)
    )
    powers = jnp.exp2((ahead - highest) * scale)
    own_powers = jnp.exp2((own - highest) * scale)
    total = jnp.sum(powers, axis=-1, keepdims=True) + jnp.sum(own_powers, axis=-1, keepdims=True)
    mixed = jnp.dot(
        powers.astype(jnp.bfloat16), tokens[:, HD:], preferred_element_type=jnp.float32
    ) + jnp.dot(own_powers.astype(jnp.bfloat16), value, preferred_element_type=jnp.float32)
    return (mixed / total).astype(jnp.bfloat16)


def fetches(hop, refs, held, kv, sem, hops, start):
    for which, source in enumerate(hops):
        copies = [
            pltpu.make_async_copy(refs[2 * which + chunk].at[:, held], kv.at[chunk], sem.at[chunk])
            for chunk in range(2)
        ]
        if start:
            @pl.when(hop == source)
            def _():
                for copy in copies:
                    copy.start()
        elif which == 0:
            for copy in copies:
                copy.wait()


def among(hop, hops):
    ours = hop == hops[0]
    for other in hops[1:]:
        ours = ours | (hop == other)
    return ours


def near_kernel(hop_ref, held_ref, length_ref, query_ref, key_ref, value_ref, *refs, hops):
    prompt_refs, (out_ref, kv, sem) = refs[: 2 * len(hops)], refs[2 * len(hops) :]
    sessions = hop_ref.shape[0]
    for i in range(sessions):
        fetches(hop_ref[i], prompt_refs, held_ref[i], kv.at[i], sem.at[i], hops, True)

    def work(i, _):
        @pl.when(among(hop_ref[i], hops))
        def _():
            fetches(hop_ref[i], prompt_refs, held_ref[i], kv.at[i], sem.at[i], hops, False)
            rows = pl.ds(pl.multiple_of(i * SLOTS, SLOTS), SLOTS)
            mixed = session_attention(
                query_ref[rows], key_ref[rows], value_ref[rows],
                kv[i].reshape(PROMPT, 2 * HD), length_ref[0, i],
            )
            for h in range(PER_GROUP):
                out_ref[rows, h * HD : (h + 1) * HD] = mixed[h * SLOTS : (h + 1) * SLOTS]

        return 0

    lax.fori_loop(0, sessions, work, 0)


def far_kernel(index_ref, hop_ref, held_ref, length_ref, query_ref, key_ref, value_ref, near_ref,
               *refs, targets, hops):
    prompt_refs, refs = refs[: 2 * len(hops)], refs[2 * len(hops) :]
    out_refs, (kv, sem) = refs[: len(targets)], refs[len(targets) :]
    head = index_ref[3]
    per_device = out_refs[0].shape[0] // SLOTS
    places = [(t, j) for t in range(len(targets)) for j in range(per_device)]
    sessions = [(head ^ targets[t]) * per_device + j for t, j in places]
    for i, session in enumerate(sessions):
        fetches(
            hop_ref[session], prompt_refs, held_ref[session], kv.at[i], sem.at[i], hops, True
        )
    for i, (session, (t, j)) in enumerate(zip(sessions, places)):
        rows = pl.ds(pl.multiple_of(session * SLOTS, SLOTS), SLOTS)
        target = slice(j * SLOTS, (j + 1) * SLOTS)
        ours = among(hop_ref[session], hops)

        @pl.when(jnp.logical_not(ours))
        def _():
            out_refs[t][target] = near_ref[rows]

        @pl.when(ours)
        def _():
            fetches(
                hop_ref[session], prompt_refs, held_ref[session], kv.at[i], sem.at[i], hops, False
            )
            mixed = session_attention(
                query_ref[rows], key_ref[rows], value_ref[rows],
                kv[i].reshape(PROMPT, 2 * HD), length_ref[0, session],
            )
            for h in range(PER_GROUP):
                out_refs[t][target, h * HD : (h + 1) * HD] = mixed[h * SLOTS : (h + 1) * SLOTS]


HBM = pl.BlockSpec(memory_space=pltpu.HBM)


def attention_call(kernel, out_specs, out_shape, places, name, scalars, arrays, prompts, hops):
    pieces = [piece for h in hops for piece in prompts[h]]
    work = places * PER_GROUP * SLOTS * (PROMPT + SLOTS) // 2
    return pl.pallas_call(
        kernel,
        in_specs=[SMEM] * len(scalars) + [VMEM] * len(arrays) + [HBM] * len(pieces),
        out_specs=out_specs,
        out_shape=out_shape,
        scratch_shapes=[
            pltpu.VMEM((places, 2, 2, PROMPT // 4, 2 * HD), jnp.bfloat16),
            pltpu.SemaphoreType.DMA((places, 2)),
        ],
        compiler_params=pltpu.CompilerParams(vmem_limit_bytes=40 << 20),
        cost_estimate=pl.CostEstimate(
            flops=4 * work * HD, bytes_accessed=places * PROMPT * 2 * HD, transcendentals=work
        ),
        name=name,
    )(*scalars, *arrays, *pieces)


def attend_near(hop, held, lengths, query, key, value, prompts, hops):
    out_shape = jax.ShapeDtypeStruct(query.shape, jnp.bfloat16)
    return attention_call(
        functools.partial(near_kernel, hops=hops),
        VMEM, out_shape, hop.shape[0], "near", (hop, held, lengths), (query, key, value),
        prompts, hops,
    )


def attend_far(index, hop, held, lengths, query, key, value, near, prompts, hops, targets):
    per_device = hop.shape[0] // KVH
    out_shape = jax.ShapeDtypeStruct((per_device * SLOTS, query.shape[1]), jnp.bfloat16)
    return attention_call(
        functools.partial(far_kernel, hops=hops, targets=targets),
        [VMEM] * len(targets), [out_shape] * len(targets), per_device * len(targets), "far",
        (index, hop, held, lengths), (query, key, value, near), prompts, hops,
    )


def output_kernel(index_ref, length_ref, states_ref, weight_ref, *refs):
    piece_refs, out_ref = refs[:-1], refs[-1]
    head = index_ref[3]
    group_width = PER_GROUP * HD
    per_device = out_ref.shape[0]
    total = per_device * SLOTS
    summed = states_ref[pl.ds(pl.multiple_of(head * total, SLOTS), total)].astype(jnp.float32)
    for by, piece_ref in enumerate(piece_refs):
        start = pl.multiple_of((head ^ by) * group_width, group_width)
        summed = summed + jnp.dot(
            piece_ref[...], weight_ref[pl.ds(start, group_width)], preferred_element_type=jnp.float32
        )
    row = lax.broadcasted_iota(jnp.int32, (SLOTS, 1), 0)
    for i in range(per_device):
        live = row < length_ref[0, head * per_device + i]
        part = summed[i * SLOTS : (i + 1) * SLOTS]
        out_ref[i] = jnp.where(live, part, 0.0).astype(jnp.bfloat16)


def output(index, lengths, states, o_weight, pieces, per_device):
    model = o_weight.shape[1]
    return pl.pallas_call(
        output_kernel,
        in_specs=[SMEM] * 2 + [VMEM] * (2 + len(pieces)),
        out_specs=VMEM,
        out_shape=jax.ShapeDtypeStruct((per_device, SLOTS, model), jnp.bfloat16),
        compiler_params=pltpu.CompilerParams(vmem_limit_bytes=40 << 20),
        cost_estimate=pl.CostEstimate(
            flops=2 * per_device * SLOTS * o_weight.size, bytes_accessed=o_weight.size * 2, transcendentals=0
        ),
        name="output",
    )(index, lengths, states, o_weight, *pieces)


def shifted(n, by):
    return [(i, i + by) for i in range(n) if 0 <= i + by < n]


def swapped(n, by):
    return [(i, i ^ by) for i in range(n)]


def line_body(
    thinker_rows,
    row_session,
    speaker_of,
    prompt_slot,
    prompt_cache,
    proj_weight,
    attn_gain,
    q_weight,
    k_weight,
    v_weight,
    o_weight,
):
    planes, plane, rep_count = lax.axis_size("sess"), KVH, 2
    blocks = planes * rep_count
    session_all = speaker_of.shape[0]
    per_plane = session_all // planes
    per_device = per_plane // plane
    slot_cap = SLOTS // blocks
    held = prompt_cache.shape[0]
    model = proj_weight.shape[1]
    width = model // 2
    z, x, c = lax.axis_index("sess"), lax.axis_index("inner"), lax.axis_index("rep")
    head = x * rep_count + c
    index = jnp.stack([z, x, c, head]).astype(jnp.int32)
    pair = ("inner", "rep")

    kept, sent = project(index, thinker_rows, proj_weight)
    came = lax.ppermute(sent, "inner", swapped(2, 1))

    own, to_core, to_x, to_far = split_heads(head.reshape(1), prompt_cache)
    from_core = lax.ppermute(to_core, pair, swapped(4, 1))
    from_x = lax.ppermute(to_x, pair, swapped(4, 2))
    from_far = lax.ppermute(to_far, pair, swapped(4, 3))
    first = stack(own[None], from_core[None])
    second = stack(from_x[None], from_far[None])

    routed = route(index, kept, came, row_session, planes, per_plane, slot_cap)
    first, _ = lax.optimization_barrier((first, routed[0]))
    arrived = [routed[0]] + [
        lax.ppermute(routed[by], "sess", swapped(planes, by)) for by in range(1, planes)
    ]
    second, arrived = lax.optimization_barrier((second, arrived))
    right, left = [first, second], [first, second]
    prompts = {0: (first, second)}
    for hop in range(1, planes):
        for chunk in range(2):
            right[chunk] = lax.ppermute(right[chunk], "sess", shifted(planes, 1))
            left[chunk] = lax.ppermute(left[chunk], "sess", shifted(planes, -1))
        prompts[-hop], prompts[hop] = tuple(right), tuple(left)

    def after(value, hop, chunk):
        return lax.optimization_barrier((value, prompts[-hop][chunk], prompts[hop][chunk]))[0]

    arrived = stack(*[a[None] for a in arrived])
    other = lax.ppermute(arrived, "inner", swapped(2, 1))
    other = after(other, 1, 1)
    slots = (
        arrived, other, lax.ppermute(arrived, "rep", swapped(2, 1)), lax.ppermute(other, "rep", swapped(2, 1))
    )
    slots = after(slots, 2, 0)
    states, query, key, value, lengths = place_rows(
        index, slots, attn_gain, (q_weight, k_weight, v_weight), per_plane, slot_cap
    )

    speakers = lax.dynamic_slice_in_dim(speaker_of, z * per_plane, per_plane)
    wanted_slot = jnp.sum(
        jnp.where(
            speakers[:, None] == jnp.arange(prompt_slot.shape[0])[None, :], prompt_slot[None, :], 0
        ),
        axis=1,
    )
    hop = wanted_slot // held - z
    which = wanted_slot % held
    near = attend_near(
        hop, which, lengths, after(query, 3, 0), key, value, prompts, (0, -1, 1, -2, 2)
    )
    run = functools.partial(attend_far, index, hop, which, lengths)
    attended = {}
    attended[2], attended[3] = run(query, key, value, near, prompts, (-3, 3), (2, 3))
    near, _ = lax.optimization_barrier((near, attended[2]))
    attended[0], attended[1] = run(query, key, value, near, prompts, (-3, 3), (0, 1))
    pieces = [attended[0]] + [
        lax.ppermute(attended[by], pair, swapped(4, by)) for by in range(1, plane)
    ]
    return output(index, lengths, states, o_weight, pieces, per_device)


def solution(mesh):
    in_specs = (
        P(("groups", "sess", "rep"), "inner"),
        P(("groups", "sess", "rep"), None),
        P("groups"),
        P("groups"),
        P(("groups", "sess"), ("inner", "rep"), None),
        P("inner", None),
        P(),
        P(),
        P(),
        P(),
        P(),
    )
    out_specs = P(("groups", "sess", "inner", "rep"), None, None)
    sizes = tuple(mesh.shape[name] for name in ("sess", "inner", "rep"))
    body = line_body if sizes == (4, 2, 2) else general_body
    return jax.shard_map(body, mesh=mesh, in_specs=in_specs, out_specs=out_specs, check_vma=False)
```

```python
import functools
import math

import jax
import jax.numpy as jnp
import numpy as np
from jax import lax
from jax.experimental import pallas as pl
from jax.experimental.pallas import tpu as pltpu
from jax.sharding import PartitionSpec as P

H = 12
KVH = 4
HD = 128
PROMPT = 1024
SLOTS = 96
PER_GROUP = H // KVH

EPSILON = 1e-06
ROPE_BASE = 1000000.0
NT = (((1,), (1,)), ((), ()))


def rope_tables(copies):
    half_width = HD // 2
    inverse = ROPE_BASE ** (-(np.arange(half_width, dtype=np.float64) * 2.0) / HD)
    angles = (PROMPT + np.arange(SLOTS, dtype=np.float64))[:, None] * inverse[None, :]
    cosine = np.concatenate([np.cos(angles), np.cos(angles)], axis=1)
    sine = np.concatenate([-np.sin(angles), np.sin(angles)], axis=1)
    return (
        np.tile(cosine, (copies, 1)).astype(np.float32),
        np.tile(sine, (copies, 1)).astype(np.float32),
    )


def states_kernel(code_ref, slots_ref, gain_ref, weight_ref, cos_ref, sin_ref,
                  states_ref, query_ref, key_ref, value_ref):
    halves, blocks, rows, width = slots_ref.shape
    total = states_ref.shape[0]
    place = lax.broadcasted_iota(jnp.int32, (total, blocks * rows), 0)
    pick = (place == code_ref[0]).astype(jnp.bfloat16)
    parts = [
        jnp.dot(
            pick,
            slots_ref[half].reshape(blocks * rows, width),
            preferred_element_type=jnp.float32,
        )
        for half in range(halves)
    ]
    widened = jnp.concatenate(parts, axis=1)
    states_ref[...] = widened.astype(jnp.bfloat16)
    factor = lax.rsqrt(jnp.mean(widened * widened, axis=-1, keepdims=True) + EPSILON)
    normed = (widened * factor * gain_ref[...].astype(jnp.float32)).astype(jnp.bfloat16)
    both = jnp.dot(normed, weight_ref[...], preferred_element_type=jnp.float32)
    cosine, sine = cos_ref[...], sin_ref[...]
    for head in range(PER_GROUP + 1):
        vector = both[:, head * HD : (head + 1) * HD]
        turned = vector * cosine + pltpu.roll(vector, HD // 2, 1) * sine
        if head < PER_GROUP:
            query_ref[:, head * HD : (head + 1) * HD] = turned.astype(jnp.bfloat16)
        else:
            key_ref[...] = turned.astype(jnp.bfloat16)
    value_ref[...] = both[:, (PER_GROUP + 1) * HD :].astype(jnp.bfloat16)


def attention_kernel(place_ref, length_ref, query_ref, key_ref, value_ref, prompt_ref, out_ref):
    session = pl.program_id(0)
    length = length_ref[session]
    scale = HD ** (-0.5) * math.log2(math.e)
    query = jnp.concatenate(
        [query_ref[:, h * HD : (h + 1) * HD] for h in range(PER_GROUP)], axis=0
    )
    ahead = lax.dot_general(query, prompt_ref[0, :, :HD], NT, preferred_element_type=jnp.float32)
    own = lax.dot_general(query, key_ref[...], NT, preferred_element_type=jnp.float32)
    row = lax.broadcasted_iota(jnp.int32, (SLOTS, SLOTS), 0)
    column = lax.broadcasted_iota(jnp.int32, (SLOTS, SLOTS), 1)
    allowed = (column <= row) & (column < length)
    own = jnp.where(jnp.concatenate([allowed] * PER_GROUP, axis=0), own, -1e30)
    highest = jnp.maximum(
        jnp.max(ahead, axis=-1, keepdims=True), jnp.max(own, axis=-1, keepdims=True)
    )
    powers = jnp.exp2((ahead - highest) * scale)
    own_powers = jnp.exp2((own - highest) * scale)
    total = jnp.sum(powers, axis=-1, keepdims=True) + jnp.sum(own_powers, axis=-1, keepdims=True)
    mixed = jnp.dot(
        powers.astype(jnp.bfloat16), prompt_ref[0, :, HD:], preferred_element_type=jnp.float32
    ) + jnp.dot(own_powers.astype(jnp.bfloat16), value_ref[...], preferred_element_type=jnp.float32)
    mixed = (mixed / total).astype(jnp.bfloat16)
    for h in range(PER_GROUP):
        out_ref[:, h * HD : (h + 1) * HD] = mixed[h * SLOTS : (h + 1) * SLOTS]


def make_states(code, slots, gain, weight, sessions, together):
    halves, blocks, rows, width = slots.shape
    steps = sessions // together
    model = halves * width
    cosine, sine = rope_tables(together)
    total = together * SLOTS
    out = jax.ShapeDtypeStruct
    row_spec = lambda w: pl.BlockSpec((total, w), lambda i: (i, 0))
    whole = lambda a: pl.BlockSpec(a.shape, lambda i: (0,) * a.ndim)
    gain = gain.reshape(1, model)
    return pl.pallas_call(
        states_kernel,
        grid=(steps,),
        in_specs=[
            pl.BlockSpec((1, 1, code.shape[2]), lambda i: (i, 0, 0)),
            pl.BlockSpec((halves, blocks, rows // steps, width), lambda i: (0, 0, i, 0)),
            whole(gain),
            whole(weight),
            whole(cosine),
            whole(sine),
        ],
        out_specs=[row_spec(model), row_spec(PER_GROUP * HD), row_spec(HD), row_spec(HD)],
        out_shape=[
            out((sessions * SLOTS, model), jnp.bfloat16),
            out((sessions * SLOTS, PER_GROUP * HD), jnp.bfloat16),
            out((sessions * SLOTS, HD), jnp.bfloat16),
            out((sessions * SLOTS, HD), jnp.bfloat16),
        ],
        compiler_params=pltpu.CompilerParams(vmem_limit_bytes=32 << 20),
        name="states",
    )(code, slots, gain, weight, jnp.asarray(cosine), jnp.asarray(sine))


def attend(place, lengths, query, key, value, prompts):
    sessions = place.shape[0]
    row_spec = lambda w: pl.BlockSpec((SLOTS, w), lambda i, place, length: (i, 0))
    return pl.pallas_call(
        attention_kernel,
        grid_spec=pltpu.PrefetchScalarGridSpec(
            num_scalar_prefetch=2,
            grid=(sessions,),
            in_specs=[
                row_spec(PER_GROUP * HD),
                row_spec(HD),
                row_spec(HD),
                pl.BlockSpec((1, PROMPT, 2 * HD), lambda i, place, length: (place[i], 0, 0)),
            ],
            out_specs=row_spec(PER_GROUP * HD),
        ),
        out_shape=jax.ShapeDtypeStruct((sessions * SLOTS, PER_GROUP * HD), jnp.bfloat16),
        compiler_params=pltpu.CompilerParams(vmem_limit_bytes=32 << 20),
        name="attend",
    )(place, lengths, query, key, value, prompts)


def general_body(
    thinker_rows,
    row_session,
    speaker_of,
    prompt_slot,
    prompt_cache,
    proj_weight,
    attn_gain,
    q_weight,
    k_weight,
    v_weight,
    o_weight,
):
    sess_count = lax.axis_size("sess")
    inner_count = lax.axis_size("inner")
    rep_count = lax.axis_size("rep")
    plane = inner_count * rep_count
    blocks = sess_count * rep_count
    session_all = speaker_of.shape[0]
    per_plane = session_all // sess_count
    per_device = per_plane // plane
    slot_cap = SLOTS // blocks
    held, tokens, channels = prompt_cache.shape
    model = proj_weight.shape[1]
    sharers = plane // KVH
    held_part = held // sharers
    sess_place = lax.axis_index("sess")
    plane_place = lax.axis_index("inner") * rep_count + lax.axis_index("rep")
    head = plane_place // sharers
    sharer = plane_place % sharers

    outgoing = jnp.transpose(
        prompt_cache.reshape(sharers, held_part, tokens, 2, KVH, HD), (4, 0, 1, 2, 3, 5)
    ).reshape(plane, held_part, tokens, 2 * HD)
    own_head = lax.all_to_all(outgoing, ("inner", "rep"), split_axis=0, concat_axis=2, tiled=True)
    own_head = own_head.reshape(held_part, plane * tokens, 2 * HD)
    prompts = lax.all_gather(own_head, "sess", axis=0, tiled=True)

    row_owner = row_session[:, 0]
    order = jnp.arange(row_owner.shape[0])
    same = row_owner[:, None] == row_owner[None, :]
    earlier = jnp.sum((same & (order[None, :] < order[:, None])).astype(jnp.int32), axis=1)
    row_slot = row_owner * slot_cap + earlier
    counts = jnp.sum(
        (row_owner[:, None] == jnp.arange(session_all)[None, :]).astype(jnp.int32), axis=0
    )
    all_counts = lax.all_gather(counts, ("sess", "rep"), axis=0, tiled=False)

    partial_sum = jnp.dot(thinker_rows, proj_weight, preferred_element_type=jnp.float32)
    width = model // inner_count
    if inner_count == 2:
        inner_place = lax.axis_index("inner")
        kept = lax.dynamic_slice_in_dim(partial_sum, inner_place * width, width, 1)
        sent = lax.dynamic_slice_in_dim(partial_sum, (1 - inner_place) * width, width, 1)
        came = lax.ppermute(sent.astype(jnp.bfloat16), "inner", [(0, 1), (1, 0)])
        own_columns = (kept + came.astype(jnp.float32)).astype(jnp.bfloat16)
    else:
        own_columns = lax.psum_scatter(
            partial_sum, "inner", scatter_dimension=1, tiled=True
        ).astype(jnp.bfloat16)
    into = (jnp.arange(session_all * slot_cap)[:, None] == row_slot[None, :]).astype(jnp.bfloat16)
    buffer = jnp.dot(into, own_columns, preferred_element_type=jnp.float32).astype(jnp.bfloat16)
    arrived = lax.all_to_all(
        buffer.reshape(sess_count, per_plane * slot_cap, width),
        "sess",
        split_axis=0,
        concat_axis=0,
        tiled=True,
    )
    spread = lax.all_gather(arrived, ("inner", "rep"), axis=0, tiled=False)
    slots = spread.reshape(inner_count, rep_count * sess_count, per_plane * slot_cap, width)

    offsets = jnp.cumsum(all_counts, axis=0) - all_counts
    lengths_all = jnp.sum(all_counts, axis=0)
    mine = lambda a: lax.dynamic_slice_in_dim(a, sess_place * per_plane, per_plane, a.ndim - 1)
    by_block = lambda a: jnp.transpose(
        mine(a).reshape(sess_count, rep_count, per_plane), (1, 0, 2)
    ).reshape(blocks, per_plane)
    lengths = mine(lengths_all)
    together = 16 // math.gcd(16, slot_cap)
    within = jnp.arange(slot_cap)
    local = (jnp.arange(per_plane) % together)[None, :, None] * SLOTS
    code = jnp.where(
        within[None, None, :] < by_block(all_counts)[:, :, None],
        by_block(offsets)[:, :, None] + within[None, None, :] + local,
        -1,
    )
    steps = per_plane // together
    code = jnp.transpose(
        code.reshape(blocks, steps, together * slot_cap), (1, 0, 2)
    ).reshape(steps, 1, blocks * together * slot_cap)

    group_width = PER_GROUP * HD
    weight = jnp.concatenate(
        [
            lax.dynamic_slice_in_dim(q_weight, head * group_width, group_width, 1),
            lax.dynamic_slice_in_dim(k_weight, head * HD, HD, 1),
            lax.dynamic_slice_in_dim(v_weight, head * HD, HD, 1),
        ],
        axis=1,
    )
    states, query, key, value = make_states(
        code, slots, attn_gain, weight, per_plane, together
    )

    wanted_slot = jnp.sum(
        jnp.where(
            mine(speaker_of)[:, None] == jnp.arange(prompt_slot.shape[0])[None, :],
            prompt_slot[None, :],
            0,
        ),
        axis=1,
    )
    place = wanted_slot // held * held_part + wanted_slot % held_part
    attended = attend(place, lengths, query, key, value, prompts)
    returned = lax.all_to_all(
        attended.reshape(plane, per_device * SLOTS, group_width),
        ("inner", "rep"),
        split_axis=0,
        concat_axis=0,
        tiled=True,
    ).reshape(KVH, sharers, per_device, SLOTS, group_width)
    first = plane_place * per_device
    if sharers > 1:
        holder = lax.dynamic_slice_in_dim(wanted_slot % held // held_part, first, per_device)
        chosen = jnp.zeros_like(returned[:, 0])
        for t in range(sharers):
            chosen = jnp.where((holder == t)[None, :, None, None], returned[:, t], chosen)
    else:
        chosen = returned[:, 0]
    gathered = jnp.transpose(chosen, (1, 2, 0, 3)).reshape(per_device * SLOTS, H * HD)
    own_states = lax.dynamic_slice_in_dim(states, first * SLOTS, per_device * SLOTS, 0)
    own_lengths = lax.dynamic_slice_in_dim(lengths, first, per_device)
    summed = own_states.astype(jnp.float32) + jnp.dot(
        gathered, o_weight, preferred_element_type=jnp.float32
    )
    live_rows = (jnp.arange(SLOTS)[None, :] < own_lengths[:, None]).reshape(-1, 1)
    return (
        jnp.where(live_rows, summed, 0.0)
        .astype(jnp.bfloat16)
        .reshape(per_device, SLOTS, model)
    )


EXTRA = 16
SMEM = pl.BlockSpec(memory_space=pltpu.SMEM)
VMEM = pl.BlockSpec(memory_space=pltpu.VMEM)
HBM = pl.BlockSpec(memory_space=pltpu.HBM)


def split_heads_kernel(head_ref, cache_ref, *out_refs):
    for by, out_ref in enumerate(out_refs):
        for side in range(2):
            start = pl.multiple_of((head_ref[0] ^ by) * HD + side * KVH * HD, HD)
            out_ref[:, :, side * HD : (side + 1) * HD] = cache_ref[:, :, pl.ds(start, HD)]


def split_heads(head, cache):
    held, tokens, _ = cache.shape
    shape = jax.ShapeDtypeStruct((held, tokens, 2 * HD), cache.dtype)
    return pl.pallas_call(
        split_heads_kernel,
        in_specs=[SMEM, VMEM],
        out_specs=[VMEM] * KVH,
        out_shape=[shape] * KVH,
        cost_estimate=pl.CostEstimate(flops=0, bytes_accessed=2 * cache.size * 2, transcendentals=0),
        name="split_heads",
    )(head, cache)


def stack_kernel(*refs):
    in_refs, out_ref = refs[:-1], refs[-1]
    place = 0
    for in_ref in in_refs:
        count = in_ref.shape[0]
        out_ref[place : place + count] = in_ref[...]
        place += count


def stack(*arrays):
    total = sum(a.shape[0] for a in arrays)
    size = sum(a.size for a in arrays)
    return pl.pallas_call(
        stack_kernel,
        in_specs=[VMEM] * len(arrays),
        out_specs=VMEM,
        out_shape=jax.ShapeDtypeStruct((total,) + arrays[0].shape[1:], arrays[0].dtype),
        cost_estimate=pl.CostEstimate(flops=0, bytes_accessed=4 * size, transcendentals=0),
        name="stack",
    )(*arrays)


def project_kernel(index_ref, rows_ref, weight_ref, kept_ref, sent_ref):
    width = kept_ref.shape[1]
    partial_sum = jnp.dot(rows_ref[...], weight_ref[...], preferred_element_type=jnp.float32)
    low, high = partial_sum[:, :width], partial_sum[:, width:]
    is_low = index_ref[1] == 0
    kept_ref[...] = jnp.where(is_low, low, high)
    sent_ref[...] = jnp.where(is_low, high, low).astype(jnp.bfloat16)


def project(index, rows, weight):
    count, width = rows.shape[0], weight.shape[1] // 2
    return pl.pallas_call(
        project_kernel,
        in_specs=[SMEM, VMEM, VMEM],
        out_specs=[VMEM] * 2,
        out_shape=[
            jax.ShapeDtypeStruct((count, width), jnp.float32),
            jax.ShapeDtypeStruct((count, width), jnp.bfloat16),
        ],
        compiler_params=pltpu.CompilerParams(vmem_limit_bytes=32 << 20),
        cost_estimate=pl.CostEstimate(
            flops=2 * count * weight.size, bytes_accessed=2 * (rows.size + weight.size), transcendentals=0
        ),
        name="project",
    )(index, rows, weight)


def route_kernel(index_ref, kept_ref, came_ref, owner_ref, *out_refs,
                 slot_cap, per_plane):
    rows = kept_ref.shape[0]
    planes = len(out_refs)
    size = out_refs[0].shape[0]
    live = per_plane * slot_cap
    columns = (kept_ref[...] + came_ref[...].astype(jnp.float32)).astype(jnp.bfloat16)
    owner_row = owner_ref[...]
    above = lax.broadcasted_iota(jnp.int32, (rows, rows), 0)
    beside = lax.broadcasted_iota(jnp.int32, (rows, rows), 1)
    owner = jnp.sum(jnp.where(above == beside, owner_row, 0), axis=1, keepdims=True)
    earlier = jnp.sum(
        jnp.where((owner == owner_row) & (above < beside), 1.0, 0.0), axis=0, keepdims=True
    ).astype(jnp.int32)
    target = lax.div(owner_row, per_plane) ^ index_ref[0]
    code = target * size + lax.rem(owner_row, per_plane) * slot_cap + earlier
    place = lax.broadcasted_iota(jnp.int32, (planes * size, rows), 0)
    into = (place == code).astype(jnp.bfloat16)
    routed = jnp.dot(into, columns, preferred_element_type=jnp.float32).astype(jnp.bfloat16)
    lane = lax.broadcasted_iota(jnp.int32, (rows, HD), 1)
    named = (lane == owner).astype(jnp.bfloat16)
    counts = jnp.dot(
        jnp.ones((EXTRA, rows), jnp.bfloat16), named, preferred_element_type=jnp.float32
    ).astype(jnp.bfloat16)
    for k, out_ref in enumerate(out_refs):
        out_ref[:live] = routed[k * size : k * size + live]
        out_ref[live:] = jnp.zeros((EXTRA, out_ref.shape[1]), jnp.bfloat16)
        out_ref[live:, :HD] = counts


def route(index, kept, came, row_session, planes, per_plane, slot_cap):
    width = kept.shape[1]
    rows = row_session.shape[0]
    size = per_plane * slot_cap + EXTRA
    return pl.pallas_call(
        functools.partial(route_kernel, slot_cap=slot_cap, per_plane=per_plane),
        in_specs=[SMEM] + [VMEM] * 3,
        out_specs=[VMEM] * planes,
        out_shape=[jax.ShapeDtypeStruct((size, width), jnp.bfloat16)] * planes,
        cost_estimate=pl.CostEstimate(
            flops=2 * planes * size * rows * width, bytes_accessed=rows * width * 8, transcendentals=0
        ),
        name="route",
    )(index, kept, came, row_session.reshape(1, rows))


def head_weights_kernel(index_ref, q_ref, k_ref, v_ref, out_ref, sem):
    copies = []
    for i, (ref, heads, place) in enumerate(
        ((q_ref, PER_GROUP, 0), (k_ref, 1, PER_GROUP), (v_ref, 1, PER_GROUP + 1))
    ):
        start = pl.multiple_of(index_ref[3] * heads * HD, HD)
        copies.append(
            pltpu.make_async_copy(
                ref.at[:, pl.ds(start, heads * HD)],
                out_ref.at[:, place * HD : (place + heads) * HD],
                sem.at[i],
            )
        )
    for copy in copies:
        copy.start()
    for copy in copies:
        copy.wait()


def head_weights(index, q_weight, k_weight, v_weight):
    model, width = q_weight.shape[0], (PER_GROUP + 2) * HD
    return pl.pallas_call(
        head_weights_kernel,
        in_specs=[SMEM] + [HBM] * 3,
        out_specs=VMEM,
        out_shape=jax.ShapeDtypeStruct((model, width), q_weight.dtype),
        scratch_shapes=[pltpu.SemaphoreType.DMA((3,))],
        cost_estimate=pl.CostEstimate(
            flops=0, bytes_accessed=4 * model * width, transcendentals=0
        ),
        name="head_weights",
    )(index, q_weight, k_weight, v_weight)


def place_kernel(index_ref, near_ref, far_ref, near_core_ref, far_core_ref, gain_ref,
                 weight_ref, cos_ref, sin_ref, states_ref, query_ref, key_ref, value_ref, length_ref, *,
                 slot_cap, together):
    z, x, c, head = [index_ref[i] for i in range(4)]
    planes, live, width = near_ref.shape
    blocks = 2 * planes
    live = live - EXTRA
    per_plane = live // slot_cap
    steps = per_plane // together
    window = together * slot_cap
    total = together * SLOTS
    counts = jnp.concatenate(
        [ref[k, live : live + 1, :HD] for ref in (near_ref, near_core_ref) for k in range(planes)],
        axis=0,
    ).astype(jnp.float32)
    kind = lambda axis: lax.broadcasted_iota(jnp.int32, (blocks, blocks), axis)
    true_block = lambda k: (z ^ (k % planes)) * 2 + (c ^ (k // planes))
    before = (true_block(kind(1)) < true_block(kind(0))).astype(jnp.float32)
    offsets = jnp.dot(before, counts, preferred_element_type=jnp.float32)
    session_lane = lax.broadcasted_iota(jnp.int32, (HD, HD), 0)
    local_lane = lax.broadcasted_iota(jnp.int32, (HD, HD), 1)
    ours = (session_lane == z * per_plane + local_lane).astype(jnp.float32)
    sums = jnp.dot(
        jnp.broadcast_to(jnp.sum(counts, axis=0, keepdims=True), (8, HD)),
        ours,
        preferred_element_type=jnp.float32,
    )
    length_ref[...] = sums[:1].astype(jnp.int32)
    cosine = jnp.concatenate([cos_ref[...]] * together, axis=0)
    sine = jnp.concatenate([sin_ref[...]] * together, axis=0)
    gain = gain_ref[...].astype(jnp.float32)
    for step in range(steps):
        slot = lax.broadcasted_iota(jnp.int32, (blocks, blocks * window), 1)
        in_block = slot % window
        spread = lax.broadcasted_iota(jnp.int32, (HD, blocks * window), 1) % window // slot_cap
        from_lane = lax.broadcasted_iota(jnp.int32, (HD, blocks * window), 0)
        expand = (from_lane == z * per_plane + step * together + spread).astype(jnp.float32)
        here = jnp.dot(counts, expand, preferred_element_type=jnp.float32).astype(jnp.int32)
        start = jnp.dot(offsets, expand, preferred_element_type=jnp.float32).astype(jnp.int32)
        within = in_block % slot_cap
        row = jnp.where(within < here, start + within + in_block // slot_cap * SLOTS, -1)
        block = lax.broadcasted_iota(jnp.int32, (blocks, blocks * window), 0)
        code = jnp.max(jnp.where(slot // window == block, row, -1), axis=0, keepdims=True)
        place = lax.broadcasted_iota(jnp.int32, (total, blocks * window), 0)
        pick = (place == code).astype(jnp.bfloat16)
        slots = slice(step * window, (step + 1) * window)
        near, far = [
            jnp.dot(
                pick,
                jnp.concatenate(
                    [ref[k, slots] for ref in refs for k in range(planes)], axis=0
                ),
                preferred_element_type=jnp.float32,
            )
            for refs in ((near_ref, near_core_ref), (far_ref, far_core_ref))
        ]
        widened = jnp.concatenate(
            [jnp.where(x == 0, near, far), jnp.where(x == 0, far, near)], axis=1
        )
        rows = slice(step * total, (step + 1) * total)
        states_ref[rows] = widened.astype(jnp.bfloat16)
        factor = lax.rsqrt(jnp.mean(widened * widened, axis=-1, keepdims=True) + EPSILON)
        normed = (widened * factor * gain).astype(jnp.bfloat16)
        both = jnp.dot(normed, weight_ref[...], preferred_element_type=jnp.float32)
        for h in range(PER_GROUP + 1):
            vector = both[:, h * HD : (h + 1) * HD]
            turned = vector * cosine + pltpu.roll(vector, HD // 2, 1) * sine
            if h < PER_GROUP:
                query_ref[rows, h * HD : (h + 1) * HD] = turned.astype(jnp.bfloat16)
            else:
                key_ref[rows] = turned.astype(jnp.bfloat16)
        value_ref[rows] = both[:, (PER_GROUP + 1) * HD :].astype(jnp.bfloat16)


def place_rows(index, slots, gain, weight, sessions, slot_cap):
    together = 16 // math.gcd(16, slot_cap)
    cosine, sine = rope_tables(1)
    model = 2 * slots[0].shape[2]
    total = sessions * SLOTS
    out = lambda w: jax.ShapeDtypeStruct((total, w), jnp.bfloat16)
    return pl.pallas_call(
        functools.partial(place_kernel, slot_cap=slot_cap, together=together),
        in_specs=[SMEM] + [VMEM] * 8,
        out_specs=[VMEM] * 5,
        out_shape=[
            out(model), out(PER_GROUP * HD), out(HD), out(HD),
            jax.ShapeDtypeStruct((1, HD), jnp.int32),
        ],
        compiler_params=pltpu.CompilerParams(vmem_limit_bytes=32 << 20),
        cost_estimate=pl.CostEstimate(
            flops=4 * total * model * 5 * HD, bytes_accessed=6 << 20, transcendentals=0
        ),
        name="place_rows",
    )(index, *slots, gain.reshape(1, model), weight, jnp.asarray(cosine), jnp.asarray(sine))


def session_attention(query, key, value, tokens, length):
    scale = HD ** (-0.5) * math.log2(math.e)
    query = jnp.concatenate([query[:, h * HD : (h + 1) * HD] for h in range(PER_GROUP)], axis=0)
    ahead = lax.dot_general(query, tokens[:, :HD], NT, preferred_element_type=jnp.float32)
    own = lax.dot_general(query, key, NT, preferred_element_type=jnp.float32)
    row = lax.broadcasted_iota(jnp.int32, (SLOTS, SLOTS), 0)
    column = lax.broadcasted_iota(jnp.int32, (SLOTS, SLOTS), 1)
    allowed = (column <= row) & (column < length)
    own = jnp.where(jnp.concatenate([allowed] * PER_GROUP, axis=0), own, -1e30)
    highest = jnp.maximum(
        jnp.max(ahead, axis=-1, keepdims=True), jnp.max(own, axis=-1, keepdims=True)
    )
    powers = jnp.exp2((ahead - highest) * scale)
    own_powers = jnp.exp2((own - highest) * scale)
    total = jnp.sum(powers, axis=-1, keepdims=True) + jnp.sum(own_powers, axis=-1, keepdims=True)
    mixed = jnp.dot(
        powers.astype(jnp.bfloat16), tokens[:, HD:], preferred_element_type=jnp.float32
    ) + jnp.dot(own_powers.astype(jnp.bfloat16), value, preferred_element_type=jnp.float32)
    return (mixed / total).astype(jnp.bfloat16)


def fetches(hop, refs, held, kv, sem, hops, start):
    for which, source in enumerate(hops):
        copies = [
            pltpu.make_async_copy(refs[2 * which + chunk].at[:, held], kv.at[chunk], sem.at[chunk])
            for chunk in range(2)
        ]
        if start:
            @pl.when(hop == source)
            def _():
                for copy in copies:
                    copy.start()
        elif which == 0:
            for copy in copies:
                copy.wait()


def among(hop, hops):
    ours = hop == hops[0]
    for other in hops[1:]:
        ours = ours | (hop == other)
    return ours


def near_kernel(hop_ref, held_ref, length_ref, query_ref, key_ref, value_ref, *refs, hops):
    prompt_refs, (out_ref, kv, sem) = refs[: 2 * len(hops)], refs[2 * len(hops) :]
    sessions = hop_ref.shape[0]
    for start in (True, False):
        for i in range(sessions):
            hop = jnp.where(among(hop_ref[i], hops), hop_ref[i], 0)
            fetches(hop, prompt_refs, held_ref[i], kv.at[i], sem.at[i], hops, start)
    for i in range(sessions):
        rows = slice(i * SLOTS, (i + 1) * SLOTS)
        mixed = session_attention(
            query_ref[rows], key_ref[rows], value_ref[rows],
            kv[i].reshape(PROMPT, 2 * HD), length_ref[0, i],
        )
        for h in range(PER_GROUP):
            out_ref[rows, h * HD : (h + 1) * HD] = mixed[h * SLOTS : (h + 1) * SLOTS]


def far_kernel(index_ref, hop_ref, held_ref, length_ref, query_ref, key_ref, value_ref, near_ref,
               *refs, targets, hops):
    prompt_refs, refs = refs[: 2 * len(hops)], refs[2 * len(hops) :]
    out_refs, (kv, sem) = refs[: len(targets)], refs[len(targets) :]
    head = index_ref[3]
    per_device = out_refs[0].shape[0] // SLOTS
    places = [(t, j) for t in range(len(targets)) for j in range(per_device)]
    sessions = [(head ^ targets[t]) * per_device + j for t, j in places]
    for i, session in enumerate(sessions):
        fetches(
            hop_ref[session], prompt_refs, held_ref[session], kv.at[i], sem.at[i], hops, True
        )
    for i, (session, (t, j)) in enumerate(zip(sessions, places)):
        rows = pl.ds(pl.multiple_of(session * SLOTS, SLOTS), SLOTS)
        target = slice(j * SLOTS, (j + 1) * SLOTS)
        ours = among(hop_ref[session], hops)

        @pl.when(jnp.logical_not(ours))
        def _():
            out_refs[t][target] = near_ref[rows]

        @pl.when(ours)
        def _():
            fetches(
                hop_ref[session], prompt_refs, held_ref[session], kv.at[i], sem.at[i], hops, False
            )
            mixed = session_attention(
                query_ref[rows], key_ref[rows], value_ref[rows],
                kv[i].reshape(PROMPT, 2 * HD), length_ref[0, session],
            )
            for h in range(PER_GROUP):
                out_refs[t][target, h * HD : (h + 1) * HD] = mixed[h * SLOTS : (h + 1) * SLOTS]


def attention_call(kernel, out_specs, out_shape, places, name, scalars, arrays, prompts, hops):
    pieces = [piece for h in hops for piece in prompts[h]]
    work = places * PER_GROUP * SLOTS * (PROMPT + SLOTS) // 2
    return pl.pallas_call(
        kernel,
        in_specs=[SMEM] * len(scalars) + [VMEM] * len(arrays) + [HBM] * len(pieces),
        out_specs=out_specs,
        out_shape=out_shape,
        scratch_shapes=[
            pltpu.VMEM((places, 2, 2, PROMPT // 4, 2 * HD), jnp.bfloat16),
            pltpu.SemaphoreType.DMA((places, 2)),
        ],
        compiler_params=pltpu.CompilerParams(vmem_limit_bytes=32 << 20),
        cost_estimate=pl.CostEstimate(
            flops=4 * work * HD, bytes_accessed=places * PROMPT * 2 * HD, transcendentals=work
        ),
        name=name,
    )(*scalars, *arrays, *pieces)


def attend_near(hop, held, lengths, query, key, value, prompts, hops):
    out_shape = jax.ShapeDtypeStruct(query.shape, jnp.bfloat16)
    return attention_call(
        functools.partial(near_kernel, hops=hops),
        VMEM, out_shape, hop.shape[0], "near", (hop, held, lengths), (query, key, value),
        prompts, hops,
    )


def attend_far(index, hop, held, lengths, query, key, value, near, prompts, hops, targets):
    per_device = hop.shape[0] // KVH
    out_shape = jax.ShapeDtypeStruct((per_device * SLOTS, query.shape[1]), jnp.bfloat16)
    return attention_call(
        functools.partial(far_kernel, hops=hops, targets=targets),
        [VMEM] * len(targets), [out_shape] * len(targets), per_device * len(targets), "far",
        (index, hop, held, lengths), (query, key, value, near), prompts, hops,
    )


def output_kernel(index_ref, length_ref, states_ref, weight_ref, *refs):
    piece_refs, out_ref = refs[:-1], refs[-1]
    head = index_ref[3]
    group_width = PER_GROUP * HD
    per_device = out_ref.shape[0]
    total = per_device * SLOTS
    summed = states_ref[pl.ds(pl.multiple_of(head * total, SLOTS), total)].astype(jnp.float32)
    for by, piece_ref in enumerate(piece_refs):
        start = pl.multiple_of((head ^ by) * group_width, group_width)
        summed = summed + jnp.dot(
            piece_ref[...], weight_ref[pl.ds(start, group_width)], preferred_element_type=jnp.float32
        )
    row = lax.broadcasted_iota(jnp.int32, (SLOTS, 1), 0)
    for i in range(per_device):
        live = row < length_ref[0, head * per_device + i]
        part = summed[i * SLOTS : (i + 1) * SLOTS]
        out_ref[i] = jnp.where(live, part, 0.0).astype(jnp.bfloat16)


def output(index, lengths, states, o_weight, pieces, per_device):
    model = o_weight.shape[1]
    return pl.pallas_call(
        output_kernel,
        in_specs=[SMEM] * 2 + [VMEM] * (2 + len(pieces)),
        out_specs=VMEM,
        out_shape=jax.ShapeDtypeStruct((per_device, SLOTS, model), jnp.bfloat16),
        compiler_params=pltpu.CompilerParams(vmem_limit_bytes=32 << 20),
        cost_estimate=pl.CostEstimate(
            flops=2 * per_device * SLOTS * o_weight.size, bytes_accessed=o_weight.size * 2, transcendentals=0
        ),
        name="output",
    )(index, lengths, states, o_weight, *pieces)


def shifted(n, by):
    return [(i, i + by) for i in range(n) if 0 <= i + by < n]


def swapped(n, by):
    return [(i, i ^ by) for i in range(n)]


def line_body(
    thinker_rows,
    row_session,
    speaker_of,
    prompt_slot,
    prompt_cache,
    proj_weight,
    attn_gain,
    q_weight,
    k_weight,
    v_weight,
    o_weight,
):
    planes, plane, rep_count = lax.axis_size("sess"), KVH, 2
    blocks = planes * rep_count
    session_all = speaker_of.shape[0]
    per_plane = session_all // planes
    per_device = per_plane // plane
    slot_cap = SLOTS // blocks
    held = prompt_cache.shape[0]
    model = proj_weight.shape[1]
    width = model // 2
    z, x, c = lax.axis_index("sess"), lax.axis_index("inner"), lax.axis_index("rep")
    head = x * rep_count + c
    index = jnp.stack([z, x, c, head]).astype(jnp.int32)
    pair = ("inner", "rep")

    kept, sent = project(index, thinker_rows, proj_weight)
    came = lax.ppermute(sent, "inner", swapped(2, 1))

    own, to_core, to_x, to_far = split_heads(head.reshape(1), prompt_cache)
    from_core = lax.ppermute(to_core, pair, swapped(4, 1))
    from_x = lax.ppermute(to_x, pair, swapped(4, 2))
    from_far = lax.ppermute(to_far, pair, swapped(4, 3))
    first = stack(own[None], from_core[None])
    second = stack(from_x[None], from_far[None])

    weight = head_weights(index, q_weight, k_weight, v_weight)
    came, weight = lax.optimization_barrier((came, weight))
    routed = route(index, kept, came, row_session, planes, per_plane, slot_cap)
    first, _ = lax.optimization_barrier((first, sent))
    arrived = [routed[0]] + [
        lax.ppermute(routed[by], "sess", swapped(planes, by)) for by in range(1, planes)
    ]
    second, arrived = lax.optimization_barrier((second, arrived))
    right, left = [first, second], [first, second]
    prompts = {0: (first, second)}

    def travel(hop):
        for chunk in range(2):
            right[chunk] = lax.ppermute(right[chunk], "sess", shifted(planes, 1))
            left[chunk] = lax.ppermute(left[chunk], "sess", shifted(planes, -1))
        prompts[-hop], prompts[hop] = tuple(right), tuple(left)

    travel(1)
    travel(2)

    def after(value, hop, chunk):
        return lax.optimization_barrier((value, prompts[-hop][chunk], prompts[hop][chunk]))[0]

    arrived = stack(*[a[None] for a in arrived])
    other = lax.ppermute(arrived, "inner", swapped(2, 1))
    other = after(other, 1, 1)
    slots = (
        arrived, other, lax.ppermute(arrived, "rep", swapped(2, 1)), lax.ppermute(other, "rep", swapped(2, 1))
    )
    slots = after(slots, 2, 0)
    states, query, key, value, lengths = place_rows(
        index, slots, attn_gain, weight, per_plane, slot_cap
    )

    travel(3)

    speakers = lax.dynamic_slice_in_dim(speaker_of, z * per_plane, per_plane)
    wanted_slot = jnp.sum(
        jnp.where(
            speakers[:, None] == jnp.arange(prompt_slot.shape[0])[None, :], prompt_slot[None, :], 0
        ),
        axis=1,
    )
    hop = wanted_slot // held - z
    which = wanted_slot % held
    near = attend_near(
        hop, which, lengths, query, key, value, prompts, (0, -1, 1, -2, 2)
    )
    run = functools.partial(attend_far, index, hop, which, lengths)
    attended = {}
    attended[2], attended[3] = run(query, key, value, near, prompts, (-3, 3), (2, 3))
    near, _ = lax.optimization_barrier((near, attended[2]))
    attended[0], attended[1] = run(query, key, value, near, prompts, (-3, 3), (0, 1))
    pieces = [attended[0]] + [
        lax.ppermute(attended[by], pair, swapped(4, by)) for by in range(1, plane)
    ]
    return output(index, lengths, states, o_weight, pieces, per_device)


def solution(mesh):
    in_specs = (
        P(("groups", "sess", "rep"), "inner"),
        P(("groups", "sess", "rep"), None),
        P("groups"),
        P("groups"),
        P(("groups", "sess"), ("inner", "rep"), None),
        P("inner", None),
        P(),
        P(),
        P(),
        P(),
        P(),
    )
    out_specs = P(("groups", "sess", "inner", "rep"), None, None)
    sizes = tuple(mesh.shape[name] for name in ("sess", "inner", "rep"))
    body = line_body if sizes == (4, 2, 2) else general_body
    return jax.shard_map(body, mesh=mesh, in_specs=in_specs, out_specs=out_specs, check_vma=False)
```

```python
import functools
import math

import jax
import jax.numpy as jnp
import numpy as np
from jax import lax
from jax.experimental import pallas as pl
from jax.experimental.pallas import tpu as pltpu
from jax.sharding import PartitionSpec as P

H = 12
KVH = 4
HD = 128
PROMPT = 1024
SLOTS = 96
PER_GROUP = H // KVH

EPSILON = 1e-06
ROPE_BASE = 1000000.0
NT = (((1,), (1,)), ((), ()))


def rope_tables(copies):
    half_width = HD // 2
    inverse = ROPE_BASE ** (-(np.arange(half_width, dtype=np.float64) * 2.0) / HD)
    angles = (PROMPT + np.arange(SLOTS, dtype=np.float64))[:, None] * inverse[None, :]
    cosine = np.concatenate([np.cos(angles), np.cos(angles)], axis=1)
    sine = np.concatenate([-np.sin(angles), np.sin(angles)], axis=1)
    return (
        np.tile(cosine, (copies, 1)).astype(np.float32),
        np.tile(sine, (copies, 1)).astype(np.float32),
    )


def states_kernel(code_ref, slots_ref, gain_ref, weight_ref, cos_ref, sin_ref,
                  states_ref, query_ref, key_ref, value_ref):
    halves, blocks, rows, width = slots_ref.shape
    total = states_ref.shape[0]
    place = lax.broadcasted_iota(jnp.int32, (total, blocks * rows), 0)
    pick = (place == code_ref[0]).astype(jnp.bfloat16)
    parts = [
        jnp.dot(
            pick,
            slots_ref[half].reshape(blocks * rows, width),
            preferred_element_type=jnp.float32,
        )
        for half in range(halves)
    ]
    widened = jnp.concatenate(parts, axis=1)
    states_ref[...] = widened.astype(jnp.bfloat16)
    factor = lax.rsqrt(jnp.mean(widened * widened, axis=-1, keepdims=True) + EPSILON)
    normed = (widened * factor * gain_ref[...].astype(jnp.float32)).astype(jnp.bfloat16)
    both = jnp.dot(normed, weight_ref[...], preferred_element_type=jnp.float32)
    cosine, sine = cos_ref[...], sin_ref[...]
    for head in range(PER_GROUP + 1):
        vector = both[:, head * HD : (head + 1) * HD]
        turned = vector * cosine + pltpu.roll(vector, HD // 2, 1) * sine
        if head < PER_GROUP:
            query_ref[:, head * HD : (head + 1) * HD] = turned.astype(jnp.bfloat16)
        else:
            key_ref[...] = turned.astype(jnp.bfloat16)
    value_ref[...] = both[:, (PER_GROUP + 1) * HD :].astype(jnp.bfloat16)


def attention_kernel(place_ref, length_ref, query_ref, key_ref, value_ref, prompt_ref, out_ref):
    session = pl.program_id(0)
    length = length_ref[session]
    scale = HD ** (-0.5) * math.log2(math.e)
    query = jnp.concatenate(
        [query_ref[:, h * HD : (h + 1) * HD] for h in range(PER_GROUP)], axis=0
    )
    ahead = lax.dot_general(query, prompt_ref[0, :, :HD], NT, preferred_element_type=jnp.float32)
    own = lax.dot_general(query, key_ref[...], NT, preferred_element_type=jnp.float32)
    row = lax.broadcasted_iota(jnp.int32, (SLOTS, SLOTS), 0)
    column = lax.broadcasted_iota(jnp.int32, (SLOTS, SLOTS), 1)
    allowed = (column <= row) & (column < length)
    own = jnp.where(jnp.concatenate([allowed] * PER_GROUP, axis=0), own, -1e30)
    highest = jnp.maximum(
        jnp.max(ahead, axis=-1, keepdims=True), jnp.max(own, axis=-1, keepdims=True)
    )
    powers = jnp.exp2((ahead - highest) * scale)
    own_powers = jnp.exp2((own - highest) * scale)
    total = jnp.sum(powers, axis=-1, keepdims=True) + jnp.sum(own_powers, axis=-1, keepdims=True)
    mixed = jnp.dot(
        powers.astype(jnp.bfloat16), prompt_ref[0, :, HD:], preferred_element_type=jnp.float32
    ) + jnp.dot(own_powers.astype(jnp.bfloat16), value_ref[...], preferred_element_type=jnp.float32)
    mixed = (mixed / total).astype(jnp.bfloat16)
    for h in range(PER_GROUP):
        out_ref[:, h * HD : (h + 1) * HD] = mixed[h * SLOTS : (h + 1) * SLOTS]


def make_states(code, slots, gain, weight, sessions, together):
    halves, blocks, rows, width = slots.shape
    steps = sessions // together
    model = halves * width
    cosine, sine = rope_tables(together)
    total = together * SLOTS
    out = jax.ShapeDtypeStruct
    row_spec = lambda w: pl.BlockSpec((total, w), lambda i: (i, 0))
    whole = lambda a: pl.BlockSpec(a.shape, lambda i: (0,) * a.ndim)
    gain = gain.reshape(1, model)
    return pl.pallas_call(
        states_kernel,
        grid=(steps,),
        in_specs=[
            pl.BlockSpec((1, 1, code.shape[2]), lambda i: (i, 0, 0)),
            pl.BlockSpec((halves, blocks, rows // steps, width), lambda i: (0, 0, i, 0)),
            whole(gain),
            whole(weight),
            whole(cosine),
            whole(sine),
        ],
        out_specs=[row_spec(model), row_spec(PER_GROUP * HD), row_spec(HD), row_spec(HD)],
        out_shape=[
            out((sessions * SLOTS, model), jnp.bfloat16),
            out((sessions * SLOTS, PER_GROUP * HD), jnp.bfloat16),
            out((sessions * SLOTS, HD), jnp.bfloat16),
            out((sessions * SLOTS, HD), jnp.bfloat16),
        ],
        compiler_params=pltpu.CompilerParams(vmem_limit_bytes=32 << 20),
        name="states",
    )(code, slots, gain, weight, jnp.asarray(cosine), jnp.asarray(sine))


def attend(place, lengths, query, key, value, prompts):
    sessions = place.shape[0]
    row_spec = lambda w: pl.BlockSpec((SLOTS, w), lambda i, place, length: (i, 0))
    return pl.pallas_call(
        attention_kernel,
        grid_spec=pltpu.PrefetchScalarGridSpec(
            num_scalar_prefetch=2,
            grid=(sessions,),
            in_specs=[
                row_spec(PER_GROUP * HD),
                row_spec(HD),
                row_spec(HD),
                pl.BlockSpec((1, PROMPT, 2 * HD), lambda i, place, length: (place[i], 0, 0)),
            ],
            out_specs=row_spec(PER_GROUP * HD),
        ),
        out_shape=jax.ShapeDtypeStruct((sessions * SLOTS, PER_GROUP * HD), jnp.bfloat16),
        compiler_params=pltpu.CompilerParams(vmem_limit_bytes=32 << 20),
        name="attend",
    )(place, lengths, query, key, value, prompts)


def general_body(
    thinker_rows,
    row_session,
    speaker_of,
    prompt_slot,
    prompt_cache,
    proj_weight,
    attn_gain,
    q_weight,
    k_weight,
    v_weight,
    o_weight,
):
    sess_count = lax.axis_size("sess")
    inner_count = lax.axis_size("inner")
    rep_count = lax.axis_size("rep")
    plane = inner_count * rep_count
    blocks = sess_count * rep_count
    session_all = speaker_of.shape[0]
    per_plane = session_all // sess_count
    per_device = per_plane // plane
    slot_cap = SLOTS // blocks
    held, tokens, channels = prompt_cache.shape
    model = proj_weight.shape[1]
    sharers = plane // KVH
    held_part = held // sharers
    sess_place = lax.axis_index("sess")
    plane_place = lax.axis_index("inner") * rep_count + lax.axis_index("rep")
    head = plane_place // sharers
    sharer = plane_place % sharers

    outgoing = jnp.transpose(
        prompt_cache.reshape(sharers, held_part, tokens, 2, KVH, HD), (4, 0, 1, 2, 3, 5)
    ).reshape(plane, held_part, tokens, 2 * HD)
    own_head = lax.all_to_all(outgoing, ("inner", "rep"), split_axis=0, concat_axis=2, tiled=True)
    own_head = own_head.reshape(held_part, plane * tokens, 2 * HD)
    prompts = lax.all_gather(own_head, "sess", axis=0, tiled=True)

    row_owner = row_session[:, 0]
    order = jnp.arange(row_owner.shape[0])
    same = row_owner[:, None] == row_owner[None, :]
    earlier = jnp.sum((same & (order[None, :] < order[:, None])).astype(jnp.int32), axis=1)
    row_slot = row_owner * slot_cap + earlier
    counts = jnp.sum(
        (row_owner[:, None] == jnp.arange(session_all)[None, :]).astype(jnp.int32), axis=0
    )
    all_counts = lax.all_gather(counts, ("sess", "rep"), axis=0, tiled=False)

    partial_sum = jnp.dot(thinker_rows, proj_weight, preferred_element_type=jnp.float32)
    width = model // inner_count
    if inner_count == 2:
        inner_place = lax.axis_index("inner")
        kept = lax.dynamic_slice_in_dim(partial_sum, inner_place * width, width, 1)
        sent = lax.dynamic_slice_in_dim(partial_sum, (1 - inner_place) * width, width, 1)
        came = lax.ppermute(sent.astype(jnp.bfloat16), "inner", [(0, 1), (1, 0)])
        own_columns = (kept + came.astype(jnp.float32)).astype(jnp.bfloat16)
    else:
        own_columns = lax.psum_scatter(
            partial_sum, "inner", scatter_dimension=1, tiled=True
        ).astype(jnp.bfloat16)
    into = (jnp.arange(session_all * slot_cap)[:, None] == row_slot[None, :]).astype(jnp.bfloat16)
    buffer = jnp.dot(into, own_columns, preferred_element_type=jnp.float32).astype(jnp.bfloat16)
    arrived = lax.all_to_all(
        buffer.reshape(sess_count, per_plane * slot_cap, width),
        "sess",
        split_axis=0,
        concat_axis=0,
        tiled=True,
    )
    spread = lax.all_gather(arrived, ("inner", "rep"), axis=0, tiled=False)
    slots = spread.reshape(inner_count, rep_count * sess_count, per_plane * slot_cap, width)

    offsets = jnp.cumsum(all_counts, axis=0) - all_counts
    lengths_all = jnp.sum(all_counts, axis=0)
    mine = lambda a: lax.dynamic_slice_in_dim(a, sess_place * per_plane, per_plane, a.ndim - 1)
    by_block = lambda a: jnp.transpose(
        mine(a).reshape(sess_count, rep_count, per_plane), (1, 0, 2)
    ).reshape(blocks, per_plane)
    lengths = mine(lengths_all)
    together = 16 // math.gcd(16, slot_cap)
    within = jnp.arange(slot_cap)
    local = (jnp.arange(per_plane) % together)[None, :, None] * SLOTS
    code = jnp.where(
        within[None, None, :] < by_block(all_counts)[:, :, None],
        by_block(offsets)[:, :, None] + within[None, None, :] + local,
        -1,
    )
    steps = per_plane // together
    code = jnp.transpose(
        code.reshape(blocks, steps, together * slot_cap), (1, 0, 2)
    ).reshape(steps, 1, blocks * together * slot_cap)

    group_width = PER_GROUP * HD
    weight = jnp.concatenate(
        [
            lax.dynamic_slice_in_dim(q_weight, head * group_width, group_width, 1),
            lax.dynamic_slice_in_dim(k_weight, head * HD, HD, 1),
            lax.dynamic_slice_in_dim(v_weight, head * HD, HD, 1),
        ],
        axis=1,
    )
    states, query, key, value = make_states(
        code, slots, attn_gain, weight, per_plane, together
    )

    wanted_slot = jnp.sum(
        jnp.where(
            mine(speaker_of)[:, None] == jnp.arange(prompt_slot.shape[0])[None, :],
            prompt_slot[None, :],
            0,
        ),
        axis=1,
    )
    place = wanted_slot // held * held_part + wanted_slot % held_part
    attended = attend(place, lengths, query, key, value, prompts)
    returned = lax.all_to_all(
        attended.reshape(plane, per_device * SLOTS, group_width),
        ("inner", "rep"),
        split_axis=0,
        concat_axis=0,
        tiled=True,
    ).reshape(KVH, sharers, per_device, SLOTS, group_width)
    first = plane_place * per_device
    if sharers > 1:
        holder = lax.dynamic_slice_in_dim(wanted_slot % held // held_part, first, per_device)
        chosen = jnp.zeros_like(returned[:, 0])
        for t in range(sharers):
            chosen = jnp.where((holder == t)[None, :, None, None], returned[:, t], chosen)
    else:
        chosen = returned[:, 0]
    gathered = jnp.transpose(chosen, (1, 2, 0, 3)).reshape(per_device * SLOTS, H * HD)
    own_states = lax.dynamic_slice_in_dim(states, first * SLOTS, per_device * SLOTS, 0)
    own_lengths = lax.dynamic_slice_in_dim(lengths, first, per_device)
    summed = own_states.astype(jnp.float32) + jnp.dot(
        gathered, o_weight, preferred_element_type=jnp.float32
    )
    live_rows = (jnp.arange(SLOTS)[None, :] < own_lengths[:, None]).reshape(-1, 1)
    return (
        jnp.where(live_rows, summed, 0.0)
        .astype(jnp.bfloat16)
        .reshape(per_device, SLOTS, model)
    )


EXTRA = 16
SMEM = pl.BlockSpec(memory_space=pltpu.SMEM)
VMEM = pl.BlockSpec(memory_space=pltpu.VMEM)
HBM = pl.BlockSpec(memory_space=pltpu.HBM)


def split_heads_kernel(head_ref, cache_ref, *out_refs):
    for by, out_ref in enumerate(out_refs):
        for side in range(2):
            start = pl.multiple_of((head_ref[0] ^ by) * HD + side * KVH * HD, HD)
            out_ref[:, :, side * HD : (side + 1) * HD] = cache_ref[:, :, pl.ds(start, HD)]


def split_heads(head, cache):
    held, tokens, _ = cache.shape
    shape = jax.ShapeDtypeStruct((held, tokens, 2 * HD), cache.dtype)
    return pl.pallas_call(
        split_heads_kernel,
        in_specs=[SMEM, VMEM],
        out_specs=[VMEM] * KVH,
        out_shape=[shape] * KVH,
        cost_estimate=pl.CostEstimate(flops=0, bytes_accessed=2 * cache.size * 2, transcendentals=0),
        name="split_heads",
    )(head, cache)


def stack_kernel(*refs):
    in_refs, out_ref = refs[:-1], refs[-1]
    place = 0
    for in_ref in in_refs:
        count = in_ref.shape[0]
        out_ref[place : place + count] = in_ref[...]
        place += count


def stack(*arrays):
    total = sum(a.shape[0] for a in arrays)
    size = sum(a.size for a in arrays)
    return pl.pallas_call(
        stack_kernel,
        in_specs=[VMEM] * len(arrays),
        out_specs=VMEM,
        out_shape=jax.ShapeDtypeStruct((total,) + arrays[0].shape[1:], arrays[0].dtype),
        cost_estimate=pl.CostEstimate(flops=0, bytes_accessed=4 * size, transcendentals=0),
        name="stack",
    )(*arrays)


def project_kernel(index_ref, rows_ref, weight_ref, kept_ref, sent_ref):
    width = kept_ref.shape[1]
    partial_sum = jnp.dot(rows_ref[...], weight_ref[...], preferred_element_type=jnp.float32)
    low, high = partial_sum[:, :width], partial_sum[:, width:]
    is_low = index_ref[1] == 0
    kept_ref[...] = jnp.where(is_low, low, high)
    sent_ref[...] = jnp.where(is_low, high, low).astype(jnp.bfloat16)


def project(index, rows, weight):
    count, width = rows.shape[0], weight.shape[1] // 2
    return pl.pallas_call(
        project_kernel,
        in_specs=[SMEM, VMEM, VMEM],
        out_specs=[VMEM] * 2,
        out_shape=[
            jax.ShapeDtypeStruct((count, width), jnp.float32),
            jax.ShapeDtypeStruct((count, width), jnp.bfloat16),
        ],
        compiler_params=pltpu.CompilerParams(vmem_limit_bytes=32 << 20),
        cost_estimate=pl.CostEstimate(
            flops=2 * count * weight.size, bytes_accessed=2 * (rows.size + weight.size), transcendentals=0
        ),
        name="project",
    )(index, rows, weight)


def route_kernel(index_ref, kept_ref, came_ref, owner_ref, *out_refs,
                 slot_cap, per_plane):
    rows = kept_ref.shape[0]
    planes = len(out_refs)
    size = out_refs[0].shape[0]
    live = per_plane * slot_cap
    columns = (kept_ref[...] + came_ref[...].astype(jnp.float32)).astype(jnp.bfloat16)
    owner_row = owner_ref[...]
    above = lax.broadcasted_iota(jnp.int32, (rows, rows), 0)
    beside = lax.broadcasted_iota(jnp.int32, (rows, rows), 1)
    owner = jnp.sum(jnp.where(above == beside, owner_row, 0), axis=1, keepdims=True)
    earlier = jnp.sum(
        jnp.where((owner == owner_row) & (above < beside), 1.0, 0.0), axis=0, keepdims=True
    ).astype(jnp.int32)
    target = lax.div(owner_row, per_plane) ^ index_ref[0]
    code = target * size + lax.rem(owner_row, per_plane) * slot_cap + earlier
    place = lax.broadcasted_iota(jnp.int32, (planes * size, rows), 0)
    into = (place == code).astype(jnp.bfloat16)
    routed = jnp.dot(into, columns, preferred_element_type=jnp.float32).astype(jnp.bfloat16)
    lane = lax.broadcasted_iota(jnp.int32, (rows, HD), 1)
    named = (lane == owner).astype(jnp.bfloat16)
    counts = jnp.dot(
        jnp.ones((EXTRA, rows), jnp.bfloat16), named, preferred_element_type=jnp.float32
    ).astype(jnp.bfloat16)
    for k, out_ref in enumerate(out_refs):
        out_ref[:live] = routed[k * size : k * size + live]
        out_ref[live:] = jnp.zeros((EXTRA, out_ref.shape[1]), jnp.bfloat16)
        out_ref[live:, :HD] = counts


def route(index, kept, came, row_session, planes, per_plane, slot_cap):
    width = kept.shape[1]
    rows = row_session.shape[0]
    size = per_plane * slot_cap + EXTRA
    return pl.pallas_call(
        functools.partial(route_kernel, slot_cap=slot_cap, per_plane=per_plane),
        in_specs=[SMEM] + [VMEM] * 3,
        out_specs=[VMEM] * planes,
        out_shape=[jax.ShapeDtypeStruct((size, width), jnp.bfloat16)] * planes,
        cost_estimate=pl.CostEstimate(
            flops=2 * planes * size * rows * width, bytes_accessed=rows * width * 8, transcendentals=0
        ),
        name="route",
    )(index, kept, came, row_session.reshape(1, rows))


def head_weights_kernel(index_ref, q_ref, k_ref, v_ref, out_ref, sem):
    copies = []
    for i, (ref, heads, place) in enumerate(
        ((q_ref, PER_GROUP, 0), (k_ref, 1, PER_GROUP), (v_ref, 1, PER_GROUP + 1))
    ):
        start = pl.multiple_of(index_ref[3] * heads * HD, HD)
        copies.append(
            pltpu.make_async_copy(
                ref.at[:, pl.ds(start, heads * HD)],
                out_ref.at[:, place * HD : (place + heads) * HD],
                sem.at[i],
            )
        )
    for copy in copies:
        copy.start()
    for copy in copies:
        copy.wait()


def head_weights(index, q_weight, k_weight, v_weight):
    model, width = q_weight.shape[0], (PER_GROUP + 2) * HD
    return pl.pallas_call(
        head_weights_kernel,
        in_specs=[SMEM] + [HBM] * 3,
        out_specs=VMEM,
        out_shape=jax.ShapeDtypeStruct((model, width), q_weight.dtype),
        scratch_shapes=[pltpu.SemaphoreType.DMA((3,))],
        cost_estimate=pl.CostEstimate(
            flops=0, bytes_accessed=4 * model * width, transcendentals=0
        ),
        name="head_weights",
    )(index, q_weight, k_weight, v_weight)


def place_kernel(index_ref, near_ref, far_ref, near_core_ref, far_core_ref, gain_ref,
                 weight_ref, cos_ref, sin_ref, states_ref, query_ref, key_ref, value_ref, length_ref, *,
                 slot_cap, together):
    z, x, c, head = [index_ref[i] for i in range(4)]
    planes, live, width = near_ref.shape
    blocks = 2 * planes
    live = live - EXTRA
    per_plane = live // slot_cap
    steps = per_plane // together
    window = together * slot_cap
    total = together * SLOTS
    counts = jnp.concatenate(
        [ref[k, live : live + 1, :HD] for ref in (near_ref, near_core_ref) for k in range(planes)],
        axis=0,
    ).astype(jnp.float32)
    kind = lambda axis: lax.broadcasted_iota(jnp.int32, (blocks, blocks), axis)
    true_block = lambda k: (z ^ (k % planes)) * 2 + (c ^ (k // planes))
    before = (true_block(kind(1)) < true_block(kind(0))).astype(jnp.float32)
    offsets = jnp.dot(before, counts, preferred_element_type=jnp.float32)
    session_lane = lax.broadcasted_iota(jnp.int32, (HD, HD), 0)
    local_lane = lax.broadcasted_iota(jnp.int32, (HD, HD), 1)
    ours = (session_lane == z * per_plane + local_lane).astype(jnp.float32)
    sums = jnp.dot(
        jnp.broadcast_to(jnp.sum(counts, axis=0, keepdims=True), (8, HD)),
        ours,
        preferred_element_type=jnp.float32,
    )
    length_ref[...] = sums[:1].astype(jnp.int32)
    cosine = jnp.concatenate([cos_ref[...]] * together, axis=0)
    sine = jnp.concatenate([sin_ref[...]] * together, axis=0)
    gain = gain_ref[...].astype(jnp.float32)
    for step in range(steps):
        slot = lax.broadcasted_iota(jnp.int32, (blocks, blocks * window), 1)
        in_block = slot % window
        spread = lax.broadcasted_iota(jnp.int32, (HD, blocks * window), 1) % window // slot_cap
        from_lane = lax.broadcasted_iota(jnp.int32, (HD, blocks * window), 0)
        expand = (from_lane == z * per_plane + step * together + spread).astype(jnp.float32)
        here = jnp.dot(counts, expand, preferred_element_type=jnp.float32).astype(jnp.int32)
        start = jnp.dot(offsets, expand, preferred_element_type=jnp.float32).astype(jnp.int32)
        within = in_block % slot_cap
        row = jnp.where(within < here, start + within + in_block // slot_cap * SLOTS, -1)
        block = lax.broadcasted_iota(jnp.int32, (blocks, blocks * window), 0)
        code = jnp.max(jnp.where(slot // window == block, row, -1), axis=0, keepdims=True)
        place = lax.broadcasted_iota(jnp.int32, (total, blocks * window), 0)
        pick = (place == code).astype(jnp.bfloat16)
        slots = slice(step * window, (step + 1) * window)
        near, far = [
            jnp.dot(
                pick,
                jnp.concatenate(
                    [ref[k, slots] for ref in refs for k in range(planes)], axis=0
                ),
                preferred_element_type=jnp.float32,
            )
            for refs in ((near_ref, near_core_ref), (far_ref, far_core_ref))
        ]
        widened = jnp.concatenate(
            [jnp.where(x == 0, near, far), jnp.where(x == 0, far, near)], axis=1
        )
        rows = slice(step * total, (step + 1) * total)
        states_ref[rows] = widened.astype(jnp.bfloat16)
        factor = lax.rsqrt(jnp.mean(widened * widened, axis=-1, keepdims=True) + EPSILON)
        normed = (widened * factor * gain).astype(jnp.bfloat16)
        both = jnp.dot(normed, weight_ref[...], preferred_element_type=jnp.float32)
        for h in range(PER_GROUP + 1):
            vector = both[:, h * HD : (h + 1) * HD]
            turned = vector * cosine + pltpu.roll(vector, HD // 2, 1) * sine
            if h < PER_GROUP:
                query_ref[rows, h * HD : (h + 1) * HD] = turned.astype(jnp.bfloat16)
            else:
                key_ref[rows] = turned.astype(jnp.bfloat16)
        value_ref[rows] = both[:, (PER_GROUP + 1) * HD :].astype(jnp.bfloat16)


def place_rows(index, slots, gain, weight, sessions, slot_cap):
    together = 16 // math.gcd(16, slot_cap)
    cosine, sine = rope_tables(1)
    model = 2 * slots[0].shape[2]
    total = sessions * SLOTS
    out = lambda w: jax.ShapeDtypeStruct((total, w), jnp.bfloat16)
    return pl.pallas_call(
        functools.partial(place_kernel, slot_cap=slot_cap, together=together),
        in_specs=[SMEM] + [VMEM] * 8,
        out_specs=[VMEM] * 5,
        out_shape=[
            out(model), out(PER_GROUP * HD), out(HD), out(HD),
            jax.ShapeDtypeStruct((1, HD), jnp.int32),
        ],
        compiler_params=pltpu.CompilerParams(vmem_limit_bytes=32 << 20),
        cost_estimate=pl.CostEstimate(
            flops=4 * total * model * 5 * HD, bytes_accessed=6 << 20, transcendentals=0
        ),
        name="place_rows",
    )(index, *slots, gain.reshape(1, model), weight, jnp.asarray(cosine), jnp.asarray(sine))


def session_attention(query, key, value, tokens, length):
    scale = HD ** (-0.5) * math.log2(math.e)
    query = jnp.concatenate([query[:, h * HD : (h + 1) * HD] for h in range(PER_GROUP)], axis=0)
    ahead = lax.dot_general(query, tokens[:, :HD], NT, preferred_element_type=jnp.float32)
    own = lax.dot_general(query, key, NT, preferred_element_type=jnp.float32)
    row = lax.broadcasted_iota(jnp.int32, (SLOTS, SLOTS), 0)
    column = lax.broadcasted_iota(jnp.int32, (SLOTS, SLOTS), 1)
    allowed = (column <= row) & (column < length)
    own = jnp.where(jnp.concatenate([allowed] * PER_GROUP, axis=0), own, -1e30)
    highest = jnp.maximum(
        jnp.max(ahead, axis=-1, keepdims=True), jnp.max(own, axis=-1, keepdims=True)
    )
    powers = jnp.exp2((ahead - highest) * scale)
    own_powers = jnp.exp2((own - highest) * scale)
    total = jnp.sum(powers, axis=-1, keepdims=True) + jnp.sum(own_powers, axis=-1, keepdims=True)
    mixed = jnp.dot(
        powers.astype(jnp.bfloat16), tokens[:, HD:], preferred_element_type=jnp.float32
    ) + jnp.dot(own_powers.astype(jnp.bfloat16), value, preferred_element_type=jnp.float32)
    return (mixed / total).astype(jnp.bfloat16)


def fetches(hop, refs, held, kv, sem, hops, start):
    for which, source in enumerate(hops):
        copies = [
            pltpu.make_async_copy(refs[2 * which + chunk].at[:, held], kv.at[chunk], sem.at[chunk])
            for chunk in range(2)
        ]
        if start:
            @pl.when(hop == source)
            def _():
                for copy in copies:
                    copy.start()
        elif which == 0:
            for copy in copies:
                copy.wait()


def among(hop, hops):
    ours = hop == hops[0]
    for other in hops[1:]:
        ours = ours | (hop == other)
    return ours


def near_kernel(hop_ref, held_ref, length_ref, query_ref, key_ref, value_ref, *refs, hops):
    prompt_refs, (out_ref, kv, sem) = refs[: 2 * len(hops)], refs[2 * len(hops) :]
    sessions = hop_ref.shape[0]
    for i in range(sessions):
        fetches(hop_ref[i], prompt_refs, held_ref[i], kv.at[i], sem.at[i], hops, True)

    def work(i, _):
        @pl.when(among(hop_ref[i], hops))
        def _():
            fetches(hop_ref[i], prompt_refs, held_ref[i], kv.at[i], sem.at[i], hops, False)
            rows = pl.ds(pl.multiple_of(i * SLOTS, SLOTS), SLOTS)
            mixed = session_attention(
                query_ref[rows], key_ref[rows], value_ref[rows],
                kv[i].reshape(PROMPT, 2 * HD), length_ref[0, i],
            )
            for h in range(PER_GROUP):
                out_ref[rows, h * HD : (h + 1) * HD] = mixed[h * SLOTS : (h + 1) * SLOTS]

        return 0

    lax.fori_loop(0, sessions, work, 0)


def far_kernel(index_ref, hop_ref, held_ref, length_ref, query_ref, key_ref, value_ref, near_ref,
               *refs, targets, hops):
    prompt_refs, refs = refs[: 2 * len(hops)], refs[2 * len(hops) :]
    out_refs, (kv, sem) = refs[: len(targets)], refs[len(targets) :]
    head = index_ref[3]
    per_device = out_refs[0].shape[0] // SLOTS
    places = [(t, j) for t in range(len(targets)) for j in range(per_device)]
    sessions = [(head ^ targets[t]) * per_device + j for t, j in places]
    for i, session in enumerate(sessions):
        fetches(
            hop_ref[session], prompt_refs, held_ref[session], kv.at[i], sem.at[i], hops, True
        )
    for i, (session, (t, j)) in enumerate(zip(sessions, places)):
        rows = pl.ds(pl.multiple_of(session * SLOTS, SLOTS), SLOTS)
        target = slice(j * SLOTS, (j + 1) * SLOTS)
        ours = among(hop_ref[session], hops)

        @pl.when(jnp.logical_not(ours))
        def _():
            out_refs[t][target] = near_ref[rows]

        @pl.when(ours)
        def _():
            fetches(
                hop_ref[session], prompt_refs, held_ref[session], kv.at[i], sem.at[i], hops, False
            )
            mixed = session_attention(
                query_ref[rows], key_ref[rows], value_ref[rows],
                kv[i].reshape(PROMPT, 2 * HD), length_ref[0, session],
            )
            for h in range(PER_GROUP):
                out_refs[t][target, h * HD : (h + 1) * HD] = mixed[h * SLOTS : (h + 1) * SLOTS]


def attention_call(kernel, out_specs, out_shape, places, name, scalars, arrays, prompts, hops):
    pieces = [piece for h in hops for piece in prompts[h]]
    work = places * PER_GROUP * SLOTS * (PROMPT + SLOTS) // 2
    return pl.pallas_call(
        kernel,
        in_specs=[SMEM] * len(scalars) + [VMEM] * len(arrays) + [HBM] * len(pieces),
        out_specs=out_specs,
        out_shape=out_shape,
        scratch_shapes=[
            pltpu.VMEM((places, 2, 2, PROMPT // 4, 2 * HD), jnp.bfloat16),
            pltpu.SemaphoreType.DMA((places, 2)),
        ],
        compiler_params=pltpu.CompilerParams(vmem_limit_bytes=32 << 20),
        cost_estimate=pl.CostEstimate(
            flops=4 * work * HD, bytes_accessed=places * PROMPT * 2 * HD, transcendentals=work
        ),
        name=name,
    )(*scalars, *arrays, *pieces)


def attend_near(hop, held, lengths, query, key, value, prompts, hops):
    out_shape = jax.ShapeDtypeStruct(query.shape, jnp.bfloat16)
    return attention_call(
        functools.partial(near_kernel, hops=hops),
        VMEM, out_shape, hop.shape[0], "near", (hop, held, lengths), (query, key, value),
        prompts, hops,
    )


def attend_far(index, hop, held, lengths, query, key, value, near, prompts, hops, targets):
    per_device = hop.shape[0] // KVH
    out_shape = jax.ShapeDtypeStruct((per_device * SLOTS, query.shape[1]), jnp.bfloat16)
    return attention_call(
        functools.partial(far_kernel, hops=hops, targets=targets),
        [VMEM] * len(targets), [out_shape] * len(targets), per_device * len(targets), "far",
        (index, hop, held, lengths), (query, key, value, near), prompts, hops,
    )


def output_kernel(index_ref, length_ref, states_ref, weight_ref, *refs):
    piece_refs, out_ref = refs[:-1], refs[-1]
    head = index_ref[3]
    group_width = PER_GROUP * HD
    per_device = out_ref.shape[0]
    total = per_device * SLOTS
    summed = states_ref[pl.ds(pl.multiple_of(head * total, SLOTS), total)].astype(jnp.float32)
    for by, piece_ref in enumerate(piece_refs):
        start = pl.multiple_of((head ^ by) * group_width, group_width)
        summed = summed + jnp.dot(
            piece_ref[...], weight_ref[pl.ds(start, group_width)], preferred_element_type=jnp.float32
        )
    row = lax.broadcasted_iota(jnp.int32, (SLOTS, 1), 0)
    for i in range(per_device):
        live = row < length_ref[0, head * per_device + i]
        part = summed[i * SLOTS : (i + 1) * SLOTS]
        out_ref[i] = jnp.where(live, part, 0.0).astype(jnp.bfloat16)


def output(index, lengths, states, o_weight, pieces, per_device):
    model = o_weight.shape[1]
    return pl.pallas_call(
        output_kernel,
        in_specs=[SMEM] * 2 + [VMEM] * (2 + len(pieces)),
        out_specs=VMEM,
        out_shape=jax.ShapeDtypeStruct((per_device, SLOTS, model), jnp.bfloat16),
        compiler_params=pltpu.CompilerParams(vmem_limit_bytes=32 << 20),
        cost_estimate=pl.CostEstimate(
            flops=2 * per_device * SLOTS * o_weight.size, bytes_accessed=o_weight.size * 2, transcendentals=0
        ),
        name="output",
    )(index, lengths, states, o_weight, *pieces)


def shifted(n, by):
    return [(i, i + by) for i in range(n) if 0 <= i + by < n]


def swapped(n, by):
    return [(i, i ^ by) for i in range(n)]


def line_body(
    thinker_rows,
    row_session,
    speaker_of,
    prompt_slot,
    prompt_cache,
    proj_weight,
    attn_gain,
    q_weight,
    k_weight,
    v_weight,
    o_weight,
):
    planes, plane, rep_count = lax.axis_size("sess"), KVH, 2
    blocks = planes * rep_count
    session_all = speaker_of.shape[0]
    per_plane = session_all // planes
    per_device = per_plane // plane
    slot_cap = SLOTS // blocks
    held = prompt_cache.shape[0]
    model = proj_weight.shape[1]
    width = model // 2
    z, x, c = lax.axis_index("sess"), lax.axis_index("inner"), lax.axis_index("rep")
    head = x * rep_count + c
    index = jnp.stack([z, x, c, head]).astype(jnp.int32)
    pair = ("inner", "rep")

    kept, sent = project(index, thinker_rows, proj_weight)
    came = lax.ppermute(sent, "inner", swapped(2, 1))

    own, to_core, to_x, to_far = split_heads(head.reshape(1), prompt_cache)
    from_core = lax.ppermute(to_core, pair, swapped(4, 1))
    from_x = lax.ppermute(to_x, pair, swapped(4, 2))
    from_far = lax.ppermute(to_far, pair, swapped(4, 3))
    first = stack(own[None], from_core[None])
    second = stack(from_x[None], from_far[None])

    weight = head_weights(index, q_weight, k_weight, v_weight)
    came, weight = lax.optimization_barrier((came, weight))
    routed = route(index, kept, came, row_session, planes, per_plane, slot_cap)
    first, _ = lax.optimization_barrier((first, sent))
    arrived = [routed[0]] + [
        lax.ppermute(routed[by], "sess", swapped(planes, by)) for by in range(1, planes)
    ]
    second, arrived = lax.optimization_barrier((second, arrived))
    right, left = [first, second], [first, second]
    prompts = {0: (first, second)}

    def travel(hop):
        for chunk in range(2):
            right[chunk] = lax.ppermute(right[chunk], "sess", shifted(planes, 1))
            left[chunk] = lax.ppermute(left[chunk], "sess", shifted(planes, -1))
        prompts[-hop], prompts[hop] = tuple(right), tuple(left)

    travel(1)
    travel(2)

    def after(value, hop, chunk):
        return lax.optimization_barrier((value, prompts[-hop][chunk], prompts[hop][chunk]))[0]

    arrived = stack(*[a[None] for a in arrived])
    other = lax.ppermute(arrived, "inner", swapped(2, 1))
    other = after(other, 1, 1)
    slots = (
        arrived, other, lax.ppermute(arrived, "rep", swapped(2, 1)), lax.ppermute(other, "rep", swapped(2, 1))
    )
    slots = after(slots, 2, 0)
    states, query, key, value, lengths = place_rows(
        index, slots, attn_gain, weight, per_plane, slot_cap
    )

    travel(3)

    speakers = lax.dynamic_slice_in_dim(speaker_of, z * per_plane, per_plane)
    wanted_slot = jnp.sum(
        jnp.where(
            speakers[:, None] == jnp.arange(prompt_slot.shape[0])[None, :], prompt_slot[None, :], 0
        ),
        axis=1,
    )
    hop = wanted_slot // held - z
    which = wanted_slot % held
    near = attend_near(
        hop, which, lengths, query, key, value, prompts, (0, -1, 1, -2, 2)
    )
    run = functools.partial(attend_far, index, hop, which, lengths)
    attended = {}
    attended[2], attended[3] = run(query, key, value, near, prompts, (-3, 3), (2, 3))
    near, _ = lax.optimization_barrier((near, attended[2]))
    attended[0], attended[1] = run(query, key, value, near, prompts, (-3, 3), (0, 1))
    pieces = [attended[0]] + [
        lax.ppermute(attended[by], pair, swapped(4, by)) for by in range(1, plane)
    ]
    return output(index, lengths, states, o_weight, pieces, per_device)


def solution(mesh):
    in_specs = (
        P(("groups", "sess", "rep"), "inner"),
        P(("groups", "sess", "rep"), None),
        P("groups"),
        P("groups"),
        P(("groups", "sess"), ("inner", "rep"), None),
        P("inner", None),
        P(),
        P(),
        P(),
        P(),
        P(),
    )
    out_specs = P(("groups", "sess", "inner", "rep"), None, None)
    sizes = tuple(mesh.shape[name] for name in ("sess", "inner", "rep"))
    body = line_body if sizes == (4, 2, 2) else general_body
    return jax.shard_map(body, mesh=mesh, in_specs=in_specs, out_specs=out_specs, check_vma=False)
```

```python
import functools
import math

import jax
import jax.numpy as jnp
import numpy as np
from jax import lax
from jax.experimental import pallas as pl
from jax.experimental.pallas import tpu as pltpu
from jax.sharding import PartitionSpec as P

H = 12
KVH = 4
HD = 128
PROMPT = 1024
SLOTS = 96
PER_GROUP = H // KVH

EPSILON = 1e-06
ROPE_BASE = 1000000.0
NT = (((1,), (1,)), ((), ()))


def rope_tables(copies):
    half_width = HD // 2
    inverse = ROPE_BASE ** (-(np.arange(half_width, dtype=np.float64) * 2.0) / HD)
    angles = (PROMPT + np.arange(SLOTS, dtype=np.float64))[:, None] * inverse[None, :]
    cosine = np.concatenate([np.cos(angles), np.cos(angles)], axis=1)
    sine = np.concatenate([-np.sin(angles), np.sin(angles)], axis=1)
    return (
        np.tile(cosine, (copies, 1)).astype(np.float32),
        np.tile(sine, (copies, 1)).astype(np.float32),
    )


def states_kernel(code_ref, slots_ref, gain_ref, weight_ref, cos_ref, sin_ref,
                  states_ref, query_ref, key_ref, value_ref):
    halves, blocks, rows, width = slots_ref.shape
    total = states_ref.shape[0]
    place = lax.broadcasted_iota(jnp.int32, (total, blocks * rows), 0)
    pick = (place == code_ref[0]).astype(jnp.bfloat16)
    parts = [
        jnp.dot(
            pick,
            slots_ref[half].reshape(blocks * rows, width),
            preferred_element_type=jnp.float32,
        )
        for half in range(halves)
    ]
    widened = jnp.concatenate(parts, axis=1)
    states_ref[...] = widened.astype(jnp.bfloat16)
    factor = lax.rsqrt(jnp.mean(widened * widened, axis=-1, keepdims=True) + EPSILON)
    normed = (widened * factor * gain_ref[...].astype(jnp.float32)).astype(jnp.bfloat16)
    both = jnp.dot(normed, weight_ref[...], preferred_element_type=jnp.float32)
    cosine, sine = cos_ref[...], sin_ref[...]
    for head in range(PER_GROUP + 1):
        vector = both[:, head * HD : (head + 1) * HD]
        turned = vector * cosine + pltpu.roll(vector, HD // 2, 1) * sine
        if head < PER_GROUP:
            query_ref[:, head * HD : (head + 1) * HD] = turned.astype(jnp.bfloat16)
        else:
            key_ref[...] = turned.astype(jnp.bfloat16)
    value_ref[...] = both[:, (PER_GROUP + 1) * HD :].astype(jnp.bfloat16)


def attention_kernel(place_ref, length_ref, query_ref, key_ref, value_ref, prompt_ref, out_ref):
    session = pl.program_id(0)
    length = length_ref[session]
    scale = HD ** (-0.5) * math.log2(math.e)
    query = jnp.concatenate(
        [query_ref[:, h * HD : (h + 1) * HD] for h in range(PER_GROUP)], axis=0
    )
    ahead = lax.dot_general(query, prompt_ref[0, :, :HD], NT, preferred_element_type=jnp.float32)
    own = lax.dot_general(query, key_ref[...], NT, preferred_element_type=jnp.float32)
    row = lax.broadcasted_iota(jnp.int32, (SLOTS, SLOTS), 0)
    column = lax.broadcasted_iota(jnp.int32, (SLOTS, SLOTS), 1)
    allowed = (column <= row) & (column < length)
    own = jnp.where(jnp.concatenate([allowed] * PER_GROUP, axis=0), own, -1e30)
    highest = jnp.maximum(
        jnp.max(ahead, axis=-1, keepdims=True), jnp.max(own, axis=-1, keepdims=True)
    )
    powers = jnp.exp2((ahead - highest) * scale)
    own_powers = jnp.exp2((own - highest) * scale)
    total = jnp.sum(powers, axis=-1, keepdims=True) + jnp.sum(own_powers, axis=-1, keepdims=True)
    mixed = jnp.dot(
        powers.astype(jnp.bfloat16), prompt_ref[0, :, HD:], preferred_element_type=jnp.float32
    ) + jnp.dot(own_powers.astype(jnp.bfloat16), value_ref[...], preferred_element_type=jnp.float32)
    mixed = (mixed / total).astype(jnp.bfloat16)
    for h in range(PER_GROUP):
        out_ref[:, h * HD : (h + 1) * HD] = mixed[h * SLOTS : (h + 1) * SLOTS]


def make_states(code, slots, gain, weight, sessions, together):
    halves, blocks, rows, width = slots.shape
    steps = sessions // together
    model = halves * width
    cosine, sine = rope_tables(together)
    total = together * SLOTS
    out = jax.ShapeDtypeStruct
    row_spec = lambda w: pl.BlockSpec((total, w), lambda i: (i, 0))
    whole = lambda a: pl.BlockSpec(a.shape, lambda i: (0,) * a.ndim)
    gain = gain.reshape(1, model)
    return pl.pallas_call(
        states_kernel,
        grid=(steps,),
        in_specs=[
            pl.BlockSpec((1, 1, code.shape[2]), lambda i: (i, 0, 0)),
            pl.BlockSpec((halves, blocks, rows // steps, width), lambda i: (0, 0, i, 0)),
            whole(gain),
            whole(weight),
            whole(cosine),
            whole(sine),
        ],
        out_specs=[row_spec(model), row_spec(PER_GROUP * HD), row_spec(HD), row_spec(HD)],
        out_shape=[
            out((sessions * SLOTS, model), jnp.bfloat16),
            out((sessions * SLOTS, PER_GROUP * HD), jnp.bfloat16),
            out((sessions * SLOTS, HD), jnp.bfloat16),
            out((sessions * SLOTS, HD), jnp.bfloat16),
        ],
        compiler_params=pltpu.CompilerParams(vmem_limit_bytes=32 << 20),
        name="states",
    )(code, slots, gain, weight, jnp.asarray(cosine), jnp.asarray(sine))


def attend(place, lengths, query, key, value, prompts):
    sessions = place.shape[0]
    row_spec = lambda w: pl.BlockSpec((SLOTS, w), lambda i, place, length: (i, 0))
    return pl.pallas_call(
        attention_kernel,
        grid_spec=pltpu.PrefetchScalarGridSpec(
            num_scalar_prefetch=2,
            grid=(sessions,),
            in_specs=[
                row_spec(PER_GROUP * HD),
                row_spec(HD),
                row_spec(HD),
                pl.BlockSpec((1, PROMPT, 2 * HD), lambda i, place, length: (place[i], 0, 0)),
            ],
            out_specs=row_spec(PER_GROUP * HD),
        ),
        out_shape=jax.ShapeDtypeStruct((sessions * SLOTS, PER_GROUP * HD), jnp.bfloat16),
        compiler_params=pltpu.CompilerParams(vmem_limit_bytes=32 << 20),
        name="attend",
    )(place, lengths, query, key, value, prompts)


def general_body(
    thinker_rows,
    row_session,
    speaker_of,
    prompt_slot,
    prompt_cache,
    proj_weight,
    attn_gain,
    q_weight,
    k_weight,
    v_weight,
    o_weight,
):
    sess_count = lax.axis_size("sess")
    inner_count = lax.axis_size("inner")
    rep_count = lax.axis_size("rep")
    plane = inner_count * rep_count
    blocks = sess_count * rep_count
    session_all = speaker_of.shape[0]
    per_plane = session_all // sess_count
    per_device = per_plane // plane
    slot_cap = SLOTS // blocks
    held, tokens, channels = prompt_cache.shape
    model = proj_weight.shape[1]
    sharers = plane // KVH
    held_part = held // sharers
    sess_place = lax.axis_index("sess")
    plane_place = lax.axis_index("inner") * rep_count + lax.axis_index("rep")
    head = plane_place // sharers
    sharer = plane_place % sharers

    outgoing = jnp.transpose(
        prompt_cache.reshape(sharers, held_part, tokens, 2, KVH, HD), (4, 0, 1, 2, 3, 5)
    ).reshape(plane, held_part, tokens, 2 * HD)
    own_head = lax.all_to_all(outgoing, ("inner", "rep"), split_axis=0, concat_axis=2, tiled=True)
    own_head = own_head.reshape(held_part, plane * tokens, 2 * HD)
    prompts = lax.all_gather(own_head, "sess", axis=0, tiled=True)

    row_owner = row_session[:, 0]
    order = jnp.arange(row_owner.shape[0])
    same = row_owner[:, None] == row_owner[None, :]
    earlier = jnp.sum((same & (order[None, :] < order[:, None])).astype(jnp.int32), axis=1)
    row_slot = row_owner * slot_cap + earlier
    counts = jnp.sum(
        (row_owner[:, None] == jnp.arange(session_all)[None, :]).astype(jnp.int32), axis=0
    )
    all_counts = lax.all_gather(counts, ("sess", "rep"), axis=0, tiled=False)

    partial_sum = jnp.dot(thinker_rows, proj_weight, preferred_element_type=jnp.float32)
    width = model // inner_count
    if inner_count == 2:
        inner_place = lax.axis_index("inner")
        kept = lax.dynamic_slice_in_dim(partial_sum, inner_place * width, width, 1)
        sent = lax.dynamic_slice_in_dim(partial_sum, (1 - inner_place) * width, width, 1)
        came = lax.ppermute(sent.astype(jnp.bfloat16), "inner", [(0, 1), (1, 0)])
        own_columns = (kept + came.astype(jnp.float32)).astype(jnp.bfloat16)
    else:
        own_columns = lax.psum_scatter(
            partial_sum, "inner", scatter_dimension=1, tiled=True
        ).astype(jnp.bfloat16)
    into = (jnp.arange(session_all * slot_cap)[:, None] == row_slot[None, :]).astype(jnp.bfloat16)
    buffer = jnp.dot(into, own_columns, preferred_element_type=jnp.float32).astype(jnp.bfloat16)
    arrived = lax.all_to_all(
        buffer.reshape(sess_count, per_plane * slot_cap, width),
        "sess",
        split_axis=0,
        concat_axis=0,
        tiled=True,
    )
    spread = lax.all_gather(arrived, ("inner", "rep"), axis=0, tiled=False)
    slots = spread.reshape(inner_count, rep_count * sess_count, per_plane * slot_cap, width)

    offsets = jnp.cumsum(all_counts, axis=0) - all_counts
    lengths_all = jnp.sum(all_counts, axis=0)
    mine = lambda a: lax.dynamic_slice_in_dim(a, sess_place * per_plane, per_plane, a.ndim - 1)
    by_block = lambda a: jnp.transpose(
        mine(a).reshape(sess_count, rep_count, per_plane), (1, 0, 2)
    ).reshape(blocks, per_plane)
    lengths = mine(lengths_all)
    together = 16 // math.gcd(16, slot_cap)
    within = jnp.arange(slot_cap)
    local = (jnp.arange(per_plane) % together)[None, :, None] * SLOTS
    code = jnp.where(
        within[None, None, :] < by_block(all_counts)[:, :, None],
        by_block(offsets)[:, :, None] + within[None, None, :] + local,
        -1,
    )
    steps = per_plane // together
    code = jnp.transpose(
        code.reshape(blocks, steps, together * slot_cap), (1, 0, 2)
    ).reshape(steps, 1, blocks * together * slot_cap)

    group_width = PER_GROUP * HD
    weight = jnp.concatenate(
        [
            lax.dynamic_slice_in_dim(q_weight, head * group_width, group_width, 1),
            lax.dynamic_slice_in_dim(k_weight, head * HD, HD, 1),
            lax.dynamic_slice_in_dim(v_weight, head * HD, HD, 1),
        ],
        axis=1,
    )
    states, query, key, value = make_states(
        code, slots, attn_gain, weight, per_plane, together
    )

    wanted_slot = jnp.sum(
        jnp.where(
            mine(speaker_of)[:, None] == jnp.arange(prompt_slot.shape[0])[None, :],
            prompt_slot[None, :],
            0,
        ),
        axis=1,
    )
    place = wanted_slot // held * held_part + wanted_slot % held_part
    attended = attend(place, lengths, query, key, value, prompts)
    returned = lax.all_to_all(
        attended.reshape(plane, per_device * SLOTS, group_width),
        ("inner", "rep"),
        split_axis=0,
        concat_axis=0,
        tiled=True,
    ).reshape(KVH, sharers, per_device, SLOTS, group_width)
    first = plane_place * per_device
    if sharers > 1:
        holder = lax.dynamic_slice_in_dim(wanted_slot % held // held_part, first, per_device)
        chosen = jnp.zeros_like(returned[:, 0])
        for t in range(sharers):
            chosen = jnp.where((holder == t)[None, :, None, None], returned[:, t], chosen)
    else:
        chosen = returned[:, 0]
    gathered = jnp.transpose(chosen, (1, 2, 0, 3)).reshape(per_device * SLOTS, H * HD)
    own_states = lax.dynamic_slice_in_dim(states, first * SLOTS, per_device * SLOTS, 0)
    own_lengths = lax.dynamic_slice_in_dim(lengths, first, per_device)
    summed = own_states.astype(jnp.float32) + jnp.dot(
        gathered, o_weight, preferred_element_type=jnp.float32
    )
    live_rows = (jnp.arange(SLOTS)[None, :] < own_lengths[:, None]).reshape(-1, 1)
    return (
        jnp.where(live_rows, summed, 0.0)
        .astype(jnp.bfloat16)
        .reshape(per_device, SLOTS, model)
    )


EXTRA = 16
SMEM = pl.BlockSpec(memory_space=pltpu.SMEM)
VMEM = pl.BlockSpec(memory_space=pltpu.VMEM)
HBM = pl.BlockSpec(memory_space=pltpu.HBM)


def split_heads_kernel(head_ref, cache_ref, *out_refs):
    for by, out_ref in enumerate(out_refs):
        for side in range(2):
            start = pl.multiple_of((head_ref[0] ^ by) * HD + side * KVH * HD, HD)
            out_ref[:, :, side * HD : (side + 1) * HD] = cache_ref[:, :, pl.ds(start, HD)]


def split_heads(head, cache):
    held, tokens, _ = cache.shape
    shape = jax.ShapeDtypeStruct((held, tokens, 2 * HD), cache.dtype)
    return pl.pallas_call(
        split_heads_kernel,
        in_specs=[SMEM, VMEM],
        out_specs=[VMEM] * KVH,
        out_shape=[shape] * KVH,
        cost_estimate=pl.CostEstimate(flops=0, bytes_accessed=2 * cache.size * 2, transcendentals=0),
        name="split_heads",
    )(head, cache)


def stack_kernel(*refs):
    in_refs, out_ref = refs[:-1], refs[-1]
    place = 0
    for in_ref in in_refs:
        count = in_ref.shape[0]
        out_ref[place : place + count] = in_ref[...]
        place += count


def stack(*arrays):
    total = sum(a.shape[0] for a in arrays)
    size = sum(a.size for a in arrays)
    return pl.pallas_call(
        stack_kernel,
        in_specs=[VMEM] * len(arrays),
        out_specs=VMEM,
        out_shape=jax.ShapeDtypeStruct((total,) + arrays[0].shape[1:], arrays[0].dtype),
        cost_estimate=pl.CostEstimate(flops=0, bytes_accessed=4 * size, transcendentals=0),
        name="stack",
    )(*arrays)


def project_kernel(index_ref, rows_ref, weight_ref, kept_ref, sent_ref):
    width = kept_ref.shape[1]
    partial_sum = jnp.dot(rows_ref[...], weight_ref[...], preferred_element_type=jnp.float32)
    low, high = partial_sum[:, :width], partial_sum[:, width:]
    is_low = index_ref[1] == 0
    kept_ref[...] = jnp.where(is_low, low, high)
    sent_ref[...] = jnp.where(is_low, high, low).astype(jnp.bfloat16)


def project(index, rows, weight):
    count, width = rows.shape[0], weight.shape[1] // 2
    return pl.pallas_call(
        project_kernel,
        in_specs=[SMEM, VMEM, VMEM],
        out_specs=[VMEM] * 2,
        out_shape=[
            jax.ShapeDtypeStruct((count, width), jnp.float32),
            jax.ShapeDtypeStruct((count, width), jnp.bfloat16),
        ],
        compiler_params=pltpu.CompilerParams(vmem_limit_bytes=32 << 20),
        cost_estimate=pl.CostEstimate(
            flops=2 * count * weight.size, bytes_accessed=2 * (rows.size + weight.size), transcendentals=0
        ),
        name="project",
    )(index, rows, weight)


def route_kernel(index_ref, kept_ref, came_ref, owner_ref, *out_refs,
                 slot_cap, per_plane):
    rows = kept_ref.shape[0]
    planes = len(out_refs)
    size = out_refs[0].shape[0]
    live = per_plane * slot_cap
    columns = (kept_ref[...] + came_ref[...].astype(jnp.float32)).astype(jnp.bfloat16)
    owner_row = owner_ref[...]
    above = lax.broadcasted_iota(jnp.int32, (rows, rows), 0)
    beside = lax.broadcasted_iota(jnp.int32, (rows, rows), 1)
    owner = jnp.sum(jnp.where(above == beside, owner_row, 0), axis=1, keepdims=True)
    earlier = jnp.sum(
        jnp.where((owner == owner_row) & (above < beside), 1.0, 0.0), axis=0, keepdims=True
    ).astype(jnp.int32)
    target = lax.div(owner_row, per_plane) ^ index_ref[0]
    code = target * size + lax.rem(owner_row, per_plane) * slot_cap + earlier
    place = lax.broadcasted_iota(jnp.int32, (planes * size, rows), 0)
    into = (place == code).astype(jnp.bfloat16)
    routed = jnp.dot(into, columns, preferred_element_type=jnp.float32).astype(jnp.bfloat16)
    lane = lax.broadcasted_iota(jnp.int32, (rows, HD), 1)
    named = (lane == owner).astype(jnp.bfloat16)
    counts = jnp.dot(
        jnp.ones((EXTRA, rows), jnp.bfloat16), named, preferred_element_type=jnp.float32
    ).astype(jnp.bfloat16)
    for k, out_ref in enumerate(out_refs):
        out_ref[:live] = routed[k * size : k * size + live]
        out_ref[live:] = jnp.zeros((EXTRA, out_ref.shape[1]), jnp.bfloat16)
        out_ref[live:, :HD] = counts


def route(index, kept, came, row_session, planes, per_plane, slot_cap):
    width = kept.shape[1]
    rows = row_session.shape[0]
    size = per_plane * slot_cap + EXTRA
    return pl.pallas_call(
        functools.partial(route_kernel, slot_cap=slot_cap, per_plane=per_plane),
        in_specs=[SMEM] + [VMEM] * 3,
        out_specs=[VMEM] * planes,
        out_shape=[jax.ShapeDtypeStruct((size, width), jnp.bfloat16)] * planes,
        cost_estimate=pl.CostEstimate(
            flops=2 * planes * size * rows * width, bytes_accessed=rows * width * 8, transcendentals=0
        ),
        name="route",
    )(index, kept, came, row_session.reshape(1, rows))


def head_weights_kernel(index_ref, q_ref, k_ref, v_ref, out_ref, sem):
    copies = []
    for i, (ref, heads, place) in enumerate(
        ((q_ref, PER_GROUP, 0), (k_ref, 1, PER_GROUP), (v_ref, 1, PER_GROUP + 1))
    ):
        start = pl.multiple_of(index_ref[3] * heads * HD, HD)
        copies.append(
            pltpu.make_async_copy(
                ref.at[:, pl.ds(start, heads * HD)],
                out_ref.at[:, place * HD : (place + heads) * HD],
                sem.at[i],
            )
        )
    for copy in copies:
        copy.start()
    for copy in copies:
        copy.wait()


def head_weights(index, q_weight, k_weight, v_weight):
    model, width = q_weight.shape[0], (PER_GROUP + 2) * HD
    return pl.pallas_call(
        head_weights_kernel,
        in_specs=[SMEM] + [HBM] * 3,
        out_specs=VMEM,
        out_shape=jax.ShapeDtypeStruct((model, width), q_weight.dtype),
        scratch_shapes=[pltpu.SemaphoreType.DMA((3,))],
        cost_estimate=pl.CostEstimate(
            flops=0, bytes_accessed=4 * model * width, transcendentals=0
        ),
        name="head_weights",
    )(index, q_weight, k_weight, v_weight)


def place_kernel(index_ref, near_ref, far_ref, near_core_ref, far_core_ref, gain_ref,
                 weight_ref, cos_ref, sin_ref, states_ref, query_ref, key_ref, value_ref, length_ref, *,
                 slot_cap, together):
    z, x, c, head = [index_ref[i] for i in range(4)]
    planes, live, width = near_ref.shape
    blocks = 2 * planes
    live = live - EXTRA
    per_plane = live // slot_cap
    steps = per_plane // together
    window = together * slot_cap
    total = together * SLOTS
    counts = jnp.concatenate(
        [ref[k, live : live + 1, :HD] for ref in (near_ref, near_core_ref) for k in range(planes)],
        axis=0,
    ).astype(jnp.float32)
    kind = lambda axis: lax.broadcasted_iota(jnp.int32, (blocks, blocks), axis)
    true_block = lambda k: (z ^ (k % planes)) * 2 + (c ^ (k // planes))
    before = (true_block(kind(1)) < true_block(kind(0))).astype(jnp.float32)
    offsets = jnp.dot(before, counts, preferred_element_type=jnp.float32)
    session_lane = lax.broadcasted_iota(jnp.int32, (HD, HD), 0)
    local_lane = lax.broadcasted_iota(jnp.int32, (HD, HD), 1)
    ours = (session_lane == z * per_plane + local_lane).astype(jnp.float32)
    sums = jnp.dot(
        jnp.broadcast_to(jnp.sum(counts, axis=0, keepdims=True), (8, HD)),
        ours,
        preferred_element_type=jnp.float32,
    )
    length_ref[...] = sums[:1].astype(jnp.int32)
    cosine = jnp.concatenate([cos_ref[...]] * together, axis=0)
    sine = jnp.concatenate([sin_ref[...]] * together, axis=0)
    gain = gain_ref[...].astype(jnp.float32)
    for step in range(steps):
        slot = lax.broadcasted_iota(jnp.int32, (blocks, blocks * window), 1)
        in_block = slot % window
        spread = lax.broadcasted_iota(jnp.int32, (HD, blocks * window), 1) % window // slot_cap
        from_lane = lax.broadcasted_iota(jnp.int32, (HD, blocks * window), 0)
        expand = (from_lane == z * per_plane + step * together + spread).astype(jnp.float32)
        here = jnp.dot(counts, expand, preferred_element_type=jnp.float32).astype(jnp.int32)
        start = jnp.dot(offsets, expand, preferred_element_type=jnp.float32).astype(jnp.int32)
        within = in_block % slot_cap
        row = jnp.where(within < here, start + within + in_block // slot_cap * SLOTS, -1)
        block = lax.broadcasted_iota(jnp.int32, (blocks, blocks * window), 0)
        code = jnp.max(jnp.where(slot // window == block, row, -1), axis=0, keepdims=True)
        place = lax.broadcasted_iota(jnp.int32, (total, blocks * window), 0)
        pick = (place == code).astype(jnp.bfloat16)
        slots = slice(step * window, (step + 1) * window)
        near, far = [
            jnp.dot(
                pick,
                jnp.concatenate(
                    [ref[k, slots] for ref in refs for k in range(planes)], axis=0
                ),
                preferred_element_type=jnp.float32,
            )
            for refs in ((near_ref, near_core_ref), (far_ref, far_core_ref))
        ]
        widened = jnp.concatenate(
            [jnp.where(x == 0, near, far), jnp.where(x == 0, far, near)], axis=1
        )
        rows = slice(step * total, (step + 1) * total)
        states_ref[rows] = widened.astype(jnp.bfloat16)
        factor = lax.rsqrt(jnp.mean(widened * widened, axis=-1, keepdims=True) + EPSILON)
        normed = (widened * factor * gain).astype(jnp.bfloat16)
        both = jnp.dot(normed, weight_ref[...], preferred_element_type=jnp.float32)
        for h in range(PER_GROUP + 1):
            vector = both[:, h * HD : (h + 1) * HD]
            turned = vector * cosine + pltpu.roll(vector, HD // 2, 1) * sine
            if h < PER_GROUP:
                query_ref[rows, h * HD : (h + 1) * HD] = turned.astype(jnp.bfloat16)
            else:
                key_ref[rows] = turned.astype(jnp.bfloat16)
        value_ref[rows] = both[:, (PER_GROUP + 1) * HD :].astype(jnp.bfloat16)


def place_rows(index, slots, gain, weight, sessions, slot_cap):
    together = 16 // math.gcd(16, slot_cap)
    cosine, sine = rope_tables(1)
    model = 2 * slots[0].shape[2]
    total = sessions * SLOTS
    out = lambda w: jax.ShapeDtypeStruct((total, w), jnp.bfloat16)
    return pl.pallas_call(
        functools.partial(place_kernel, slot_cap=slot_cap, together=together),
        in_specs=[SMEM] + [VMEM] * 8,
        out_specs=[VMEM] * 5,
        out_shape=[
            out(model), out(PER_GROUP * HD), out(HD), out(HD),
            jax.ShapeDtypeStruct((1, HD), jnp.int32),
        ],
        compiler_params=pltpu.CompilerParams(vmem_limit_bytes=32 << 20),
        cost_estimate=pl.CostEstimate(
            flops=4 * total * model * 5 * HD, bytes_accessed=6 << 20, transcendentals=0
        ),
        name="place_rows",
    )(index, *slots, gain.reshape(1, model), weight, jnp.asarray(cosine), jnp.asarray(sine))


def session_attention(query, key, value, tokens, length):
    scale = HD ** (-0.5) * math.log2(math.e)
    query = jnp.concatenate([query[:, h * HD : (h + 1) * HD] for h in range(PER_GROUP)], axis=0)
    ahead = lax.dot_general(query, tokens[:, :HD], NT, preferred_element_type=jnp.float32)
    own = lax.dot_general(query, key, NT, preferred_element_type=jnp.float32)
    row = lax.broadcasted_iota(jnp.int32, (SLOTS, SLOTS), 0)
    column = lax.broadcasted_iota(jnp.int32, (SLOTS, SLOTS), 1)
    allowed = (column <= row) & (column < length)
    own = jnp.where(jnp.concatenate([allowed] * PER_GROUP, axis=0), own, -1e30)
    highest = jnp.maximum(
        jnp.max(ahead, axis=-1, keepdims=True), jnp.max(own, axis=-1, keepdims=True)
    )
    powers = jnp.exp2((ahead - highest) * scale)
    own_powers = jnp.exp2((own - highest) * scale)
    total = jnp.sum(powers, axis=-1, keepdims=True) + jnp.sum(own_powers, axis=-1, keepdims=True)
    mixed = jnp.dot(
        powers.astype(jnp.bfloat16), tokens[:, HD:], preferred_element_type=jnp.float32
    ) + jnp.dot(own_powers.astype(jnp.bfloat16), value, preferred_element_type=jnp.float32)
    return (mixed / total).astype(jnp.bfloat16)


def fetches(hop, refs, held, kv, sem, hops, start):
    for which, source in enumerate(hops):
        copies = [
            pltpu.make_async_copy(refs[2 * which + chunk].at[:, held], kv.at[chunk], sem.at[chunk])
            for chunk in range(2)
        ]
        if start:
            @pl.when(hop == source)
            def _():
                for copy in copies:
                    copy.start()
        elif which == 0:
            for copy in copies:
                copy.wait()


def among(hop, hops):
    ours = hop == hops[0]
    for other in hops[1:]:
        ours = ours | (hop == other)
    return ours


def near_kernel(hop_ref, held_ref, length_ref, query_ref, key_ref, value_ref, *refs, hops):
    prompt_refs, (out_ref, kv, sem) = refs[: 2 * len(hops)], refs[2 * len(hops) :]
    sessions = hop_ref.shape[0]
    for i in range(sessions):
        fetches(hop_ref[i], prompt_refs, held_ref[i], kv.at[i], sem.at[i], hops, True)

    def work(i, _):
        @pl.when(among(hop_ref[i], hops))
        def _():
            fetches(hop_ref[i], prompt_refs, held_ref[i], kv.at[i], sem.at[i], hops, False)
            rows = pl.ds(pl.multiple_of(i * SLOTS, SLOTS), SLOTS)
            mixed = session_attention(
                query_ref[rows], key_ref[rows], value_ref[rows],
                kv[i].reshape(PROMPT, 2 * HD), length_ref[0, i],
            )
            for h in range(PER_GROUP):
                out_ref[rows, h * HD : (h + 1) * HD] = mixed[h * SLOTS : (h + 1) * SLOTS]

        return 0

    lax.fori_loop(0, sessions, work, 0)


def far_kernel(index_ref, hop_ref, held_ref, length_ref, query_ref, key_ref, value_ref, near_ref,
               *refs, targets, hops):
    prompt_refs, refs = refs[: 2 * len(hops)], refs[2 * len(hops) :]
    out_refs, (kv, sem) = refs[: len(targets)], refs[len(targets) :]
    head = index_ref[3]
    per_device = out_refs[0].shape[0] // SLOTS
    places = [(t, j) for t in range(len(targets)) for j in range(per_device)]
    sessions = [(head ^ targets[t]) * per_device + j for t, j in places]
    for i, session in enumerate(sessions):
        fetches(
            hop_ref[session], prompt_refs, held_ref[session], kv.at[i], sem.at[i], hops, True
        )
    for i, (session, (t, j)) in enumerate(zip(sessions, places)):
        rows = pl.ds(pl.multiple_of(session * SLOTS, SLOTS), SLOTS)
        target = slice(j * SLOTS, (j + 1) * SLOTS)
        ours = among(hop_ref[session], hops)

        @pl.when(jnp.logical_not(ours))
        def _():
            out_refs[t][target] = near_ref[rows]

        @pl.when(ours)
        def _():
            fetches(
                hop_ref[session], prompt_refs, held_ref[session], kv.at[i], sem.at[i], hops, False
            )
            mixed = session_attention(
                query_ref[rows], key_ref[rows], value_ref[rows],
                kv[i].reshape(PROMPT, 2 * HD), length_ref[0, session],
            )
            for h in range(PER_GROUP):
                out_refs[t][target, h * HD : (h + 1) * HD] = mixed[h * SLOTS : (h + 1) * SLOTS]


def attention_call(kernel, out_specs, out_shape, places, name, scalars, arrays, prompts, hops):
    pieces = [piece for h in hops for piece in prompts[h]]
    work = places * PER_GROUP * SLOTS * (PROMPT + SLOTS) // 2
    return pl.pallas_call(
        kernel,
        in_specs=[SMEM] * len(scalars) + [VMEM] * len(arrays) + [HBM] * len(pieces),
        out_specs=out_specs,
        out_shape=out_shape,
        scratch_shapes=[
            pltpu.VMEM((places, 2, 2, PROMPT // 4, 2 * HD), jnp.bfloat16),
            pltpu.SemaphoreType.DMA((places, 2)),
        ],
        compiler_params=pltpu.CompilerParams(vmem_limit_bytes=32 << 20),
        cost_estimate=pl.CostEstimate(
            flops=4 * work * HD, bytes_accessed=places * PROMPT * 2 * HD, transcendentals=work
        ),
        name=name,
    )(*scalars, *arrays, *pieces)


def attend_near(hop, held, lengths, query, key, value, prompts, hops):
    out_shape = jax.ShapeDtypeStruct(query.shape, jnp.bfloat16)
    return attention_call(
        functools.partial(near_kernel, hops=hops),
        VMEM, out_shape, hop.shape[0], "near", (hop, held, lengths), (query, key, value),
        prompts, hops,
    )


def attend_far(index, hop, held, lengths, query, key, value, near, prompts, hops, targets):
    per_device = hop.shape[0] // KVH
    out_shape = jax.ShapeDtypeStruct((per_device * SLOTS, query.shape[1]), jnp.bfloat16)
    return attention_call(
        functools.partial(far_kernel, hops=hops, targets=targets),
        [VMEM] * len(targets), [out_shape] * len(targets), per_device * len(targets), "far",
        (index, hop, held, lengths), (query, key, value, near), prompts, hops,
    )


def output_kernel(index_ref, length_ref, states_ref, weight_ref, *refs):
    piece_refs, out_ref = refs[:-1], refs[-1]
    head = index_ref[3]
    group_width = PER_GROUP * HD
    per_device = out_ref.shape[0]
    total = per_device * SLOTS
    summed = states_ref[pl.ds(pl.multiple_of(head * total, SLOTS), total)].astype(jnp.float32)
    for by, piece_ref in enumerate(piece_refs):
        start = pl.multiple_of((head ^ by) * group_width, group_width)
        summed = summed + jnp.dot(
            piece_ref[...], weight_ref[pl.ds(start, group_width)], preferred_element_type=jnp.float32
        )
    row = lax.broadcasted_iota(jnp.int32, (SLOTS, 1), 0)
    for i in range(per_device):
        live = row < length_ref[0, head * per_device + i]
        part = summed[i * SLOTS : (i + 1) * SLOTS]
        out_ref[i] = jnp.where(live, part, 0.0).astype(jnp.bfloat16)


def output(index, lengths, states, o_weight, pieces, per_device):
    model = o_weight.shape[1]
    return pl.pallas_call(
        output_kernel,
        in_specs=[SMEM] * 2 + [VMEM] * (2 + len(pieces)),
        out_specs=VMEM,
        out_shape=jax.ShapeDtypeStruct((per_device, SLOTS, model), jnp.bfloat16),
        compiler_params=pltpu.CompilerParams(vmem_limit_bytes=32 << 20),
        cost_estimate=pl.CostEstimate(
            flops=2 * per_device * SLOTS * o_weight.size, bytes_accessed=o_weight.size * 2, transcendentals=0
        ),
        name="output",
    )(index, lengths, states, o_weight, *pieces)


def shifted(n, by):
    return [(i, i + by) for i in range(n) if 0 <= i + by < n]


def swapped(n, by):
    return [(i, i ^ by) for i in range(n)]


def line_body(
    thinker_rows,
    row_session,
    speaker_of,
    prompt_slot,
    prompt_cache,
    proj_weight,
    attn_gain,
    q_weight,
    k_weight,
    v_weight,
    o_weight,
):
    planes, plane, rep_count = lax.axis_size("sess"), KVH, 2
    blocks = planes * rep_count
    session_all = speaker_of.shape[0]
    per_plane = session_all // planes
    per_device = per_plane // plane
    slot_cap = SLOTS // blocks
    held = prompt_cache.shape[0]
    model = proj_weight.shape[1]
    width = model // 2
    z, x, c = lax.axis_index("sess"), lax.axis_index("inner"), lax.axis_index("rep")
    head = x * rep_count + c
    index = jnp.stack([z, x, c, head]).astype(jnp.int32)
    pair = ("inner", "rep")

    kept, sent = project(index, thinker_rows, proj_weight)
    came = lax.ppermute(sent, "inner", swapped(2, 1))

    own, to_core, to_x, to_far = split_heads(head.reshape(1), prompt_cache)
    from_core = lax.ppermute(to_core, pair, swapped(4, 1))
    from_x = lax.ppermute(to_x, pair, swapped(4, 2))
    from_far = lax.ppermute(to_far, pair, swapped(4, 3))
    first = stack(own[None], from_core[None])
    second = stack(from_x[None], from_far[None])

    weight = head_weights(index, q_weight, k_weight, v_weight)
    came, weight = lax.optimization_barrier((came, weight))
    routed = route(index, kept, came, row_session, planes, per_plane, slot_cap)
    first, _ = lax.optimization_barrier((first, sent))
    arrived = [routed[0]] + [
        lax.ppermute(routed[by], "sess", swapped(planes, by)) for by in range(1, planes)
    ]
    second, arrived = lax.optimization_barrier((second, arrived))
    right, left = [first, second], [first, second]
    prompts = {0: (first, second)}

    def travel(hop):
        for chunk in range(2):
            right[chunk] = lax.ppermute(right[chunk], "sess", shifted(planes, 1))
            left[chunk] = lax.ppermute(left[chunk], "sess", shifted(planes, -1))
        prompts[-hop], prompts[hop] = tuple(right), tuple(left)

    travel(1)
    travel(2)

    def after(value, hop, chunk):
        return lax.optimization_barrier((value, prompts[-hop][chunk], prompts[hop][chunk]))[0]

    arrived = stack(*[a[None] for a in arrived])
    other = lax.ppermute(arrived, "inner", swapped(2, 1))
    other = after(other, 1, 1)
    slots = (
        arrived, other, lax.ppermute(arrived, "rep", swapped(2, 1)), lax.ppermute(other, "rep", swapped(2, 1))
    )
    slots = after(slots, 2, 0)
    states, query, key, value, lengths = place_rows(
        index, slots, attn_gain, weight, per_plane, slot_cap
    )

    travel(3)

    speakers = lax.dynamic_slice_in_dim(speaker_of, z * per_plane, per_plane)
    wanted_slot = jnp.sum(
        jnp.where(
            speakers[:, None] == jnp.arange(prompt_slot.shape[0])[None, :], prompt_slot[None, :], 0
        ),
        axis=1,
    )
    hop = wanted_slot // held - z
    which = wanted_slot % held
    near = attend_near(
        hop, which, lengths, query, key, value, prompts, (0, -1, 1, -2, 2)
    )
    run = functools.partial(attend_far, index, hop, which, lengths)
    attended = run(query, key, value, near, prompts, (-3, 3), tuple(range(plane)))
    pieces = [attended[0]] + [
        lax.ppermute(attended[by], pair, swapped(4, by)) for by in range(1, plane)
    ]
    return output(index, lengths, states, o_weight, pieces, per_device)


def solution(mesh):
    in_specs = (
        P(("groups", "sess", "rep"), "inner"),
        P(("groups", "sess", "rep"), None),
        P("groups"),
        P("groups"),
        P(("groups", "sess"), ("inner", "rep"), None),
        P("inner", None),
        P(),
        P(),
        P(),
        P(),
        P(),
    )
    out_specs = P(("groups", "sess", "inner", "rep"), None, None)
    sizes = tuple(mesh.shape[name] for name in ("sess", "inner", "rep"))
    body = line_body if sizes == (4, 2, 2) else general_body
    return jax.shard_map(body, mesh=mesh, in_specs=in_specs, out_specs=out_specs, check_vma=False)
```
